32 devices in a mesh: batch: 8 (over z, y), ffn: 4 (over x, core).
Axes of the slice: x: 2, y: 2, z: 4, core: 2. Of those that a mesh axis runs over, the one named last changes fastest.
Arguments:
- tokens: bfloat16 [50112, 768], P(('batch', 'ffn')), may hold values from -6 to 6
- text_lengths: int32 [192], P(('batch', 'ffn')), may hold values from 8 to 64
- routes: int32 [50112, 1], P(('batch', 'ffn')), may hold values from 0 to 7; in each aligned block of 1566 rows (0 to 1565, 1566 to 3131, ...) at most 261 rows name the same one
- group_map: int32 [8], replicated, may hold values from 0 to 2, as said below
- gain_one: float32 [768], replicated, may hold values from 0.1 to 1.9
- w_qkv: bfloat16 [768, 2304], replicated, may hold values from -0.3125 to 0.3125
- w_proj: bfloat16 [768, 768], replicated, may hold values from -0.875 to 0.875
- gain_two: float32 [768], replicated, may hold values from 0.1 to 1.9
- w_in: bfloat16 [8, 768, 3072], P('batch', None, 'ffn'), as said below
- w_back: bfloat16 [8, 3072, 768], P('batch', 'ffn'), as said below
- cotangent: bfloat16 [50112, 768], P(('batch', 'ffn')), may hold values from -6 to 6
Outputs:
- block_out: float32 [50112, 768], P(('batch', 'ffn'))
- input_grad: float32 [50112, 768], P(('batch', 'ffn'))
- grad_gain_one: float32 [768], replicated
- grad_w_qkv: float32 [768, 2304], replicated
- grad_w_proj: float32 [768, 768], replicated
- grad_gain_two: float32 [768], replicated
- grad_w_in: float32 [8, 768, 3072], P('batch', None, 'ffn')
- grad_w_back: float32 [8, 3072, 768], P('batch', 'ffn')
The draws below stay inside these ranges and needn't reach their ends.
Inputs may be any that keep to these rules, and one draw needn't show every extreme that they name: `routes`: among the rows of one device each index of batch is named by at most 261 rows, and by exactly 261 rows in some devices' rows. `group_map`: every expert is hosted by at least one index of batch; the numbers of indices hosting each expert differ by at most one. w_in[i] equals w_in[j] whenever group_map[i] equals group_map[j]. w_back[i] equals w_back[j] whenever group_map[i] equals group_map[j].
All inputs are finite; a program needn't handle non-finite values.
Results may differ from the reference program's by a relative error of at most 0.015.
The reference program's roundings to bfloat16 on the way count: a program that leaves them out, or rounds other values in their place, can miss the bound.
Values may be sent and summed in bfloat16 or wider, within the bound.
A program may use at most 256 MiB of HBM per device.

```python
import math
import jax
import jax.numpy as jnp
import numpy as np
from jax import lax

D = 768
HEADS = 12
HEAD_DIM = 64
FF = 3072
EXPERTS = 3
PATCHES = 197
TEXT = 64
SEQ_DEV = 6
SEQ_LEN = 261
TOK_DEV = 1566
PAIRS = 192
TOKENS = 50112
CAP = 261
N_BATCH = 8


def group_law(key):
    shuffled = jax.random.permutation(jax.random.fold_in(key, 11), N_BATCH)
    return (shuffled % EXPERTS).astype(jnp.int32)


def draw_group_map(key, part):
    return group_law(key)


def draw_w_in(key, part):
    groups = group_law(key)
    base = jax.random.normal(jax.random.fold_in(key, 23), (EXPERTS, D, FF), jnp.float32)
    base = jnp.clip(base, -6.0, 6.0) * D ** (-0.5)
    return base[groups].astype(jnp.bfloat16)


def draw_w_back(key, part):
    groups = group_law(key)
    base = jax.random.normal(jax.random.fold_in(key, 37), (EXPERTS, FF, D), jnp.float32)
    base = jnp.clip(base, -6.0, 6.0) * (FF // 2) ** (-0.5)
    return base[groups].astype(jnp.bfloat16)


def touch_ends(values, rng, smallest, top_value):
    longest = values.shape.index(max(values.shape))
    spots = []
    for shift in (0, 1):
        where = [jax.random.randint(jax.random.fold_in(rng, axis), (), 0, length) for axis, length in enumerate(values.shape)]
        where[longest] = (where[longest] + shift) % values.shape[longest]
        spots.append(tuple(where))
    return values.at[spots[0]].set(smallest).at[spots[1]].set(top_value)


def shard_levels(rng, shape, cuts, least, largest):
    loudness = 1.0
    for dim, parts in cuts:
        draws = jax.random.uniform(jax.random.fold_in(jax.random.fold_in(rng, 6), dim), (parts,), jnp.float32, least / len(cuts), largest / len(cuts))
        loudness = loudness * jnp.repeat(jnp.exp(draws), shape[dim] // parts).reshape((-1,) + (1,) * (len(shape) - 1 - dim))
    return loudness


def routed_block(own_key, own, number, rows, amount, top, bound, slope):
    order = jax.random.permutation(own_key, amount)
    crowded, usual = load_shares(amount, rows * top, bound, slope, True), load_shares(amount, rows * top, bound, slope, False)
    places = jnp.arange(amount)

    def named(tallies, turn):
        used = int((tallies > 0).sum())
        fixed = max(1, used // 4)
        moved = fixed + (places - fixed + turn * (used - fixed)) % max(1, amount - fixed)
        return jnp.zeros((amount,), jnp.int32).at[order[jnp.where(places < fixed, places, moved)]].set(jnp.asarray(tallies, jnp.int32))

    tallies = jnp.where(number % 4 == 0, named(crowded, number // 4), named(usual, number - number // 4 - 1))
    mixed = jax.random.permutation(jax.random.fold_in(own, 3), amount)
    source_of, taker = mixed[0:amount // 2 * 2:2], mixed[1:amount // 2 * 2:2]
    slack = jnp.minimum(tallies[source_of] - 1, bound - tallies[taker]) // 2
    slack = jnp.where((source_of == order[0]) | (taker == order[0]) | (tallies[taker] == 0), 0, jnp.maximum(slack, 0))
    moved = jax.random.randint(jax.random.fold_in(own, 4), (amount // 2,), 0, 1 << 20) % (slack + 1)
    tallies = tallies.at[source_of].add(-moved).at[taker].add(moved)
    labels = jnp.searchsorted(jnp.cumsum(tallies), jnp.arange(rows * top), side="right").astype(jnp.int32)
    table = labels.reshape(top, rows).T
    table = table[jax.random.permutation(jax.random.fold_in(own, 1), rows)]
    turn = jax.random.randint(jax.random.fold_in(own, 2), (rows, 1), 0, top)
    return jnp.take_along_axis(table, (jnp.arange(top)[None, :] + turn) % top, axis=1)


def load_shares(amount, total, reach, skew, full):
    weights = [(1 << 20) // math.isqrt(rank ** skew) + 1 for rank in range(1, amount + 1)]
    largest = reach if full else min(reach, max(-(-total // amount), total * weights[0] // sum(weights)))
    least = 1 if total - largest >= amount - 1 else 0
    holding, spare = [largest] + [least] * (amount - 1), total - largest - least * (amount - 1)
    while spare > 0:
        movable = [i for i in range(1, amount) if holding[i] < largest] or [i for i in range(1, amount) if holding[i] < reach]
        mass, budget = sum([weights[i] for i in movable]), spare
        for i in movable:
            addition = min(reach - holding[i], max(1, budget * weights[i] // mass), spare)
            holding[i] = holding[i] + addition
            spare = spare - addition
    return np.array(holding)


def scatter_about(own_key, dims, scale, bound, cuts=(), held_as=jnp.bfloat16):
    drawn = jax.random.normal(own_key, dims, jnp.float32) * scale
    if len(cuts) > 0:
        drawn = shard_levels(own_key, dims, cuts, -0.22, 0.18) * drawn
    return jnp.clip(drawn, min=-bound, max=bound).astype(held_as)


def setup_inputs(seed: int = 0) -> dict:
    splits = jax.random.split(jax.random.key(seed), 12)
    tokens = scatter_about(splits[0], (TOKENS, D), 1.0, 6.0, ((0, 32),))
    text_lengths = touch_ends(jax.random.randint(splits[1], (PAIRS,), 8, TEXT + 1), jax.random.fold_in(splits[1], 1), 8, TEXT).astype(jnp.int32)
    routes_keys = jax.random.split(jax.random.fold_in(splits[2], 1), TOKENS // TOK_DEV)
    routes_turns = jax.random.permutation(jax.random.fold_in(splits[2], 3), TOKENS // TOK_DEV)
    routes = jax.vmap(lambda own, number: routed_block(jax.random.fold_in(splits[2], 2), own, number, TOK_DEV, N_BATCH, 1, CAP, 1))(routes_keys, routes_turns).reshape((TOKENS, 1))
    group_map = draw_group_map(jax.random.fold_in(splits[11], 71), 0)
    gain_one = jnp.clip(1.0 + 0.18 * jax.random.normal(splits[4], (D,), jnp.float32), 0.1, 1.9)
    w_qkv = scatter_about(splits[5], (D, 3 * D), (D // 2) ** -0.5, 0.3125)
    w_proj = scatter_about(splits[6], (D, D), (D // 16) ** -0.5, 0.875)
    gain_two = jnp.clip(1.0 + 0.18 * jax.random.normal(splits[7], (D,), jnp.float32), 0.1, 1.9)
    w_in = draw_w_in(jax.random.fold_in(splits[11], 71), 0)
    w_back = draw_w_back(jax.random.fold_in(splits[11], 71), 0)
    cotangent = scatter_about(splits[10], (TOKENS, D), 1.0, 6.0, ((0, 32),))
    return dict(tokens=tokens, text_lengths=text_lengths, routes=routes, group_map=group_map, gain_one=gain_one, w_qkv=w_qkv, w_proj=w_proj, gain_two=gain_two, w_in=w_in, w_back=w_back, cotangent=cotangent)


@jax.custom_vjp
def low(v):
    return lax.optimization_barrier(v.astype(jnp.bfloat16)).astype(jnp.float32)

@jax.custom_vjp
def low_back(v):
    return v

def low_keep(v):
    return (low(v), None)

def low_pass(kept, grad):
    return (grad,)

def back_keep(v):
    return (v, None)

def back_low(kept, grad):
    return (low(grad),)
low.defvjp(low_keep, low_pass)
low_back.defvjp(back_keep, back_low)
highest = lax.Precision.HIGHEST
epsilon = 1e-05

def norm_rows(values, gain):
    average = lax.optimization_barrier(jnp.mean(values, axis=-1, keepdims=True))
    centred = values - average
    variance = lax.optimization_barrier(jnp.mean(centred * centred, axis=-1, keepdims=True))
    return centred * lax.rsqrt(variance + epsilon) * gain

def layer_block(params, token_rows, lengths, expert_of):
    gain_one, w_qkv, w_proj, gain_two, w_in, w_back = params
    normed_one = low(norm_rows(token_rows, gain_one))
    qkv_rows = low_back(low(jnp.dot(normed_one, w_qkv, precision=highest)))
    split_rows = qkv_rows.reshape(SEQ_DEV, SEQ_LEN, 3, HEADS, HEAD_DIM)
    queries = split_rows[:, :, 0]
    key_rows = split_rows[:, :, 1]
    value_rows = split_rows[:, :, 2]
    scores = jnp.einsum('sqhd,skhd->shqk', queries, key_rows, precision=highest) * HEAD_DIM ** (-0.5)
    scores = low_back(scores)
    position = jnp.arange(SEQ_LEN, dtype=jnp.int32)
    visible = position[None, :] < PATCHES + lengths[:, None]
    scores = jnp.where(visible[:, None, None, :], scores, -1e+30)
    attn_probs = low(jax.nn.softmax(scores, axis=-1))
    context = jnp.einsum('shqk,skhd->sqhd', attn_probs, value_rows, precision=highest).reshape(TOK_DEV, D)
    context = low_back(low(context))
    attended = low_back(jnp.dot(context, w_proj, precision=highest))
    middle = token_rows + attended
    normed_two = low_back(low(norm_rows(middle, gain_two)))
    combined = jnp.zeros_like(middle)
    for expert in range(EXPERTS):
        inner_act = low_back(jnp.dot(normed_two, w_in[expert], precision=highest))
        hidden = low_back(low(jax.nn.gelu(inner_act, approximate=False)))
        branch = jnp.dot(hidden, w_back[expert], precision=highest)
        chosen = (expert_of == expert).astype(jnp.float32)[:, None]
        combined = combined + chosen * branch
    combined = low_back(low(combined))
    return middle + combined

def reference(tokens, text_lengths, routes, group_map, gain_one, w_qkv, w_proj, gain_two, w_in, w_back, cotangent):
    num_blocks = TOKENS // TOK_DEV
    expert_of = group_map[routes[:, 0]].reshape(num_blocks, TOK_DEV)
    lengths = text_lengths.reshape(num_blocks, SEQ_DEV)
    token_rows = tokens.astype(jnp.float32).reshape(num_blocks, TOK_DEV, D)
    hosting = (group_map[None, :] == jnp.arange(EXPERTS, dtype=jnp.int32)[:, None]).astype(jnp.int32)
    first_host = jnp.argmax(hosting, axis=1).astype(jnp.int32)
    params_in = (gain_one.astype(jnp.float32), w_qkv.astype(jnp.float32), w_proj.astype(jnp.float32), gain_two.astype(jnp.float32), w_in[first_host].astype(jnp.float32), w_back[first_host].astype(jnp.float32))

    def forward(inputs, params):

        def one_block(pieces):
            return layer_block(params, pieces[0], pieces[1], pieces[2])
        return lax.map(jax.checkpoint(one_block), (inputs, lengths, expert_of))
    output, pullback = jax.vjp(forward, token_rows, params_in)
    grad_inputs, gradients = pullback(cotangent.astype(jnp.float32).reshape(num_blocks, TOK_DEV, D))
    return (output.reshape(TOKENS, D), grad_inputs.reshape(TOKENS, D), gradients[0], gradients[1], gradients[2], gradients[3], gradients[4][group_map], gradients[5][group_map])
```

```python
import functools
import math

import jax
import jax.numpy as jnp
from jax import lax
from jax.experimental import pallas as pl
from jax.experimental.pallas import tpu as pltpu
from jax.sharding import PartitionSpec as P

D = 768
HEADS = 12
HEAD_DIM = 64
EXPERTS = 3
PATCHES = 197
SEQ_DEV = 6
SEQ_LEN = 261
TOK_DEV = 1566
ROWS = 1584
SORTED = 1568
WIN = 288
TILE = 528
LANES = 1664
EPS = 1e-05
F32 = jnp.float32
BF16 = jnp.bfloat16
I32 = jnp.int32
CONTRACT_LANES = (((1,), (1,)), ((), ()))
CONTRACT_ROWS = (((0,), (0,)), ((), ()))


def params(**extra):
    return pltpu.CompilerParams(vmem_limit_bytes=60 << 20, **extra)


def cost(flops, moved):
    return pl.CostEstimate(flops=int(flops), bytes_accessed=int(moved), transcendentals=0)


def dot(a, b, dims=(((1,), (0,)), ((), ()))):
    return lax.dot_general(a, b, dims, preferred_element_type=F32)


def full(shape):
    zeros = (0,) * len(shape)
    return pl.BlockSpec(shape, lambda *_: zeros)


def once(shape):
    zeros = (0,) * len(shape)
    return pl.BlockSpec(shape, lambda *_: zeros, pipeline_mode=pl.Buffered(1))


def row_mask(start, rows, limit):
    return start + lax.broadcasted_iota(I32, (rows, 1), 0) < limit


def norm_parts(values):
    average = jnp.mean(values, axis=-1, keepdims=True)
    centred = values - average
    variance = jnp.mean(centred * centred, axis=-1, keepdims=True)
    inverse = lax.rsqrt(variance + EPS)
    return centred * inverse, inverse


def norm_pull(grad_normed, gain, normal, inverse):
    scaled = grad_normed * gain
    mean_grad = jnp.mean(scaled, axis=-1, keepdims=True)
    mean_proj = jnp.mean(scaled * normal, axis=-1, keepdims=True)
    return inverse * (scaled - mean_grad - normal * mean_proj)


def route_kernel(n_batch, gm_ref, routes_ref, pos_ref, offs_ref):
    routes = routes_ref[...]
    lane = lax.broadcasted_iota(I32, (8, LANES), 1)
    sub = lax.broadcasted_iota(I32, (8, LANES), 0)
    expert = jnp.zeros((1, LANES), I32)
    for b in range(n_batch):
        expert = jnp.where(routes == b, gm_ref[b], expert)
    live = lane < TOK_DEV
    hot = jnp.where((jnp.broadcast_to(expert, (8, LANES)) == sub) & live, 1, 0)
    count = hot
    step = 1
    while step < LANES:
        count = count + jnp.where(lane >= step, pltpu.roll(count, step, 1), 0)
        step *= 2
    totals = [jnp.sum(hot[e : e + 1, :], axis=1, keepdims=True) for e in range(EXPERTS)]
    starts = [jnp.zeros((1, 1), I32)]
    for e in range(EXPERTS):
        starts.append(starts[-1] + totals[e])
    pos = jnp.zeros((1, LANES), I32)
    for e in range(EXPERTS):
        pos = pos + jnp.where(hot[e : e + 1, :] > 0, count[e : e + 1, :] - 1 + starts[e], 0)
    pos_ref[...] = jnp.where(live[0:1, :], pos, -1)
    slot = lax.broadcasted_iota(I32, (1, 128), 1)
    offs = jnp.zeros((1, 128), I32)
    for e in range(EXPERTS + 1):
        offs = jnp.where(slot == e, starts[e], offs)
    offs_ref[...] = offs


def route_rows(routes_row, group_map):
    n_batch = group_map.shape[0]
    return pl.pallas_call(
        functools.partial(route_kernel, n_batch),
        out_shape=(
            jax.ShapeDtypeStruct((1, LANES), I32),
            jax.ShapeDtypeStruct((1, 128), I32),
        ),
        in_specs=[
            pl.BlockSpec(memory_space=pltpu.SMEM),
            pl.BlockSpec(memory_space=pltpu.VMEM),
        ],
        out_specs=(
            pl.BlockSpec(memory_space=pltpu.VMEM),
            pl.BlockSpec(memory_space=pltpu.VMEM),
        ),
        compiler_params=params(),
        name="route",
    )(group_map, routes_row)


SORT_TILE = 224


def sort_into(out_ref, rows_ref, pos_ref):
    pos = pos_ref[0:1, 0:ROWS]
    for i in range(SORTED // SORT_TILE):
        want = i * SORT_TILE + lax.broadcasted_iota(I32, (SORT_TILE, ROWS), 0)
        hot = jnp.where(pos == want, 1.0, 0.0).astype(BF16)
        out_ref[i * SORT_TILE : (i + 1) * SORT_TILE, :] = dot(hot, rows_ref[...]).astype(BF16)


def sort_kernel(rows_ref, pos_ref, out_ref, held):
    held[1552:ROWS, :] = jnp.zeros((ROWS - 1552, D), BF16)
    held[0:TOK_DEV, :] = rows_ref[...]
    sort_into(out_ref, held, pos_ref)


def sort_rows(rows, pos):
    return pl.pallas_call(
        sort_kernel,
        out_shape=jax.ShapeDtypeStruct((SORTED, D), BF16),
        scratch_shapes=[pltpu.VMEM((ROWS, D), BF16)],
        compiler_params=params(),
        cost_estimate=cost(2 * SORTED * ROWS * D, 4 * ROWS * D),
        name="sort_rows",
    )(rows, pos)


def qkv_kernel(tok_ref, gain_ref, w_ref, out_ref):
    normal, _ = norm_parts(tok_ref[...].astype(F32))
    keep = row_mask(pl.program_id(0) * TILE, TILE, TOK_DEV)
    normed = jnp.where(keep, normal * gain_ref[...], 0.0).astype(BF16)
    out_ref[...] = dot(normed, w_ref[...]).astype(BF16)


def qkv_rows(tokens, gain, w_qkv):
    return pl.pallas_call(
        qkv_kernel,
        grid=(ROWS // TILE,),
        out_shape=jax.ShapeDtypeStruct((ROWS, 3 * D), BF16),
        in_specs=[
            pl.BlockSpec((TILE, D), lambda i: (i, 0)),
            full((1, D)),
            once((D, 3 * D)),
        ],
        out_specs=pl.BlockSpec((TILE, 3 * D), lambda i: (i, 0)),
        compiler_params=params(),
        cost_estimate=cost(2 * ROWS * D * 3 * D, 2 * ROWS * D * 4),
        name="qkv",
    )(tokens, gain, w_qkv)


def window(pair):
    first = pair * SEQ_LEN
    start = first // 16 * 16
    return start, first - start


def attend_kernel(len_ref, qkv_ref, ctx_ref, lse_ref, stat):
    pair = pl.program_id(0)
    start, skip = window(pair)
    start = pl.multiple_of(start, 16)

    @pl.when(pair == 0)
    def _():
        ctx_ref[...] = jnp.zeros_like(ctx_ref)

    key = lax.broadcasted_iota(I32, (1, WIN), 1)
    seen = (key >= skip) & (key < skip + PATCHES + len_ref[pair])
    bias = jnp.where(seen, 0.0, -1e30)
    row = lax.broadcasted_iota(I32, (WIN, 1), 0)
    mine = (row >= skip) & (row < skip + SEQ_LEN)
    lane = lax.broadcasted_iota(I32, (WIN, 128), 1)
    stat[...] = jnp.zeros_like(stat)
    for hp in range(HEADS // 2):
        cols = slice(hp * 128, hp * 128 + 128)
        q = qkv_ref[pl.ds(start, WIN), hp * 128 : hp * 128 + 128]
        k = qkv_ref[pl.ds(start, WIN), D + hp * 128 : D + hp * 128 + 128]
        v = qkv_ref[pl.ds(start, WIN), 2 * D + hp * 128 : 2 * D + hp * 128 + 128]
        q = q * jnp.asarray(HEAD_DIM**-0.5, BF16)
        pieces = []
        for half in range(2):
            inside = (lane < 64) if half == 0 else (lane >= 64)
            qh = jnp.where(inside, q, jnp.zeros_like(q))
            scores = dot(qh, k, CONTRACT_LANES) + bias
            peak = jnp.max(scores, axis=1, keepdims=True)
            weight = jnp.exp(scores - peak).astype(BF16)
            vh = jnp.where(inside, v, jnp.ones_like(v))
            mixed = dot(weight, vh)
            total = pltpu.roll(mixed, 64, 1)
            pieces.append(mixed / total)
            one = total[:, 0:1] if half == 0 else mixed[:, 0:1]
            head = hp * 2 + half
            stat[0:WIN, :] = jnp.where(lane == head, peak + jnp.log(one), stat[0:WIN, :])
        ctx = jnp.where(lane < 64, pieces[0], pieces[1]).astype(BF16)
        old = ctx_ref[pl.ds(start, WIN), cols]
        ctx_ref[pl.ds(start, WIN), cols] = jnp.where(mine, ctx, old)
    lse_ref[0] = jnp.transpose(stat[...])[0:16, :]


def attend(qkv, lengths):
    return pl.pallas_call(
        attend_kernel,
        grid=(SEQ_DEV,),
        out_shape=(
            jax.ShapeDtypeStruct((ROWS, D), BF16),
            jax.ShapeDtypeStruct((SEQ_DEV, 16, 384), F32),
        ),
        in_specs=[
            pl.BlockSpec(memory_space=pltpu.SMEM),
            once((ROWS, 3 * D)),
        ],
        out_specs=(
            full((ROWS, D)),
            pl.BlockSpec((1, 16, 384), lambda s: (s, 0, 0)),
        ),
        scratch_shapes=[pltpu.VMEM((384, 128), F32)],
        compiler_params=params(),
        cost_estimate=cost(72 * 4 * WIN * 384 * 128, 2 * ROWS * D * 4),
        name="attend",
    )(lengths, qkv)


def middle_kernel(ctx_ref, w_ref, tok_ref, gain_ref, pos_ref, mid_ref, out_ref, held):
    held[1552:ROWS, :] = jnp.zeros((ROWS - 1552, D), BF16)
    for i in range(3):
        top = min(TILE * (i + 1), TOK_DEV)
        rows = slice(TILE * i, top)
        attended = dot(ctx_ref[rows, :], w_ref[...])
        middle = tok_ref[rows, :].astype(F32) + attended
        mid_ref[rows, :] = middle
        normal, _ = norm_parts(middle)
        held[rows, :] = (normal * gain_ref[...]).astype(BF16)
    sort_into(out_ref, held, pos_ref)


def middle_rows(ctx, w_proj, tokens, gain, pos):
    return pl.pallas_call(
        middle_kernel,
        out_shape=(
            jax.ShapeDtypeStruct((TOK_DEV, D), F32),
            jax.ShapeDtypeStruct((SORTED, D), BF16),
        ),
        scratch_shapes=[pltpu.VMEM((ROWS, D), BF16)],
        compiler_params=params(),
        cost_estimate=cost(2 * SORTED * ROWS * D + 2 * ROWS * D * D, 12 * ROWS * D),
        name="middle",
    )(ctx, w_proj, tokens, gain, pos)


HALF = 384
FF_DEV = 768


def gelu_both(u):
    below = 0.5 * (1.0 + lax.erf(u * (1.0 / math.sqrt(2.0))))
    density = jnp.exp(-0.5 * u * u) * (1.0 / math.sqrt(2.0 * math.pi))
    return u * below, below + u * density


def expert_kernel(
    n_src,
    offs_ref,
    hosts_ref,
    x_ref,
    g_ref,
    wi_hbm,
    wb_hbm,
    out_ref,
    gx_ref,
    dwi_hbm,
    dwb_hbm,
    wi,
    wb,
    acc_i,
    acc_b,
    sems,
):
    src = pl.program_id(0)

    def weight_copies():
        for e in range(EXPERTS):
            for p in range(2):
                host = hosts_ref[e * 2 + p]
                part = pl.ds(p * HALF, HALF)
                yield pltpu.make_async_copy(
                    wi_hbm.at[host], wi.at[e, :, part], sems.at[e * 4 + p * 2]
                )
                yield pltpu.make_async_copy(
                    wb_hbm.at[host], wb.at[e, part, :], sems.at[e * 4 + p * 2 + 1]
                )

    @pl.when(src == 0)
    def _():
        for copy in weight_copies():
            copy.start()
        acc_i[...] = jnp.zeros_like(acc_i)
        acc_b[...] = jnp.zeros_like(acc_b)
        for copy in weight_copies():
            copy.wait()

    tail = slice(SORTED - 16, SORTED)
    out_ref[0, tail, :] = jnp.zeros((16, D), BF16)
    gx_ref[0, tail, :] = jnp.zeros((16, D), BF16)

    def visit(e, low, first, last, size):
        start = pl.multiple_of(jnp.minimum(low, SORTED - size), 16)
        rows = pl.ds(start, size)
        row = start + lax.broadcasted_iota(I32, (size, 1), 0)
        mine = (row >= jnp.maximum(first, low)) & (row < last)
        x = jnp.where(mine, x_ref[0, rows, :], jnp.zeros((), BF16))
        g = jnp.where(mine, g_ref[0, rows, :], jnp.zeros((), BF16))
        inner = dot(x, wi[e])
        hidden, slope = gelu_both(inner)
        hidden = hidden.astype(BF16)
        branch = dot(hidden, wb[e]).astype(BF16)
        grad_hidden = dot(g, wb[e], CONTRACT_LANES).astype(BF16)
        grad_inner = (grad_hidden.astype(F32) * slope).astype(BF16)
        grad_x = dot(grad_inner, wi[e], CONTRACT_LANES).astype(BF16)
        out_ref[0, rows, :] = jnp.where(mine, branch, out_ref[0, rows, :])
        gx_ref[0, rows, :] = jnp.where(mine, grad_x, gx_ref[0, rows, :])
        acc_b[e] += dot(hidden, g, CONTRACT_ROWS)
        acc_i[e] += dot(x, grad_inner, CONTRACT_ROWS)

    for e in range(EXPERTS):
        first = offs_ref[src * 4 + e]
        last = offs_ref[src * 4 + e + 1]
        base = first // 16 * 16
        span = last - base
        span = jnp.where(last > first, span, 0)
        big = span // 256

        @pl.loop(0, big)
        def _(i):
            visit(e, base + i * 256, first, last, 256)

        rest = base + big * 256
        small = (span - big * 256 + 127) // 128

        @pl.loop(0, small)
        def _(i):
            visit(e, rest + i * 128, first, last, 128)

    @pl.when(src == n_src - 1)
    def _():
        copies = []
        for e in range(EXPERTS):
            wi[e] = acc_i[e].astype(BF16)
            wb[e] = acc_b[e].astype(BF16)
            copies.append(pltpu.make_async_copy(wi.at[e], dwi_hbm.at[e], sems.at[e * 2]))
            copies.append(pltpu.make_async_copy(wb.at[e], dwb_hbm.at[e], sems.at[e * 2 + 1]))
            copies[-2].start()
            copies[-1].start()
        for copy in copies:
            copy.wait()


def experts(offs, hosts, x, g, wi, wb):
    n_src = x.shape[0]
    block = pl.BlockSpec((1, SORTED, D), lambda s, *_: (s, 0, 0))
    any_space = pl.BlockSpec(memory_space=pl.ANY)
    return pl.pallas_call(
        functools.partial(expert_kernel, n_src),
        grid_spec=pltpu.PrefetchScalarGridSpec(
            num_scalar_prefetch=2,
            grid=(n_src,),
            in_specs=[block, block, any_space, any_space],
            out_specs=[block, block, any_space, any_space],
            scratch_shapes=[
                pltpu.VMEM((EXPERTS, D, FF_DEV), BF16),
                pltpu.VMEM((EXPERTS, FF_DEV, D), BF16),
                pltpu.VMEM((EXPERTS, D, FF_DEV), F32),
                pltpu.VMEM((EXPERTS, FF_DEV, D), F32),
                pltpu.SemaphoreType.DMA((EXPERTS * 4,)),
            ],
        ),
        out_shape=(
            jax.ShapeDtypeStruct((n_src, SORTED, D), BF16),
            jax.ShapeDtypeStruct((n_src, SORTED, D), BF16),
            jax.ShapeDtypeStruct((EXPERTS, D, FF_DEV), BF16),
            jax.ShapeDtypeStruct((EXPERTS, FF_DEV, D), BF16),
        ),
        compiler_params=params(),
        cost_estimate=cost(12 * n_src * SORTED * D * FF_DEV, 8 * n_src * SORTED * D),
        name="experts",
    )(offs, hosts, x, g, wi, wb)


def unsort(pos_col, src):
    want = lax.broadcasted_iota(I32, (pos_col.shape[0], SORTED), 1)
    hot = jnp.where(pos_col == want, 1.0, 0.0).astype(BF16)
    return dot(hot, src)


def back_kernel(
    a_ref,
    b_ref,
    c_ref,
    pos_ref,
    mid_ref,
    cot_ref,
    gain_ref,
    ctx_ref,
    w_ref,
    gm_ref,
    gctx_ref,
    dw_ref,
    dg_ref,
    total,
):
    step = pl.program_id(0)

    @pl.when(step == 0)
    def _():
        both = a_ref[...].astype(F32) + b_ref[...].astype(F32) + c_ref[...].astype(F32)
        total[...] = both.astype(BF16)
        dw_ref[...] = jnp.zeros_like(dw_ref)
        dg_ref[...] = jnp.zeros_like(dg_ref)

    keep = row_mask(step * TILE, TILE, TOK_DEV)
    grad_normed = unsort(pos_ref[...], total[...])
    middle = jnp.where(keep, mid_ref[...], 0.0)
    normal, inverse = norm_parts(middle)
    dg_ref[...] += jnp.sum(grad_normed * normal, axis=0, keepdims=True)
    part = norm_pull(grad_normed, gain_ref[...], normal, inverse)
    grad_middle = jnp.where(keep, cot_ref[...].astype(F32) + part, 0.0)
    gm_ref[...] = grad_middle
    low = grad_middle.astype(BF16)
    dw_ref[...] += dot(ctx_ref[...], low, CONTRACT_ROWS)
    gctx_ref[...] = dot(low, w_ref[...], CONTRACT_LANES).astype(BF16)


def back_rows(a, b, c, pos_col, middle, cot, gain, ctx, w_proj):
    tile = pl.BlockSpec((TILE, D), lambda i: (i, 0))
    return pl.pallas_call(
        back_kernel,
        grid=(ROWS // TILE,),
        out_shape=(
            jax.ShapeDtypeStruct((TOK_DEV, D), F32),
            jax.ShapeDtypeStruct((ROWS, D), BF16),
            jax.ShapeDtypeStruct((D, D), F32),
            jax.ShapeDtypeStruct((1, D), F32),
        ),
        in_specs=[
            once((SORTED, D)),
            once((SORTED, D)),
            once((SORTED, D)),
            pl.BlockSpec((TILE, 1), lambda i: (i, 0)),
            tile,
            tile,
            full((1, D)),
            tile,
            once((D, D)),
        ],
        out_specs=(tile, tile, full((D, D)), full((1, D))),
        scratch_shapes=[pltpu.VMEM((SORTED, D), BF16)],
        compiler_params=params(),
        cost_estimate=cost(2 * ROWS * D * (SORTED + 2 * D), 24 * ROWS * D),
        name="back",
    )(a, b, c, pos_col, middle, cot, gain, ctx, w_proj)


def finish_kernel(a_ref, b_ref, c_ref, pos_ref, mid_ref, out_ref, total):
    @pl.when(pl.program_id(0) == 0)
    def _():
        both = a_ref[...].astype(F32) + b_ref[...].astype(F32) + c_ref[...].astype(F32)
        total[...] = both.astype(BF16)

    out_ref[...] = mid_ref[...] + unsort(pos_ref[...], total[...])


def finish_rows(a, b, c, pos_col, middle):
    tile = pl.BlockSpec((TILE, D), lambda i: (i, 0))
    return pl.pallas_call(
        finish_kernel,
        grid=(ROWS // TILE,),
        out_shape=jax.ShapeDtypeStruct((TOK_DEV, D), F32),
        in_specs=[
            once((SORTED, D)),
            once((SORTED, D)),
            once((SORTED, D)),
            pl.BlockSpec((TILE, 1), lambda i: (i, 0)),
            tile,
        ],
        out_specs=tile,
        scratch_shapes=[pltpu.VMEM((SORTED, D), BF16)],
        compiler_params=params(),
        cost_estimate=cost(2 * ROWS * D * SORTED, 14 * ROWS * D),
        name="finish",
    )(a, b, c, pos_col, middle)


def attend_back_kernel(len_ref, qkv_ref, gctx_ref, lse_ref, out_ref):
    pair = pl.program_id(0)
    start, skip = window(pair)
    start = pl.multiple_of(start, 16)

    @pl.when(pair == 0)
    def _():
        out_ref[...] = jnp.zeros_like(out_ref)

    row = lax.broadcasted_iota(I32, (WIN, 1), 0)
    mine = (row >= skip) & (row < skip + SEQ_LEN)
    bias = jnp.where((row >= skip) & (row < skip + PATCHES + len_ref[pair]), 0.0, -1e30)
    lane = lax.broadcasted_iota(I32, (WIN, 128), 1)
    scale = jnp.asarray(HEAD_DIM**-0.5, BF16)
    for hp in range(HEADS // 2):
        spots = [slice(part * D + hp * 128, part * D + hp * 128 + 128) for part in range(3)]
        q, k, v = [qkv_ref[pl.ds(start, WIN), spot] for spot in spots]
        q = q * scale
        ks = k * scale
        go = gctx_ref[pl.ds(start, WIN), hp * 128 : hp * 128 + 128]
        q = jnp.where(mine, q, jnp.zeros_like(q))
        go = jnp.where(mine, go, jnp.zeros_like(go))
        grads = []
        for half in range(2):
            head = hp * 2 + half
            inside = (lane < 64) if half == 0 else (lane >= 64)
            qh = jnp.where(inside, q, jnp.zeros_like(q))
            gh = jnp.where(inside, go, jnp.zeros_like(go))
            scores = dot(k, qh, CONTRACT_LANES)
            probs = jnp.exp(scores + bias - lse_ref[0, head : head + 1, 0:WIN])
            grad_probs = dot(v, gh, CONTRACT_LANES)
            delta = jnp.sum(probs * grad_probs, axis=0, keepdims=True)
            grad_scores = (probs * (grad_probs - delta)).astype(BF16)
            grad_v = dot(probs.astype(BF16), go)
            grad_k = dot(grad_scores, q)
            grad_q = dot(grad_scores, ks, CONTRACT_ROWS)
            grads.append((grad_q, grad_k, grad_v))
        for spot, low, high in zip(spots, grads[0], grads[1]):
            new = jnp.where(lane < 64, low, high).astype(BF16)
            old = out_ref[pl.ds(start, WIN), spot]
            out_ref[pl.ds(start, WIN), spot] = jnp.where(mine, new, old)


def attend_back(qkv, gctx, lse, lengths):
    return pl.pallas_call(
        attend_back_kernel,
        grid=(SEQ_DEV,),
        out_shape=jax.ShapeDtypeStruct((ROWS, 3 * D), BF16),
        in_specs=[
            pl.BlockSpec(memory_space=pltpu.SMEM),
            once((ROWS, 3 * D)),
            once((ROWS, D)),
            pl.BlockSpec((1, 16, 384), lambda s: (s, 0, 0)),
        ],
        out_specs=full((ROWS, 3 * D)),
        compiler_params=params(),
        cost_estimate=cost(72 * 10 * WIN * 384 * 128, 2 * ROWS * D * 7),
        name="attend_back",
    )(lengths, qkv, gctx, lse)


def first_back_kernel(tok_ref, gain_ref, gq_ref, w_ref, gm_ref, ig_ref, dw_ref, dg_ref):
    step = pl.program_id(0)

    @pl.when(step == 0)
    def _():
        dw_ref[...] = jnp.zeros_like(dw_ref)
        dg_ref[...] = jnp.zeros_like(dg_ref)

    keep = row_mask(step * TILE, TILE, TOK_DEV)
    tokens = jnp.where(keep, tok_ref[...].astype(F32), 0.0)
    normal, inverse = norm_parts(tokens)
    normed = (normal * gain_ref[...]).astype(BF16)
    grad_qkv = gq_ref[...]
    dw_ref[...] += dot(normed, grad_qkv, CONTRACT_ROWS)
    grad_normed = dot(grad_qkv, w_ref[...], CONTRACT_LANES)
    dg_ref[...] += jnp.sum(grad_normed * normal, axis=0, keepdims=True)
    ig_ref[...] = gm_ref[...] + norm_pull(grad_normed, gain_ref[...], normal, inverse)


def first_back(tokens, gain, grad_qkv, w_qkv, grad_middle):
    tile = pl.BlockSpec((TILE, D), lambda i: (i, 0))
    return pl.pallas_call(
        first_back_kernel,
        grid=(ROWS // TILE,),
        out_shape=(
            jax.ShapeDtypeStruct((TOK_DEV, D), F32),
            jax.ShapeDtypeStruct((D, 3 * D), F32),
            jax.ShapeDtypeStruct((1, D), F32),
        ),
        in_specs=[
            tile,
            full((1, D)),
            pl.BlockSpec((TILE, 3 * D), lambda i: (i, 0)),
            once((D, 3 * D)),
            tile,
        ],
        out_specs=(tile, full((D, 3 * D)), full((1, D))),
        compiler_params=params(),
        cost_estimate=cost(4 * ROWS * D * 3 * D, 16 * ROWS * D),
        name="first_back",
    )(tokens, gain, grad_qkv, w_qkv, grad_middle)


def swap(rows, bit):
    pairs = [(f, f ^ bit) for f in range(4)]
    return lax.ppermute(rows, "ffn", pairs)


def spread(rows):
    near = swap(rows, 1)
    far = swap(rows, 2)
    return [rows, near, far, swap(far, 1)]


def body(
    tokens,
    text_lengths,
    routes,
    group_map,
    gain_one,
    w_qkv,
    w_proj,
    gain_two,
    w_in,
    w_back,
    cotangent,
):
    n_batch = lax.axis_size("batch")
    own = lax.axis_index("batch")
    gain_one = gain_one.reshape(1, D)
    gain_two = gain_two.reshape(1, D)
    own_expert = group_map[own]
    order = jnp.arange(n_batch, dtype=I32)
    rank = jnp.sum(jnp.where((group_map == own_expert) & (order < own), 1, 0))
    part = jnp.minimum(rank, 1)
    hosting = group_map[None, :] == jnp.arange(EXPERTS, dtype=I32)[:, None]
    first_host = jnp.min(jnp.where(hosting, order[None, :], n_batch), axis=1)
    later = hosting & (order[None, :] > first_host[:, None])
    second_host = jnp.min(jnp.where(later, order[None, :], n_batch), axis=1)
    hosts = jnp.stack([first_host, second_host], axis=1).reshape(2 * EXPERTS)

    wi_part = lax.dynamic_slice(w_in[0], (0, part * HALF), (D, HALF))
    wb_part = lax.dynamic_slice(w_back[0], (part * HALF, 0), (HALF, D))
    wi_all = lax.all_gather(wi_part, "batch", axis=0)
    wb_all = lax.all_gather(wb_part, "batch", axis=0)

    routes_row = jnp.pad(routes.reshape(1, TOK_DEV), ((0, 0), (0, LANES - TOK_DEV)))
    pos, offs = route_rows(routes_row, group_map)
    pos_col = pos.reshape(LANES, 1)[0:ROWS]
    offs_all = jnp.concatenate([o[0, 0:4] for o in spread(offs)])

    grads_sorted = sort_rows(cotangent, pos)
    g_all = jnp.stack(spread(grads_sorted))

    qkv = qkv_rows(tokens, gain_one, w_qkv)
    context, lse = attend(qkv, text_lengths)
    middle, sending = middle_rows(context, w_proj, tokens, gain_two, pos)
    x_all = jnp.stack(spread(sending))

    out, gx, dwi, dwb = experts(offs_all, hosts, x_all, g_all, wi_all, wb_all)

    def collect(parts):
        near = swap(parts[1], 1)
        far = (parts[2].astype(F32) + swap(parts[3], 1).astype(F32)).astype(BF16)
        return parts[0], near, swap(far, 2)

    grad_middle, gctx, dw_proj, dg_two = back_rows(
        *collect(gx), pos_col, middle, cotangent, gain_two, context, w_proj
    )
    block_out = finish_rows(*collect(out), pos_col, middle)
    grad_qkv = attend_back(qkv, gctx, lse, text_lengths)
    input_grad, dw_qkv, dg_one = first_back(tokens, gain_one, grad_qkv, w_qkv, grad_middle)

    def settle(grad, dim):
        share = lax.psum_scatter(grad, "batch", scatter_dimension=dim, tiled=True)
        whole = lax.all_gather(share, "batch", axis=dim, tiled=True)
        return lax.dynamic_index_in_dim(whole, own_expert, 0, keepdims=True).astype(F32)

    grad_w_in = settle(dwi, 1)
    grad_w_back = settle(dwb, 1)
    summed_qkv, summed_proj = lax.psum(
        (dw_qkv.astype(BF16), dw_proj.astype(BF16)), ("batch", "ffn")
    )
    gains = lax.psum(jnp.concatenate([dg_one, dg_two], axis=0), ("batch", "ffn"))
    return (
        block_out,
        input_grad,
        gains[0],
        summed_qkv.astype(F32),
        summed_proj.astype(F32),
        gains[1],
        grad_w_in,
        grad_w_back,
    )


def solution(mesh):
    placed = (
        P(("batch", "ffn"), None),
        P(("batch", "ffn")),
        P(("batch", "ffn"), None),
        P(),
        P(),
        P(),
        P(),
        P(),
        P("batch", None, "ffn"),
        P("batch", "ffn", None),
        P(("batch", "ffn"), None),
    )
    return jax.shard_map(
        body,
        mesh=mesh,
        in_specs=placed,
        out_specs=(
            P(("batch", "ffn"), None),
            P(("batch", "ffn"), None),
            P(),
            P(),
            P(),
            P(),
            P("batch", None, "ffn"),
            P("batch", "ffn", None),
        ),
        check_vma=False,
    )
```

```python
import functools
import math

import jax
import jax.numpy as jnp
from jax import lax
from jax.experimental import pallas as pl
from jax.experimental.pallas import tpu as pltpu
from jax.sharding import PartitionSpec as P

D = 768
HEADS = 12
HEAD_DIM = 64
EXPERTS = 3
PATCHES = 197
SEQ_DEV = 6
SEQ_LEN = 261
TOK_DEV = 1566
ROWS = 1584
SORTED = 1616
WIN = 288
TILE = 528
LANES = 1664
EPS = 1e-05
F32 = jnp.float32
BF16 = jnp.bfloat16
I32 = jnp.int32
CONTRACT_LANES = (((1,), (1,)), ((), ()))
CONTRACT_ROWS = (((0,), (0,)), ((), ()))


def params(**extra):
    return pltpu.CompilerParams(vmem_limit_bytes=60 << 20, **extra)


def cost(flops, moved):
    return pl.CostEstimate(flops=int(flops), bytes_accessed=int(moved), transcendentals=0)


def dot(a, b, dims=(((1,), (0,)), ((), ()))):
    return lax.dot_general(a, b, dims, preferred_element_type=F32)


def full(shape):
    zeros = (0,) * len(shape)
    return pl.BlockSpec(shape, lambda *_: zeros)


def once(shape):
    zeros = (0,) * len(shape)
    return pl.BlockSpec(shape, lambda *_: zeros, pipeline_mode=pl.Buffered(1))


def row_mask(start, rows, limit):
    return start + lax.broadcasted_iota(I32, (rows, 1), 0) < limit


def norm_parts(values):
    average = jnp.mean(values, axis=-1, keepdims=True)
    centred = values - average
    variance = jnp.mean(centred * centred, axis=-1, keepdims=True)
    inverse = lax.rsqrt(variance + EPS)
    return centred * inverse, inverse


def norm_pull(grad_normed, gain, normal, inverse):
    scaled = grad_normed * gain
    mean_grad = jnp.mean(scaled, axis=-1, keepdims=True)
    mean_proj = jnp.mean(scaled * normal, axis=-1, keepdims=True)
    return inverse * (scaled - mean_grad - normal * mean_proj)


def route_kernel(n_batch, gm_ref, routes_ref, pos_ref, offs_ref):
    routes = routes_ref[...]
    lane = lax.broadcasted_iota(I32, (8, LANES), 1)
    sub = lax.broadcasted_iota(I32, (8, LANES), 0)
    expert = jnp.zeros((1, LANES), I32)
    for b in range(n_batch):
        expert = jnp.where(routes == b, gm_ref[b], expert)
    live = lane < TOK_DEV
    hot = jnp.where((jnp.broadcast_to(expert, (8, LANES)) == sub) & live, 1, 0)
    count = hot
    step = 1
    while step < LANES:
        count = count + jnp.where(lane >= step, pltpu.roll(count, step, 1), 0)
        step *= 2
    totals = [jnp.sum(hot[e : e + 1, :], axis=1, keepdims=True) for e in range(EXPERTS)]
    starts = [jnp.zeros((1, 1), I32)]
    for e in range(EXPERTS):
        starts.append(starts[-1] + (totals[e] + 15) // 16 * 16)
    pos = jnp.zeros((1, LANES), I32)
    for e in range(EXPERTS):
        pos = pos + jnp.where(hot[e : e + 1, :] > 0, count[e : e + 1, :] - 1 + starts[e], 0)
    pos_ref[...] = jnp.where(live[0:1, :], pos, -1)
    slot = lax.broadcasted_iota(I32, (1, 128), 1)
    offs = jnp.zeros((1, 128), I32)
    for e in range(EXPERTS + 1):
        offs = jnp.where(slot == e, starts[e], offs)
    offs_ref[...] = offs


def route_rows(routes_row, group_map):
    n_batch = group_map.shape[0]
    return pl.pallas_call(
        functools.partial(route_kernel, n_batch),
        out_shape=(
            jax.ShapeDtypeStruct((1, LANES), I32),
            jax.ShapeDtypeStruct((1, 128), I32),
        ),
        in_specs=[
            pl.BlockSpec(memory_space=pltpu.SMEM),
            pl.BlockSpec(memory_space=pltpu.VMEM),
        ],
        out_specs=(
            pl.BlockSpec(memory_space=pltpu.VMEM),
            pl.BlockSpec(memory_space=pltpu.VMEM),
        ),
        compiler_params=params(),
        name="route",
    )(group_map, routes_row)


SORT_TILES = (336, 336, 336, 336, 272)


def sort_into(out_ref, rows_ref, pos_ref):
    pos = pos_ref[0:1, 0:ROWS]
    top = 0
    for size in SORT_TILES:
        want = top + lax.broadcasted_iota(I32, (size, ROWS), 0)
        hot = jnp.where(pos == want, 1.0, 0.0).astype(BF16)
        out_ref[top : top + size, :] = dot(hot, rows_ref[...]).astype(BF16)
        top += size


def sort_kernel(rows_ref, pos_ref, out_ref, held):
    held[1552:ROWS, :] = jnp.zeros((ROWS - 1552, D), BF16)
    held[0:TOK_DEV, :] = rows_ref[...]
    sort_into(out_ref, held, pos_ref)


def sort_rows(rows, pos):
    return pl.pallas_call(
        sort_kernel,
        out_shape=jax.ShapeDtypeStruct((SORTED, D), BF16),
        scratch_shapes=[pltpu.VMEM((ROWS, D), BF16)],
        compiler_params=params(),
        cost_estimate=cost(2 * SORTED * ROWS * D, 4 * ROWS * D),
        name="sort_rows",
    )(rows, pos)


def qkv_kernel(tok_ref, gain_ref, w_ref, out_ref):
    normal, _ = norm_parts(tok_ref[...].astype(F32))
    keep = row_mask(pl.program_id(0) * TILE, TILE, TOK_DEV)
    normed = jnp.where(keep, normal * gain_ref[...], 0.0).astype(BF16)
    out_ref[...] = dot(normed, w_ref[...]).astype(BF16)


def qkv_rows(tokens, gain, w_qkv):
    return pl.pallas_call(
        qkv_kernel,
        grid=(ROWS // TILE,),
        out_shape=jax.ShapeDtypeStruct((ROWS, 3 * D), BF16),
        in_specs=[
            pl.BlockSpec((TILE, D), lambda i: (i, 0)),
            full((1, D)),
            once((D, 3 * D)),
        ],
        out_specs=pl.BlockSpec((TILE, 3 * D), lambda i: (i, 0)),
        compiler_params=params(),
        cost_estimate=cost(2 * ROWS * D * 3 * D, 2 * ROWS * D * 4),
        name="qkv",
    )(tokens, gain, w_qkv)


def window(pair):
    first = pair * SEQ_LEN
    start = first // 16 * 16
    return start, first - start


def attend_kernel(len_ref, qkv_ref, ctx_ref, lse_ref, stat):
    pair = pl.program_id(0)
    start, skip = window(pair)
    start = pl.multiple_of(start, 16)

    @pl.when(pair == 0)
    def _():
        ctx_ref[...] = jnp.zeros_like(ctx_ref)

    key = lax.broadcasted_iota(I32, (1, WIN), 1)
    seen = (key >= skip) & (key < skip + PATCHES + len_ref[pair])
    bias = jnp.where(seen, 0.0, -1e30)
    row = lax.broadcasted_iota(I32, (WIN, 1), 0)
    mine = (row >= skip) & (row < skip + SEQ_LEN)
    lane = lax.broadcasted_iota(I32, (WIN, 128), 1)
    stat[...] = jnp.zeros_like(stat)
    for hp in range(HEADS // 2):
        cols = slice(hp * 128, hp * 128 + 128)
        q = qkv_ref[pl.ds(start, WIN), hp * 128 : hp * 128 + 128]
        k = qkv_ref[pl.ds(start, WIN), D + hp * 128 : D + hp * 128 + 128]
        v = qkv_ref[pl.ds(start, WIN), 2 * D + hp * 128 : 2 * D + hp * 128 + 128]
        q = q * jnp.asarray(HEAD_DIM**-0.5, BF16)
        pieces = []
        for half in range(2):
            inside = (lane < 64) if half == 0 else (lane >= 64)
            qh = jnp.where(inside, q, jnp.zeros_like(q))
            scores = dot(qh, k, CONTRACT_LANES) + bias
            peak = jnp.max(scores, axis=1, keepdims=True)
            weight = jnp.exp(scores - peak).astype(BF16)
            vh = jnp.where(inside, v, jnp.ones_like(v))
            mixed = dot(weight, vh)
            total = pltpu.roll(mixed, 64, 1)
            pieces.append(mixed / total)
            one = total[:, 0:1] if half == 0 else mixed[:, 0:1]
            head = hp * 2 + half
            stat[0:WIN, :] = jnp.where(lane == head, peak + jnp.log(one), stat[0:WIN, :])
        ctx = jnp.where(lane < 64, pieces[0], pieces[1]).astype(BF16)
        old = ctx_ref[pl.ds(start, WIN), cols]
        ctx_ref[pl.ds(start, WIN), cols] = jnp.where(mine, ctx, old)
    lse_ref[0] = jnp.transpose(stat[...])[0:16, :]


def attend(qkv, lengths):
    return pl.pallas_call(
        attend_kernel,
        grid=(SEQ_DEV,),
        out_shape=(
            jax.ShapeDtypeStruct((ROWS, D), BF16),
            jax.ShapeDtypeStruct((SEQ_DEV, 16, 384), F32),
        ),
        in_specs=[
            pl.BlockSpec(memory_space=pltpu.SMEM),
            once((ROWS, 3 * D)),
        ],
        out_specs=(
            full((ROWS, D)),
            pl.BlockSpec((1, 16, 384), lambda s: (s, 0, 0)),
        ),
        scratch_shapes=[pltpu.VMEM((384, 128), F32)],
        compiler_params=params(),
        cost_estimate=cost(72 * 4 * WIN * 384 * 128, 2 * ROWS * D * 4),
        name="attend",
    )(lengths, qkv)


def middle_kernel(ctx_ref, w_ref, tok_ref, gain_ref, pos_ref, mid_ref, out_ref, held):
    held[1552:ROWS, :] = jnp.zeros((ROWS - 1552, D), BF16)
    for i in range(3):
        top = min(TILE * (i + 1), TOK_DEV)
        rows = slice(TILE * i, top)
        attended = dot(ctx_ref[rows, :], w_ref[...])
        middle = tok_ref[rows, :].astype(F32) + attended
        mid_ref[rows, :] = middle
        normal, _ = norm_parts(middle)
        held[rows, :] = (normal * gain_ref[...]).astype(BF16)
    sort_into(out_ref, held, pos_ref)


def middle_rows(ctx, w_proj, tokens, gain, pos):
    return pl.pallas_call(
        middle_kernel,
        out_shape=(
            jax.ShapeDtypeStruct((TOK_DEV, D), F32),
            jax.ShapeDtypeStruct((SORTED, D), BF16),
        ),
        scratch_shapes=[pltpu.VMEM((ROWS, D), BF16)],
        compiler_params=params(),
        cost_estimate=cost(2 * SORTED * ROWS * D + 2 * ROWS * D * D, 12 * ROWS * D),
        name="middle",
    )(ctx, w_proj, tokens, gain, pos)


HALF = 384
FF_DEV = 768


def gelu_both(u):
    below = 0.5 * (1.0 + lax.erf(u * (1.0 / math.sqrt(2.0))))
    density = jnp.exp(-0.5 * u * u) * (1.0 / math.sqrt(2.0 * math.pi))
    return u * below, below + u * density


MERGED = 2 * SORTED + 256


def expert_kernel(n_slots, carried, offs_ref, hosts_ref, *refs):
    refs = list(refs)

    def take(count):
        head = refs[:count]
        del refs[:count]
        return head

    xs, gs = take(2), take(2)
    wi_hbm, wb_hbm = take(1), take(n_slots)
    before = take(2) if carried else None
    outs, gxs = take(2), take(2)
    dwi_ref, dwb_ref = take(2)
    xm, gm, wi, wb, acc_i, acc_b, sems = refs
    expert = pl.program_id(0)
    slot = expert % 2

    def weight_copies(e, buffer, start):
        for p in range(2):
            host = hosts_ref[e * 4 + p]
            part = pl.ds(p * HALF, HALF)
            copy = pltpu.make_async_copy(
                wi_hbm[0].at[host], wi.at[buffer, :, part], sems.at[buffer, p, 0]
            )
            if start:
                copy.start()
            else:
                copy.wait()
            if not start or n_slots == 1:
                source = wb_hbm[0].at[host if n_slots == 1 else 0]
                copy = pltpu.make_async_copy(
                    source, wb.at[buffer, part, :], sems.at[buffer, p, 1]
                )
                if start:
                    copy.start()
                else:
                    copy.wait()
            else:
                for j in range(n_slots):

                    slot = hosts_ref[e * 4 + 2 + p]

                    @pl.when(slot // 2 == j)
                    def _(j=j, slot=slot):
                        pltpu.make_async_copy(
                            wb_hbm[j].at[slot % 2], wb.at[buffer, part, :], sems.at[buffer, p, 1]
                        ).start()

    @pl.when(expert == 0)
    def _():
        weight_copies(0, 0, True)

    @pl.when(expert + 1 < EXPERTS)
    def _():
        weight_copies(expert + 1, 1 - slot, True)

    def blocks(count, act):
        @pl.loop(0, count)
        def _(i):
            act(pl.multiple_of(i * 16, 16))

    @pl.when(expert == 0)
    def _():
        for s in range(2):
            live = pl.multiple_of(offs_ref[s * 4 + EXPERTS], 16)

            def clear(at, s=s, live=live):
                rows = pl.ds(pl.multiple_of(live + at, 16), 16)
                outs[s][rows, :] = jnp.zeros((16, D), BF16)
                gxs[s][rows, :] = jnp.zeros((16, D), BF16)

            blocks((SORTED - live) // 16, clear)

    if carried:
        acc_i[...] = before[0][0].astype(F32)
        acc_b[...] = before[1][0].astype(F32)
    else:
        acc_i[...] = jnp.zeros_like(acc_i)
        acc_b[...] = jnp.zeros_like(acc_b)

    places = []
    total = jnp.int32(0)
    for s in range(2):
        first = pl.multiple_of(offs_ref[s * 4 + expert], 16)
        size = offs_ref[s * 4 + expert + 1] - first
        places.append((first, total, size // 16))

        def gather(at, s=s, first=first, total=total):
            here = pl.ds(pl.multiple_of(first + at, 16), 16)
            there = pl.ds(pl.multiple_of(total + at, 16), 16)
            xm[there, :] = xs[s][here, :]
            gm[there, :] = gs[s][here, :]

        blocks(size // 16, gather)
        total = total + size
    span = pl.multiple_of(total, 16)

    def blank(at):
        there = pl.ds(pl.multiple_of(span + at, 16), 16)
        xm[there, :] = jnp.zeros((16, D), BF16)
        gm[there, :] = jnp.zeros((16, D), BF16)

    blocks((256 - span % 256) // 16, blank)
    weight_copies(expert, slot, False)
    w_in, w_back = wi.at[slot], wb.at[slot]

    @pl.loop(0, (span + 255) // 256)
    def _(i):
        rows = pl.ds(pl.multiple_of(i * 256, 256), 256)
        x, g = xm[rows, :], gm[rows, :]
        inner = dot(x, w_in[...])
        hidden, slope = gelu_both(inner)
        hidden = hidden.astype(BF16)
        grad_hidden = dot(g, w_back[...], CONTRACT_LANES).astype(BF16)
        grad_inner = (grad_hidden.astype(F32) * slope).astype(BF16)
        xm[rows, :] = dot(hidden, w_back[...]).astype(BF16)
        gm[rows, :] = dot(grad_inner, w_in[...], CONTRACT_LANES).astype(BF16)
        acc_b[...] += dot(hidden, g, CONTRACT_ROWS)
        acc_i[...] += dot(x, grad_inner, CONTRACT_ROWS)

    dwi_ref[0] = acc_i[...].astype(BF16)
    dwb_ref[0] = acc_b[...].astype(BF16)
    for s in range(2):
        first, base, count = places[s]

        def hand_back(at, s=s, first=first, base=base):
            here = pl.ds(pl.multiple_of(first + at, 16), 16)
            there = pl.ds(pl.multiple_of(base + at, 16), 16)
            outs[s][here, :] = xm[there, :]
            gxs[s][here, :] = gm[there, :]

        blocks(count, hand_back)


def experts(offs, hosts, xs, gs, wi, wb, before=None):
    whole = once((SORTED, D))
    any_space = pl.BlockSpec(memory_space=pl.ANY)
    weight = pl.BlockSpec((1, D, FF_DEV), lambda e, *_: (e, 0, 0))
    carried = before is not None
    n_slots = len(wb)
    rows = jax.ShapeDtypeStruct((SORTED, D), BF16)
    grad = jax.ShapeDtypeStruct((EXPERTS, D, FF_DEV), BF16)
    return pl.pallas_call(
        functools.partial(expert_kernel, n_slots, carried),
        grid_spec=pltpu.PrefetchScalarGridSpec(
            num_scalar_prefetch=2,
            grid=(EXPERTS,),
            in_specs=[whole] * 4 + [any_space] * (1 + n_slots) + [weight] * (2 * carried),
            out_specs=[whole] * 4 + [weight] * 2,
            scratch_shapes=[
                pltpu.VMEM((MERGED, D), BF16),
                pltpu.VMEM((MERGED, D), BF16),
                pltpu.VMEM((2, D, FF_DEV), BF16),
                pltpu.VMEM((2, FF_DEV, D), BF16),
                pltpu.VMEM((D, FF_DEV), F32),
                pltpu.VMEM((FF_DEV, D), F32),
                pltpu.SemaphoreType.DMA((2, 2, 2)),
            ],
        ),
        out_shape=(rows,) * 4 + (grad,) * 2,
        compiler_params=params(),
        cost_estimate=cost(24 * SORTED * D * FF_DEV, 16 * SORTED * D),
        name="experts",
    )(offs, hosts, *xs, *gs, wi, *wb, *(before or ()))


def unsort(pos_col, src):
    want = lax.broadcasted_iota(I32, (pos_col.shape[0], SORTED), 1)
    hot = jnp.where(pos_col == want, 1.0, 0.0).astype(BF16)
    return dot(hot, src)


def back_kernel(
    a_ref,
    b_ref,
    c_ref,
    pos_ref,
    mid_ref,
    cot_ref,
    gain_ref,
    ctx_ref,
    w_ref,
    gm_ref,
    gctx_ref,
    dw_ref,
    dg_ref,
    total,
    acc,
):
    step = pl.program_id(0)

    @pl.when(step == 0)
    def _():
        both = a_ref[...].astype(F32) + b_ref[...].astype(F32) + c_ref[...].astype(F32)
        total[...] = both.astype(BF16)
        acc[...] = jnp.zeros_like(acc)
        dg_ref[...] = jnp.zeros_like(dg_ref)

    keep = row_mask(step * TILE, TILE, TOK_DEV)
    grad_normed = unsort(pos_ref[...], total[...])
    middle = jnp.where(keep, mid_ref[...], 0.0)
    normal, inverse = norm_parts(middle)
    dg_ref[...] += jnp.sum(grad_normed * normal, axis=0, keepdims=True)
    part = norm_pull(grad_normed, gain_ref[...], normal, inverse)
    grad_middle = jnp.where(keep, cot_ref[...].astype(F32) + part, 0.0)
    gm_ref[...] = grad_middle
    low = grad_middle.astype(BF16)
    acc[...] += dot(ctx_ref[...], low, CONTRACT_ROWS)
    dw_ref[...] = acc[...].astype(BF16)
    gctx_ref[...] = dot(low, w_ref[...], CONTRACT_LANES).astype(BF16)


def back_rows(a, b, c, pos_col, middle, cot, gain, ctx, w_proj):
    tile = pl.BlockSpec((TILE, D), lambda i: (i, 0))
    return pl.pallas_call(
        back_kernel,
        grid=(ROWS // TILE,),
        out_shape=(
            jax.ShapeDtypeStruct((TOK_DEV, D), F32),
            jax.ShapeDtypeStruct((ROWS, D), BF16),
            jax.ShapeDtypeStruct((D, D), BF16),
            jax.ShapeDtypeStruct((1, D), F32),
        ),
        in_specs=[
            once((SORTED, D)),
            once((SORTED, D)),
            once((SORTED, D)),
            pl.BlockSpec((TILE, 1), lambda i: (i, 0)),
            tile,
            tile,
            full((1, D)),
            tile,
            once((D, D)),
        ],
        out_specs=(tile, tile, full((D, D)), full((1, D))),
        scratch_shapes=[pltpu.VMEM((SORTED, D), BF16), pltpu.VMEM((D, D), F32)],
        compiler_params=params(),
        cost_estimate=cost(2 * ROWS * D * (SORTED + 2 * D), 24 * ROWS * D),
        name="back",
    )(a, b, c, pos_col, middle, cot, gain, ctx, w_proj)


def finish_kernel(a_ref, b_ref, c_ref, pos_ref, mid_ref, out_ref, total):
    @pl.when(pl.program_id(0) == 0)
    def _():
        both = a_ref[...].astype(F32) + b_ref[...].astype(F32) + c_ref[...].astype(F32)
        total[...] = both.astype(BF16)

    out_ref[...] = mid_ref[...] + unsort(pos_ref[...], total[...])


def finish_rows(a, b, c, pos_col, middle):
    tile = pl.BlockSpec((TILE, D), lambda i: (i, 0))
    return pl.pallas_call(
        finish_kernel,
        grid=(ROWS // TILE,),
        out_shape=jax.ShapeDtypeStruct((TOK_DEV, D), F32),
        in_specs=[
            once((SORTED, D)),
            once((SORTED, D)),
            once((SORTED, D)),
            pl.BlockSpec((TILE, 1), lambda i: (i, 0)),
            tile,
        ],
        out_specs=tile,
        scratch_shapes=[pltpu.VMEM((SORTED, D), BF16)],
        compiler_params=params(),
        cost_estimate=cost(2 * ROWS * D * SORTED, 14 * ROWS * D),
        name="finish",
    )(a, b, c, pos_col, middle)


def attend_back_kernel(len_ref, qkv_ref, gctx_ref, lse_ref, out_ref):
    pair = pl.program_id(0)
    start, skip = window(pair)
    start = pl.multiple_of(start, 16)

    @pl.when(pair == 0)
    def _():
        out_ref[...] = jnp.zeros_like(out_ref)

    row = lax.broadcasted_iota(I32, (WIN, 1), 0)
    mine = (row >= skip) & (row < skip + SEQ_LEN)
    bias = jnp.where((row >= skip) & (row < skip + PATCHES + len_ref[pair]), 0.0, -1e30)
    lane = lax.broadcasted_iota(I32, (WIN, 128), 1)
    scale = jnp.asarray(HEAD_DIM**-0.5, BF16)
    for hp in range(HEADS // 2):
        spots = [slice(part * D + hp * 128, part * D + hp * 128 + 128) for part in range(3)]
        q, k, v = [qkv_ref[pl.ds(start, WIN), spot] for spot in spots]
        q = q * scale
        ks = k * scale
        go = gctx_ref[pl.ds(start, WIN), hp * 128 : hp * 128 + 128]
        q = jnp.where(mine, q, jnp.zeros_like(q))
        go = jnp.where(mine, go, jnp.zeros_like(go))
        grads = []
        for half in range(2):
            head = hp * 2 + half
            inside = (lane < 64) if half == 0 else (lane >= 64)
            qh = jnp.where(inside, q, jnp.zeros_like(q))
            gh = jnp.where(inside, go, jnp.zeros_like(go))
            scores = dot(k, qh, CONTRACT_LANES)
            probs = jnp.exp(scores + bias - lse_ref[0, head : head + 1, 0:WIN])
            grad_probs = dot(v, gh, CONTRACT_LANES)
            delta = jnp.sum(probs * grad_probs, axis=0, keepdims=True)
            grad_scores = (probs * (grad_probs - delta)).astype(BF16)
            grad_v = dot(probs.astype(BF16), go)
            grad_k = dot(grad_scores, q)
            grad_q = dot(grad_scores, ks, CONTRACT_ROWS)
            grads.append((grad_q, grad_k, grad_v))
        for spot, low, high in zip(spots, grads[0], grads[1]):
            new = jnp.where(lane < 64, low, high).astype(BF16)
            old = out_ref[pl.ds(start, WIN), spot]
            out_ref[pl.ds(start, WIN), spot] = jnp.where(mine, new, old)


def attend_back(qkv, gctx, lse, lengths):
    return pl.pallas_call(
        attend_back_kernel,
        grid=(SEQ_DEV,),
        out_shape=jax.ShapeDtypeStruct((ROWS, 3 * D), BF16),
        in_specs=[
            pl.BlockSpec(memory_space=pltpu.SMEM),
            once((ROWS, 3 * D)),
            once((ROWS, D)),
            pl.BlockSpec((1, 16, 384), lambda s: (s, 0, 0)),
        ],
        out_specs=full((ROWS, 3 * D)),
        compiler_params=params(),
        cost_estimate=cost(72 * 10 * WIN * 384 * 128, 2 * ROWS * D * 7),
        name="attend_back",
    )(lengths, qkv, gctx, lse)


def first_back_kernel(tok_ref, gain_ref, gq_ref, w_ref, gm_ref, ig_ref, dw_ref, dg_ref, acc):
    step = pl.program_id(0)

    @pl.when(step == 0)
    def _():
        acc[...] = jnp.zeros_like(acc)
        dg_ref[...] = jnp.zeros_like(dg_ref)

    keep = row_mask(step * TILE, TILE, TOK_DEV)
    tokens = jnp.where(keep, tok_ref[...].astype(F32), 0.0)
    normal, inverse = norm_parts(tokens)
    normed = (normal * gain_ref[...]).astype(BF16)
    grad_qkv = gq_ref[...]
    acc[...] += dot(normed, grad_qkv, CONTRACT_ROWS)

    @pl.when(step == ROWS // TILE - 1)
    def _():
        dw_ref[...] = acc[...].astype(BF16)

    grad_normed = dot(grad_qkv, w_ref[...], CONTRACT_LANES)
    dg_ref[...] += jnp.sum(grad_normed * normal, axis=0, keepdims=True)
    ig_ref[...] = gm_ref[...] + norm_pull(grad_normed, gain_ref[...], normal, inverse)


def first_back(tokens, gain, grad_qkv, w_qkv, grad_middle):
    tile = pl.BlockSpec((TILE, D), lambda i: (i, 0))
    return pl.pallas_call(
        first_back_kernel,
        grid=(ROWS // TILE,),
        out_shape=(
            jax.ShapeDtypeStruct((TOK_DEV, D), F32),
            jax.ShapeDtypeStruct((D, 3 * D), BF16),
            jax.ShapeDtypeStruct((1, D), F32),
        ),
        in_specs=[
            tile,
            full((1, D)),
            pl.BlockSpec((TILE, 3 * D), lambda i: (i, 0)),
            once((D, 3 * D)),
            tile,
        ],
        out_specs=(tile, full((D, 3 * D)), full((1, D))),
        scratch_shapes=[pltpu.VMEM((D, 3 * D), F32)],
        compiler_params=params(),
        cost_estimate=cost(4 * ROWS * D * 3 * D, 16 * ROWS * D),
        name="first_back",
    )(tokens, gain, grad_qkv, w_qkv, grad_middle)


def swap(rows, bit):
    pairs = [(f, f ^ bit) for f in range(4)]
    return lax.ppermute(rows, "ffn", pairs)


def spread(rows):
    near = swap(rows, 1)
    far = swap(rows, 2)
    return [rows, near, far, swap(far, 1)]


def cross(rows, bits):
    return lax.ppermute(rows, "batch", [(b, b ^ bits) for b in range(8)])


def tie(value, *others):
    return lax.optimization_barrier((value, *others))[0]


CHUNK = D // 8


Z_GROUPS = [[0, 2, 4, 6], [1, 3, 5, 7]]


def deliver_kernel(gm_ref, in_ref, back_ref, out_ref):
    for b in range(8):
        e = gm_ref[b]
        out_ref[b, 0] = in_ref[e]
        total = sum(back_ref[e, z].astype(F32) for z in range(4))
        out_ref[b, 1] = total.astype(BF16)


def deliver(grad_in, grad_back, group_map):
    vmem = pl.BlockSpec(memory_space=pltpu.VMEM)
    return pl.pallas_call(
        deliver_kernel,
        out_shape=jax.ShapeDtypeStruct((8, 2, CHUNK, D), BF16),
        in_specs=[pl.BlockSpec(memory_space=pltpu.SMEM), vmem, vmem],
        out_specs=vmem,
        compiler_params=params(),
        cost_estimate=cost(0, 6 << 20),
        name="deliver",
    )(group_map, grad_in, grad_back)


def cross_y(dwb, own):
    y = own % 2
    cut = dwb.reshape(EXPERTS, 4, 2, CHUNK, D)
    there = cross(lax.dynamic_index_in_dim(cut, 1 - y, 2, keepdims=False), 1)
    mine = lax.dynamic_index_in_dim(cut, y, 2, keepdims=False)
    return (mine.astype(F32) + there.astype(F32)).astype(BF16)


def cross_z(rows):
    return lax.all_to_all(
        rows, "batch", split_axis=1, concat_axis=1, axis_index_groups=Z_GROUPS, tiled=True
    )


AXES = ("x", "y", "z")
ORDERS = (("x", "y", "z"), ("y", "z", "x"), ("z", "x", "y"))
WIDE = 4 * D
COLOUR = WIDE // 3
QUARTER = COLOUR // 4
GAIN_ROWS = 8


def total_kernel(
    qkv_ref, proj_ref, gain_ref, out_ref, gain_out_ref, near, held, came, gain_in, send_sems, recv_sems
):
    batch, ffn = lax.axis_index("batch"), lax.axis_index("ffn")
    z, y, x, c = batch // 2, batch % 2, ffn // 2, ffn % 2
    place = {"x": x, "y": y, "z": z}

    def peer(axis, k=1):
        if axis == "c":
            return (batch, ffn ^ 1)
        if axis == "x":
            return (batch, ffn ^ 2)
        if axis == "y":
            return (batch ^ 1, ffn)
        return (batch ^ (2 * k), ffn)

    peers = [peer("c"), peer("x"), peer("y")] + [peer("z", k) for k in (1, 2, 3)]
    barrier = pltpu.get_barrier_semaphore()
    for device in peers:
        pl.semaphore_signal(barrier, inc=1, device_id=device, device_id_type=pl.DeviceIdType.MESH)
    pl.semaphore_wait(barrier, len(peers))

    used = [0]

    def send(src, dst, device):
        number = used[0]
        used[0] += 1
        copy = pltpu.make_async_remote_copy(
            src_ref=src,
            dst_ref=dst,
            send_sem=send_sems.at[number],
            recv_sem=recv_sems.at[number],
            device_id=device,
            device_id_type=pl.DeviceIdType.MESH,
        )
        copy.start()
        return copy

    give = pl.ds(pl.multiple_of((1 - c) * 384, 16), 384)
    keep = pl.ds(pl.multiple_of(c * 384, 16), 384)
    first = [
        send(qkv_ref.at[give, :], near.at[:, 0 : 3 * D], peer("c")),
        send(proj_ref.at[give, :], near.at[:, 3 * D : WIDE], peer("c")),
        send(gain_ref, gain_in.at[0], peer("c")),
    ]
    for copy in first:
        copy.wait()
    held[:, 0 : 3 * D] = (
        qkv_ref[keep, :].astype(F32) + near[:, 0 : 3 * D].astype(F32)
    ).astype(BF16)
    held[:, 3 * D : WIDE] = (
        proj_ref[keep, :].astype(F32) + near[:, 3 * D : WIDE].astype(F32)
    ).astype(BF16)
    gain_out_ref[...] = gain_ref[...] + gain_in[0]

    top = [0, 0, 0]
    left = [COLOUR * i for i in range(3)]
    rows, cols = [384] * 3, [COLOUR] * 3
    gain_slot = 1
    for step in range(3):
        flying = []
        for i in range(3):
            axis = ORDERS[i][step]
            if axis == "z":
                for k in (1, 2, 3):
                    there = pl.ds(pl.multiple_of(left[i] + (z ^ k) * QUARTER, 128), QUARTER)
                    live = pl.ds(top[i], rows[i])
                    flying.append(
                        send(
                            held.at[live, there],
                            came.at[i, k - 1, 0 : rows[i], 0:QUARTER],
                            peer("z", k),
                        )
                    )
            else:
                half = rows[i] // 2
                there = pl.ds(pl.multiple_of(top[i] + (1 - place[axis]) * half, 16), half)
                flying.append(
                    send(
                        held.at[there, pl.ds(left[i], cols[i])],
                        came.at[i, 3 if axis == "x" else 4, 0:half, 0 : cols[i]],
                        peer(axis),
                    )
                )
        gain_axis = AXES[step]
        if gain_axis == "z":
            flying += [send(gain_out_ref, gain_in.at[gain_slot + k - 1], peer("z", k)) for k in (1, 2, 3)]
        else:
            flying.append(send(gain_out_ref, gain_in.at[gain_slot], peer(gain_axis)))
        for copy in flying:
            copy.wait()
        for i in range(3):
            axis = ORDERS[i][step]
            if axis == "z":
                left[i] = pl.multiple_of(left[i] + z * QUARTER, 128)
                cols[i] = QUARTER
                spots = (0, 1, 2)
            else:
                rows[i] = rows[i] // 2
                top[i] = pl.multiple_of(top[i] + place[axis] * rows[i], 16)
                spots = (3,) if axis == "x" else (4,)
            spot = (pl.ds(top[i], rows[i]), pl.ds(left[i], cols[i]))
            total = held[spot].astype(F32)
            for number in spots:
                total = total + came[i, number, 0 : rows[i], 0 : cols[i]].astype(F32)
            held[spot] = total.astype(BF16)
        if gain_axis == "z":
            gain_out_ref[...] = (
                (gain_out_ref[...] + gain_in[gain_slot])
                + gain_in[gain_slot + 1]
                + gain_in[gain_slot + 2]
            )
        else:
            gain_out_ref[...] = gain_out_ref[...] + gain_in[gain_slot]
            gain_slot += 1

    base = c * 384
    for i in range(3):
        spot = (pl.ds(top[i], rows[i]), pl.ds(left[i], cols[i]))
        out_ref[pl.ds(pl.multiple_of(base + top[i], 16), rows[i]), spot[1]] = held[spot]
    for step in (2, 1, 0):
        flying = []
        for i in range(3):
            axis = ORDERS[i][step]
            mine = out_ref.at[
                pl.ds(pl.multiple_of(base + top[i], 16), rows[i]), pl.ds(left[i], cols[i])
            ]
            for k in (1, 2, 3) if axis == "z" else (1,):
                flying.append(send(mine, mine, peer(axis, k)))
        for copy in flying:
            copy.wait()
        for i in range(3):
            axis = ORDERS[i][step]
            if axis == "z":
                left[i] = COLOUR * i
                cols[i] = COLOUR
            else:
                top[i] = top[i] - place[axis] * rows[i]
                rows[i] = rows[i] * 2
                if rows[i] == 384:
                    top[i] = 0
    mine = out_ref.at[pl.ds(pl.multiple_of(base, 16), 384), :]
    send(mine, mine, peer("c")).wait()


COPIES = 3 + 2 * (2 + 3 + 2 + 3 + 2 + 3) // 2 + 5 + 15 + 1


def total_over_all(dw_qkv, dw_proj, gains):
    vmem = pl.BlockSpec(memory_space=pltpu.VMEM)
    return pl.pallas_call(
        total_kernel,
        out_shape=(
            jax.ShapeDtypeStruct((D, WIDE), BF16),
            jax.ShapeDtypeStruct((GAIN_ROWS, D), F32),
        ),
        in_specs=[vmem] * 3,
        out_specs=(vmem, vmem),
        scratch_shapes=[
            pltpu.VMEM((384, WIDE), BF16),
            pltpu.VMEM((384, WIDE), BF16),
            pltpu.VMEM((3, 5, 384, COLOUR), BF16),
            pltpu.VMEM((6, GAIN_ROWS, D), F32),
            pltpu.SemaphoreType.DMA((COPIES,)),
            pltpu.SemaphoreType.DMA((COPIES,)),
        ],
        compiler_params=params(collective_id=0, has_side_effects=True),
        name="total",
    )(dw_qkv, dw_proj, gains)


def body(
    tokens,
    text_lengths,
    routes,
    group_map,
    gain_one,
    w_qkv,
    w_proj,
    gain_two,
    w_in,
    w_back,
    cotangent,
):
    n_batch = lax.axis_size("batch")
    own = lax.axis_index("batch")
    gain_one = gain_one.reshape(1, D)
    gain_two = gain_two.reshape(1, D)
    own_expert = group_map[own]
    order = jnp.arange(n_batch, dtype=I32)
    rank = jnp.sum(jnp.where((group_map == own_expert) & (order < own), 1, 0))
    part = jnp.minimum(rank, 1)
    hosting = group_map[None, :] == jnp.arange(EXPERTS, dtype=I32)[:, None]
    first_host = jnp.min(jnp.where(hosting, order[None, :], n_batch), axis=1)
    later = hosting & (order[None, :] > first_host[:, None])
    second_host = jnp.min(jnp.where(later, order[None, :], n_batch), axis=1)
    hosts = jnp.stack([first_host, second_host], axis=1).reshape(2 * EXPERTS)

    wi_part = lax.dynamic_slice(w_in[0], (0, part * HALF), (D, HALF))
    wb_part = lax.dynamic_slice(w_back[0], (part * HALF, 0), (HALF, D))
    small = n_batch == 8
    wi_all = lax.all_gather(wi_part, "batch", axis=0)
    if small:
        column = jnp.stack([wb_part, cross(wb_part, 1)])
        wb_all = [column] + [cross(column, 2 * k) for k in (1, 2, 3)]
        slots = hosts ^ own
    else:
        wb_all = [lax.all_gather(wb_part, "batch", axis=0)]
        slots = hosts
    hosts = jnp.stack([hosts.reshape(EXPERTS, 2), slots.reshape(EXPERTS, 2)], axis=1).reshape(-1)

    routes_row = jnp.pad(routes.reshape(1, TOK_DEV), ((0, 0), (0, LANES - TOK_DEV)))
    pos, offs = route_rows(routes_row, group_map)
    pos_col = pos.reshape(LANES, 1)[0:ROWS]
    offs_at = [o[0, 0:4] for o in spread(offs)]

    grads_sorted = sort_rows(cotangent, pos)
    g = spread(grads_sorted)
    tokens = tie(tokens, grads_sorted)

    qkv = qkv_rows(tokens, gain_one, w_qkv)
    if small:
        qkv = tie(qkv, column)
    context, lse = attend(qkv, text_lengths)
    context = tie(context, g[2], g[1], *(wb_all[1:2] if small else []))
    middle, sending = middle_rows(context, w_proj, tokens, gain_two, pos)
    x = spread(sending)

    def run(pair, before):
        return experts(
            jnp.concatenate([offs_at[i] for i in pair]),
            hosts,
            [x[i] for i in pair],
            [g[i] for i in pair],
            wi_all,
            wb_all,
            before,
        )

    def add(a, b):
        return (a.astype(F32) + b.astype(F32)).astype(BF16)

    out2, out3, gx2, gx3, dwi, dwb = run((2, 3), None)
    gx_half = add(gx2, swap(gx3, 1))
    x[0] = tie(x[0], gx_half)
    gx_far = swap(gx_half, 2)
    out0, out1, gx0, gx1, dwi, dwb = run((0, 1), (dwi, dwb))
    gx_near = swap(gx1, 1)
    out_near = swap(out1, 1)
    out_far = swap(tie(add(out2, swap(out3, 1)), gx_far), 2)
    if small:
        share_in = lax.psum_scatter(dwi, "batch", scatter_dimension=1, tiled=True)
        share_back = cross_y(dwb, own)

    grad_middle, gctx, dw_proj, dg_two = back_rows(
        gx0, gx_near, gx_far, pos_col, middle, cotangent, gain_two, context, w_proj
    )
    if small:
        gctx = tie(gctx, share_back)
        share_back = cross_z(share_back)
    grad_qkv = attend_back(qkv, gctx, lse, text_lengths)
    input_grad, dw_qkv, dg_one = first_back(tokens, gain_one, grad_qkv, w_qkv, grad_middle)
    block_out = finish_rows(out0, out_near, out_far, pos_col, middle)

    if small:
        share_in = tie(share_in, grad_qkv)
        pieces = lax.all_to_all(
            deliver(share_in, share_back, group_map),
            "batch",
            split_axis=0,
            concat_axis=0,
            tiled=True,
        )
        grad_w_in = pieces[:, 0].reshape(1, D, D).astype(F32)
        grad_w_back = pieces[:, 1].reshape(1, D, D).astype(F32)
        gains = jnp.concatenate([dg_one, dg_two, jnp.zeros((GAIN_ROWS - 2, D), F32)], axis=0)
        summed, gains = total_over_all(dw_qkv, dw_proj, gains)
        summed_qkv, summed_proj = summed[:, 0 : 3 * D], summed[:, 3 * D : WIDE]
    else:

        def settle_any(grad):
            share = lax.psum_scatter(grad, "batch", scatter_dimension=1, tiled=True)
            whole = lax.all_gather(share, "batch", axis=1, tiled=True)
            return lax.dynamic_index_in_dim(whole, own_expert, 0, keepdims=True).astype(F32)

        grad_w_in = settle_any(dwi)
        grad_w_back = settle_any(dwb)
        summed_qkv, summed_proj = lax.psum((dw_qkv, dw_proj), ("batch", "ffn"))
        gains = lax.psum(jnp.concatenate([dg_one, dg_two], axis=0), ("batch", "ffn"))
    return (
        block_out,
        input_grad,
        gains[0],
        summed_qkv.astype(F32),
        summed_proj.astype(F32),
        gains[1],
        grad_w_in,
        grad_w_back,
    )


def solution(mesh):
    placed = (
        P(("batch", "ffn"), None),
        P(("batch", "ffn")),
        P(("batch", "ffn"), None),
        P(),
        P(),
        P(),
        P(),
        P(),
        P("batch", None, "ffn"),
        P("batch", "ffn", None),
        P(("batch", "ffn"), None),
    )
    return jax.shard_map(
        body,
        mesh=mesh,
        in_specs=placed,
        out_specs=(
            P(("batch", "ffn"), None),
            P(("batch", "ffn"), None),
            P(),
            P(),
            P(),
            P(),
            P("batch", None, "ffn"),
            P("batch", "ffn", None),
        ),
        check_vma=False,
    )
```

```python
import functools
import math

import jax
import jax.numpy as jnp
from jax import lax
from jax.experimental import pallas as pl
from jax.experimental.pallas import tpu as pltpu
from jax.sharding import PartitionSpec as P

D = 768
HEADS = 12
HEAD_DIM = 64
EXPERTS = 3
PATCHES = 197
SEQ_DEV = 6
SEQ_LEN = 261
TOK_DEV = 1566
ROWS = 1584
SORTED = 1616
WIN = 288
TILE = 528
LANES = 1664
EPS = 1e-05
F32 = jnp.float32
BF16 = jnp.bfloat16
I32 = jnp.int32
CONTRACT_LANES = (((1,), (1,)), ((), ()))
CONTRACT_ROWS = (((0,), (0,)), ((), ()))


def params(**extra):
    return pltpu.CompilerParams(vmem_limit_bytes=60 << 20, **extra)


def cost(flops, moved):
    return pl.CostEstimate(flops=int(flops), bytes_accessed=int(moved), transcendentals=0)


def dot(a, b, dims=(((1,), (0,)), ((), ()))):
    return lax.dot_general(a, b, dims, preferred_element_type=F32)


def full(shape):
    zeros = (0,) * len(shape)
    return pl.BlockSpec(shape, lambda *_: zeros)


def once(shape):
    zeros = (0,) * len(shape)
    return pl.BlockSpec(shape, lambda *_: zeros, pipeline_mode=pl.Buffered(1))


def row_mask(start, rows, limit):
    return start + lax.broadcasted_iota(I32, (rows, 1), 0) < limit


def norm_parts(values):
    average = jnp.mean(values, axis=-1, keepdims=True)
    centred = values - average
    variance = jnp.mean(centred * centred, axis=-1, keepdims=True)
    inverse = lax.rsqrt(variance + EPS)
    return centred * inverse, inverse


def norm_pull(grad_normed, gain, normal, inverse):
    scaled = grad_normed * gain
    mean_grad = jnp.mean(scaled, axis=-1, keepdims=True)
    mean_proj = jnp.mean(scaled * normal, axis=-1, keepdims=True)
    return inverse * (scaled - mean_grad - normal * mean_proj)


def route_kernel(n_batch, gm_ref, routes_ref, pos_ref, offs_ref):
    routes = routes_ref[...]
    lane = lax.broadcasted_iota(I32, (8, LANES), 1)
    sub = lax.broadcasted_iota(I32, (8, LANES), 0)
    expert = jnp.zeros((1, LANES), I32)
    for b in range(n_batch):
        expert = jnp.where(routes == b, gm_ref[b], expert)
    live = lane < TOK_DEV
    hot = jnp.where((jnp.broadcast_to(expert, (8, LANES)) == sub) & live, 1, 0)
    count = hot
    step = 1
    while step < LANES:
        count = count + jnp.where(lane >= step, pltpu.roll(count, step, 1), 0)
        step *= 2
    totals = [jnp.sum(hot[e : e + 1, :], axis=1, keepdims=True) for e in range(EXPERTS)]
    starts = [jnp.zeros((1, 1), I32)]
    for e in range(EXPERTS):
        starts.append(starts[-1] + (totals[e] + 15) // 16 * 16)
    pos = jnp.zeros((1, LANES), I32)
    for e in range(EXPERTS):
        pos = pos + jnp.where(hot[e : e + 1, :] > 0, count[e : e + 1, :] - 1 + starts[e], 0)
    pos_ref[...] = jnp.where(live[0:1, :], pos, -1)
    slot = lax.broadcasted_iota(I32, (1, 128), 1)
    offs = jnp.zeros((1, 128), I32)
    for e in range(EXPERTS + 1):
        offs = jnp.where(slot == e, starts[e], offs)
    offs_ref[...] = offs


def route_rows(routes_row, group_map):
    n_batch = group_map.shape[0]
    return pl.pallas_call(
        functools.partial(route_kernel, n_batch),
        out_shape=(
            jax.ShapeDtypeStruct((1, LANES), I32),
            jax.ShapeDtypeStruct((1, 128), I32),
        ),
        in_specs=[
            pl.BlockSpec(memory_space=pltpu.SMEM),
            pl.BlockSpec(memory_space=pltpu.VMEM),
        ],
        out_specs=(
            pl.BlockSpec(memory_space=pltpu.VMEM),
            pl.BlockSpec(memory_space=pltpu.VMEM),
        ),
        compiler_params=params(),
        name="route",
    )(group_map, routes_row)


SORT_TILES = (336, 336, 336, 336, 272)


def window(pair):
    first = pair * SEQ_LEN
    start = first // 16 * 16
    return start, first - start


def attend_pair(pair, length, qkv_ref, ctx_ref, lse_ref, stat):
    start, skip = window(pair)
    start = pl.multiple_of(start, 16)
    key = lax.broadcasted_iota(I32, (1, WIN), 1)
    seen = (key >= skip) & (key < skip + PATCHES + length)
    bias = jnp.where(seen, 0.0, -1e30)
    row = lax.broadcasted_iota(I32, (WIN, 1), 0)
    mine = (row >= skip) & (row < skip + SEQ_LEN)
    lane = lax.broadcasted_iota(I32, (WIN, 128), 1)
    stat[...] = jnp.zeros_like(stat)
    for hp in range(HEADS // 2):
        cols = slice(hp * 128, hp * 128 + 128)
        q = qkv_ref[pl.ds(start, WIN), hp * 128 : hp * 128 + 128]
        k = qkv_ref[pl.ds(start, WIN), D + hp * 128 : D + hp * 128 + 128]
        v = qkv_ref[pl.ds(start, WIN), 2 * D + hp * 128 : 2 * D + hp * 128 + 128]
        q = q * jnp.asarray(HEAD_DIM**-0.5, BF16)
        pieces = []
        for half in range(2):
            inside = (lane < 64) if half == 0 else (lane >= 64)
            qh = jnp.where(inside, q, jnp.zeros_like(q))
            scores = dot(qh, k, CONTRACT_LANES) + bias
            peak = jnp.max(scores, axis=1, keepdims=True)
            weight = jnp.exp(scores - peak).astype(BF16)
            vh = jnp.where(inside, v, jnp.ones_like(v))
            mixed = dot(weight, vh)
            total = pltpu.roll(mixed, 64, 1)
            pieces.append(mixed / total)
            one = total[:, 0:1] if half == 0 else mixed[:, 0:1]
            head = hp * 2 + half
            stat[0:WIN, :] = jnp.where(lane == head, peak + jnp.log(one), stat[0:WIN, :])
        ctx = jnp.where(lane < 64, pieces[0], pieces[1]).astype(BF16)
        old = ctx_ref[pl.ds(start, WIN), cols]
        ctx_ref[pl.ds(start, WIN), cols] = jnp.where(mine, ctx, old)
    lse_ref[pair] = jnp.transpose(stat[...])[0:16, :]


MESH = pl.DeviceIdType.MESH
HALF = 384
FF_DEV = 768
HOPS = [(way, hop) for hop in (1, 2, 3) for way in (1, -1)]


def front_kernel(
    small,
    len_ref,
    pos_ref,
    tok_ref,
    cot_ref,
    gain_one_ref,
    w_qkv_ref,
    w_proj_ref,
    gain_two_ref,
    wi_hbm,
    wb_hbm,
    qkv_hbm,
    ctx_hbm,
    lse_hbm,
    mid_hbm,
    g_hbm,
    x_hbm,
    wi_all,
    wb_all,
    qkv,
    ctx,
    lse,
    mid,
    g_sorted,
    x_sorted,
    held,
    stat,
    local_sems,
    send_sems,
    recv_sems,
    hop_send,
    hop_recv,
    pass_send,
    pass_recv,
):
    batch, ffn = lax.axis_index("batch"), lax.axis_index("ffn")
    z, y = batch // 2, batch % 2
    near, far = (batch, ffn ^ 1), (batch, ffn ^ 2)
    across = (batch ^ 1, ffn)

    barrier = pltpu.get_barrier_semaphore()
    for device in [near, far] + ([across] if small else []):
        pl.semaphore_signal(barrier, inc=1, device_id=device, device_id_type=MESH)
    if small:
        for way in (1, -1):

            @pl.when((z + way >= 0) & (z + way <= 3))
            def _(way=way):
                pl.semaphore_signal(
                    barrier, inc=1, device_id=(batch + 2 * way, ffn), device_id_type=MESH
                )

        inner = jnp.where((z == 0) | (z == 3), 1, 2)
        pl.semaphore_wait(barrier, 3 + inner)
    else:
        pl.semaphore_wait(barrier, 2)

    local_count = [0]
    waiting = []

    def local(src, dst):
        number = local_count[0]
        local_count[0] += 1
        copy = pltpu.make_async_copy(src, dst, local_sems.at[number])
        copy.start()
        waiting.append(copy)

    used = [0]

    def send(src, dst, device):
        number = used[0]
        used[0] += 1
        copy = pltpu.make_async_remote_copy(
            src_ref=src,
            dst_ref=dst,
            send_sem=send_sems.at[number],
            recv_sem=recv_sems.at[number],
            device_id=device,
            device_id_type=MESH,
        )
        copy.start()
        return copy

    part, whole = (wi_hbm, wb_hbm), (wi_all, wb_all)

    def valid(origin):
        return (origin >= 0) & (origin <= 3)

    def hop_copy(a, way, hop, origin, device):
        slot = whole[a].at[origin * 2 + y]
        number = HOPS.index((way, hop))
        return pltpu.make_async_remote_copy(
            src_ref=part[a] if hop == 1 else slot,
            dst_ref=slot,
            send_sem=hop_send.at[a, number],
            recv_sem=hop_recv.at[a, number],
            device_id=device,
            device_id_type=MESH,
        )

    def hop_go(a, hop, finish=False):
        for way in (1, -1):
            origin = z - way * (hop - 1)

            @pl.when(valid(origin) & valid(z + way))
            def _(way=way, origin=origin):
                copy = hop_copy(a, way, hop, origin, (batch + 2 * way, ffn))
                if finish:
                    copy.wait_send()
                else:
                    copy.start()

    def pass_copy(a, way, hop, origin, column):
        slot = whole[a].at[origin * 2 + column]
        number = HOPS.index((way, hop))
        return pltpu.make_async_remote_copy(
            src_ref=slot,
            dst_ref=slot,
            send_sem=pass_send.at[a, number],
            recv_sem=pass_recv.at[a, number],
            device_id=across,
            device_id_type=MESH,
        )

    def hop_came(a, hop):
        for way in (1, -1):
            origin = z - way * hop

            @pl.when(valid(origin))
            def _(way=way, origin=origin):
                hop_copy(a, way, hop, origin, (batch, ffn)).wait_recv()

        if hop < 3:
            hop_go(a, hop + 1)
        for way in (1, -1):
            origin = z - way * hop

            @pl.when(valid(origin))
            def _(way=way, origin=origin):
                pass_copy(a, way, hop, origin, y).start()

    own_over = []
    if small:
        for a in range(2):
            hop_go(a, 1)
            own_over.append(send(part[a], whole[a].at[batch], across))
            local(part[a], whole[a].at[batch])

    exchanged = []

    def sort_and_send(rows_ref, out_ref, out_hbm):
        pos = pos_ref[0:1, 0:ROWS]
        top = 0
        sent = []
        for size in SORT_TILES:
            want = top + lax.broadcasted_iota(I32, (size, ROWS), 0)
            hot = jnp.where(pos == want, 1.0, 0.0).astype(BF16)
            rows = pl.ds(top, size)
            out_ref[rows, :] = dot(hot, rows_ref[...]).astype(BF16)
            sent.append(send(out_ref.at[rows], out_hbm.at[2, rows], far))
            exchanged.append(send(out_ref.at[rows], out_hbm.at[1, rows], near))
            local(out_ref.at[rows], out_hbm.at[0, rows])
            top += size
        return sent

    def hand_on(sent, out_hbm):
        top = 0
        for copy, size in zip(sent, SORT_TILES):
            rows = pl.ds(top, size)
            copy.wait()
            exchanged.append(send(out_hbm.at[2, rows], out_hbm.at[3, rows], near))
            top += size

    held[1552:ROWS, :] = jnp.zeros((ROWS - 1552, D), BF16)
    held[0:TOK_DEV, :] = cot_ref[...]
    g_sent = sort_and_send(held, g_sorted, g_hbm)

    for i in range(3):
        top = min(TILE * (i + 1), TOK_DEV)
        rows = slice(TILE * i, top)
        normal, _ = norm_parts(tok_ref[rows, :].astype(F32))
        normed = (normal * gain_one_ref[...]).astype(BF16)
        qkv[rows, :] = dot(normed, w_qkv_ref[...]).astype(BF16)
    tail = slice(TOK_DEV, ROWS)
    qkv[tail, :] = jnp.zeros((ROWS - TOK_DEV, 3 * D), BF16)
    ctx[1552:ROWS, :] = jnp.zeros((ROWS - 1552, D), BF16)
    local(qkv, qkv_hbm)
    if small:
        hop_came(0, 1)

    @pl.loop(0, SEQ_DEV)
    def _(pair):
        attend_pair(pair, len_ref[pair], qkv, ctx, lse, stat)
        if small:

            @pl.when(pair == 1)
            def _():
                hop_came(1, 1)

            @pl.when(pair == 4)
            def _():
                hop_came(0, 2)

    local(ctx, ctx_hbm)
    local(lse, lse_hbm)
    for i in range(3):
        top = min(TILE * (i + 1), TOK_DEV)
        rows = slice(TILE * i, top)
        middle = tok_ref[rows, :].astype(F32) + dot(ctx[rows, :], w_proj_ref[...])
        mid[rows, :] = middle
        normal, _ = norm_parts(middle)
        held[rows, :] = (normal * gain_two_ref[...]).astype(BF16)
    local(mid, mid_hbm)
    if small:
        hop_came(1, 2)
    x_sent = sort_and_send(held, x_sorted, x_hbm)
    hand_on(g_sent, g_hbm)
    if small:
        hop_came(0, 3)
        hop_came(1, 3)
    hand_on(x_sent, x_hbm)
    for copy in exchanged + own_over:
        copy.wait()
    if small:
        for a in range(2):
            for hop in (1, 2, 3):
                hop_go(a, hop, finish=True)
            for way, hop in HOPS:
                origin = z - way * hop

                @pl.when(valid(origin))
                def _(a=a, way=way, hop=hop, origin=origin):
                    pass_copy(a, way, hop, origin, y).wait_send()
                    pass_copy(a, way, hop, origin, 1 - y).wait_recv()

    for copy in waiting:
        copy.wait()


def front(small, lengths, pos, tokens, cot, gain_one, w_qkv, w_proj, gain_two, wi, wb):
    vmem = pl.BlockSpec(memory_space=pltpu.VMEM)
    any_space = pl.BlockSpec(memory_space=pl.ANY)
    tiles = len(SORT_TILES)
    copies = 6 * tiles + 2
    dma = pltpu.SemaphoreType.DMA
    return pl.pallas_call(
        functools.partial(front_kernel, small),
        out_shape=(
            jax.ShapeDtypeStruct((ROWS, 3 * D), BF16),
            jax.ShapeDtypeStruct((ROWS, D), BF16),
            jax.ShapeDtypeStruct((SEQ_DEV, 16, 384), F32),
            jax.ShapeDtypeStruct((TOK_DEV, D), F32),
            jax.ShapeDtypeStruct((4, SORTED, D), BF16),
            jax.ShapeDtypeStruct((4, SORTED, D), BF16),
            jax.ShapeDtypeStruct((8, D, HALF), BF16),
            jax.ShapeDtypeStruct((8, HALF, D), BF16),
        ),
        in_specs=[pl.BlockSpec(memory_space=pltpu.SMEM)] + [vmem] * 7 + [any_space] * 2,
        out_specs=(any_space,) * 8,
        scratch_shapes=[
            pltpu.VMEM((ROWS, 3 * D), BF16),
            pltpu.VMEM((ROWS, D), BF16),
            pltpu.VMEM((SEQ_DEV, 16, 384), F32),
            pltpu.VMEM((TOK_DEV, D), F32),
            pltpu.VMEM((SORTED, D), BF16),
            pltpu.VMEM((SORTED, D), BF16),
            pltpu.VMEM((ROWS, D), BF16),
            pltpu.VMEM((384, 128), F32),
            dma((2 * tiles + 6,)),
            dma((copies,)),
            dma((copies,)),
            dma((2, 6)),
            dma((2, 6)),
            dma((2, 6)),
            dma((2, 6)),
        ],
        compiler_params=params(collective_id=1, has_side_effects=True),
        name="front",
    )(lengths, pos, tokens, cot, gain_one, w_qkv, w_proj, gain_two, wi, wb)


def gelu_both(u):
    below = 0.5 * (1.0 + lax.erf(u * (1.0 / math.sqrt(2.0))))
    density = jnp.exp(-0.5 * u * u) * (1.0 / math.sqrt(2.0 * math.pi))
    return u * below, below + u * density


MERGED = 2 * SORTED + 256


def expert_kernel(carried, offs_ref, hosts_ref, *refs):
    refs = list(refs)

    def take(count):
        head = refs[:count]
        del refs[:count]
        return head

    xs, gs = take(2), take(2)
    wi_hbm, wb_hbm = take(2)
    before = take(2) if carried else None
    outs, gxs = take(2), take(2)
    dwi_ref, dwb_ref = take(2)
    xm, gm, wi, wb, acc_i, acc_b, sems = refs
    expert = pl.program_id(0)
    slot = expert % 2

    def weight_copies(e, buffer, start):
        for p in range(2):
            host = hosts_ref[e * 2 + p]
            part = pl.ds(p * HALF, HALF)
            for number, source, target in (
                (0, wi_hbm.at[host], wi.at[buffer, :, part]),
                (1, wb_hbm.at[host], wb.at[buffer, part, :]),
            ):
                copy = pltpu.make_async_copy(source, target, sems.at[buffer, p, number])
                if start:
                    copy.start()
                else:
                    copy.wait()

    @pl.when(expert == 0)
    def _():
        weight_copies(0, 0, True)

    @pl.when(expert + 1 < EXPERTS)
    def _():
        weight_copies(expert + 1, 1 - slot, True)

    def blocks(count, act):
        @pl.loop(0, count)
        def _(i):
            act(pl.multiple_of(i * 16, 16))

    @pl.when(expert == 0)
    def _():
        for s in range(2):
            live = pl.multiple_of(offs_ref[s * 4 + EXPERTS], 16)

            def clear(at, s=s, live=live):
                rows = pl.ds(pl.multiple_of(live + at, 16), 16)
                outs[s][rows, :] = jnp.zeros((16, D), BF16)
                gxs[s][rows, :] = jnp.zeros((16, D), BF16)

            blocks((SORTED - live) // 16, clear)

    if carried:
        acc_i[...] = before[0][0].astype(F32)
        acc_b[...] = before[1][0].astype(F32)
    else:
        acc_i[...] = jnp.zeros_like(acc_i)
        acc_b[...] = jnp.zeros_like(acc_b)

    places = []
    total = jnp.int32(0)
    for s in range(2):
        first = pl.multiple_of(offs_ref[s * 4 + expert], 16)
        size = offs_ref[s * 4 + expert + 1] - first
        places.append((first, total, size // 16))

        def gather(at, s=s, first=first, total=total):
            here = pl.ds(pl.multiple_of(first + at, 16), 16)
            there = pl.ds(pl.multiple_of(total + at, 16), 16)
            xm[there, :] = xs[s][0, here, :]
            gm[there, :] = gs[s][0, here, :]

        blocks(size // 16, gather)
        total = total + size
    span = pl.multiple_of(total, 16)

    def blank(at):
        there = pl.ds(pl.multiple_of(span + at, 16), 16)
        xm[there, :] = jnp.zeros((16, D), BF16)
        gm[there, :] = jnp.zeros((16, D), BF16)

    blocks((256 - span % 256) // 16, blank)
    weight_copies(expert, slot, False)
    w_in, w_back = wi.at[slot], wb.at[slot]

    @pl.loop(0, (span + 255) // 256)
    def _(i):
        rows = pl.ds(pl.multiple_of(i * 256, 256), 256)
        x, g = xm[rows, :], gm[rows, :]
        inner = dot(x, w_in[...])
        hidden, slope = gelu_both(inner)
        hidden = hidden.astype(BF16)
        grad_hidden = dot(g, w_back[...], CONTRACT_LANES).astype(BF16)
        grad_inner = (grad_hidden.astype(F32) * slope).astype(BF16)
        xm[rows, :] = dot(hidden, w_back[...]).astype(BF16)
        gm[rows, :] = dot(grad_inner, w_in[...], CONTRACT_LANES).astype(BF16)
        acc_b[...] += dot(hidden, g, CONTRACT_ROWS)
        acc_i[...] += dot(x, grad_inner, CONTRACT_ROWS)

    dwi_ref[0] = acc_i[...].astype(BF16)
    dwb_ref[0] = acc_b[...].astype(BF16)
    for s in range(2):
        first, base, count = places[s]

        def hand_back(at, s=s, first=first, base=base):
            here = pl.ds(pl.multiple_of(first + at, 16), 16)
            there = pl.ds(pl.multiple_of(base + at, 16), 16)
            outs[s][here, :] = xm[there, :]
            gxs[s][here, :] = gm[there, :]

        blocks(count, hand_back)


def experts(sources, offs, hosts, x, g, wi, wb, before=None):
    whole = once((SORTED, D))
    any_space = pl.BlockSpec(memory_space=pl.ANY)
    weight = pl.BlockSpec((1, D, FF_DEV), lambda e, *_: (e, 0, 0))
    carried = before is not None
    rows = jax.ShapeDtypeStruct((SORTED, D), BF16)
    grad = jax.ShapeDtypeStruct((EXPERTS, D, FF_DEV), BF16)

    def source(i):
        return pl.BlockSpec(
            (1, SORTED, D), lambda e, *_: (i, 0, 0), pipeline_mode=pl.Buffered(1)
        )

    picked = [source(i) for i in sources]
    return pl.pallas_call(
        functools.partial(expert_kernel, carried),
        grid_spec=pltpu.PrefetchScalarGridSpec(
            num_scalar_prefetch=2,
            grid=(EXPERTS,),
            in_specs=picked + picked + [any_space] * 2 + [weight] * (2 * carried),
            out_specs=[whole] * 4 + [weight] * 2,
            scratch_shapes=[
                pltpu.VMEM((MERGED, D), BF16),
                pltpu.VMEM((MERGED, D), BF16),
                pltpu.VMEM((2, D, FF_DEV), BF16),
                pltpu.VMEM((2, FF_DEV, D), BF16),
                pltpu.VMEM((D, FF_DEV), F32),
                pltpu.VMEM((FF_DEV, D), F32),
                pltpu.SemaphoreType.DMA((2, 2, 2)),
            ],
        ),
        out_shape=(rows,) * 4 + (grad,) * 2,
        compiler_params=params(),
        cost_estimate=cost(24 * SORTED * D * FF_DEV, 16 * SORTED * D),
        name="experts",
    )(offs, hosts, x, x, g, g, wi, wb, *(before or ()))


def unsort(pos_col, src):
    want = lax.broadcasted_iota(I32, (pos_col.shape[0], SORTED), 1)
    hot = jnp.where(pos_col == want, 1.0, 0.0).astype(BF16)
    return dot(hot, src)


def back_kernel(
    a_ref,
    b_ref,
    c_ref,
    pos_ref,
    mid_ref,
    cot_ref,
    gain_ref,
    ctx_ref,
    w_ref,
    gm_ref,
    gctx_ref,
    dw_ref,
    dg_ref,
    total,
    acc,
):
    step = pl.program_id(0)

    @pl.when(step == 0)
    def _():
        both = a_ref[...].astype(F32) + b_ref[...].astype(F32) + c_ref[...].astype(F32)
        total[...] = both.astype(BF16)
        acc[...] = jnp.zeros_like(acc)
        dg_ref[...] = jnp.zeros_like(dg_ref)

    keep = row_mask(step * TILE, TILE, TOK_DEV)
    grad_normed = unsort(pos_ref[...], total[...])
    middle = jnp.where(keep, mid_ref[...], 0.0)
    normal, inverse = norm_parts(middle)
    dg_ref[...] += jnp.sum(grad_normed * normal, axis=0, keepdims=True)
    part = norm_pull(grad_normed, gain_ref[...], normal, inverse)
    grad_middle = jnp.where(keep, cot_ref[...].astype(F32) + part, 0.0)
    gm_ref[...] = grad_middle
    low = grad_middle.astype(BF16)
    acc[...] += dot(ctx_ref[...], low, CONTRACT_ROWS)
    dw_ref[...] = acc[...].astype(BF16)
    gctx_ref[...] = dot(low, w_ref[...], CONTRACT_LANES).astype(BF16)


def back_rows(a, b, c, pos_col, middle, cot, gain, ctx, w_proj):
    tile = pl.BlockSpec((TILE, D), lambda i: (i, 0))
    return pl.pallas_call(
        back_kernel,
        grid=(ROWS // TILE,),
        out_shape=(
            jax.ShapeDtypeStruct((TOK_DEV, D), F32),
            jax.ShapeDtypeStruct((ROWS, D), BF16),
            jax.ShapeDtypeStruct((D, D), BF16),
            jax.ShapeDtypeStruct((1, D), F32),
        ),
        in_specs=[
            once((SORTED, D)),
            once((SORTED, D)),
            once((SORTED, D)),
            pl.BlockSpec((TILE, 1), lambda i: (i, 0)),
            tile,
            tile,
            full((1, D)),
            tile,
            once((D, D)),
        ],
        out_specs=(tile, tile, full((D, D)), full((1, D))),
        scratch_shapes=[pltpu.VMEM((SORTED, D), BF16), pltpu.VMEM((D, D), F32)],
        compiler_params=params(),
        cost_estimate=cost(2 * ROWS * D * (SORTED + 2 * D), 24 * ROWS * D),
        name="back",
    )(a, b, c, pos_col, middle, cot, gain, ctx, w_proj)


def finish_kernel(a_ref, b_ref, c_ref, pos_ref, mid_ref, out_ref, total):
    @pl.when(pl.program_id(0) == 0)
    def _():
        both = a_ref[...].astype(F32) + b_ref[...].astype(F32) + c_ref[...].astype(F32)
        total[...] = both.astype(BF16)

    out_ref[...] = mid_ref[...] + unsort(pos_ref[...], total[...])


def finish_rows(a, b, c, pos_col, middle):
    tile = pl.BlockSpec((TILE, D), lambda i: (i, 0))
    return pl.pallas_call(
        finish_kernel,
        grid=(ROWS // TILE,),
        out_shape=jax.ShapeDtypeStruct((TOK_DEV, D), F32),
        in_specs=[
            once((SORTED, D)),
            once((SORTED, D)),
            once((SORTED, D)),
            pl.BlockSpec((TILE, 1), lambda i: (i, 0)),
            tile,
        ],
        out_specs=tile,
        scratch_shapes=[pltpu.VMEM((SORTED, D), BF16)],
        compiler_params=params(),
        cost_estimate=cost(2 * ROWS * D * SORTED, 14 * ROWS * D),
        name="finish",
    )(a, b, c, pos_col, middle)


def attend_back_kernel(len_ref, qkv_ref, gctx_ref, lse_ref, out_ref):
    pair = pl.program_id(0)
    start, skip = window(pair)
    start = pl.multiple_of(start, 16)

    @pl.when(pair == 0)
    def _():
        out_ref[...] = jnp.zeros_like(out_ref)

    row = lax.broadcasted_iota(I32, (WIN, 1), 0)
    mine = (row >= skip) & (row < skip + SEQ_LEN)
    bias = jnp.where((row >= skip) & (row < skip + PATCHES + len_ref[pair]), 0.0, -1e30)
    lane = lax.broadcasted_iota(I32, (WIN, 128), 1)
    scale = jnp.asarray(HEAD_DIM**-0.5, BF16)
    for hp in range(HEADS // 2):
        spots = [slice(part * D + hp * 128, part * D + hp * 128 + 128) for part in range(3)]
        q, k, v = [qkv_ref[pl.ds(start, WIN), spot] for spot in spots]
        q = q * scale
        ks = k * scale
        go = gctx_ref[pl.ds(start, WIN), hp * 128 : hp * 128 + 128]
        q = jnp.where(mine, q, jnp.zeros_like(q))
        go = jnp.where(mine, go, jnp.zeros_like(go))
        grads = []
        for half in range(2):
            head = hp * 2 + half
            inside = (lane < 64) if half == 0 else (lane >= 64)
            qh = jnp.where(inside, q, jnp.zeros_like(q))
            gh = jnp.where(inside, go, jnp.zeros_like(go))
            scores = dot(k, qh, CONTRACT_LANES)
            probs = jnp.exp(scores + bias - lse_ref[0, head : head + 1, 0:WIN])
            grad_probs = dot(v, gh, CONTRACT_LANES)
            delta = jnp.sum(probs * grad_probs, axis=0, keepdims=True)
            grad_scores = (probs * (grad_probs - delta)).astype(BF16)
            grad_v = dot(probs.astype(BF16), go)
            grad_k = dot(grad_scores, q)
            grad_q = dot(grad_scores, ks, CONTRACT_ROWS)
            grads.append((grad_q, grad_k, grad_v))
        for spot, low, high in zip(spots, grads[0], grads[1]):
            new = jnp.where(lane < 64, low, high).astype(BF16)
            old = out_ref[pl.ds(start, WIN), spot]
            out_ref[pl.ds(start, WIN), spot] = jnp.where(mine, new, old)


def attend_back(qkv, gctx, lse, lengths):
    return pl.pallas_call(
        attend_back_kernel,
        grid=(SEQ_DEV,),
        out_shape=jax.ShapeDtypeStruct((ROWS, 3 * D), BF16),
        in_specs=[
            pl.BlockSpec(memory_space=pltpu.SMEM),
            once((ROWS, 3 * D)),
            once((ROWS, D)),
            pl.BlockSpec((1, 16, 384), lambda s: (s, 0, 0)),
        ],
        out_specs=full((ROWS, 3 * D)),
        compiler_params=params(),
        cost_estimate=cost(72 * 10 * WIN * 384 * 128, 2 * ROWS * D * 7),
        name="attend_back",
    )(lengths, qkv, gctx, lse)


def first_back_kernel(tok_ref, gain_ref, gq_ref, w_ref, gm_ref, ig_ref, dw_ref, dg_ref, acc):
    step = pl.program_id(0)

    @pl.when(step == 0)
    def _():
        acc[...] = jnp.zeros_like(acc)
        dg_ref[...] = jnp.zeros_like(dg_ref)

    keep = row_mask(step * TILE, TILE, TOK_DEV)
    tokens = jnp.where(keep, tok_ref[...].astype(F32), 0.0)
    normal, inverse = norm_parts(tokens)
    normed = (normal * gain_ref[...]).astype(BF16)
    grad_qkv = gq_ref[...]
    acc[...] += dot(normed, grad_qkv, CONTRACT_ROWS)

    @pl.when(step == ROWS // TILE - 1)
    def _():
        dw_ref[...] = acc[...].astype(BF16)

    grad_normed = dot(grad_qkv, w_ref[...], CONTRACT_LANES)
    dg_ref[...] += jnp.sum(grad_normed * normal, axis=0, keepdims=True)
    ig_ref[...] = gm_ref[...] + norm_pull(grad_normed, gain_ref[...], normal, inverse)


def first_back(tokens, gain, grad_qkv, w_qkv, grad_middle):
    tile = pl.BlockSpec((TILE, D), lambda i: (i, 0))
    return pl.pallas_call(
        first_back_kernel,
        grid=(ROWS // TILE,),
        out_shape=(
            jax.ShapeDtypeStruct((TOK_DEV, D), F32),
            jax.ShapeDtypeStruct((D, 3 * D), BF16),
            jax.ShapeDtypeStruct((1, D), F32),
        ),
        in_specs=[
            tile,
            full((1, D)),
            pl.BlockSpec((TILE, 3 * D), lambda i: (i, 0)),
            once((D, 3 * D)),
            tile,
        ],
        out_specs=(tile, full((D, 3 * D)), full((1, D))),
        scratch_shapes=[pltpu.VMEM((D, 3 * D), F32)],
        compiler_params=params(),
        cost_estimate=cost(4 * ROWS * D * 3 * D, 16 * ROWS * D),
        name="first_back",
    )(tokens, gain, grad_qkv, w_qkv, grad_middle)


def swap(rows, bit):
    pairs = [(f, f ^ bit) for f in range(4)]
    return lax.ppermute(rows, "ffn", pairs)


def spread(rows):
    near = swap(rows, 1)
    far = swap(rows, 2)
    return [rows, near, far, swap(far, 1)]


def cross(rows, bits):
    return lax.ppermute(rows, "batch", [(b, b ^ bits) for b in range(8)])


def tie(value, *others):
    return lax.optimization_barrier((value, *others))[0]


CHUNK = D // 8


Z_GROUPS = [[0, 2, 4, 6], [1, 3, 5, 7]]


def deliver_kernel(gm_ref, in_ref, back_ref, out_ref):
    for b in range(8):
        e = gm_ref[b]
        out_ref[b, 0] = in_ref[e]
        total = sum(back_ref[e, z].astype(F32) for z in range(4))
        out_ref[b, 1] = total.astype(BF16)


def deliver(grad_in, grad_back, group_map):
    vmem = pl.BlockSpec(memory_space=pltpu.VMEM)
    return pl.pallas_call(
        deliver_kernel,
        out_shape=jax.ShapeDtypeStruct((8, 2, CHUNK, D), BF16),
        in_specs=[pl.BlockSpec(memory_space=pltpu.SMEM), vmem, vmem],
        out_specs=vmem,
        compiler_params=params(),
        cost_estimate=cost(0, 6 << 20),
        name="deliver",
    )(group_map, grad_in, grad_back)


def cross_y(dwb, own):
    y = own % 2
    cut = dwb.reshape(EXPERTS, 4, 2, CHUNK, D)
    there = cross(lax.dynamic_index_in_dim(cut, 1 - y, 2, keepdims=False), 1)
    mine = lax.dynamic_index_in_dim(cut, y, 2, keepdims=False)
    return (mine.astype(F32) + there.astype(F32)).astype(BF16)


def cross_z(rows):
    return lax.all_to_all(
        rows, "batch", split_axis=1, concat_axis=1, axis_index_groups=Z_GROUPS, tiled=True
    )


AXES = ("x", "y", "z")
ORDERS = (("x", "y", "z"), ("y", "z", "x"), ("z", "x", "y"))
WIDE = 4 * D
COLOUR = WIDE // 3
QUARTER = COLOUR // 4
GAIN_ROWS = 8


def total_kernel(
    qkv_ref, proj_ref, gain_ref, out_ref, gain_out_ref, near, held, came, gain_in, send_sems, recv_sems
):
    batch, ffn = lax.axis_index("batch"), lax.axis_index("ffn")
    z, y, x, c = batch // 2, batch % 2, ffn // 2, ffn % 2
    place = {"x": x, "y": y, "z": z}

    def peer(axis, k=1):
        if axis == "c":
            return (batch, ffn ^ 1)
        if axis == "x":
            return (batch, ffn ^ 2)
        if axis == "y":
            return (batch ^ 1, ffn)
        return (batch ^ (2 * k), ffn)

    peers = [peer("c"), peer("x"), peer("y")] + [peer("z", k) for k in (1, 2, 3)]
    barrier = pltpu.get_barrier_semaphore()
    for device in peers:
        pl.semaphore_signal(barrier, inc=1, device_id=device, device_id_type=pl.DeviceIdType.MESH)
    pl.semaphore_wait(barrier, len(peers))

    used = [0]

    def send(src, dst, device):
        number = used[0]
        used[0] += 1
        copy = pltpu.make_async_remote_copy(
            src_ref=src,
            dst_ref=dst,
            send_sem=send_sems.at[number],
            recv_sem=recv_sems.at[number],
            device_id=device,
            device_id_type=pl.DeviceIdType.MESH,
        )
        copy.start()
        return copy

    give = pl.ds(pl.multiple_of((1 - c) * 384, 16), 384)
    keep = pl.ds(pl.multiple_of(c * 384, 16), 384)
    first = [
        send(qkv_ref.at[give, :], near.at[:, 0 : 3 * D], peer("c")),
        send(proj_ref.at[give, :], near.at[:, 3 * D : WIDE], peer("c")),
        send(gain_ref, gain_in.at[0], peer("c")),
    ]
    for copy in first:
        copy.wait()
    held[:, 0 : 3 * D] = (
        qkv_ref[keep, :].astype(F32) + near[:, 0 : 3 * D].astype(F32)
    ).astype(BF16)
    held[:, 3 * D : WIDE] = (
        proj_ref[keep, :].astype(F32) + near[:, 3 * D : WIDE].astype(F32)
    ).astype(BF16)
    gain_out_ref[...] = gain_ref[...] + gain_in[0]

    top = [0, 0, 0]
    left = [COLOUR * i for i in range(3)]
    rows, cols = [384] * 3, [COLOUR] * 3
    gain_slot = 1
    for step in range(3):
        flying = []
        for i in range(3):
            axis = ORDERS[i][step]
            if axis == "z":
                for k in (1, 2, 3):
                    there = pl.ds(pl.multiple_of(left[i] + (z ^ k) * QUARTER, 128), QUARTER)
                    live = pl.ds(top[i], rows[i])
                    flying.append(
                        send(
                            held.at[live, there],
                            came.at[i, k - 1, 0 : rows[i], 0:QUARTER],
                            peer("z", k),
                        )
                    )
            else:
                half = rows[i] // 2
                there = pl.ds(pl.multiple_of(top[i] + (1 - place[axis]) * half, 16), half)
                flying.append(
                    send(
                        held.at[there, pl.ds(left[i], cols[i])],
                        came.at[i, 3 if axis == "x" else 4, 0:half, 0 : cols[i]],
                        peer(axis),
                    )
                )
        gain_axis = AXES[step]
        if gain_axis == "z":
            flying += [send(gain_out_ref, gain_in.at[gain_slot + k - 1], peer("z", k)) for k in (1, 2, 3)]
        else:
            flying.append(send(gain_out_ref, gain_in.at[gain_slot], peer(gain_axis)))
        for copy in flying:
            copy.wait()
        for i in range(3):
            axis = ORDERS[i][step]
            if axis == "z":
                left[i] = pl.multiple_of(left[i] + z * QUARTER, 128)
                cols[i] = QUARTER
                spots = (0, 1, 2)
            else:
                rows[i] = rows[i] // 2
                top[i] = pl.multiple_of(top[i] + place[axis] * rows[i], 16)
                spots = (3,) if axis == "x" else (4,)
            spot = (pl.ds(top[i], rows[i]), pl.ds(left[i], cols[i]))
            total = held[spot].astype(F32)
            for number in spots:
                total = total + came[i, number, 0 : rows[i], 0 : cols[i]].astype(F32)
            held[spot] = total.astype(BF16)
        if gain_axis == "z":
            gain_out_ref[...] = (
                (gain_out_ref[...] + gain_in[gain_slot])
                + gain_in[gain_slot + 1]
                + gain_in[gain_slot + 2]
            )
        else:
            gain_out_ref[...] = gain_out_ref[...] + gain_in[gain_slot]
            gain_slot += 1

    base = c * 384
    for i in range(3):
        spot = (pl.ds(top[i], rows[i]), pl.ds(left[i], cols[i]))
        out_ref[pl.ds(pl.multiple_of(base + top[i], 16), rows[i]), spot[1]] = held[spot]
    for step in (2, 1, 0):
        flying = []
        for i in range(3):
            axis = ORDERS[i][step]
            mine = out_ref.at[
                pl.ds(pl.multiple_of(base + top[i], 16), rows[i]), pl.ds(left[i], cols[i])
            ]
            for k in (1, 2, 3) if axis == "z" else (1,):
                flying.append(send(mine, mine, peer(axis, k)))
        for copy in flying:
            copy.wait()
        for i in range(3):
            axis = ORDERS[i][step]
            if axis == "z":
                left[i] = COLOUR * i
                cols[i] = COLOUR
            else:
                top[i] = top[i] - place[axis] * rows[i]
                rows[i] = rows[i] * 2
                if rows[i] == 384:
                    top[i] = 0
    mine = out_ref.at[pl.ds(pl.multiple_of(base, 16), 384), :]
    send(mine, mine, peer("c")).wait()


COPIES = 3 + 2 * (2 + 3 + 2 + 3 + 2 + 3) // 2 + 5 + 15 + 1


def total_over_all(dw_qkv, dw_proj, gains):
    vmem = pl.BlockSpec(memory_space=pltpu.VMEM)
    return pl.pallas_call(
        total_kernel,
        out_shape=(
            jax.ShapeDtypeStruct((D, WIDE), BF16),
            jax.ShapeDtypeStruct((GAIN_ROWS, D), F32),
        ),
        in_specs=[vmem] * 3,
        out_specs=(vmem, vmem),
        scratch_shapes=[
            pltpu.VMEM((384, WIDE), BF16),
            pltpu.VMEM((384, WIDE), BF16),
            pltpu.VMEM((3, 5, 384, COLOUR), BF16),
            pltpu.VMEM((6, GAIN_ROWS, D), F32),
            pltpu.SemaphoreType.DMA((COPIES,)),
            pltpu.SemaphoreType.DMA((COPIES,)),
        ],
        compiler_params=params(collective_id=0, has_side_effects=True),
        name="total",
    )(dw_qkv, dw_proj, gains)


def body(
    tokens,
    text_lengths,
    routes,
    group_map,
    gain_one,
    w_qkv,
    w_proj,
    gain_two,
    w_in,
    w_back,
    cotangent,
):
    n_batch = lax.axis_size("batch")
    own = lax.axis_index("batch")
    gain_one = gain_one.reshape(1, D)
    gain_two = gain_two.reshape(1, D)
    own_expert = group_map[own]
    order = jnp.arange(n_batch, dtype=I32)
    rank = jnp.sum(jnp.where((group_map == own_expert) & (order < own), 1, 0))
    part = jnp.minimum(rank, 1)
    hosting = group_map[None, :] == jnp.arange(EXPERTS, dtype=I32)[:, None]
    first_host = jnp.min(jnp.where(hosting, order[None, :], n_batch), axis=1)
    later = hosting & (order[None, :] > first_host[:, None])
    second_host = jnp.min(jnp.where(later, order[None, :], n_batch), axis=1)
    hosts = jnp.stack([first_host, second_host], axis=1).reshape(2 * EXPERTS)

    wi_part = lax.dynamic_slice(w_in[0], (0, part * HALF), (D, HALF))
    wb_part = lax.dynamic_slice(w_back[0], (part * HALF, 0), (HALF, D))
    small = n_batch == 8

    routes_row = jnp.pad(routes.reshape(1, TOK_DEV), ((0, 0), (0, LANES - TOK_DEV)))
    pos, offs = route_rows(routes_row, group_map)
    pos_col = pos.reshape(LANES, 1)[0:ROWS]
    offs_at = [o[0, 0:4] for o in spread(offs)]

    qkv, context, lse, middle, g, x, wi_all, wb_all = front(
        small, text_lengths, pos, tokens, cotangent, gain_one, w_qkv, w_proj, gain_two, wi_part, wb_part
    )
    if not small:
        wi_all = lax.all_gather(wi_part, "batch", axis=0)
        wb_all = lax.all_gather(wb_part, "batch", axis=0)

    def run(pair, x, before):
        return experts(
            pair,
            jnp.concatenate([offs_at[i] for i in pair]),
            hosts,
            x,
            g,
            wi_all,
            wb_all,
            before,
        )

    def add(a, b):
        return (a.astype(F32) + b.astype(F32)).astype(BF16)

    out2, out3, gx2, gx3, dwi, dwb = run((2, 3), x, None)
    gx_half = add(gx2, swap(gx3, 1))
    gx_far = swap(gx_half, 2)
    out0, out1, gx0, gx1, dwi, dwb = run((0, 1), tie(x, gx_half), (dwi, dwb))
    gx_near = swap(gx1, 1)
    out_near = swap(out1, 1)
    out_far = swap(tie(add(out2, swap(out3, 1)), gx_far), 2)
    if small:
        share_in = lax.psum_scatter(dwi, "batch", scatter_dimension=1, tiled=True)
        share_back = cross_y(dwb, own)

    grad_middle, gctx, dw_proj, dg_two = back_rows(
        gx0, gx_near, gx_far, pos_col, middle, cotangent, gain_two, context, w_proj
    )
    if small:
        gctx = tie(gctx, share_back)
        share_back = cross_z(share_back)
    grad_qkv = attend_back(qkv, gctx, lse, text_lengths)
    input_grad, dw_qkv, dg_one = first_back(tokens, gain_one, grad_qkv, w_qkv, grad_middle)
    block_out = finish_rows(out0, out_near, out_far, pos_col, middle)

    if small:
        share_in = tie(share_in, grad_qkv)
        pieces = lax.all_to_all(
            deliver(share_in, share_back, group_map),
            "batch",
            split_axis=0,
            concat_axis=0,
            tiled=True,
        )
        grad_w_in = pieces[:, 0].reshape(1, D, D).astype(F32)
        grad_w_back = pieces[:, 1].reshape(1, D, D).astype(F32)
        gains = jnp.concatenate([dg_one, dg_two, jnp.zeros((GAIN_ROWS - 2, D), F32)], axis=0)
        summed, gains = total_over_all(dw_qkv, dw_proj, gains)
        summed_qkv, summed_proj = summed[:, 0 : 3 * D], summed[:, 3 * D : WIDE]
    else:

        def settle_any(grad):
            share = lax.psum_scatter(grad, "batch", scatter_dimension=1, tiled=True)
            whole = lax.all_gather(share, "batch", axis=1, tiled=True)
            return lax.dynamic_index_in_dim(whole, own_expert, 0, keepdims=True).astype(F32)

        grad_w_in = settle_any(dwi)
        grad_w_back = settle_any(dwb)
        summed_qkv, summed_proj = lax.psum((dw_qkv, dw_proj), ("batch", "ffn"))
        gains = lax.psum(jnp.concatenate([dg_one, dg_two], axis=0), ("batch", "ffn"))
    return (
        block_out,
        input_grad,
        gains[0],
        summed_qkv.astype(F32),
        summed_proj.astype(F32),
        gains[1],
        grad_w_in,
        grad_w_back,
    )


def solution(mesh):
    placed = (
        P(("batch", "ffn"), None),
        P(("batch", "ffn")),
        P(("batch", "ffn"), None),
        P(),
        P(),
        P(),
        P(),
        P(),
        P("batch", None, "ffn"),
        P("batch", "ffn", None),
        P(("batch", "ffn"), None),
    )
    return jax.shard_map(
        body,
        mesh=mesh,
        in_specs=placed,
        out_specs=(
            P(("batch", "ffn"), None),
            P(("batch", "ffn"), None),
            P(),
            P(),
            P(),
            P(),
            P("batch", None, "ffn"),
            P("batch", "ffn", None),
        ),
        check_vma=False,
    )
```

```python
import functools
import math

import jax
import jax.numpy as jnp
from jax import lax
from jax.experimental import pallas as pl
from jax.experimental.pallas import tpu as pltpu
from jax.sharding import PartitionSpec as P

D = 768
HEADS = 12
HEAD_DIM = 64
EXPERTS = 3
PATCHES = 197
SEQ_DEV = 6
SEQ_LEN = 261
TOK_DEV = 1566
ROWS = 1584
SORTED = 1616
WIN = 288
TILE = 528
LANES = 1664
EPS = 1e-05
F32 = jnp.float32
BF16 = jnp.bfloat16
I32 = jnp.int32
CONTRACT_LANES = (((1,), (1,)), ((), ()))
CONTRACT_ROWS = (((0,), (0,)), ((), ()))


def params(**extra):
    return pltpu.CompilerParams(vmem_limit_bytes=60 << 20, **extra)


def cost(flops, moved):
    return pl.CostEstimate(flops=int(flops), bytes_accessed=int(moved), transcendentals=0)


def dot(a, b, dims=(((1,), (0,)), ((), ()))):
    return lax.dot_general(a, b, dims, preferred_element_type=F32)


def full(shape):
    zeros = (0,) * len(shape)
    return pl.BlockSpec(shape, lambda *_: zeros)


def once(shape):
    zeros = (0,) * len(shape)
    return pl.BlockSpec(shape, lambda *_: zeros, pipeline_mode=pl.Buffered(1))


def row_mask(start, rows, limit):
    return start + lax.broadcasted_iota(I32, (rows, 1), 0) < limit


def norm_parts(values):
    average = jnp.mean(values, axis=-1, keepdims=True)
    centred = values - average
    variance = jnp.mean(centred * centred, axis=-1, keepdims=True)
    inverse = lax.rsqrt(variance + EPS)
    return centred * inverse, inverse


def norm_pull(grad_normed, gain, normal, inverse):
    scaled = grad_normed * gain
    mean_grad = jnp.mean(scaled, axis=-1, keepdims=True)
    mean_proj = jnp.mean(scaled * normal, axis=-1, keepdims=True)
    return inverse * (scaled - mean_grad - normal * mean_proj)


def route_kernel(n_batch, gm_ref, routes_ref, pos_ref, offs_ref):
    routes = routes_ref[...]
    lane = lax.broadcasted_iota(I32, (8, LANES), 1)
    sub = lax.broadcasted_iota(I32, (8, LANES), 0)
    expert = jnp.zeros((1, LANES), I32)
    for b in range(n_batch):
        expert = jnp.where(routes == b, gm_ref[b], expert)
    live = lane < TOK_DEV
    hot = jnp.where((jnp.broadcast_to(expert, (8, LANES)) == sub) & live, 1, 0)
    count = hot
    step = 1
    while step < LANES:
        count = count + jnp.where(lane >= step, pltpu.roll(count, step, 1), 0)
        step *= 2
    totals = [jnp.sum(hot[e : e + 1, :], axis=1, keepdims=True) for e in range(EXPERTS)]
    starts = [jnp.zeros((1, 1), I32)]
    for e in range(EXPERTS):
        starts.append(starts[-1] + (totals[e] + 15) // 16 * 16)
    pos = jnp.zeros((1, LANES), I32)
    for e in range(EXPERTS):
        pos = pos + jnp.where(hot[e : e + 1, :] > 0, count[e : e + 1, :] - 1 + starts[e], 0)
    pos_ref[...] = jnp.where(live[0:1, :], pos, -1)
    slot = lax.broadcasted_iota(I32, (1, 128), 1)
    offs = jnp.zeros((1, 128), I32)
    for e in range(EXPERTS + 1):
        offs = jnp.where(slot == e, starts[e], offs)
    offs_ref[...] = offs


def route_rows(routes_row, group_map):
    n_batch = group_map.shape[0]
    return pl.pallas_call(
        functools.partial(route_kernel, n_batch),
        out_shape=(
            jax.ShapeDtypeStruct((1, LANES), I32),
            jax.ShapeDtypeStruct((1, 128), I32),
        ),
        in_specs=[
            pl.BlockSpec(memory_space=pltpu.SMEM),
            pl.BlockSpec(memory_space=pltpu.VMEM),
        ],
        out_specs=(
            pl.BlockSpec(memory_space=pltpu.VMEM),
            pl.BlockSpec(memory_space=pltpu.VMEM),
        ),
        compiler_params=params(),
        name="route",
    )(group_map, routes_row)


SORT_TILES = (336, 336, 336, 336, 272)


def window(pair):
    first = pair * SEQ_LEN
    start = first // 16 * 16
    return start, first - start


def attend_pair(pair, length, qkv_ref, ctx_ref, lse_ref, stat):
    start, skip = window(pair)
    start = pl.multiple_of(start, 16)
    key = lax.broadcasted_iota(I32, (1, WIN), 1)
    seen = (key >= skip) & (key < skip + PATCHES + length)
    bias = jnp.where(seen, 0.0, -1e30)
    row = lax.broadcasted_iota(I32, (WIN, 1), 0)
    mine = (row >= skip) & (row < skip + SEQ_LEN)
    lane = lax.broadcasted_iota(I32, (WIN, 128), 1)
    stat[...] = jnp.zeros_like(stat)
    for hp in range(HEADS // 2):
        cols = slice(hp * 128, hp * 128 + 128)
        q = qkv_ref[pl.ds(start, WIN), hp * 128 : hp * 128 + 128]
        k = qkv_ref[pl.ds(start, WIN), D + hp * 128 : D + hp * 128 + 128]
        v = qkv_ref[pl.ds(start, WIN), 2 * D + hp * 128 : 2 * D + hp * 128 + 128]
        q = q * jnp.asarray(HEAD_DIM**-0.5, BF16)
        pieces = []
        for half in range(2):
            inside = (lane < 64) if half == 0 else (lane >= 64)
            qh = jnp.where(inside, q, jnp.zeros_like(q))
            scores = dot(qh, k, CONTRACT_LANES) + bias
            peak = jnp.max(scores, axis=1, keepdims=True)
            weight = jnp.exp(scores - peak).astype(BF16)
            vh = jnp.where(inside, v, jnp.ones_like(v))
            mixed = dot(weight, vh)
            total = pltpu.roll(mixed, 64, 1)
            pieces.append(mixed / total)
            one = total[:, 0:1] if half == 0 else mixed[:, 0:1]
            head = hp * 2 + half
            stat[0:WIN, :] = jnp.where(lane == head, peak + jnp.log(one), stat[0:WIN, :])
        ctx = jnp.where(lane < 64, pieces[0], pieces[1]).astype(BF16)
        old = ctx_ref[pl.ds(start, WIN), cols]
        ctx_ref[pl.ds(start, WIN), cols] = jnp.where(mine, ctx, old)
    lse_ref[pair] = jnp.transpose(stat[...])[0:16, :]


MESH = pl.DeviceIdType.MESH
HALF = 384
FF_DEV = 768
HOPS = [(way, hop) for hop in (1, 2, 3) for way in (1, -1)]


def front_kernel(
    small,
    len_ref,
    pos_ref,
    tok_ref,
    cot_ref,
    gain_one_ref,
    w_qkv_ref,
    w_proj_ref,
    gain_two_ref,
    wi_hbm,
    wb_hbm,
    qkv_hbm,
    ctx_hbm,
    lse_hbm,
    mid_hbm,
    g_hbm,
    x_hbm,
    wi_all,
    wb_all,
    qkv,
    ctx,
    lse,
    mid,
    g_sorted,
    x_sorted,
    held,
    stat,
    local_sems,
    send_sems,
    recv_sems,
    hop_send,
    hop_recv,
    pass_send,
    pass_recv,
):
    batch, ffn = lax.axis_index("batch"), lax.axis_index("ffn")
    z, y = batch // 2, batch % 2
    near, far = (batch, ffn ^ 1), (batch, ffn ^ 2)
    across = (batch ^ 1, ffn)

    barrier = pltpu.get_barrier_semaphore()
    for device in [near, far] + ([across] if small else []):
        pl.semaphore_signal(barrier, inc=1, device_id=device, device_id_type=MESH)
    if small:
        for way in (1, -1):

            @pl.when((z + way >= 0) & (z + way <= 3))
            def _(way=way):
                pl.semaphore_signal(
                    barrier, inc=1, device_id=(batch + 2 * way, ffn), device_id_type=MESH
                )

        inner = jnp.where((z == 0) | (z == 3), 1, 2)
        pl.semaphore_wait(barrier, 3 + inner)
    else:
        pl.semaphore_wait(barrier, 2)

    local_count = [0]
    waiting = []

    def local(src, dst):
        number = local_count[0]
        local_count[0] += 1
        copy = pltpu.make_async_copy(src, dst, local_sems.at[number])
        copy.start()
        waiting.append(copy)

    used = [0]

    def send(src, dst, device):
        number = used[0]
        used[0] += 1
        copy = pltpu.make_async_remote_copy(
            src_ref=src,
            dst_ref=dst,
            send_sem=send_sems.at[number],
            recv_sem=recv_sems.at[number],
            device_id=device,
            device_id_type=MESH,
        )
        copy.start()
        return copy

    part, whole = (wi_hbm, wb_hbm), (wi_all, wb_all)

    def valid(origin):
        return (origin >= 0) & (origin <= 3)

    def hop_copy(a, way, hop, origin, device):
        slot = whole[a].at[origin * 2 + y]
        number = HOPS.index((way, hop))
        return pltpu.make_async_remote_copy(
            src_ref=part[a] if hop == 1 else slot,
            dst_ref=slot,
            send_sem=hop_send.at[a, number],
            recv_sem=hop_recv.at[a, number],
            device_id=device,
            device_id_type=MESH,
        )

    def hop_go(a, hop, finish=False):
        for way in (1, -1):
            origin = z - way * (hop - 1)

            @pl.when(valid(origin) & valid(z + way))
            def _(way=way, origin=origin):
                copy = hop_copy(a, way, hop, origin, (batch + 2 * way, ffn))
                if finish:
                    copy.wait_send()
                else:
                    copy.start()

    def pass_copy(a, way, hop, origin, column):
        slot = whole[a].at[origin * 2 + column]
        number = HOPS.index((way, hop))
        return pltpu.make_async_remote_copy(
            src_ref=slot,
            dst_ref=slot,
            send_sem=pass_send.at[a, number],
            recv_sem=pass_recv.at[a, number],
            device_id=across,
            device_id_type=MESH,
        )

    def hop_came(a, hop):
        for way in (1, -1):
            origin = z - way * hop

            @pl.when(valid(origin))
            def _(way=way, origin=origin):
                hop_copy(a, way, hop, origin, (batch, ffn)).wait_recv()

        if hop < 3:
            hop_go(a, hop + 1)
        for way in (1, -1):
            origin = z - way * hop

            @pl.when(valid(origin))
            def _(way=way, origin=origin):
                pass_copy(a, way, hop, origin, y).start()

    own_over = []
    if small:
        for a in range(2):
            hop_go(a, 1)
            own_over.append(send(part[a], whole[a].at[batch], across))
            local(part[a], whole[a].at[batch])

    exchanged = []

    def sort_and_send(rows_ref, out_ref, out_hbm):
        pos = pos_ref[0:1, 0:ROWS]
        top = 0
        sent = []
        for size in SORT_TILES:
            want = top + lax.broadcasted_iota(I32, (size, ROWS), 0)
            hot = jnp.where(pos == want, 1.0, 0.0).astype(BF16)
            rows = pl.ds(top, size)
            out_ref[rows, :] = dot(hot, rows_ref[...]).astype(BF16)
            sent.append(send(out_ref.at[rows], out_hbm.at[2, rows], far))
            exchanged.append(send(out_ref.at[rows], out_hbm.at[1, rows], near))
            local(out_ref.at[rows], out_hbm.at[0, rows])
            top += size
        return sent

    def hand_on(sent, out_hbm):
        top = 0
        for copy, size in zip(sent, SORT_TILES):
            rows = pl.ds(top, size)
            copy.wait()
            exchanged.append(send(out_hbm.at[2, rows], out_hbm.at[3, rows], near))
            top += size

    held[1552:ROWS, :] = jnp.zeros((ROWS - 1552, D), BF16)
    held[0:TOK_DEV, :] = cot_ref[...]
    g_sent = sort_and_send(held, g_sorted, g_hbm)

    for i in range(3):
        top = min(TILE * (i + 1), TOK_DEV)
        rows = slice(TILE * i, top)
        normal, _ = norm_parts(tok_ref[rows, :].astype(F32))
        normed = (normal * gain_one_ref[...]).astype(BF16)
        qkv[rows, :] = dot(normed, w_qkv_ref[...]).astype(BF16)
    tail = slice(TOK_DEV, ROWS)
    qkv[tail, :] = jnp.zeros((ROWS - TOK_DEV, 3 * D), BF16)
    ctx[1552:ROWS, :] = jnp.zeros((ROWS - 1552, D), BF16)
    local(qkv, qkv_hbm)
    if small:
        hop_came(0, 1)

    @pl.loop(0, SEQ_DEV)
    def _(pair):
        attend_pair(pair, len_ref[pair], qkv, ctx, lse, stat)
        if small:

            @pl.when(pair == 1)
            def _():
                hop_came(1, 1)

            @pl.when(pair == 4)
            def _():
                hop_came(0, 2)

    local(ctx, ctx_hbm)
    local(lse, lse_hbm)
    for i in range(3):
        top = min(TILE * (i + 1), TOK_DEV)
        rows = slice(TILE * i, top)
        middle = tok_ref[rows, :].astype(F32) + dot(ctx[rows, :], w_proj_ref[...])
        mid[rows, :] = middle
        normal, _ = norm_parts(middle)
        held[rows, :] = (normal * gain_two_ref[...]).astype(BF16)
    local(mid, mid_hbm)
    if small:
        hop_came(1, 2)
    x_sent = sort_and_send(held, x_sorted, x_hbm)
    hand_on(g_sent, g_hbm)
    if small:
        hop_came(0, 3)
        hop_came(1, 3)
    hand_on(x_sent, x_hbm)
    for copy in exchanged + own_over:
        copy.wait()
    if small:
        for a in range(2):
            for hop in (1, 2, 3):
                hop_go(a, hop, finish=True)
            for way, hop in HOPS:
                origin = z - way * hop

                @pl.when(valid(origin))
                def _(a=a, way=way, hop=hop, origin=origin):
                    pass_copy(a, way, hop, origin, y).wait_send()
                    pass_copy(a, way, hop, origin, 1 - y).wait_recv()

    for copy in waiting:
        copy.wait()


def front(small, lengths, pos, tokens, cot, gain_one, w_qkv, w_proj, gain_two, wi, wb):
    vmem = pl.BlockSpec(memory_space=pltpu.VMEM)
    any_space = pl.BlockSpec(memory_space=pl.ANY)
    tiles = len(SORT_TILES)
    copies = 6 * tiles + 2
    dma = pltpu.SemaphoreType.DMA
    return pl.pallas_call(
        functools.partial(front_kernel, small),
        out_shape=(
            jax.ShapeDtypeStruct((ROWS, 3 * D), BF16),
            jax.ShapeDtypeStruct((ROWS, D), BF16),
            jax.ShapeDtypeStruct((SEQ_DEV, 16, 384), F32),
            jax.ShapeDtypeStruct((TOK_DEV, D), F32),
            jax.ShapeDtypeStruct((4, SORTED, D), BF16),
            jax.ShapeDtypeStruct((4, SORTED, D), BF16),
            jax.ShapeDtypeStruct((8, D, HALF), BF16),
            jax.ShapeDtypeStruct((8, HALF, D), BF16),
        ),
        in_specs=[pl.BlockSpec(memory_space=pltpu.SMEM)] + [vmem] * 7 + [any_space] * 2,
        out_specs=(any_space,) * 8,
        scratch_shapes=[
            pltpu.VMEM((ROWS, 3 * D), BF16),
            pltpu.VMEM((ROWS, D), BF16),
            pltpu.VMEM((SEQ_DEV, 16, 384), F32),
            pltpu.VMEM((TOK_DEV, D), F32),
            pltpu.VMEM((SORTED, D), BF16),
            pltpu.VMEM((SORTED, D), BF16),
            pltpu.VMEM((ROWS, D), BF16),
            pltpu.VMEM((384, 128), F32),
            dma((2 * tiles + 6,)),
            dma((copies,)),
            dma((copies,)),
            dma((2, 6)),
            dma((2, 6)),
            dma((2, 6)),
            dma((2, 6)),
        ],
        compiler_params=params(collective_id=1, has_side_effects=True),
        name="front",
    )(lengths, pos, tokens, cot, gain_one, w_qkv, w_proj, gain_two, wi, wb)


def gelu_both(u):
    below = 0.5 * (1.0 + lax.erf(u * (1.0 / math.sqrt(2.0))))
    density = jnp.exp(-0.5 * u * u) * (1.0 / math.sqrt(2.0 * math.pi))
    return u * below, below + u * density


MERGED = 2 * SORTED + 256


def expert_kernel(carried, offs_ref, hosts_ref, *refs):
    refs = list(refs)

    def take(count):
        head = refs[:count]
        del refs[:count]
        return head

    xs, gs = take(2), take(2)
    wi_hbm, wb_hbm = take(2)
    before = take(2) if carried else None
    outs, gxs = take(2), take(2)
    dwi_ref, dwb_ref = take(2)
    xm, gm, wi, wb, acc_i, acc_b, sems = refs
    expert = pl.program_id(0)
    slot = expert % 2

    def weight_copies(e, buffer, start):
        for p in range(2):
            host = hosts_ref[e * 2 + p]
            part = pl.ds(p * HALF, HALF)
            for number, source, target in (
                (0, wi_hbm.at[host], wi.at[buffer, :, part]),
                (1, wb_hbm.at[host], wb.at[buffer, part, :]),
            ):
                copy = pltpu.make_async_copy(source, target, sems.at[buffer, p, number])
                if start:
                    copy.start()
                else:
                    copy.wait()

    @pl.when(expert == 0)
    def _():
        weight_copies(0, 0, True)

    @pl.when(expert + 1 < EXPERTS)
    def _():
        weight_copies(expert + 1, 1 - slot, True)

    def blocks(count, act):
        @pl.loop(0, count)
        def _(i):
            act(pl.multiple_of(i * 16, 16))

    @pl.when(expert == 0)
    def _():
        for s in range(2):
            live = pl.multiple_of(offs_ref[s * 4 + EXPERTS], 16)

            def clear(at, s=s, live=live):
                rows = pl.ds(pl.multiple_of(live + at, 16), 16)
                outs[s][rows, :] = jnp.zeros((16, D), BF16)
                gxs[s][rows, :] = jnp.zeros((16, D), BF16)

            blocks((SORTED - live) // 16, clear)

    if carried:
        acc_i[...] = before[0][0].astype(F32)
        acc_b[...] = before[1][0].astype(F32)
    else:
        acc_i[...] = jnp.zeros_like(acc_i)
        acc_b[...] = jnp.zeros_like(acc_b)

    places = []
    total = jnp.int32(0)
    for s in range(2):
        first = pl.multiple_of(offs_ref[s * 4 + expert], 16)
        size = offs_ref[s * 4 + expert + 1] - first
        places.append((first, total, size // 16))

        def gather(at, s=s, first=first, total=total):
            here = pl.ds(pl.multiple_of(first + at, 16), 16)
            there = pl.ds(pl.multiple_of(total + at, 16), 16)
            xm[there, :] = xs[s][0, here, :]
            gm[there, :] = gs[s][0, here, :]

        blocks(size // 16, gather)
        total = total + size
    span = pl.multiple_of(total, 16)

    def blank(at):
        there = pl.ds(pl.multiple_of(span + at, 16), 16)
        xm[there, :] = jnp.zeros((16, D), BF16)
        gm[there, :] = jnp.zeros((16, D), BF16)

    blocks((256 - span % 256) // 16, blank)
    weight_copies(expert, slot, False)
    w_in, w_back = wi.at[slot], wb.at[slot]

    @pl.loop(0, (span + 255) // 256)
    def _(i):
        rows = pl.ds(pl.multiple_of(i * 256, 256), 256)
        x, g = xm[rows, :], gm[rows, :]
        inner = dot(x, w_in[...])
        hidden, slope = gelu_both(inner)
        hidden = hidden.astype(BF16)
        grad_hidden = dot(g, w_back[...], CONTRACT_LANES).astype(BF16)
        grad_inner = (grad_hidden.astype(F32) * slope).astype(BF16)
        xm[rows, :] = dot(hidden, w_back[...]).astype(BF16)
        gm[rows, :] = dot(grad_inner, w_in[...], CONTRACT_LANES).astype(BF16)
        acc_b[...] += dot(hidden, g, CONTRACT_ROWS)
        acc_i[...] += dot(x, grad_inner, CONTRACT_ROWS)

    dwi_ref[0] = acc_i[...].astype(BF16)
    dwb_ref[0] = acc_b[...].astype(BF16)
    for s in range(2):
        first, base, count = places[s]

        def hand_back(at, s=s, first=first, base=base):
            here = pl.ds(pl.multiple_of(first + at, 16), 16)
            there = pl.ds(pl.multiple_of(base + at, 16), 16)
            outs[s][here, :] = xm[there, :]
            gxs[s][here, :] = gm[there, :]

        blocks(count, hand_back)


def experts(sources, offs, hosts, x, g, wi, wb, before=None):
    whole = once((SORTED, D))
    any_space = pl.BlockSpec(memory_space=pl.ANY)
    weight = pl.BlockSpec((1, D, FF_DEV), lambda e, *_: (e, 0, 0))
    carried = before is not None
    rows = jax.ShapeDtypeStruct((SORTED, D), BF16)
    grad = jax.ShapeDtypeStruct((EXPERTS, D, FF_DEV), BF16)

    def source(i):
        return pl.BlockSpec(
            (1, SORTED, D), lambda e, *_: (i, 0, 0), pipeline_mode=pl.Buffered(1)
        )

    picked = [source(i) for i in sources]
    return pl.pallas_call(
        functools.partial(expert_kernel, carried),
        grid_spec=pltpu.PrefetchScalarGridSpec(
            num_scalar_prefetch=2,
            grid=(EXPERTS,),
            in_specs=picked + picked + [any_space] * 2 + [weight] * (2 * carried),
            out_specs=[whole] * 4 + [weight] * 2,
            scratch_shapes=[
                pltpu.VMEM((MERGED, D), BF16),
                pltpu.VMEM((MERGED, D), BF16),
                pltpu.VMEM((2, D, FF_DEV), BF16),
                pltpu.VMEM((2, FF_DEV, D), BF16),
                pltpu.VMEM((D, FF_DEV), F32),
                pltpu.VMEM((FF_DEV, D), F32),
                pltpu.SemaphoreType.DMA((2, 2, 2)),
            ],
        ),
        out_shape=(rows,) * 4 + (grad,) * 2,
        compiler_params=params(),
        cost_estimate=cost(24 * SORTED * D * FF_DEV, 16 * SORTED * D),
        name="experts",
    )(offs, hosts, x, x, g, g, wi, wb, *(before or ()))


def swap(rows, bit):
    pairs = [(f, f ^ bit) for f in range(4)]
    return lax.ppermute(rows, "ffn", pairs)


def spread(rows):
    near = swap(rows, 1)
    far = swap(rows, 2)
    return [rows, near, far, swap(far, 1)]


def tie(value, *others):
    return lax.optimization_barrier((value, *others))[0]


class Wire:
    def __init__(self, send_sems, recv_sems):
        self.send_sems, self.recv_sems, self.used = send_sems, recv_sems, 0

    def send(self, src, dst, device):
        number = self.used
        self.used += 1
        copy = pltpu.make_async_remote_copy(
            src_ref=src,
            dst_ref=dst,
            send_sem=self.send_sems.at[number],
            recv_sem=self.recv_sems.at[number],
            device_id=device,
            device_id_type=MESH,
        )
        copy.start()
        return copy


class Mover:
    def __init__(self, sems):
        self.sems, self.used = sems, 0

    def go(self, src, dst):
        number = self.used
        self.used += 1
        copy = pltpu.make_async_copy(src, dst, self.sems.at[number])
        copy.start()
        return copy


def greet(peers):
    barrier = pltpu.get_barrier_semaphore()
    for device in peers:
        pl.semaphore_signal(barrier, inc=1, device_id=device, device_id_type=MESH)
    pl.semaphore_wait(barrier, len(peers))


def wait_all(copies):
    for copy in copies:
        copy.wait()


def token_tiles():
    for i in range(3):
        yield slice(TILE * i, min(TILE * (i + 1), TOK_DEV))


def unsort(pos_col, src):
    want = lax.broadcasted_iota(I32, (pos_col.shape[0], SORTED), 1)
    hot = jnp.where(pos_col == want, 1.0, 0.0).astype(BF16)
    return dot(hot, src)


def attend_back_pair(pair, length, qkv_ref, gctx_ref, lse_ref, out_ref):
    start, skip = window(pair)
    start = pl.multiple_of(start, 16)
    row = lax.broadcasted_iota(I32, (WIN, 1), 0)
    mine = (row >= skip) & (row < skip + SEQ_LEN)
    bias = jnp.where((row >= skip) & (row < skip + PATCHES + length), 0.0, -1e30)
    lane = lax.broadcasted_iota(I32, (WIN, 128), 1)
    scale = jnp.asarray(HEAD_DIM**-0.5, BF16)
    for hp in range(HEADS // 2):
        spots = [slice(part * D + hp * 128, part * D + hp * 128 + 128) for part in range(3)]
        q, k, v = [qkv_ref[pl.ds(start, WIN), spot] for spot in spots]
        q = q * scale
        ks = k * scale
        go = gctx_ref[pl.ds(start, WIN), hp * 128 : hp * 128 + 128]
        q = jnp.where(mine, q, jnp.zeros_like(q))
        go = jnp.where(mine, go, jnp.zeros_like(go))
        grads = []
        for half in range(2):
            head = hp * 2 + half
            inside = (lane < 64) if half == 0 else (lane >= 64)
            qh = jnp.where(inside, q, jnp.zeros_like(q))
            gh = jnp.where(inside, go, jnp.zeros_like(go))
            scores = dot(k, qh, CONTRACT_LANES)
            probs = jnp.exp(scores + bias - lse_ref[pair, head : head + 1, 0:WIN])
            grad_probs = dot(v, gh, CONTRACT_LANES)
            delta = jnp.sum(probs * grad_probs, axis=0, keepdims=True)
            grad_scores = (probs * (grad_probs - delta)).astype(BF16)
            grad_v = dot(probs.astype(BF16), go)
            grad_k = dot(grad_scores, q)
            grad_q = dot(grad_scores, ks, CONTRACT_ROWS)
            grads.append((grad_q, grad_k, grad_v))
        for spot, low, high in zip(spots, grads[0], grads[1]):
            new = jnp.where(lane < 64, low, high).astype(BF16)
            old = out_ref[pl.ds(start, WIN), spot]
            out_ref[pl.ds(start, WIN), spot] = jnp.where(mine, new, old)


CHUNK = D // 8
TURNS = (2, 3, 1, 0)


def rear_kernel(
    small,
    len_ref,
    pos_ref,
    gain_one_ref,
    gain_two_ref,
    w_ref,
    lse_ref,
    gx0_hbm,
    gx1_hbm,
    gx2_hbm,
    mid_hbm,
    cot_hbm,
    ctx_hbm,
    qkv_hbm,
    tok_hbm,
    out1_hbm,
    out2_hbm,
    out3_hbm,
    dwi_hbm,
    dwb_hbm,
    gm_hbm,
    gq_hbm,
    dwq_hbm,
    dwp_hbm,
    dg_ref,
    share_hbm,
    near_hbm,
    far_hbm,
    wide,
    mid,
    cot,
    ctx,
    gctx,
    qkv,
    half_a,
    half_b,
    own_rows,
    came_y,
    came_z,
    acc,
    dwp,
    local_sems,
    send_sems,
    recv_sems,
    z_send,
    z_recv,
):
    batch, ffn = lax.axis_index("batch"), lax.axis_index("ffn")
    z, y = batch // 2, batch % 2
    near, far, across = (batch, ffn ^ 1), (batch, ffn ^ 2), (batch ^ 1, ffn)
    along = {k: (batch ^ (2 * k), ffn) for k in (1, 2, 3)}
    greet([near, far] + ([across] + list(along.values()) if small else []))
    wire, mover = Wire(send_sems, recv_sems), Mover(local_sems)

    parts_near = wire.send(gx1_hbm, wide.at[:, D : 2 * D], near)
    near_sent = wire.send(out3_hbm, half_b, near)
    half_in = mover.go(out2_hbm, half_a)
    over_y = {}
    own_in = {}
    if small:
        for turn in TURNS:
            there = pl.ds(pl.multiple_of(((z ^ turn) * 2 + 1 - y) * CHUNK, 16), CHUNK)
            over_y[turn] = [
                wire.send(grad.at[:, there, :], came_y.at[turn, i], across)
                for i, grad in enumerate((dwi_hbm, dwb_hbm))
            ]
    parts_in = [
        mover.go(part, wide.at[:, i * D : i * D + D])
        for i, part in ((0, gx0_hbm), (2, gx2_hbm))
    ]
    rows_in = [mover.go(mid_hbm, mid), mover.go(cot_hbm, cot), mover.go(ctx_hbm, ctx)]
    qkv_in = mover.go(qkv_hbm, qkv)
    if small:
        for turn in TURNS:
            here = pl.ds(pl.multiple_of(((z ^ turn) * 2 + y) * CHUNK, 16), CHUNK)
            own_in[turn] = [
                mover.go(grad.at[:, here, :], own_rows.at[turn, i])
                for i, grad in enumerate((dwi_hbm, dwb_hbm))
            ]
    sent = [wire.send(out1_hbm, near_hbm, near)]
    stored = []

    def z_copy(turn, i):
        return pltpu.make_async_remote_copy(
            src_ref=came_y.at[turn, i],
            dst_ref=came_z.at[turn - 1, i],
            send_sem=z_send.at[turn - 1, i],
            recv_sem=z_recv.at[turn - 1, i],
            device_id=along[turn],
            device_id_type=MESH,
        )

    def take_turn(turn, i):
        if not small:
            return
        over_y[turn][i].wait()
        own_in[turn][i].wait()
        for e in range(EXPERTS):
            came_y[turn, i, e] = (
                came_y[turn, i, e].astype(F32) + own_rows[turn, i, e].astype(F32)
            ).astype(BF16)
        if turn:
            z_copy(turn, i).start()

    wait_all(parts_in + rows_in + [parts_near])
    top = 0
    for size in SORT_TILES:
        rows = slice(top, top + size)
        wide[rows, 0:D] = (
            wide[rows, 0:D].astype(F32)
            + wide[rows, D : 2 * D].astype(F32)
            + wide[rows, 2 * D : 3 * D].astype(F32)
        ).astype(BF16)
        top += size
    half_in.wait()
    near_sent.wait()
    half_a[...] = (half_a[...].astype(F32) + half_b[...].astype(F32)).astype(BF16)
    sent.append(wire.send(half_a, far_hbm, far))

    gctx[1552:ROWS, :] = jnp.zeros((ROWS - 1552, D), BF16)
    grad_gain = jnp.zeros((1, D), F32)
    for i, rows in enumerate(token_tiles()):
        grad_normed = unsort(pos_ref[rows, :], wide[:, 0:D])
        normal, inverse = norm_parts(mid[rows, :])
        grad_gain = grad_gain + jnp.sum(grad_normed * normal, axis=0, keepdims=True)
        part = norm_pull(grad_normed, gain_two_ref[...], normal, inverse)
        grad_middle = cot[rows, :].astype(F32) + part
        mid[rows, :] = grad_middle
        low = grad_middle.astype(BF16)
        product = dot(ctx[rows, :], low, CONTRACT_ROWS)
        if i == 0:
            acc[...] = product
        elif i == 1:
            acc[...] += product
        else:
            dwp[...] = (acc[...] + product).astype(BF16)
        gctx[rows, :] = dot(low, w_ref[...], CONTRACT_LANES).astype(BF16)
        if i < 2:
            take_turn(2, i)
    dg_ref[...] = grad_gain
    stored.append(mover.go(mid, gm_hbm))
    stored.append(mover.go(dwp, dwp_hbm))
    tok_in = mover.go(tok_hbm, cot)
    wide[1552:SORTED, :] = jnp.zeros((SORTED - 1552, 3 * D), BF16)
    qkv_in.wait()
    take_turn(3, 0)

    @pl.loop(0, SEQ_DEV)
    def _(pair):
        attend_back_pair(pair, len_ref[pair], qkv, gctx, lse_ref, wide)
        for when, turn, i in ((1, 3, 1), (3, 1, 0), (4, 1, 1)):

            @pl.when(pair == when)
            def _(turn=turn, i=i):
                take_turn(turn, i)

    stored.append(mover.go(wide.at[0:ROWS, :], gq_hbm))
    tok_in.wait()
    for rows in token_tiles():
        normal, _ = norm_parts(cot[rows, :].astype(F32))
        gctx[rows, :] = (normal * gain_one_ref[...]).astype(BF16)
    for i in range(3):
        cols = slice(i * D, i * D + D)
        qkv[0:D, cols] = dot(gctx[...], wide[0:ROWS, cols], CONTRACT_ROWS).astype(BF16)
    stored.append(mover.go(qkv.at[0:D, :], dwq_hbm))
    if small:
        take_turn(0, 0)
        take_turn(0, 1)
        wait_all([z_copy(turn, i) for turn in TURNS[:3] for i in range(2)])
        for i in range(2):
            for e in range(EXPERTS):
                total = came_y[0, i, e].astype(F32)
                for k in range(3):
                    total = total + came_z[k, i, e].astype(F32)
                came_y[0, i, e] = total.astype(BF16)
        stored.append(mover.go(came_y.at[0], share_hbm))
    wait_all(sent + stored)


def rear(small, lengths, pos_col, gain_one, gain_two, w_proj, lse, *arrays):
    vmem = pl.BlockSpec(memory_space=pltpu.VMEM)
    any_space = pl.BlockSpec(memory_space=pl.ANY)
    dma = pltpu.SemaphoreType.DMA
    copies = 12
    return pl.pallas_call(
        functools.partial(rear_kernel, small),
        out_shape=(
            jax.ShapeDtypeStruct((TOK_DEV, D), F32),
            jax.ShapeDtypeStruct((ROWS, 3 * D), BF16),
            jax.ShapeDtypeStruct((D, 3 * D), BF16),
            jax.ShapeDtypeStruct((D, D), BF16),
            jax.ShapeDtypeStruct((1, D), F32),
            jax.ShapeDtypeStruct((2, EXPERTS, CHUNK, D), BF16),
            jax.ShapeDtypeStruct((SORTED, D), BF16),
            jax.ShapeDtypeStruct((SORTED, D), BF16),
        ),
        in_specs=[pl.BlockSpec(memory_space=pltpu.SMEM)] + [vmem] * 5 + [any_space] * len(arrays),
        out_specs=(any_space,) * 4 + (vmem,) + (any_space,) * 3,
        scratch_shapes=[
            pltpu.VMEM((SORTED, 3 * D), BF16),
            pltpu.VMEM((TOK_DEV, D), F32),
            pltpu.VMEM((TOK_DEV, D), BF16),
            pltpu.VMEM((ROWS, D), BF16),
            pltpu.VMEM((ROWS, D), BF16),
            pltpu.VMEM((ROWS, 3 * D), BF16),
            pltpu.VMEM((SORTED, D), BF16),
            pltpu.VMEM((SORTED, D), BF16),
            pltpu.VMEM((4, 2, EXPERTS, CHUNK, D), BF16),
            pltpu.VMEM((4, 2, EXPERTS, CHUNK, D), BF16),
            pltpu.VMEM((3, 2, EXPERTS, CHUNK, D), BF16),
            pltpu.VMEM((D, D), F32),
            pltpu.VMEM((D, D), BF16),
            dma((24,)),
            dma((copies,)),
            dma((copies,)),
            dma((3, 2)),
            dma((3, 2)),
        ],
        compiler_params=params(collective_id=2, has_side_effects=True),
        name="rear",
    )(lengths, pos_col, gain_one, gain_two, w_proj, lse, *arrays)


ORDERS = (("x", "y", "z"), ("y", "x", "z"))
WIDE = 4 * D
COLOUR = WIDE // 2
QUARTER = COLOUR // 4
GAIN_ROWS = 8


def last_kernel(
    small,
    group_ref,
    pos_ref,
    gain_ref,
    w_ref,
    dg_two_ref,
    tok_hbm,
    gq_hbm,
    gm_hbm,
    mid_hbm,
    out0_hbm,
    out1_hbm,
    out2_hbm,
    dwq_hbm,
    dwp_hbm,
    share_hbm,
    ig_hbm,
    bo_hbm,
    sum_ref,
    gains_ref,
    pieces_ref,
    tok,
    gq,
    gm,
    mid,
    outs,
    share,
    stage,
    near_rows,
    held,
    came_z,
    came_xy,
    gain_in,
    local_sems,
    send_sems,
    recv_sems,
):
    batch, ffn = lax.axis_index("batch"), lax.axis_index("ffn")
    z, y, x, c = batch // 2, batch % 2, ffn // 2, ffn % 2
    place = {"x": x, "y": y, "z": z}
    mover = Mover(local_sems)

    def peer(axis, k=1):
        if axis == "c":
            return (batch, ffn ^ 1)
        if axis == "x":
            return (batch, ffn ^ 2)
        if axis == "y":
            return (batch ^ 1, ffn)
        return (batch ^ (2 * k), ffn)

    flying = []
    top = [0, 0]
    left = [COLOUR * i for i in range(2)]
    rows, cols = [384] * 2, [COLOUR] * 2
    base = pl.multiple_of(c * 384, 16)
    if small:
        greet([peer("c"), peer("x")] + [(batch ^ j, ffn) for j in range(1, 8)])
        wire = Wire(send_sems, recv_sems)
        share_in = mover.go(share_hbm, share)
        give = pl.ds(pl.multiple_of((1 - c) * 384, 16), 384)
        keep = pl.ds(base, 384)
        to_core = [
            wire.send(dwq_hbm.at[give, :], near_rows.at[:, 0 : 3 * D], peer("c")),
            wire.send(dwp_hbm.at[give, :], near_rows.at[:, 3 * D : WIDE], peer("c")),
        ]
        kept = [
            mover.go(dwq_hbm.at[keep, :], held.at[:, 0 : 3 * D]),
            mover.go(dwp_hbm.at[keep, :], held.at[:, 3 * D : WIDE]),
        ]
    loads = [mover.go(tok_hbm, tok), mover.go(gq_hbm, gq), mover.go(gm_hbm, gm)]
    later = [mover.go(mid_hbm, mid)] + [
        mover.go(part, outs.at[i]) for i, part in enumerate((out0_hbm, out1_hbm, out2_hbm))
    ]
    handed = []
    if small:
        share_in.wait()
        for j in range(8):
            expert = group_ref[batch ^ j]
            for i in range(2):
                stage[j, i] = share[i, expert]
            if j:
                handed.append(wire.send(stage.at[j], pieces_ref.at[batch], (batch ^ j, ffn)))
        pieces_ref[batch] = stage[0]

    def core_done():
        wait_all(to_core + kept)
        for i in range(4):
            lanes = slice(i * D, i * D + D)
            held[:, lanes] = (
                held[:, lanes].astype(F32) + near_rows[:, lanes].astype(F32)
            ).astype(BF16)

    def sum_go(step):
        for i in range(2):
            axis = ORDERS[i][step]
            if axis == "z":
                live = pl.ds(top[i], rows[i])
                for k in (1, 2, 3):
                    there = pl.ds(pl.multiple_of(left[i] + (z ^ k) * QUARTER, 128), QUARTER)
                    flying.append(
                        wire.send(
                            held.at[live, there], came_z.at[i, k - 1, 0 : rows[i]], peer("z", k)
                        )
                    )
            else:
                half = rows[i] // 2
                there = pl.ds(pl.multiple_of(top[i] + (1 - place[axis]) * half, 16), half)
                flying.append(
                    wire.send(
                        held.at[there, pl.ds(left[i], cols[i])],
                        came_xy.at[i, 0 if axis == "x" else 1, 0:half, 0 : cols[i]],
                        peer(axis),
                    )
                )

    def sum_done(step):
        wait_all(flying)
        flying.clear()
        for i in range(2):
            axis = ORDERS[i][step]
            if axis == "z":
                left[i] = pl.multiple_of(left[i] + z * QUARTER, 128)
                cols[i] = QUARTER
                terms = [came_z[i, k, 0 : rows[i]] for k in range(3)]
            else:
                rows[i] = rows[i] // 2
                top[i] = pl.multiple_of(top[i] + place[axis] * rows[i], 16)
                terms = [came_xy[i, 0 if axis == "x" else 1, 0 : rows[i], 0 : cols[i]]]
            spot = (pl.ds(top[i], rows[i]), pl.ds(left[i], cols[i]))
            total = held[spot].astype(F32)
            for term in terms:
                total = total + term.astype(F32)
            held[spot] = total.astype(BF16)

    def spread_go(step):
        for i in range(2):
            axis = ORDERS[i][step]
            mine = sum_ref.at[
                pl.ds(pl.multiple_of(base + top[i], 16), rows[i]), pl.ds(left[i], cols[i])
            ]
            for k in (1, 2, 3) if axis == "z" else (1,):
                flying.append(wire.send(mine, mine, peer(axis, k)))

    def spread_done(step):
        wait_all(flying)
        flying.clear()
        for i in range(2):
            axis = ORDERS[i][step]
            if axis == "z":
                left[i] = COLOUR * i
                cols[i] = COLOUR
            else:
                top[i] = top[i] - place[axis] * rows[i]
                rows[i] = rows[i] * 2

    def gains_go(axis, slot):
        for k in (1, 2, 3) if axis == "z" else (1,):
            flying.append(wire.send(gains_ref, gain_in.at[slot + k - 1], peer(axis, k)))

    def gains_done(axis, slot):
        total = gains_ref[...]
        for k in (0, 1, 2) if axis == "z" else (0,):
            total = total + gain_in[slot + k]
        gains_ref[...] = total

    tiles = list(token_tiles())
    grad_gain = jnp.zeros((1, D), F32)
    stored = []

    def first_back(part):
        normal, inverse = norm_parts(tok[part, :].astype(F32))
        grad_normed = dot(gq[part, :], w_ref[...], CONTRACT_LANES)
        gain_part = jnp.sum(grad_normed * normal, axis=0, keepdims=True)
        pulled = norm_pull(grad_normed, gain_ref[...], normal, inverse)
        gm[part, :] = gm[part, :] + pulled
        stored.append(mover.go(gm.at[part], ig_hbm.at[part]))
        return gain_part

    def finish(part):
        mid[part, :] = mid[part, :] + unsort(pos_ref[part, :], outs[0])
        stored.append(mover.go(mid.at[part], bo_hbm.at[part]))

    wait_all(loads)
    grad_gain = grad_gain + first_back(tiles[0])
    if small:
        core_done()
        sum_go(0)
    grad_gain = grad_gain + first_back(tiles[1])
    grad_gain = grad_gain + first_back(tiles[2])
    gains_ref[0:1, :] = grad_gain
    gains_ref[1:2, :] = dg_two_ref[...]
    gains_ref[2:GAIN_ROWS, :] = jnp.zeros((GAIN_ROWS - 2, D), F32)
    if small:
        gains_go("c", 0)
        sum_done(0)
        gains_done("c", 0)
        gains_go("x", 1)
        sum_go(1)
    wait_all(later)
    at = 0
    for size in SORT_TILES:
        part = slice(at, at + size)
        outs[0, part] = (
            outs[0, part].astype(F32) + outs[1, part].astype(F32) + outs[2, part].astype(F32)
        ).astype(BF16)
        at += size
    finish(tiles[0])
    if small:
        sum_done(1)
        gains_done("x", 1)
        gains_go("y", 2)
        sum_go(2)
    finish(tiles[1])
    if small:
        sum_done(2)
        gains_done("y", 2)
        for i in range(2):
            spot = (pl.ds(top[i], rows[i]), pl.ds(left[i], cols[i]))
            sum_ref[pl.ds(pl.multiple_of(base + top[i], 16), rows[i]), spot[1]] = held[spot]
        gains_go("z", 3)
        spread_go(2)
    finish(tiles[2])
    if small:
        spread_done(2)
        gains_done("z", 3)
        spread_go(1)
        spread_done(1)
        spread_go(0)
        spread_done(0)
        mine = sum_ref.at[pl.ds(base, 384), :]
        wire.send(mine, mine, peer("c")).wait()
        wait_all(handed)
    wait_all(stored)


def last(small, group_map, pos_col, gain_one, w_qkv, dg_two, *arrays):
    vmem = pl.BlockSpec(memory_space=pltpu.VMEM)
    any_space = pl.BlockSpec(memory_space=pl.ANY)
    dma = pltpu.SemaphoreType.DMA
    copies = 2 + 7 + 10 + 10 + 6 + 1
    extra = dict(collective_id=3, has_side_effects=True) if small else {}
    return pl.pallas_call(
        functools.partial(last_kernel, small),
        out_shape=(
            jax.ShapeDtypeStruct((TOK_DEV, D), F32),
            jax.ShapeDtypeStruct((TOK_DEV, D), F32),
            jax.ShapeDtypeStruct((D, WIDE), BF16),
            jax.ShapeDtypeStruct((GAIN_ROWS, D), F32),
            jax.ShapeDtypeStruct((8, 2, CHUNK, D), BF16),
        ),
        in_specs=[pl.BlockSpec(memory_space=pltpu.SMEM)] + [vmem] * 4 + [any_space] * len(arrays),
        out_specs=(any_space,) * 2 + (vmem,) * 3,
        scratch_shapes=[
            pltpu.VMEM((TOK_DEV, D), BF16),
            pltpu.VMEM((ROWS, 3 * D), BF16),
            pltpu.VMEM((TOK_DEV, D), F32),
            pltpu.VMEM((TOK_DEV, D), F32),
            pltpu.VMEM((3, SORTED, D), BF16),
            pltpu.VMEM((2, EXPERTS, CHUNK, D), BF16),
            pltpu.VMEM((8, 2, CHUNK, D), BF16),
            pltpu.VMEM((384, WIDE), BF16),
            pltpu.VMEM((384, WIDE), BF16),
            pltpu.VMEM((2, 3, 96, QUARTER), BF16),
            pltpu.VMEM((2, 2, 192, COLOUR), BF16),
            pltpu.VMEM((6, GAIN_ROWS, D), F32),
            dma((16,)),
            dma((copies,)),
            dma((copies,)),
        ],
        compiler_params=params(**extra),
        name="last",
    )(group_map, pos_col, gain_one, w_qkv, dg_two, *arrays)


def body(
    tokens,
    text_lengths,
    routes,
    group_map,
    gain_one,
    w_qkv,
    w_proj,
    gain_two,
    w_in,
    w_back,
    cotangent,
):
    n_batch = lax.axis_size("batch")
    own = lax.axis_index("batch")
    gain_one = gain_one.reshape(1, D)
    gain_two = gain_two.reshape(1, D)
    own_expert = group_map[own]
    order = jnp.arange(n_batch, dtype=I32)
    rank = jnp.sum(jnp.where((group_map == own_expert) & (order < own), 1, 0))
    part = jnp.minimum(rank, 1)
    hosting = group_map[None, :] == jnp.arange(EXPERTS, dtype=I32)[:, None]
    first_host = jnp.min(jnp.where(hosting, order[None, :], n_batch), axis=1)
    later = hosting & (order[None, :] > first_host[:, None])
    second_host = jnp.min(jnp.where(later, order[None, :], n_batch), axis=1)
    hosts = jnp.stack([first_host, second_host], axis=1).reshape(2 * EXPERTS)

    wi_part = lax.dynamic_slice(w_in[0], (0, part * HALF), (D, HALF))
    wb_part = lax.dynamic_slice(w_back[0], (part * HALF, 0), (HALF, D))
    small = n_batch == 8

    routes_row = jnp.pad(routes.reshape(1, TOK_DEV), ((0, 0), (0, LANES - TOK_DEV)))
    pos, offs = route_rows(routes_row, group_map)
    pos_col = pos.reshape(LANES, 1)[0:ROWS]
    offs_at = [o[0, 0:4] for o in spread(offs)]

    qkv, context, lse, middle, g, x, wi_all, wb_all = front(
        small, text_lengths, pos, tokens, cotangent, gain_one, w_qkv, w_proj, gain_two, wi_part, wb_part
    )
    if not small:
        wi_all = lax.all_gather(wi_part, "batch", axis=0)
        wb_all = lax.all_gather(wb_part, "batch", axis=0)

    def run(pair, x, before):
        return experts(
            pair,
            jnp.concatenate([offs_at[i] for i in pair]),
            hosts,
            x,
            g,
            wi_all,
            wb_all,
            before,
        )

    def add(a, b):
        return (a.astype(F32) + b.astype(F32)).astype(BF16)

    out2, out3, gx2, gx3, dwi, dwb = run((2, 3), x, None)
    gx_half = add(gx2, swap(gx3, 1))
    gx_far = swap(gx_half, 2)
    out0, out1, gx0, gx1, dwi, dwb = run((0, 1), tie(x, gx_half), (dwi, dwb))
    grad_middle, grad_qkv, dw_qkv, dw_proj, dg_two, share, out_near, out_far = rear(
        small,
        text_lengths,
        pos_col,
        gain_one,
        gain_two,
        w_proj,
        lse,
        gx0,
        gx1,
        gx_far,
        middle,
        cotangent,
        context,
        qkv,
        tokens,
        out1,
        out2,
        out3,
        dwi,
        dwb,
    )
    input_grad, block_out, summed, gains, pieces = last(
        small,
        group_map,
        pos_col,
        gain_one,
        w_qkv,
        dg_two,
        tokens,
        grad_qkv,
        grad_middle,
        middle,
        out0,
        out_near,
        out_far,
        dw_qkv,
        dw_proj,
        share,
    )
    if small:
        grad_w_in = pieces[:, 0].reshape(1, D, D).astype(F32)
        grad_w_back = pieces[:, 1].reshape(1, D, D).astype(F32)
        summed_qkv, summed_proj = summed[:, 0 : 3 * D], summed[:, 3 * D : WIDE]
    else:

        def settle_any(grad):
            share = lax.psum_scatter(grad, "batch", scatter_dimension=1, tiled=True)
            whole = lax.all_gather(share, "batch", axis=1, tiled=True)
            return lax.dynamic_index_in_dim(whole, own_expert, 0, keepdims=True).astype(F32)

        grad_w_in = settle_any(dwi)
        grad_w_back = settle_any(dwb)
        summed_qkv, summed_proj = lax.psum((dw_qkv, dw_proj), ("batch", "ffn"))
        gains = lax.psum(gains, ("batch", "ffn"))
    return (
        block_out,
        input_grad,
        gains[0],
        summed_qkv.astype(F32),
        summed_proj.astype(F32),
        gains[1],
        grad_w_in,
        grad_w_back,
    )


def solution(mesh):
    placed = (
        P(("batch", "ffn"), None),
        P(("batch", "ffn")),
        P(("batch", "ffn"), None),
        P(),
        P(),
        P(),
        P(),
        P(),
        P("batch", None, "ffn"),
        P("batch", "ffn", None),
        P(("batch", "ffn"), None),
    )
    return jax.shard_map(
        body,
        mesh=mesh,
        in_specs=placed,
        out_specs=(
            P(("batch", "ffn"), None),
            P(("batch", "ffn"), None),
            P(),
            P(),
            P(),
            P(),
            P("batch", None, "ffn"),
            P("batch", "ffn", None),
        ),
        check_vma=False,
    )
```

```python
import functools
import math

import jax
import jax.numpy as jnp
from jax import lax
from jax.experimental import pallas as pl
from jax.experimental.pallas import tpu as pltpu
from jax.sharding import PartitionSpec as P

D = 768
HEADS = 12
HEAD_DIM = 64
EXPERTS = 3
PATCHES = 197
SEQ_DEV = 6
SEQ_LEN = 261
TOK_DEV = 1566
ROWS = 1584
SORTED = 1616
WIN = 288
TILE = 528
LANES = 1664
EPS = 1e-05
F32 = jnp.float32
BF16 = jnp.bfloat16
I32 = jnp.int32
CONTRACT_LANES = (((1,), (1,)), ((), ()))
CONTRACT_ROWS = (((0,), (0,)), ((), ()))


def params(**extra):
    return pltpu.CompilerParams(vmem_limit_bytes=60 << 20, **extra)


def cost(flops, moved):
    return pl.CostEstimate(flops=int(flops), bytes_accessed=int(moved), transcendentals=0)


def dot(a, b, dims=(((1,), (0,)), ((), ()))):
    return lax.dot_general(a, b, dims, preferred_element_type=F32)


def full(shape):
    zeros = (0,) * len(shape)
    return pl.BlockSpec(shape, lambda *_: zeros)


def once(shape):
    zeros = (0,) * len(shape)
    return pl.BlockSpec(shape, lambda *_: zeros, pipeline_mode=pl.Buffered(1))


def row_mask(start, rows, limit):
    return start + lax.broadcasted_iota(I32, (rows, 1), 0) < limit


def norm_parts(values):
    average = jnp.mean(values, axis=-1, keepdims=True)
    centred = values - average
    variance = jnp.mean(centred * centred, axis=-1, keepdims=True)
    inverse = lax.rsqrt(variance + EPS)
    return centred * inverse, inverse


def norm_pull(grad_normed, gain, normal, inverse):
    scaled = grad_normed * gain
    mean_grad = jnp.mean(scaled, axis=-1, keepdims=True)
    mean_proj = jnp.mean(scaled * normal, axis=-1, keepdims=True)
    return inverse * (scaled - mean_grad - normal * mean_proj)


def route_rows(n_batch, gm_ref, routes_ref, pos_ref, col_ref, offs_ref):
    routes = routes_ref[...]
    lane = lax.broadcasted_iota(I32, (8, LANES), 1)
    sub = lax.broadcasted_iota(I32, (8, LANES), 0)
    expert = jnp.zeros((1, LANES), I32)
    for b in range(n_batch):
        expert = jnp.where(routes == b, gm_ref[b], expert)
    live = lane < TOK_DEV
    hot = jnp.where((jnp.broadcast_to(expert, (8, LANES)) == sub) & live, 1, 0)
    count = hot
    step = 1
    while step < LANES:
        count = count + jnp.where(lane >= step, pltpu.roll(count, step, 1), 0)
        step *= 2
    totals = [jnp.sum(hot[e : e + 1, :], axis=1, keepdims=True) for e in range(EXPERTS)]
    starts = [jnp.zeros((1, 1), I32)]
    for e in range(EXPERTS):
        starts.append(starts[-1] + (totals[e] + 15) // 16 * 16)
    pos = jnp.zeros((1, LANES), I32)
    for e in range(EXPERTS):
        pos = pos + jnp.where(hot[e : e + 1, :] > 0, count[e : e + 1, :] - 1 + starts[e], 0)
    pos = jnp.where(live[0:1, :], pos, -1)
    pos_ref[...] = pos
    wide = jnp.broadcast_to(pos.astype(F32), (128, LANES))
    col_ref[...] = jnp.transpose(wide).astype(I32)
    slot = lax.broadcasted_iota(I32, (1, 128), 1)
    offs = jnp.zeros((1, 128), I32)
    for e in range(EXPERTS + 1):
        offs = jnp.where(slot == e, starts[e], offs)
    offs_ref[...] = offs


SORT_TILES = (336, 336, 336, 336, 272)


def window(pair):
    first = pair * SEQ_LEN
    start = first // 16 * 16
    return start, first - start


def attend_pair(pair, length, qkv_ref, ctx_ref, lse_ref, stat):
    start, skip = window(pair)
    start = pl.multiple_of(start, 16)
    key = lax.broadcasted_iota(I32, (1, WIN), 1)
    seen = (key >= skip) & (key < skip + PATCHES + length)
    bias = jnp.where(seen, 0.0, -1e30)
    row = lax.broadcasted_iota(I32, (WIN, 1), 0)
    mine = (row >= skip) & (row < skip + SEQ_LEN)
    lane = lax.broadcasted_iota(I32, (WIN, 128), 1)
    stat[...] = jnp.zeros_like(stat)
    for hp in range(HEADS // 2):
        cols = slice(hp * 128, hp * 128 + 128)
        q = qkv_ref[pl.ds(start, WIN), hp * 128 : hp * 128 + 128]
        k = qkv_ref[pl.ds(start, WIN), D + hp * 128 : D + hp * 128 + 128]
        v = qkv_ref[pl.ds(start, WIN), 2 * D + hp * 128 : 2 * D + hp * 128 + 128]
        q = q * jnp.asarray(HEAD_DIM**-0.5, BF16)
        pieces = []
        for half in range(2):
            inside = (lane < 64) if half == 0 else (lane >= 64)
            qh = jnp.where(inside, q, jnp.zeros_like(q))
            scores = dot(qh, k, CONTRACT_LANES) + bias
            peak = jnp.max(scores, axis=1, keepdims=True)
            weight = jnp.exp(scores - peak).astype(BF16)
            vh = jnp.where(inside, v, jnp.ones_like(v))
            mixed = dot(weight, vh)
            total = pltpu.roll(mixed, 64, 1)
            pieces.append(mixed / total)
            one = total[:, 0:1] if half == 0 else mixed[:, 0:1]
            head = hp * 2 + half
            stat[0:WIN, :] = jnp.where(lane == head, peak + jnp.log(one), stat[0:WIN, :])
        ctx = jnp.where(lane < 64, pieces[0], pieces[1]).astype(BF16)
        old = ctx_ref[pl.ds(start, WIN), cols]
        ctx_ref[pl.ds(start, WIN), cols] = jnp.where(mine, ctx, old)
    lse_ref[pair] = jnp.transpose(stat[...])[0:16, :]


MESH = pl.DeviceIdType.MESH
HALF = 384
FF_DEV = 768
HOPS = [(way, hop) for hop in (1, 2, 3) for way in (1, -1)]


def front_kernel(
    small,
    n_batch,
    len_ref,
    group_ref,
    routes_ref,
    tok_ref,
    cot_ref,
    gain_one_ref,
    w_qkv_ref,
    w_proj_ref,
    gain_two_ref,
    w_in_ref,
    w_back_ref,
    qkv_hbm,
    ctx_hbm,
    lse_hbm,
    mid_hbm,
    g_hbm,
    x_hbm,
    wi_all,
    wb_all,
    offs_all,
    col_ref,
    qkv,
    ctx,
    lse,
    mid,
    g_sorted,
    x_sorted,
    held,
    stat,
    pos_ref,
    offs,
    wi_part,
    wb_part,
    local_sems,
    send_sems,
    recv_sems,
    hop_send,
    hop_recv,
    pass_send,
    pass_recv,
):
    batch, ffn = lax.axis_index("batch"), lax.axis_index("ffn")
    z, y = batch // 2, batch % 2
    near, far, cater = (batch, ffn ^ 1), (batch, ffn ^ 2), (batch, ffn ^ 3)
    across = (batch ^ 1, ffn)

    barrier = pltpu.get_barrier_semaphore()
    for device in [near, far, cater] + ([across] if small else []):
        pl.semaphore_signal(barrier, inc=1, device_id=device, device_id_type=MESH)
    if small:
        for way in (1, -1):

            @pl.when((z + way >= 0) & (z + way <= 3))
            def _(way=way):
                pl.semaphore_signal(
                    barrier, inc=1, device_id=(batch + 2 * way, ffn), device_id_type=MESH
                )

        inner = jnp.where((z == 0) | (z == 3), 1, 2)
        pl.semaphore_wait(barrier, 4 + inner)
    else:
        pl.semaphore_wait(barrier, 3)

    local_count = [0]
    waiting = []

    def local(src, dst):
        number = local_count[0]
        local_count[0] += 1
        copy = pltpu.make_async_copy(src, dst, local_sems.at[number])
        copy.start()
        waiting.append(copy)

    used = [0]

    def send(src, dst, device):
        number = used[0]
        used[0] += 1
        copy = pltpu.make_async_remote_copy(
            src_ref=src,
            dst_ref=dst,
            send_sem=send_sems.at[number],
            recv_sem=recv_sems.at[number],
            device_id=device,
            device_id_type=MESH,
        )
        copy.start()
        return copy

    part, whole = (wi_part, wb_part), (wi_all, wb_all)

    def valid(origin):
        return (origin >= 0) & (origin <= 3)

    def hop_copy(a, way, hop, origin, device):
        slot = whole[a].at[origin * 2 + y]
        number = HOPS.index((way, hop))
        return pltpu.make_async_remote_copy(
            src_ref=part[a] if hop == 1 else slot,
            dst_ref=slot,
            send_sem=hop_send.at[a, number],
            recv_sem=hop_recv.at[a, number],
            device_id=device,
            device_id_type=MESH,
        )

    def hop_go(a, hop, finish=False):
        for way in (1, -1):
            origin = z - way * (hop - 1)

            @pl.when(valid(origin) & valid(z + way))
            def _(way=way, origin=origin):
                copy = hop_copy(a, way, hop, origin, (batch + 2 * way, ffn))
                if finish:
                    copy.wait_send()
                else:
                    copy.start()

    def pass_copy(a, way, hop, origin, column):
        slot = whole[a].at[origin * 2 + column]
        number = HOPS.index((way, hop))
        return pltpu.make_async_remote_copy(
            src_ref=slot,
            dst_ref=slot,
            send_sem=pass_send.at[a, number],
            recv_sem=pass_recv.at[a, number],
            device_id=across,
            device_id_type=MESH,
        )

    def hop_came(a, hop):
        for way in (1, -1):
            origin = z - way * hop

            @pl.when(valid(origin))
            def _(way=way, origin=origin):
                hop_copy(a, way, hop, origin, (batch, ffn)).wait_recv()

        if hop < 3:
            hop_go(a, hop + 1)
        for way in (1, -1):
            origin = z - way * hop

            @pl.when(valid(origin))
            def _(way=way, origin=origin):
                pass_copy(a, way, hop, origin, y).start()

    own_over = []
    if small:
        rank = jnp.int32(0)
        for b in range(n_batch):
            same = (group_ref[b] == group_ref[batch]) & (b < batch)
            rank = rank + jnp.where(same, 1, 0)
        wi_part[...] = jnp.where(rank == 0, w_in_ref[0, :, 0:HALF], w_in_ref[0, :, HALF:FF_DEV])
        wb_part[...] = jnp.where(rank == 0, w_back_ref[0, 0:HALF, :], w_back_ref[0, HALF:FF_DEV, :])
        for a in range(2):
            hop_go(a, 1)
            own_over.append(send(part[a], whole[a].at[batch], across))
            local(part[a], whole[a].at[batch])

    exchanged = []
    route_rows(n_batch, group_ref, routes_ref, pos_ref, col_ref, offs)
    for slot, device in ((1, near), (2, far), (3, cater)):
        exchanged.append(send(offs, offs_all.at[pl.ds(slot, 1), :], device))
    local(offs, offs_all.at[pl.ds(0, 1), :])

    def sort_and_send(rows_ref, out_ref, out_hbm):
        pos = pos_ref[0:1, 0:ROWS]
        top = 0
        sent = []
        for size in SORT_TILES:
            want = top + lax.broadcasted_iota(I32, (size, ROWS), 0)
            hot = jnp.where(pos == want, 1.0, 0.0).astype(BF16)
            rows = pl.ds(top, size)
            out_ref[rows, :] = dot(hot, rows_ref[...]).astype(BF16)
            sent.append(send(out_ref.at[rows], out_hbm.at[2, rows], far))
            exchanged.append(send(out_ref.at[rows], out_hbm.at[1, rows], near))
            local(out_ref.at[rows], out_hbm.at[0, rows])
            top += size
        return sent

    def hand_on(sent, out_hbm):
        top = 0
        for copy, size in zip(sent, SORT_TILES):
            rows = pl.ds(top, size)
            copy.wait()
            exchanged.append(send(out_hbm.at[2, rows], out_hbm.at[3, rows], near))
            top += size

    held[1552:ROWS, :] = jnp.zeros((ROWS - 1552, D), BF16)
    held[0:TOK_DEV, :] = cot_ref[...]
    g_sent = sort_and_send(held, g_sorted, g_hbm)

    for i in range(3):
        top = min(TILE * (i + 1), TOK_DEV)
        rows = slice(TILE * i, top)
        normal, _ = norm_parts(tok_ref[rows, :].astype(F32))
        normed = (normal * gain_one_ref[...].reshape(1, D)).astype(BF16)
        qkv[rows, :] = dot(normed, w_qkv_ref[...]).astype(BF16)
    tail = slice(TOK_DEV, ROWS)
    qkv[tail, :] = jnp.zeros((ROWS - TOK_DEV, 3 * D), BF16)
    ctx[1552:ROWS, :] = jnp.zeros((ROWS - 1552, D), BF16)
    local(qkv, qkv_hbm)
    if small:
        hop_came(0, 1)

    @pl.loop(0, SEQ_DEV)
    def _(pair):
        attend_pair(pair, len_ref[pair], qkv, ctx, lse, stat)
        if small:

            @pl.when(pair == 1)
            def _():
                hop_came(1, 1)

            @pl.when(pair == 4)
            def _():
                hop_came(0, 2)

    local(ctx, ctx_hbm)
    local(lse, lse_hbm)
    for i in range(3):
        top = min(TILE * (i + 1), TOK_DEV)
        rows = slice(TILE * i, top)
        middle = tok_ref[rows, :].astype(F32) + dot(ctx[rows, :], w_proj_ref[...])
        mid[rows, :] = middle
        normal, _ = norm_parts(middle)
        held[rows, :] = (normal * gain_two_ref[...].reshape(1, D)).astype(BF16)
    local(mid, mid_hbm)
    if small:
        hop_came(1, 2)
    x_sent = sort_and_send(held, x_sorted, x_hbm)
    hand_on(g_sent, g_hbm)
    if small:
        hop_came(0, 3)
        hop_came(1, 3)
    hand_on(x_sent, x_hbm)
    for copy in exchanged + own_over:
        copy.wait()
    if small:
        for a in range(2):
            for hop in (1, 2, 3):
                hop_go(a, hop, finish=True)
            for way, hop in HOPS:
                origin = z - way * hop

                @pl.when(valid(origin))
                def _(a=a, way=way, hop=hop, origin=origin):
                    pass_copy(a, way, hop, origin, y).wait_send()
                    pass_copy(a, way, hop, origin, 1 - y).wait_recv()

    for copy in waiting:
        copy.wait()


def front(small, lengths, group_map, routes, tokens, *arrays):
    vmem = pl.BlockSpec(memory_space=pltpu.VMEM)
    any_space = pl.BlockSpec(memory_space=pl.ANY)
    tiles = len(SORT_TILES)
    copies = 6 * tiles + 2 + 3
    dma = pltpu.SemaphoreType.DMA
    return pl.pallas_call(
        functools.partial(front_kernel, small, group_map.shape[0]),
        out_shape=(
            jax.ShapeDtypeStruct((ROWS, 3 * D), BF16),
            jax.ShapeDtypeStruct((ROWS, D), BF16),
            jax.ShapeDtypeStruct((SEQ_DEV, 16, 384), F32),
            jax.ShapeDtypeStruct((TOK_DEV, D), F32),
            jax.ShapeDtypeStruct((4, SORTED, D), BF16),
            jax.ShapeDtypeStruct((4, SORTED, D), BF16),
            jax.ShapeDtypeStruct((8, D, HALF), BF16),
            jax.ShapeDtypeStruct((8, HALF, D), BF16),
            jax.ShapeDtypeStruct((4, 128), I32),
            jax.ShapeDtypeStruct((LANES, 128), I32),
        ),
        in_specs=[pl.BlockSpec(memory_space=pltpu.SMEM)] * 2 + [vmem] * (2 + len(arrays)),
        out_specs=(any_space,) * 8 + (vmem,) * 2,
        scratch_shapes=[
            pltpu.VMEM((ROWS, 3 * D), BF16),
            pltpu.VMEM((ROWS, D), BF16),
            pltpu.VMEM((SEQ_DEV, 16, 384), F32),
            pltpu.VMEM((TOK_DEV, D), F32),
            pltpu.VMEM((SORTED, D), BF16),
            pltpu.VMEM((SORTED, D), BF16),
            pltpu.VMEM((ROWS, D), BF16),
            pltpu.VMEM((384, 128), F32),
            pltpu.VMEM((1, LANES), I32),
            pltpu.VMEM((1, 128), I32),
            pltpu.VMEM((D, HALF), BF16),
            pltpu.VMEM((HALF, D), BF16),
            dma((2 * tiles + 7,)),
            dma((copies,)),
            dma((copies,)),
            dma((2, 6)),
            dma((2, 6)),
            dma((2, 6)),
            dma((2, 6)),
        ],
        compiler_params=params(collective_id=1, has_side_effects=True),
        name="front",
    )(lengths, group_map, routes, tokens, *arrays)


def gelu_both(u):
    below = 0.5 * (1.0 + lax.erf(u * (1.0 / math.sqrt(2.0))))
    density = jnp.exp(-0.5 * u * u) * (1.0 / math.sqrt(2.0 * math.pi))
    return u * below, below + u * density


MERGED = 2 * SORTED + 256


def expert_kernel(sources, carried, n_batch, offs_ref, group_ref, *refs):
    refs = list(refs)

    def take(count):
        head = refs[:count]
        del refs[:count]
        return head

    xs, gs = take(2), take(2)
    wi_hbm, wb_hbm = take(2)
    before = take(2) if carried else None
    outs, gxs = take(2), take(2)
    dwi_ref, dwb_ref = take(2)
    xm, gm, wi, wb, acc_i, acc_b, hosts_ref, sems = refs
    expert = pl.program_id(0)
    slot = expert % 2

    def weight_copies(e, buffer, start):
        for p in range(2):
            host = hosts_ref[e * 2 + p]
            part = pl.ds(p * HALF, HALF)
            for number, source, target in (
                (0, wi_hbm.at[host], wi.at[buffer, :, part]),
                (1, wb_hbm.at[host], wb.at[buffer, part, :]),
            ):
                copy = pltpu.make_async_copy(source, target, sems.at[buffer, p, number])
                if start:
                    copy.start()
                else:
                    copy.wait()

    @pl.when(expert == 0)
    def _():
        for e in range(EXPERTS):
            first_host, second_host = jnp.int32(n_batch), jnp.int32(n_batch)
            for b in reversed(range(n_batch)):
                hosting = group_ref[b] == e
                second_host = jnp.where(hosting, first_host, second_host)
                first_host = jnp.where(hosting, b, first_host)
            hosts_ref[2 * e] = first_host
            hosts_ref[2 * e + 1] = second_host
        weight_copies(0, 0, True)

    @pl.when(expert + 1 < EXPERTS)
    def _():
        weight_copies(expert + 1, 1 - slot, True)

    def blocks(count, act):
        @pl.loop(0, count)
        def _(i):
            act(pl.multiple_of(i * 16, 16))

    @pl.when(expert == 0)
    def _():
        for s in range(2):
            live = pl.multiple_of(offs_ref[sources[s], EXPERTS], 16)

            def clear(at, s=s, live=live):
                rows = pl.ds(pl.multiple_of(live + at, 16), 16)
                outs[s][rows, :] = jnp.zeros((16, D), BF16)
                gxs[s][rows, :] = jnp.zeros((16, D), BF16)

            blocks((SORTED - live) // 16, clear)

    if carried:
        acc_i[...] = before[0][0].astype(F32)
        acc_b[...] = before[1][0].astype(F32)
    else:
        acc_i[...] = jnp.zeros_like(acc_i)
        acc_b[...] = jnp.zeros_like(acc_b)

    places = []
    total = jnp.int32(0)
    for s in range(2):
        first = pl.multiple_of(offs_ref[sources[s], expert], 16)
        size = offs_ref[sources[s], expert + 1] - first
        places.append((first, total, size // 16))

        def gather(at, s=s, first=first, total=total):
            here = pl.ds(pl.multiple_of(first + at, 16), 16)
            there = pl.ds(pl.multiple_of(total + at, 16), 16)
            xm[there, :] = xs[s][0, here, :]
            gm[there, :] = gs[s][0, here, :]

        blocks(size // 16, gather)
        total = total + size
    span = pl.multiple_of(total, 16)

    def blank(at):
        there = pl.ds(pl.multiple_of(span + at, 16), 16)
        xm[there, :] = jnp.zeros((16, D), BF16)
        gm[there, :] = jnp.zeros((16, D), BF16)

    blocks((256 - span % 256) // 16, blank)
    weight_copies(expert, slot, False)
    w_in, w_back = wi.at[slot], wb.at[slot]

    @pl.loop(0, (span + 255) // 256)
    def _(i):
        rows = pl.ds(pl.multiple_of(i * 256, 256), 256)
        x, g = xm[rows, :], gm[rows, :]
        inner = dot(x, w_in[...])
        hidden, slope = gelu_both(inner)
        hidden = hidden.astype(BF16)
        grad_hidden = dot(g, w_back[...], CONTRACT_LANES).astype(BF16)
        grad_inner = (grad_hidden.astype(F32) * slope).astype(BF16)
        xm[rows, :] = dot(hidden, w_back[...]).astype(BF16)
        gm[rows, :] = dot(grad_inner, w_in[...], CONTRACT_LANES).astype(BF16)
        acc_b[...] += dot(hidden, g, CONTRACT_ROWS)
        acc_i[...] += dot(x, grad_inner, CONTRACT_ROWS)

    dwi_ref[0] = acc_i[...].astype(BF16)
    dwb_ref[0] = acc_b[...].astype(BF16)
    for s in range(2):
        first, base, count = places[s]

        def hand_back(at, s=s, first=first, base=base):
            here = pl.ds(pl.multiple_of(first + at, 16), 16)
            there = pl.ds(pl.multiple_of(base + at, 16), 16)
            outs[s][here, :] = xm[there, :]
            gxs[s][here, :] = gm[there, :]

        blocks(count, hand_back)


def experts(sources, offs, group_map, x, g, wi, wb, before=None):
    whole = once((SORTED, D))
    any_space = pl.BlockSpec(memory_space=pl.ANY)
    weight = pl.BlockSpec((1, D, FF_DEV), lambda e, *_: (e, 0, 0))
    carried = before is not None
    rows = jax.ShapeDtypeStruct((SORTED, D), BF16)
    grad = jax.ShapeDtypeStruct((EXPERTS, D, FF_DEV), BF16)

    def source(i):
        return pl.BlockSpec(
            (1, SORTED, D), lambda e, *_: (i, 0, 0), pipeline_mode=pl.Buffered(1)
        )

    picked = [source(i) for i in sources]
    return pl.pallas_call(
        functools.partial(expert_kernel, sources, carried, group_map.shape[0]),
        grid_spec=pltpu.PrefetchScalarGridSpec(
            num_scalar_prefetch=2,
            grid=(EXPERTS,),
            in_specs=picked + picked + [any_space] * 2 + [weight] * (2 * carried),
            out_specs=[whole] * 4 + [weight] * 2,
            scratch_shapes=[
                pltpu.VMEM((MERGED, D), BF16),
                pltpu.VMEM((MERGED, D), BF16),
                pltpu.VMEM((2, D, FF_DEV), BF16),
                pltpu.VMEM((2, FF_DEV, D), BF16),
                pltpu.VMEM((D, FF_DEV), F32),
                pltpu.VMEM((FF_DEV, D), F32),
                pltpu.SMEM((2 * EXPERTS,), I32),
                pltpu.SemaphoreType.DMA((2, 2, 2)),
            ],
        ),
        out_shape=(rows,) * 4 + (grad,) * 2,
        compiler_params=params(),
        cost_estimate=cost(24 * SORTED * D * FF_DEV, 16 * SORTED * D),
        name="experts",
    )(offs, group_map, x, x, g, g, wi, wb, *(before or ()))


def swap(rows, bit):
    pairs = [(f, f ^ bit) for f in range(4)]
    return lax.ppermute(rows, "ffn", pairs)


def tie(value, *others):
    return lax.optimization_barrier((value, *others))[0]


class Wire:
    def __init__(self, send_sems, recv_sems):
        self.send_sems, self.recv_sems, self.used = send_sems, recv_sems, 0

    def send(self, src, dst, device):
        number = self.used
        self.used += 1
        copy = pltpu.make_async_remote_copy(
            src_ref=src,
            dst_ref=dst,
            send_sem=self.send_sems.at[number],
            recv_sem=self.recv_sems.at[number],
            device_id=device,
            device_id_type=MESH,
        )
        copy.start()
        return copy


class Mover:
    def __init__(self, sems):
        self.sems, self.used = sems, 0

    def go(self, src, dst):
        number = self.used
        self.used += 1
        copy = pltpu.make_async_copy(src, dst, self.sems.at[number])
        copy.start()
        return copy


def greet(peers):
    barrier = pltpu.get_barrier_semaphore()
    for device in peers:
        pl.semaphore_signal(barrier, inc=1, device_id=device, device_id_type=MESH)
    pl.semaphore_wait(barrier, len(peers))


def wait_all(copies):
    for copy in copies:
        copy.wait()


def token_tiles():
    for i in range(3):
        yield slice(TILE * i, min(TILE * (i + 1), TOK_DEV))


def unsort(pos_col, src):
    want = lax.broadcasted_iota(I32, (pos_col.shape[0], SORTED), 1)
    hot = jnp.where(pos_col == want, 1.0, 0.0).astype(BF16)
    return dot(hot, src)


def attend_back_pair(pair, length, qkv_ref, gctx_ref, lse_ref, out_ref):
    start, skip = window(pair)
    start = pl.multiple_of(start, 16)
    row = lax.broadcasted_iota(I32, (WIN, 1), 0)
    mine = (row >= skip) & (row < skip + SEQ_LEN)
    bias = jnp.where((row >= skip) & (row < skip + PATCHES + length), 0.0, -1e30)
    lane = lax.broadcasted_iota(I32, (WIN, 128), 1)
    scale = jnp.asarray(HEAD_DIM**-0.5, BF16)
    for hp in range(HEADS // 2):
        spots = [slice(part * D + hp * 128, part * D + hp * 128 + 128) for part in range(3)]
        q, k, v = [qkv_ref[pl.ds(start, WIN), spot] for spot in spots]
        q = q * scale
        ks = k * scale
        go = gctx_ref[pl.ds(start, WIN), hp * 128 : hp * 128 + 128]
        q = jnp.where(mine, q, jnp.zeros_like(q))
        go = jnp.where(mine, go, jnp.zeros_like(go))
        grads = []
        for half in range(2):
            head = hp * 2 + half
            inside = (lane < 64) if half == 0 else (lane >= 64)
            qh = jnp.where(inside, q, jnp.zeros_like(q))
            gh = jnp.where(inside, go, jnp.zeros_like(go))
            scores = dot(k, qh, CONTRACT_LANES)
            probs = jnp.exp(scores + bias - lse_ref[pair, head : head + 1, 0:WIN])
            grad_probs = dot(v, gh, CONTRACT_LANES)
            delta = jnp.sum(probs * grad_probs, axis=0, keepdims=True)
            grad_scores = (probs * (grad_probs - delta)).astype(BF16)
            grad_v = dot(probs.astype(BF16), go)
            grad_k = dot(grad_scores, q)
            grad_q = dot(grad_scores, ks, CONTRACT_ROWS)
            grads.append((grad_q, grad_k, grad_v))
        for spot, low, high in zip(spots, grads[0], grads[1]):
            new = jnp.where(lane < 64, low, high).astype(BF16)
            old = out_ref[pl.ds(start, WIN), spot]
            out_ref[pl.ds(start, WIN), spot] = jnp.where(mine, new, old)


CHUNK = D // 8
TURNS = (2, 3, 1, 0)


def rear_kernel(
    small,
    len_ref,
    pos_ref,
    gain_one_ref,
    gain_two_ref,
    w_ref,
    lse_ref,
    gx0_hbm,
    gx1_hbm,
    gx2_hbm,
    mid_hbm,
    cot_hbm,
    ctx_hbm,
    qkv_hbm,
    tok_hbm,
    out1_hbm,
    out2_hbm,
    out3_hbm,
    dwi_hbm,
    dwb_hbm,
    gm_hbm,
    gq_hbm,
    dwq_hbm,
    dwp_hbm,
    dg_ref,
    share_hbm,
    near_hbm,
    far_hbm,
    wide,
    mid,
    cot,
    ctx,
    gctx,
    qkv,
    half_a,
    half_b,
    own_rows,
    came_y,
    came_z,
    acc,
    dwp,
    local_sems,
    send_sems,
    recv_sems,
    z_send,
    z_recv,
):
    batch, ffn = lax.axis_index("batch"), lax.axis_index("ffn")
    z, y = batch // 2, batch % 2
    near, far, across = (batch, ffn ^ 1), (batch, ffn ^ 2), (batch ^ 1, ffn)
    along = {k: (batch ^ (2 * k), ffn) for k in (1, 2, 3)}
    greet([near, far] + ([across] + list(along.values()) if small else []))
    wire, mover = Wire(send_sems, recv_sems), Mover(local_sems)

    parts_near = wire.send(gx1_hbm, wide.at[:, D : 2 * D], near)
    near_sent = wire.send(out3_hbm, half_b, near)
    half_in = mover.go(out2_hbm, half_a)
    over_y = {}
    own_in = {}
    if small:
        for turn in TURNS:
            there = pl.ds(pl.multiple_of(((z ^ turn) * 2 + 1 - y) * CHUNK, 16), CHUNK)
            over_y[turn] = [
                wire.send(grad.at[:, there, :], came_y.at[turn, i], across)
                for i, grad in enumerate((dwi_hbm, dwb_hbm))
            ]
    parts_in = [
        mover.go(part, wide.at[:, i * D : i * D + D])
        for i, part in ((0, gx0_hbm), (2, gx2_hbm))
    ]
    rows_in = [mover.go(mid_hbm, mid), mover.go(cot_hbm, cot), mover.go(ctx_hbm, ctx)]
    qkv_in = mover.go(qkv_hbm, qkv)
    if small:
        for turn in TURNS:
            here = pl.ds(pl.multiple_of(((z ^ turn) * 2 + y) * CHUNK, 16), CHUNK)
            own_in[turn] = [
                mover.go(grad.at[:, here, :], own_rows.at[turn, i])
                for i, grad in enumerate((dwi_hbm, dwb_hbm))
            ]
    sent = [wire.send(out1_hbm, near_hbm, near)]
    stored = []

    def z_copy(turn, i):
        return pltpu.make_async_remote_copy(
            src_ref=came_y.at[turn, i],
            dst_ref=came_z.at[turn - 1, i],
            send_sem=z_send.at[turn - 1, i],
            recv_sem=z_recv.at[turn - 1, i],
            device_id=along[turn],
            device_id_type=MESH,
        )

    def take_turn(turn, i):
        if not small:
            return
        over_y[turn][i].wait()
        own_in[turn][i].wait()
        for e in range(EXPERTS):
            came_y[turn, i, e] = (
                came_y[turn, i, e].astype(F32) + own_rows[turn, i, e].astype(F32)
            ).astype(BF16)
        if turn:
            z_copy(turn, i).start()

    wait_all(parts_in + rows_in + [parts_near])
    top = 0
    for size in SORT_TILES:
        rows = slice(top, top + size)
        wide[rows, 0:D] = (
            wide[rows, 0:D].astype(F32)
            + wide[rows, D : 2 * D].astype(F32)
            + wide[rows, 2 * D : 3 * D].astype(F32)
        ).astype(BF16)
        top += size
    half_in.wait()
    near_sent.wait()
    half_a[...] = (half_a[...].astype(F32) + half_b[...].astype(F32)).astype(BF16)
    sent.append(wire.send(half_a, far_hbm, far))

    gctx[1552:ROWS, :] = jnp.zeros((ROWS - 1552, D), BF16)
    grad_gain = jnp.zeros((1, D), F32)
    for i, rows in enumerate(token_tiles()):
        grad_normed = unsort(pos_ref[rows, 0:1], wide[:, 0:D])
        normal, inverse = norm_parts(mid[rows, :])
        grad_gain = grad_gain + jnp.sum(grad_normed * normal, axis=0, keepdims=True)
        part = norm_pull(grad_normed, gain_two_ref[...].reshape(1, D), normal, inverse)
        grad_middle = cot[rows, :].astype(F32) + part
        mid[rows, :] = grad_middle
        low = grad_middle.astype(BF16)
        product = dot(ctx[rows, :], low, CONTRACT_ROWS)
        if i == 0:
            acc[...] = product
        elif i == 1:
            acc[...] += product
        else:
            dwp[...] = (acc[...] + product).astype(BF16)
        gctx[rows, :] = dot(low, w_ref[...], CONTRACT_LANES).astype(BF16)
        if i < 2:
            take_turn(2, i)
    dg_ref[...] = grad_gain
    stored.append(mover.go(mid, gm_hbm))
    stored.append(mover.go(dwp, dwp_hbm))
    tok_in = mover.go(tok_hbm, cot)
    wide[1552:SORTED, :] = jnp.zeros((SORTED - 1552, 3 * D), BF16)
    qkv_in.wait()
    take_turn(3, 0)

    @pl.loop(0, SEQ_DEV)
    def _(pair):
        attend_back_pair(pair, len_ref[pair], qkv, gctx, lse_ref, wide)
        for when, turn, i in ((1, 3, 1), (3, 1, 0), (4, 1, 1)):

            @pl.when(pair == when)
            def _(turn=turn, i=i):
                take_turn(turn, i)

    stored.append(mover.go(wide.at[0:ROWS, :], gq_hbm))
    tok_in.wait()
    for rows in token_tiles():
        normal, _ = norm_parts(cot[rows, :].astype(F32))
        gctx[rows, :] = (normal * gain_one_ref[...].reshape(1, D)).astype(BF16)
    for i in range(3):
        cols = slice(i * D, i * D + D)
        qkv[0:D, cols] = dot(gctx[...], wide[0:ROWS, cols], CONTRACT_ROWS).astype(BF16)
    stored.append(mover.go(qkv.at[0:D, :], dwq_hbm))
    if small:
        take_turn(0, 0)
        take_turn(0, 1)
        wait_all([z_copy(turn, i) for turn in TURNS[:3] for i in range(2)])
        for i in range(2):
            for e in range(EXPERTS):
                total = came_y[0, i, e].astype(F32)
                for k in range(3):
                    total = total + came_z[k, i, e].astype(F32)
                came_y[0, i, e] = total.astype(BF16)
        stored.append(mover.go(came_y.at[0], share_hbm))
    wait_all(sent + stored)


def rear(small, lengths, pos_col, gain_one, gain_two, w_proj, lse, *arrays):
    vmem = pl.BlockSpec(memory_space=pltpu.VMEM)
    any_space = pl.BlockSpec(memory_space=pl.ANY)
    dma = pltpu.SemaphoreType.DMA
    copies = 12
    return pl.pallas_call(
        functools.partial(rear_kernel, small),
        out_shape=(
            jax.ShapeDtypeStruct((TOK_DEV, D), F32),
            jax.ShapeDtypeStruct((ROWS, 3 * D), BF16),
            jax.ShapeDtypeStruct((D, 3 * D), BF16),
            jax.ShapeDtypeStruct((D, D), BF16),
            jax.ShapeDtypeStruct((1, D), F32),
            jax.ShapeDtypeStruct((2, EXPERTS, CHUNK, D), BF16),
            jax.ShapeDtypeStruct((SORTED, D), BF16),
            jax.ShapeDtypeStruct((SORTED, D), BF16),
        ),
        in_specs=[pl.BlockSpec(memory_space=pltpu.SMEM)] + [vmem] * 5 + [any_space] * len(arrays),
        out_specs=(any_space,) * 4 + (vmem,) + (any_space,) * 3,
        scratch_shapes=[
            pltpu.VMEM((SORTED, 3 * D), BF16),
            pltpu.VMEM((TOK_DEV, D), F32),
            pltpu.VMEM((TOK_DEV, D), BF16),
            pltpu.VMEM((ROWS, D), BF16),
            pltpu.VMEM((ROWS, D), BF16),
            pltpu.VMEM((ROWS, 3 * D), BF16),
            pltpu.VMEM((SORTED, D), BF16),
            pltpu.VMEM((SORTED, D), BF16),
            pltpu.VMEM((4, 2, EXPERTS, CHUNK, D), BF16),
            pltpu.VMEM((4, 2, EXPERTS, CHUNK, D), BF16),
            pltpu.VMEM((3, 2, EXPERTS, CHUNK, D), BF16),
            pltpu.VMEM((D, D), F32),
            pltpu.VMEM((D, D), BF16),
            dma((24,)),
            dma((copies,)),
            dma((copies,)),
            dma((3, 2)),
            dma((3, 2)),
        ],
        compiler_params=params(collective_id=2, has_side_effects=True),
        name="rear",
    )(lengths, pos_col, gain_one, gain_two, w_proj, lse, *arrays)


ORDERS = (("x", "y", "z"), ("y", "x", "z"))
WIDE = 4 * D
COLOUR = WIDE // 2
QUARTER = COLOUR // 4
GAIN_ROWS = 8


def last_kernel(
    small,
    group_ref,
    pos_ref,
    gain_ref,
    w_ref,
    dg_two_ref,
    tok_hbm,
    gq_hbm,
    gm_hbm,
    mid_hbm,
    out0_hbm,
    out1_hbm,
    out2_hbm,
    dwq_hbm,
    dwp_hbm,
    share_hbm,
    ig_hbm,
    bo_hbm,
    sum_ref,
    gains_ref,
    pieces_ref,
    tok,
    gq,
    gm,
    mid,
    outs,
    share,
    stage,
    near_rows,
    held,
    came_z,
    came_xy,
    gain_in,
    local_sems,
    send_sems,
    recv_sems,
):
    batch, ffn = lax.axis_index("batch"), lax.axis_index("ffn")
    z, y, x, c = batch // 2, batch % 2, ffn // 2, ffn % 2
    place = {"x": x, "y": y, "z": z}
    mover = Mover(local_sems)

    def peer(axis, k=1):
        if axis == "c":
            return (batch, ffn ^ 1)
        if axis == "x":
            return (batch, ffn ^ 2)
        if axis == "y":
            return (batch ^ 1, ffn)
        return (batch ^ (2 * k), ffn)

    flying = []
    top = [0, 0]
    left = [COLOUR * i for i in range(2)]
    rows, cols = [384] * 2, [COLOUR] * 2
    base = pl.multiple_of(c * 384, 16)
    if small:
        greet([peer("c"), peer("x")] + [(batch ^ j, ffn) for j in range(1, 8)])
        wire = Wire(send_sems, recv_sems)
        share_in = mover.go(share_hbm, share)
        give = pl.ds(pl.multiple_of((1 - c) * 384, 16), 384)
        keep = pl.ds(base, 384)
        to_core = [
            wire.send(dwq_hbm.at[give, :], near_rows.at[:, 0 : 3 * D], peer("c")),
            wire.send(dwp_hbm.at[give, :], near_rows.at[:, 3 * D : WIDE], peer("c")),
        ]
        kept = [
            mover.go(dwq_hbm.at[keep, :], held.at[:, 0 : 3 * D]),
            mover.go(dwp_hbm.at[keep, :], held.at[:, 3 * D : WIDE]),
        ]
    loads = [mover.go(tok_hbm, tok), mover.go(gq_hbm, gq), mover.go(gm_hbm, gm)]
    later = [mover.go(mid_hbm, mid)] + [
        mover.go(part, outs.at[i]) for i, part in enumerate((out0_hbm, out1_hbm, out2_hbm))
    ]
    handed = []

    def hand_out(i):
        for j in range(1, 8):
            handed.append(
                wire.send(stage.at[j, i], pieces_ref.at[batch, i], (batch ^ j, ffn))
            )

    if small:
        share_in.wait()
        for j in range(8):
            expert = group_ref[batch ^ j]
            for i in range(2):
                stage[j, i] = share[i, expert]
        hand_out(0)
        pieces_ref[batch] = stage[0]

    def core_done():
        wait_all(to_core + kept)
        for i in range(4):
            lanes = slice(i * D, i * D + D)
            held[:, lanes] = (
                held[:, lanes].astype(F32) + near_rows[:, lanes].astype(F32)
            ).astype(BF16)

    def sum_go(step):
        for i in range(2):
            axis = ORDERS[i][step]
            if axis == "z":
                live = pl.ds(top[i], rows[i])
                for k in (1, 2, 3):
                    there = pl.ds(pl.multiple_of(left[i] + (z ^ k) * QUARTER, 128), QUARTER)
                    flying.append(
                        wire.send(
                            held.at[live, there], came_z.at[i, k - 1, 0 : rows[i]], peer("z", k)
                        )
                    )
            else:
                half = rows[i] // 2
                there = pl.ds(pl.multiple_of(top[i] + (1 - place[axis]) * half, 16), half)
                flying.append(
                    wire.send(
                        held.at[there, pl.ds(left[i], cols[i])],
                        came_xy.at[i, 0 if axis == "x" else 1, 0:half, 0 : cols[i]],
                        peer(axis),
                    )
                )

    def sum_done(step):
        wait_all(flying)
        flying.clear()
        for i in range(2):
            axis = ORDERS[i][step]
            if axis == "z":
                left[i] = pl.multiple_of(left[i] + z * QUARTER, 128)
                cols[i] = QUARTER
                terms = [came_z[i, k, 0 : rows[i]] for k in range(3)]
            else:
                rows[i] = rows[i] // 2
                top[i] = pl.multiple_of(top[i] + place[axis] * rows[i], 16)
                terms = [came_xy[i, 0 if axis == "x" else 1, 0 : rows[i], 0 : cols[i]]]
            spot = (pl.ds(top[i], rows[i]), pl.ds(left[i], cols[i]))
            total = held[spot].astype(F32)
            for term in terms:
                total = total + term.astype(F32)
            held[spot] = total.astype(BF16)

    def spread_go(step):
        for i in range(2):
            axis = ORDERS[i][step]
            mine = sum_ref.at[
                pl.ds(pl.multiple_of(base + top[i], 16), rows[i]), pl.ds(left[i], cols[i])
            ]
            for k in (1, 2, 3) if axis == "z" else (1,):
                flying.append(wire.send(mine, mine, peer(axis, k)))

    def spread_done(step):
        wait_all(flying)
        flying.clear()
        for i in range(2):
            axis = ORDERS[i][step]
            if axis == "z":
                left[i] = COLOUR * i
                cols[i] = COLOUR
            else:
                top[i] = top[i] - place[axis] * rows[i]
                rows[i] = rows[i] * 2

    def gains_go(axis, slot):
        for k in (1, 2, 3) if axis == "z" else (1,):
            flying.append(wire.send(gains_ref, gain_in.at[slot + k - 1], peer(axis, k)))

    def gains_done(axis, slot):
        total = gains_ref[...]
        for k in (0, 1, 2) if axis == "z" else (0,):
            total = total + gain_in[slot + k]
        gains_ref[...] = total

    tiles = list(token_tiles())
    grad_gain = jnp.zeros((1, D), F32)
    stored = []

    def first_back(part):
        normal, inverse = norm_parts(tok[part, :].astype(F32))
        grad_normed = dot(gq[part, :], w_ref[...], CONTRACT_LANES)
        gain_part = jnp.sum(grad_normed * normal, axis=0, keepdims=True)
        pulled = norm_pull(grad_normed, gain_ref[...].reshape(1, D), normal, inverse)
        gm[part, :] = gm[part, :] + pulled
        stored.append(mover.go(gm.at[part], ig_hbm.at[part]))
        return gain_part

    def finish(part):
        mid[part, :] = mid[part, :] + unsort(pos_ref[part, 0:1], outs[0])
        stored.append(mover.go(mid.at[part], bo_hbm.at[part]))

    wait_all(loads)
    grad_gain = grad_gain + first_back(tiles[0])
    if small:
        core_done()
        sum_go(0)
    grad_gain = grad_gain + first_back(tiles[1])
    grad_gain = grad_gain + first_back(tiles[2])
    gains_ref[0:1, :] = grad_gain
    gains_ref[1:2, :] = dg_two_ref[...]
    gains_ref[2:GAIN_ROWS, :] = jnp.zeros((GAIN_ROWS - 2, D), F32)
    if small:
        gains_go("c", 0)
        sum_done(0)
        gains_done("c", 0)
        gains_go("x", 1)
        sum_go(1)
    wait_all(later)
    at = 0
    for size in SORT_TILES:
        part = slice(at, at + size)
        outs[0, part] = (
            outs[0, part].astype(F32) + outs[1, part].astype(F32) + outs[2, part].astype(F32)
        ).astype(BF16)
        at += size
    finish(tiles[0])
    if small:
        sum_done(1)
        gains_done("x", 1)
        gains_go("y", 2)
        sum_go(2)
    finish(tiles[1])
    if small:
        sum_done(2)
        gains_done("y", 2)
        for i in range(2):
            spot = (pl.ds(top[i], rows[i]), pl.ds(left[i], cols[i]))
            sum_ref[pl.ds(pl.multiple_of(base + top[i], 16), rows[i]), spot[1]] = held[spot]
        gains_go("z", 3)
        spread_go(2)
    finish(tiles[2])
    if small:
        spread_done(2)
        gains_done("z", 3)
        spread_go(1)
        hand_out(1)
        spread_done(1)
        spread_go(0)
        spread_done(0)
        mine = sum_ref.at[pl.ds(base, 384), :]
        wire.send(mine, mine, peer("c")).wait()
        wait_all(handed)
    wait_all(stored)


def last(small, group_map, pos_col, gain_one, w_qkv, dg_two, *arrays):
    vmem = pl.BlockSpec(memory_space=pltpu.VMEM)
    any_space = pl.BlockSpec(memory_space=pl.ANY)
    dma = pltpu.SemaphoreType.DMA
    copies = 2 + 14 + 10 + 10 + 6 + 1
    extra = dict(collective_id=3, has_side_effects=True) if small else {}
    return pl.pallas_call(
        functools.partial(last_kernel, small),
        out_shape=(
            jax.ShapeDtypeStruct((TOK_DEV, D), F32),
            jax.ShapeDtypeStruct((TOK_DEV, D), F32),
            jax.ShapeDtypeStruct((D, WIDE), BF16),
            jax.ShapeDtypeStruct((GAIN_ROWS, D), F32),
            jax.ShapeDtypeStruct((8, 2, CHUNK, D), BF16),
        ),
        in_specs=[pl.BlockSpec(memory_space=pltpu.SMEM)] + [vmem] * 4 + [any_space] * len(arrays),
        out_specs=(any_space,) * 2 + (vmem,) * 3,
        scratch_shapes=[
            pltpu.VMEM((TOK_DEV, D), BF16),
            pltpu.VMEM((ROWS, 3 * D), BF16),
            pltpu.VMEM((TOK_DEV, D), F32),
            pltpu.VMEM((TOK_DEV, D), F32),
            pltpu.VMEM((3, SORTED, D), BF16),
            pltpu.VMEM((2, EXPERTS, CHUNK, D), BF16),
            pltpu.VMEM((8, 2, CHUNK, D), BF16),
            pltpu.VMEM((384, WIDE), BF16),
            pltpu.VMEM((384, WIDE), BF16),
            pltpu.VMEM((2, 3, 96, QUARTER), BF16),
            pltpu.VMEM((2, 2, 192, COLOUR), BF16),
            pltpu.VMEM((6, GAIN_ROWS, D), F32),
            dma((16,)),
            dma((copies,)),
            dma((copies,)),
        ],
        compiler_params=params(**extra),
        name="last",
    )(group_map, pos_col, gain_one, w_qkv, dg_two, *arrays)


def close_kernel(
    sum_ref, gains_ref, pieces_ref, ig_ref, bo_ref, *outs
):
    qkv_ref, proj_ref, one_ref, two_ref, wi_ref, wb_ref, ig_out, bo_out = outs
    qkv_ref[...] = sum_ref[:, 0 : 3 * D].astype(F32)
    proj_ref[...] = sum_ref[:, 3 * D : WIDE].astype(F32)
    one_ref[...] = gains_ref[0:1, :].reshape(D)
    two_ref[...] = gains_ref[1:2, :].reshape(D)
    wi_ref[0] = pieces_ref[0, 0].astype(F32)
    wb_ref[0] = pieces_ref[0, 1].astype(F32)
    ig_out[...] = ig_ref[...]
    bo_out[...] = bo_ref[...]


def close(summed, gains, pieces, input_grad, block_out):
    row = pl.BlockSpec((CHUNK, D), lambda i: (i, 0))
    tokens = pl.BlockSpec((200, D), lambda i: (i, 0))
    weight = pl.BlockSpec((1, CHUNK, D), lambda i: (0, i, 0))
    rows = jax.ShapeDtypeStruct((TOK_DEV, D), F32)
    return pl.pallas_call(
        close_kernel,
        grid=(8,),
        out_shape=(
            jax.ShapeDtypeStruct((D, 3 * D), F32),
            jax.ShapeDtypeStruct((D, D), F32),
            jax.ShapeDtypeStruct((D,), F32),
            jax.ShapeDtypeStruct((D,), F32),
            jax.ShapeDtypeStruct((1, D, D), F32),
            jax.ShapeDtypeStruct((1, D, D), F32),
            rows,
            rows,
        ),
        in_specs=[
            pl.BlockSpec((CHUNK, WIDE), lambda i: (i, 0)),
            full((GAIN_ROWS, D)),
            pl.BlockSpec((1, 2, CHUNK, D), lambda i: (i, 0, 0, 0)),
            tokens,
            tokens,
        ],
        out_specs=(
            pl.BlockSpec((CHUNK, 3 * D), lambda i: (i, 0)),
            row,
            full((D,)),
            full((D,)),
            weight,
            weight,
            tokens,
            tokens,
        ),
        compiler_params=params(),
        name="close",
    )(summed, gains, pieces, input_grad, block_out)


def body(
    tokens,
    text_lengths,
    routes,
    group_map,
    gain_one,
    w_qkv,
    w_proj,
    gain_two,
    w_in,
    w_back,
    cotangent,
):
    n_batch = lax.axis_size("batch")
    own = lax.axis_index("batch")
    small = n_batch == 8
    routes_row = jnp.pad(routes.reshape(1, TOK_DEV), ((0, 0), (0, LANES - TOK_DEV)))
    qkv, context, lse, middle, g, x, wi_all, wb_all, offs, pos_col = front(
        small,
        text_lengths,
        group_map,
        routes_row,
        tokens,
        cotangent,
        gain_one,
        w_qkv,
        w_proj,
        gain_two,
        w_in,
        w_back,
    )
    if not small:
        own_expert = group_map[own]
        order = jnp.arange(n_batch, dtype=I32)
        rank = jnp.sum(jnp.where((group_map == own_expert) & (order < own), 1, 0))
        part = jnp.minimum(rank, 1)
        wi_part = lax.dynamic_slice(w_in[0], (0, part * HALF), (D, HALF))
        wb_part = lax.dynamic_slice(w_back[0], (part * HALF, 0), (HALF, D))
        wi_all = lax.all_gather(wi_part, "batch", axis=0)
        wb_all = lax.all_gather(wb_part, "batch", axis=0)

    def run(pair, x, before):
        return experts(
            pair,
            offs,
            group_map,
            x,
            g,
            wi_all,
            wb_all,
            before,
        )

    def add(a, b):
        return (a.astype(F32) + b.astype(F32)).astype(BF16)

    out2, out3, gx2, gx3, dwi, dwb = run((2, 3), x, None)
    gx_half = add(gx2, swap(gx3, 1))
    gx_far = swap(gx_half, 2)
    out0, out1, gx0, gx1, dwi, dwb = run((0, 1), tie(x, gx_half), (dwi, dwb))
    grad_middle, grad_qkv, dw_qkv, dw_proj, dg_two, share, out_near, out_far = rear(
        small,
        text_lengths,
        pos_col,
        gain_one,
        gain_two,
        w_proj,
        lse,
        gx0,
        gx1,
        gx_far,
        middle,
        cotangent,
        context,
        qkv,
        tokens,
        out1,
        out2,
        out3,
        dwi,
        dwb,
    )
    input_grad, block_out, summed, gains, pieces = last(
        small,
        group_map,
        pos_col,
        gain_one,
        w_qkv,
        dg_two,
        tokens,
        grad_qkv,
        grad_middle,
        middle,
        out0,
        out_near,
        out_far,
        dw_qkv,
        dw_proj,
        share,
    )
    if small:
        summed_qkv, summed_proj, gain_a, gain_b, grad_w_in, grad_w_back, input_grad, block_out = close(
            summed, gains, pieces, input_grad, block_out
        )
        gains = (gain_a, gain_b)
    else:

        def settle_any(grad):
            share = lax.psum_scatter(grad, "batch", scatter_dimension=1, tiled=True)
            whole = lax.all_gather(share, "batch", axis=1, tiled=True)
            return lax.dynamic_index_in_dim(whole, own_expert, 0, keepdims=True).astype(F32)

        grad_w_in = settle_any(dwi)
        grad_w_back = settle_any(dwb)
        summed_qkv, summed_proj = lax.psum((dw_qkv, dw_proj), ("batch", "ffn"))
        gains = lax.psum(gains, ("batch", "ffn"))
    return (
        block_out,
        input_grad,
        gains[0],
        summed_qkv.astype(F32),
        summed_proj.astype(F32),
        gains[1],
        grad_w_in,
        grad_w_back,
    )


def solution(mesh):
    placed = (
        P(("batch", "ffn"), None),
        P(("batch", "ffn")),
        P(("batch", "ffn"), None),
        P(),
        P(),
        P(),
        P(),
        P(),
        P("batch", None, "ffn"),
        P("batch", "ffn", None),
        P(("batch", "ffn"), None),
    )
    return jax.shard_map(
        body,
        mesh=mesh,
        in_specs=placed,
        out_specs=(
            P(("batch", "ffn"), None),
            P(("batch", "ffn"), None),
            P(),
            P(),
            P(),
            P(),
            P("batch", None, "ffn"),
            P("batch", "ffn", None),
        ),
        check_vma=False,
    )
```

```python
import functools
import math

import jax
import jax.numpy as jnp
from jax import lax
from jax.experimental import pallas as pl
from jax.experimental.pallas import tpu as pltpu
from jax.sharding import PartitionSpec as P

D = 768
HEADS = 12
HEAD_DIM = 64
EXPERTS = 3
PATCHES = 197
SEQ_DEV = 6
SEQ_LEN = 261
TOK_DEV = 1566
ROWS = 1584
SORTED = 1616
WIN = 288
TILE = 528
LANES = 1664
EPS = 1e-05
F32 = jnp.float32
BF16 = jnp.bfloat16
I32 = jnp.int32
CONTRACT_LANES = (((1,), (1,)), ((), ()))
CONTRACT_ROWS = (((0,), (0,)), ((), ()))


def params(**extra):
    return pltpu.CompilerParams(vmem_limit_bytes=60 << 20, **extra)


def cost(flops, moved):
    return pl.CostEstimate(flops=int(flops), bytes_accessed=int(moved), transcendentals=0)


def dot(a, b, dims=(((1,), (0,)), ((), ()))):
    return lax.dot_general(a, b, dims, preferred_element_type=F32)


def full(shape):
    zeros = (0,) * len(shape)
    return pl.BlockSpec(shape, lambda *_: zeros)


def once(shape):
    zeros = (0,) * len(shape)
    return pl.BlockSpec(shape, lambda *_: zeros, pipeline_mode=pl.Buffered(1))


def row_mask(start, rows, limit):
    return start + lax.broadcasted_iota(I32, (rows, 1), 0) < limit


def norm_parts(values):
    average = jnp.mean(values, axis=-1, keepdims=True)
    centred = values - average
    variance = jnp.mean(centred * centred, axis=-1, keepdims=True)
    inverse = lax.rsqrt(variance + EPS)
    return centred * inverse, inverse


def norm_pull(grad_normed, gain, normal, inverse):
    scaled = grad_normed * gain
    mean_grad = jnp.mean(scaled, axis=-1, keepdims=True)
    mean_proj = jnp.mean(scaled * normal, axis=-1, keepdims=True)
    return inverse * (scaled - mean_grad - normal * mean_proj)


def route_rows(n_batch, gm_ref, routes_ref, pos_ref, col_ref, offs_ref):
    routes = routes_ref[...]
    lane = lax.broadcasted_iota(I32, (8, LANES), 1)
    sub = lax.broadcasted_iota(I32, (8, LANES), 0)
    expert = jnp.zeros((1, LANES), I32)
    for b in range(n_batch):
        expert = jnp.where(routes == b, gm_ref[b], expert)
    live = lane < TOK_DEV
    hot = jnp.where((jnp.broadcast_to(expert, (8, LANES)) == sub) & live, 1, 0)
    count = hot
    step = 1
    while step < LANES:
        count = count + jnp.where(lane >= step, pltpu.roll(count, step, 1), 0)
        step *= 2
    totals = [jnp.sum(hot[e : e + 1, :], axis=1, keepdims=True) for e in range(EXPERTS)]
    starts = [jnp.zeros((1, 1), I32)]
    for e in range(EXPERTS):
        starts.append(starts[-1] + (totals[e] + 15) // 16 * 16)
    pos = jnp.zeros((1, LANES), I32)
    for e in range(EXPERTS):
        pos = pos + jnp.where(hot[e : e + 1, :] > 0, count[e : e + 1, :] - 1 + starts[e], 0)
    pos = jnp.where(live[0:1, :], pos, -1)
    pos_ref[...] = pos
    wide = jnp.broadcast_to(pos.astype(F32), (128, LANES))
    col_ref[...] = jnp.transpose(wide).astype(I32)
    slot = lax.broadcasted_iota(I32, (1, 128), 1)
    offs = jnp.zeros((1, 128), I32)
    for e in range(EXPERTS + 1):
        offs = jnp.where(slot == e, starts[e], offs)
    offs_ref[...] = offs


SORT_TILES = (336, 336, 336, 336, 272)


def window(pair):
    first = pair * SEQ_LEN
    start = first // 16 * 16
    return start, first - start


def head_cols(hp, part):
    return pl.ds(pl.multiple_of(part * D + hp * 128, 128), 128)


def attend_pair(pair, length, qkv_ref, ctx_ref, lse_ref, stat):
    start, skip = window(pair)
    start = pl.multiple_of(start, 16)
    key = lax.broadcasted_iota(I32, (1, WIN), 1)
    seen = (key >= skip) & (key < skip + PATCHES + length)
    bias = jnp.where(seen, 0.0, -1e30)
    row = lax.broadcasted_iota(I32, (WIN, 1), 0)
    mine = (row >= skip) & (row < skip + SEQ_LEN)
    lane = lax.broadcasted_iota(I32, (WIN, 128), 1)
    stat[...] = jnp.zeros_like(stat)
    @pl.loop(0, HEADS // 2)
    def _(hp):
        q, k, v = [qkv_ref[pl.ds(start, WIN), head_cols(hp, part)] for part in range(3)]
        cols = head_cols(hp, 0)
        q = q * jnp.asarray(HEAD_DIM**-0.5, BF16)
        pieces = []
        for half in range(2):
            inside = (lane < 64) if half == 0 else (lane >= 64)
            qh = jnp.where(inside, q, jnp.zeros_like(q))
            scores = dot(qh, k, CONTRACT_LANES) + bias
            peak = jnp.max(scores, axis=1, keepdims=True)
            weight = jnp.exp(scores - peak).astype(BF16)
            vh = jnp.where(inside, v, jnp.ones_like(v))
            mixed = dot(weight, vh)
            total = pltpu.roll(mixed, 64, 1)
            pieces.append(mixed / total)
            one = total[:, 0:1] if half == 0 else mixed[:, 0:1]
            head = hp * 2 + half
            stat[0:WIN, :] = jnp.where(lane == head, peak + jnp.log(one), stat[0:WIN, :])
        ctx = jnp.where(lane < 64, pieces[0], pieces[1]).astype(BF16)
        old = ctx_ref[pl.ds(start, WIN), cols]
        ctx_ref[pl.ds(start, WIN), cols] = jnp.where(mine, ctx, old)
    lse_ref[pair] = jnp.transpose(stat[...])[0:16, :]


MESH = pl.DeviceIdType.MESH
HALF = 384
FF_DEV = 768
HOPS = [(way, hop) for hop in (1, 2, 3) for way in (1, -1)]


def front_kernel(
    small,
    n_batch,
    len_ref,
    group_ref,
    routes_ref,
    tok_ref,
    cot_ref,
    gain_one_ref,
    w_qkv_ref,
    w_proj_ref,
    gain_two_ref,
    w_in_ref,
    w_back_ref,
    qkv_hbm,
    ctx_hbm,
    lse_hbm,
    mid_hbm,
    g_hbm,
    x_hbm,
    wi_all,
    wb_all,
    offs_all,
    col_ref,
    qkv,
    ctx,
    lse,
    mid,
    g_sorted,
    x_sorted,
    held,
    stat,
    pos_ref,
    offs,
    wi_part,
    wb_part,
    local_sems,
    send_sems,
    recv_sems,
    hop_send,
    hop_recv,
    pass_send,
    pass_recv,
):
    batch, ffn = lax.axis_index("batch"), lax.axis_index("ffn")
    z, y = batch // 2, batch % 2
    near, far, cater = (batch, ffn ^ 1), (batch, ffn ^ 2), (batch, ffn ^ 3)
    across = (batch ^ 1, ffn)

    barrier = pltpu.get_barrier_semaphore()
    for device in [near, far, cater] + ([across] if small else []):
        pl.semaphore_signal(barrier, inc=1, device_id=device, device_id_type=MESH)
    if small:
        for way in (1, -1):

            @pl.when((z + way >= 0) & (z + way <= 3))
            def _(way=way):
                pl.semaphore_signal(
                    barrier, inc=1, device_id=(batch + 2 * way, ffn), device_id_type=MESH
                )

        inner = jnp.where((z == 0) | (z == 3), 1, 2)
        pl.semaphore_wait(barrier, 4 + inner)
    else:
        pl.semaphore_wait(barrier, 3)

    local_count = [0]
    waiting = []

    def local(src, dst):
        number = local_count[0]
        local_count[0] += 1
        copy = pltpu.make_async_copy(src, dst, local_sems.at[number])
        copy.start()
        waiting.append(copy)

    used = [0]

    def send(src, dst, device):
        number = used[0]
        used[0] += 1
        copy = pltpu.make_async_remote_copy(
            src_ref=src,
            dst_ref=dst,
            send_sem=send_sems.at[number],
            recv_sem=recv_sems.at[number],
            device_id=device,
            device_id_type=MESH,
        )
        copy.start()
        return copy

    part, whole = (wi_part, wb_part), (wi_all, wb_all)

    def valid(origin):
        return (origin >= 0) & (origin <= 3)

    def hop_copy(a, way, hop, origin, device):
        slot = whole[a].at[origin * 2 + y]
        number = HOPS.index((way, hop))
        return pltpu.make_async_remote_copy(
            src_ref=part[a] if hop == 1 else slot,
            dst_ref=slot,
            send_sem=hop_send.at[a, number],
            recv_sem=hop_recv.at[a, number],
            device_id=device,
            device_id_type=MESH,
        )

    def hop_go(a, hop, finish=False):
        for way in (1, -1):
            origin = z - way * (hop - 1)

            @pl.when(valid(origin) & valid(z + way))
            def _(way=way, origin=origin):
                copy = hop_copy(a, way, hop, origin, (batch + 2 * way, ffn))
                if finish:
                    copy.wait_send()
                else:
                    copy.start()

    def pass_copy(a, way, hop, origin, column):
        slot = whole[a].at[origin * 2 + column]
        number = HOPS.index((way, hop))
        return pltpu.make_async_remote_copy(
            src_ref=slot,
            dst_ref=slot,
            send_sem=pass_send.at[a, number],
            recv_sem=pass_recv.at[a, number],
            device_id=across,
            device_id_type=MESH,
        )

    def hop_came(a, hop):
        for way in (1, -1):
            origin = z - way * hop

            @pl.when(valid(origin))
            def _(way=way, origin=origin):
                hop_copy(a, way, hop, origin, (batch, ffn)).wait_recv()

        if hop < 3:
            hop_go(a, hop + 1)
        for way in (1, -1):
            origin = z - way * hop

            @pl.when(valid(origin))
            def _(way=way, origin=origin):
                pass_copy(a, way, hop, origin, y).start()

    own_over = []
    if small:
        rank = jnp.int32(0)
        for b in range(n_batch):
            same = (group_ref[b] == group_ref[batch]) & (b < batch)
            rank = rank + jnp.where(same, 1, 0)
        wi_part[...] = jnp.where(rank == 0, w_in_ref[0, :, 0:HALF], w_in_ref[0, :, HALF:FF_DEV])
        wb_part[...] = jnp.where(rank == 0, w_back_ref[0, 0:HALF, :], w_back_ref[0, HALF:FF_DEV, :])
        for a in range(2):
            hop_go(a, 1)
            own_over.append(send(part[a], whole[a].at[batch], across))
            local(part[a], whole[a].at[batch])

    exchanged = []
    route_rows(n_batch, group_ref, routes_ref, pos_ref, col_ref, offs)
    for slot, device in ((1, near), (2, far), (3, cater)):
        exchanged.append(send(offs, offs_all.at[pl.ds(slot, 1), :], device))
    local(offs, offs_all.at[pl.ds(0, 1), :])

    def sort_and_send(rows_ref, out_ref, out_hbm):
        pos = pos_ref[0:1, 0:ROWS]
        top = 0
        sent = []
        for size in SORT_TILES:
            want = top + lax.broadcasted_iota(I32, (size, ROWS), 0)
            hot = jnp.where(pos == want, 1.0, 0.0).astype(BF16)
            rows = pl.ds(top, size)
            out_ref[rows, :] = dot(hot, rows_ref[...]).astype(BF16)
            sent.append(send(out_ref.at[rows], out_hbm.at[2, rows], far))
            exchanged.append(send(out_ref.at[rows], out_hbm.at[1, rows], near))
            local(out_ref.at[rows], out_hbm.at[0, rows])
            top += size
        return sent

    def hand_on(sent, out_hbm):
        top = 0
        for copy, size in zip(sent, SORT_TILES):
            rows = pl.ds(top, size)
            copy.wait()
            exchanged.append(send(out_hbm.at[2, rows], out_hbm.at[3, rows], near))
            top += size

    held[1552:ROWS, :] = jnp.zeros((ROWS - 1552, D), BF16)
    held[0:TOK_DEV, :] = cot_ref[...]
    g_sent = sort_and_send(held, g_sorted, g_hbm)

    for i in range(3):
        top = min(TILE * (i + 1), TOK_DEV)
        rows = slice(TILE * i, top)
        normal, _ = norm_parts(tok_ref[rows, :].astype(F32))
        normed = (normal * gain_one_ref[...].reshape(1, D)).astype(BF16)
        qkv[rows, :] = dot(normed, w_qkv_ref[...]).astype(BF16)
    tail = slice(TOK_DEV, ROWS)
    qkv[tail, :] = jnp.zeros((ROWS - TOK_DEV, 3 * D), BF16)
    ctx[1552:ROWS, :] = jnp.zeros((ROWS - 1552, D), BF16)
    local(qkv, qkv_hbm)
    if small:
        hop_came(0, 1)

    @pl.loop(0, SEQ_DEV)
    def _(pair):
        attend_pair(pair, len_ref[pair], qkv, ctx, lse, stat)
        if small:

            @pl.when(pair == 1)
            def _():
                hop_came(1, 1)

            @pl.when(pair == 4)
            def _():
                hop_came(0, 2)

    local(ctx, ctx_hbm)
    local(lse, lse_hbm)
    for i in range(3):
        top = min(TILE * (i + 1), TOK_DEV)
        rows = slice(TILE * i, top)
        middle = tok_ref[rows, :].astype(F32) + dot(ctx[rows, :], w_proj_ref[...])
        mid[rows, :] = middle
        normal, _ = norm_parts(middle)
        held[rows, :] = (normal * gain_two_ref[...].reshape(1, D)).astype(BF16)
    local(mid, mid_hbm)
    if small:
        hop_came(1, 2)
    x_sent = sort_and_send(held, x_sorted, x_hbm)
    hand_on(g_sent, g_hbm)
    if small:
        hop_came(0, 3)
        hop_came(1, 3)
    hand_on(x_sent, x_hbm)
    for copy in exchanged + own_over:
        copy.wait()
    if small:
        for a in range(2):
            for hop in (1, 2, 3):
                hop_go(a, hop, finish=True)
            for way, hop in HOPS:
                origin = z - way * hop

                @pl.when(valid(origin))
                def _(a=a, way=way, hop=hop, origin=origin):
                    pass_copy(a, way, hop, origin, y).wait_send()
                    pass_copy(a, way, hop, origin, 1 - y).wait_recv()

    for copy in waiting:
        copy.wait()


def front(small, lengths, group_map, routes, tokens, *arrays):
    vmem = pl.BlockSpec(memory_space=pltpu.VMEM)
    any_space = pl.BlockSpec(memory_space=pl.ANY)
    tiles = len(SORT_TILES)
    copies = 6 * tiles + 2 + 3
    dma = pltpu.SemaphoreType.DMA
    return pl.pallas_call(
        functools.partial(front_kernel, small, group_map.shape[0]),
        out_shape=(
            jax.ShapeDtypeStruct((ROWS, 3 * D), BF16),
            jax.ShapeDtypeStruct((ROWS, D), BF16),
            jax.ShapeDtypeStruct((SEQ_DEV, 16, 384), F32),
            jax.ShapeDtypeStruct((TOK_DEV, D), F32),
            jax.ShapeDtypeStruct((4, SORTED, D), BF16),
            jax.ShapeDtypeStruct((4, SORTED, D), BF16),
            jax.ShapeDtypeStruct((8, D, HALF), BF16),
            jax.ShapeDtypeStruct((8, HALF, D), BF16),
            jax.ShapeDtypeStruct((4, 128), I32),
            jax.ShapeDtypeStruct((LANES, 128), I32),
        ),
        in_specs=[pl.BlockSpec(memory_space=pltpu.SMEM)] * 2 + [vmem] * (2 + len(arrays)),
        out_specs=(any_space,) * 8 + (vmem,) * 2,
        scratch_shapes=[
            pltpu.VMEM((ROWS, 3 * D), BF16),
            pltpu.VMEM((ROWS, D), BF16),
            pltpu.VMEM((SEQ_DEV, 16, 384), F32),
            pltpu.VMEM((TOK_DEV, D), F32),
            pltpu.VMEM((SORTED, D), BF16),
            pltpu.VMEM((SORTED, D), BF16),
            pltpu.VMEM((ROWS, D), BF16),
            pltpu.VMEM((384, 128), F32),
            pltpu.VMEM((1, LANES), I32),
            pltpu.VMEM((1, 128), I32),
            pltpu.VMEM((D, HALF), BF16),
            pltpu.VMEM((HALF, D), BF16),
            dma((2 * tiles + 7,)),
            dma((copies,)),
            dma((copies,)),
            dma((2, 6)),
            dma((2, 6)),
            dma((2, 6)),
            dma((2, 6)),
        ],
        compiler_params=params(collective_id=1, has_side_effects=True),
        name="front",
    )(lengths, group_map, routes, tokens, *arrays)


def gelu_both(u):
    below = 0.5 * (1.0 + lax.erf(u * (1.0 / math.sqrt(2.0))))
    density = jnp.exp(-0.5 * u * u) * (1.0 / math.sqrt(2.0 * math.pi))
    return u * below, below + u * density


MERGED = 2 * SORTED + 256
HEAD = 800
CHUNK = D // 8


def expert_kernel(sources, first, count, rows, carried, joined, cut, n_batch, offs_ref, group_ref, *refs):
    refs = list(refs)

    def take(count):
        head = refs[:count]
        del refs[:count]
        return head

    xs, gs = take(2), take(2)
    wi_hbm, wb_hbm = take(2)
    before = take(2) if carried else None
    earlier = take(4) if joined else None
    outs, gxs = take(2), take(2)
    dwi_ref, dwb_ref = take(2)
    xm, gm, wi, wb, acc_i, acc_b, hosts_ref, sems, join_sems = refs
    step = pl.program_id(0)
    expert = first + step
    slot = step % 2

    def join_copies():
        for number, (source, target) in enumerate(zip(earlier, outs + gxs)):
            yield pltpu.make_async_copy(source, target.at[0:HEAD, :], join_sems.at[number])

    def weight_copies(e, buffer, start):
        for p in range(2):
            host = hosts_ref[e * 2 + p]
            part = pl.ds(p * HALF, HALF)
            for number, source, target in (
                (0, wi_hbm.at[host], wi.at[buffer, :, part]),
                (1, wb_hbm.at[host], wb.at[buffer, part, :]),
            ):
                copy = pltpu.make_async_copy(source, target, sems.at[buffer, p, number])
                if start:
                    copy.start()
                else:
                    copy.wait()

    @pl.when(step == 0)
    def _():
        for e in range(EXPERTS):
            first_host, second_host = jnp.int32(n_batch), jnp.int32(n_batch)
            for b in reversed(range(n_batch)):
                hosting = group_ref[b] == e
                second_host = jnp.where(hosting, first_host, second_host)
                first_host = jnp.where(hosting, b, first_host)
            hosts_ref[2 * e] = first_host
            hosts_ref[2 * e + 1] = second_host
        weight_copies(first, 0, True)
        if joined:
            for copy in join_copies():
                copy.start()

    @pl.when(step + 1 < count)
    def _():
        weight_copies(expert + 1, 1 - slot, True)

    def blocks(count, act):
        @pl.loop(0, count)
        def _(i):
            act(pl.multiple_of(i * 16, 16))

    @pl.when((step == 0) & (rows == SORTED))
    def _():
        for s in range(2):
            live = pl.multiple_of(offs_ref[sources[s], EXPERTS], 16)

            def clear(at, s=s, live=live):
                spot = pl.ds(pl.multiple_of(live + at, 16), 16)
                outs[s][spot, :] = jnp.zeros((16, D), BF16)
                gxs[s][spot, :] = jnp.zeros((16, D), BF16)

            blocks((SORTED - live) // 16, clear)

    if carried:
        acc_i[...] = before[0][0].astype(F32)
        acc_b[...] = before[1][0].astype(F32)
    else:
        acc_i[...] = jnp.zeros_like(acc_i)
        acc_b[...] = jnp.zeros_like(acc_b)

    places = []
    total = jnp.int32(0)
    for s in range(2):
        begin = pl.multiple_of(offs_ref[sources[s], expert], 16)
        size = offs_ref[sources[s], expert + 1] - begin
        places.append((begin, total, size // 16))

        def gather(at, s=s, begin=begin, total=total):
            here = pl.ds(pl.multiple_of(begin + at, 16), 16)
            there = pl.ds(pl.multiple_of(total + at, 16), 16)
            xm[there, :] = xs[s][0, here, :]
            gm[there, :] = gs[s][0, here, :]

        blocks(size // 16, gather)
        total = total + size
    span = pl.multiple_of(total, 16)

    def blank(at):
        there = pl.ds(pl.multiple_of(span + at, 16), 16)
        xm[there, :] = jnp.zeros((16, D), BF16)
        gm[there, :] = jnp.zeros((16, D), BF16)

    blocks((256 - span % 256) // 16, blank)
    weight_copies(expert, slot, False)
    w_in, w_back = wi.at[slot], wb.at[slot]

    @pl.loop(0, (span + 255) // 256)
    def _(i):
        spot = pl.ds(pl.multiple_of(i * 256, 256), 256)
        x, g = xm[spot, :], gm[spot, :]
        inner = dot(x, w_in[...])
        hidden, slope = gelu_both(inner)
        hidden = hidden.astype(BF16)
        grad_hidden = dot(g, w_back[...], CONTRACT_LANES).astype(BF16)
        grad_inner = (grad_hidden.astype(F32) * slope).astype(BF16)
        xm[spot, :] = dot(hidden, w_back[...]).astype(BF16)
        gm[spot, :] = dot(grad_inner, w_in[...], CONTRACT_LANES).astype(BF16)
        acc_b[...] += dot(hidden, g, CONTRACT_ROWS)
        acc_i[...] += dot(x, grad_inner, CONTRACT_ROWS)

    if cut:
        y = lax.axis_index("batch") % 2
        for i, acc in enumerate((acc_i, acc_b)):
            for z in range(4):
                for ref, column in ((dwi_ref, 1 - y), (dwb_ref, y)):
                    part = pl.ds(pl.multiple_of((z * 2 + column) * CHUNK, 16), CHUNK)
                    ref[i, z] = acc[part, :].astype(BF16)
    else:
        dwi_ref[0] = acc_i[...].astype(BF16)
        dwb_ref[0] = acc_b[...].astype(BF16)
    if joined:

        @pl.when(step == 0)
        def _():
            for copy in join_copies():
                copy.wait()

    for s in range(2):
        begin, base, blocks_of = places[s]

        def hand_back(at, s=s, begin=begin, base=base):
            here = pl.ds(pl.multiple_of(begin + at, 16), 16)
            there = pl.ds(pl.multiple_of(base + at, 16), 16)
            outs[s][here, :] = xm[there, :]
            gxs[s][here, :] = gm[there, :]

        blocks(blocks_of, hand_back)


def experts(
    sources, offs, group_map, x, g, wi, wb, before=None, earlier=None, first=0, count=EXPERTS, cut=False
):
    rows = HEAD if cut else SORTED
    whole = once((rows, D))
    any_space = pl.BlockSpec(memory_space=pl.ANY)
    carried, joined = before is not None, earlier is not None
    out = jax.ShapeDtypeStruct((rows, D), BF16)

    def source(i):
        return pl.BlockSpec((1, rows, D), lambda e, *_: (i, 0, 0), pipeline_mode=pl.Buffered(1))

    carry = pl.BlockSpec((1, D, FF_DEV), lambda e, *_: (first + e, 0, 0))
    if cut:
        weight = once((2, 4, CHUNK, D))
        grad = jax.ShapeDtypeStruct((2, 4, CHUNK, D), BF16)
    else:
        weight = pl.BlockSpec((1, D, FF_DEV), lambda e, *_: (e, 0, 0))
        grad = jax.ShapeDtypeStruct((count, D, FF_DEV), BF16)
    picked = [source(i) for i in sources]
    kernel = functools.partial(
        expert_kernel, sources, first, count, rows, carried, joined, cut, group_map.shape[0]
    )
    return pl.pallas_call(
        kernel,
        grid_spec=pltpu.PrefetchScalarGridSpec(
            num_scalar_prefetch=2,
            grid=(count,),
            in_specs=picked
            + picked
            + [any_space] * 2
            + [carry] * (2 * carried)
            + [any_space] * (4 * joined),
            out_specs=[whole] * 4 + [weight] * 2,
            scratch_shapes=[
                pltpu.VMEM((MERGED, D), BF16),
                pltpu.VMEM((MERGED, D), BF16),
                pltpu.VMEM((2, D, FF_DEV), BF16),
                pltpu.VMEM((2, FF_DEV, D), BF16),
                pltpu.VMEM((D, FF_DEV), F32),
                pltpu.VMEM((FF_DEV, D), F32),
                pltpu.SMEM((2 * EXPERTS,), I32),
                pltpu.SemaphoreType.DMA((2, 2, 2)),
                pltpu.SemaphoreType.DMA((4,)),
            ],
        ),
        out_shape=(out,) * 4 + (grad,) * 2,
        compiler_params=params(),
        cost_estimate=cost(8 * count * SORTED * D * FF_DEV, 16 * SORTED * D),
        name="experts",
    )(offs, group_map, x, x, g, g, wi, wb, *(before or ()), *(earlier or ()))


def swap(rows, bit):
    pairs = [(f, f ^ bit) for f in range(4)]
    return lax.ppermute(rows, "ffn", pairs)


def tie(value, *others):
    return lax.optimization_barrier((value, *others))[0]


class Wire:
    def __init__(self, send_sems, recv_sems):
        self.send_sems, self.recv_sems, self.used = send_sems, recv_sems, 0

    def send(self, src, dst, device):
        number = self.used
        self.used += 1
        copy = pltpu.make_async_remote_copy(
            src_ref=src,
            dst_ref=dst,
            send_sem=self.send_sems.at[number],
            recv_sem=self.recv_sems.at[number],
            device_id=device,
            device_id_type=MESH,
        )
        copy.start()
        return copy


class Mover:
    def __init__(self, sems):
        self.sems, self.used = sems, 0

    def go(self, src, dst):
        number = self.used
        self.used += 1
        copy = pltpu.make_async_copy(src, dst, self.sems.at[number])
        copy.start()
        return copy


def greet(peers):
    barrier = pltpu.get_barrier_semaphore()
    for device in peers:
        pl.semaphore_signal(barrier, inc=1, device_id=device, device_id_type=MESH)
    pl.semaphore_wait(barrier, len(peers))


def wait_all(copies):
    for copy in copies:
        copy.wait()


def token_tiles():
    for i in range(3):
        yield slice(TILE * i, min(TILE * (i + 1), TOK_DEV))


def unsort(pos_col, src):
    want = lax.broadcasted_iota(I32, (pos_col.shape[0], SORTED), 1)
    hot = jnp.where(pos_col == want, 1.0, 0.0).astype(BF16)
    return dot(hot, src)


def attend_back_pair(pair, length, qkv_ref, gctx_ref, lse_ref, out_ref):
    start, skip = window(pair)
    start = pl.multiple_of(start, 16)
    row = lax.broadcasted_iota(I32, (WIN, 1), 0)
    mine = (row >= skip) & (row < skip + SEQ_LEN)
    bias = jnp.where((row >= skip) & (row < skip + PATCHES + length), 0.0, -1e30)
    lane = lax.broadcasted_iota(I32, (WIN, 128), 1)
    scale = jnp.asarray(HEAD_DIM**-0.5, BF16)
    @pl.loop(0, HEADS // 2)
    def _(hp):
        spots = [head_cols(hp, part) for part in range(3)]
        q, k, v = [qkv_ref[pl.ds(start, WIN), spot] for spot in spots]
        q = q * scale
        ks = k * scale
        go = gctx_ref[pl.ds(start, WIN), spots[0]]
        q = jnp.where(mine, q, jnp.zeros_like(q))
        go = jnp.where(mine, go, jnp.zeros_like(go))
        grads = []
        for half in range(2):
            head = hp * 2 + half
            inside = (lane < 64) if half == 0 else (lane >= 64)
            qh = jnp.where(inside, q, jnp.zeros_like(q))
            gh = jnp.where(inside, go, jnp.zeros_like(go))
            scores = dot(k, qh, CONTRACT_LANES)
            probs = jnp.exp(scores + bias - lse_ref[pair, pl.ds(head, 1), 0:WIN])
            grad_probs = dot(v, gh, CONTRACT_LANES)
            delta = jnp.sum(probs * grad_probs, axis=0, keepdims=True)
            grad_scores = (probs * (grad_probs - delta)).astype(BF16)
            grad_v = dot(probs.astype(BF16), go)
            grad_k = dot(grad_scores, q)
            grad_q = dot(grad_scores, ks, CONTRACT_ROWS)
            grads.append((grad_q, grad_k, grad_v))
        for spot, low, high in zip(spots, grads[0], grads[1]):
            new = jnp.where(lane < 64, low, high).astype(BF16)
            old = out_ref[pl.ds(start, WIN), spot]
            out_ref[pl.ds(start, WIN), spot] = jnp.where(mine, new, old)


TURNS = (2, 3, 1, 0)


def rear_kernel(
    small,
    len_ref,
    pos_ref,
    gain_one_ref,
    gain_two_ref,
    w_ref,
    lse_ref,
    gx0_hbm,
    gx1_hbm,
    gx2_hbm,
    mid_hbm,
    cot_hbm,
    ctx_hbm,
    qkv_hbm,
    tok_hbm,
    out1_hbm,
    out2_hbm,
    out3_hbm,
    dwi_hbm,
    dwb_hbm,
    first_came,
    first_own,
    gm_hbm,
    gq_hbm,
    dwq_hbm,
    dwp_hbm,
    dg_ref,
    share_hbm,
    near_hbm,
    far_hbm,
    wide,
    mid,
    cot,
    ctx,
    gctx,
    qkv,
    half_a,
    half_b,
    own_rows,
    came_y,
    came_z,
    acc,
    dwp,
    local_sems,
    send_sems,
    recv_sems,
    z_send,
    z_recv,
):
    batch, ffn = lax.axis_index("batch"), lax.axis_index("ffn")
    z, y = batch // 2, batch % 2
    near, far, across = (batch, ffn ^ 1), (batch, ffn ^ 2), (batch ^ 1, ffn)
    along = {k: (batch ^ (2 * k), ffn) for k in (1, 2, 3)}
    greet([near, far] + ([across] + list(along.values()) if small else []))
    wire, mover = Wire(send_sems, recv_sems), Mover(local_sems)

    parts_near = wire.send(gx1_hbm, wide.at[:, D : 2 * D], near)
    near_sent = wire.send(out3_hbm, half_b, near)
    half_in = mover.go(out2_hbm, half_a)
    over_y = {}
    own_in = {}
    if small:
        for turn in TURNS:
            there = pl.ds(pl.multiple_of(((z ^ turn) * 2 + 1 - y) * CHUNK, 16), CHUNK)
            over_y[turn] = [
                wire.send(grad.at[:, there, :], came_y.at[turn, i, 1:EXPERTS], across)
                for i, grad in enumerate((dwi_hbm, dwb_hbm))
            ]
    first_in = {}
    if small:
        for turn in TURNS:
            first_in[turn] = [
                mover.go(first_came.at[:, z ^ turn], came_y.at[turn, :, 0]),
                mover.go(first_own.at[:, z ^ turn], own_rows.at[turn, :, 0]),
            ]
    parts_in = [
        mover.go(part, wide.at[:, i * D : i * D + D])
        for i, part in ((0, gx0_hbm), (2, gx2_hbm))
    ]
    rows_in = [mover.go(mid_hbm, mid), mover.go(cot_hbm, cot), mover.go(ctx_hbm, ctx)]
    qkv_in = mover.go(qkv_hbm, qkv)
    if small:
        for turn in TURNS:
            here = pl.ds(pl.multiple_of(((z ^ turn) * 2 + y) * CHUNK, 16), CHUNK)
            own_in[turn] = [
                mover.go(grad.at[:, here, :], own_rows.at[turn, i, 1:EXPERTS])
                for i, grad in enumerate((dwi_hbm, dwb_hbm))
            ]
    sent = [wire.send(out1_hbm, near_hbm, near)]
    stored = []

    def z_copy(turn, i):
        return pltpu.make_async_remote_copy(
            src_ref=came_y.at[turn, i, 1:EXPERTS],
            dst_ref=came_z.at[turn - 1, i, 1:EXPERTS],
            send_sem=z_send.at[turn - 1, i],
            recv_sem=z_recv.at[turn - 1, i],
            device_id=along[turn],
            device_id_type=MESH,
        )

    def take_turn(turn, i):
        if not small:
            return
        over_y[turn][i].wait()
        own_in[turn][i].wait()
        for e in range(1, EXPERTS):
            came_y[turn, i, e] = (
                came_y[turn, i, e].astype(F32) + own_rows[turn, i, e].astype(F32)
            ).astype(BF16)
        if turn:
            z_copy(turn, i).start()

    first_z = []
    if small:
        for turn in TURNS:
            wait_all(first_in[turn])
            for i in range(2):
                came_y[turn, i, 0] = (
                    came_y[turn, i, 0].astype(F32) + own_rows[turn, i, 0].astype(F32)
                ).astype(BF16)
            if turn:
                first_z.append(
                    wire.send(came_y.at[turn, :, 0], came_z.at[turn - 1, :, 0], along[turn])
                )
    wait_all(parts_in + rows_in + [parts_near])
    top = 0
    for size in SORT_TILES:
        rows = slice(top, top + size)
        wide[rows, 0:D] = (
            wide[rows, 0:D].astype(F32)
            + wide[rows, D : 2 * D].astype(F32)
            + wide[rows, 2 * D : 3 * D].astype(F32)
        ).astype(BF16)
        top += size
    half_in.wait()
    near_sent.wait()
    half_a[...] = (half_a[...].astype(F32) + half_b[...].astype(F32)).astype(BF16)
    sent.append(wire.send(half_a, far_hbm, far))

    gctx[1552:ROWS, :] = jnp.zeros((ROWS - 1552, D), BF16)
    grad_gain = jnp.zeros((1, D), F32)
    for i, rows in enumerate(token_tiles()):
        grad_normed = unsort(pos_ref[rows, 0:1], wide[:, 0:D])
        normal, inverse = norm_parts(mid[rows, :])
        grad_gain = grad_gain + jnp.sum(grad_normed * normal, axis=0, keepdims=True)
        part = norm_pull(grad_normed, gain_two_ref[...].reshape(1, D), normal, inverse)
        grad_middle = cot[rows, :].astype(F32) + part
        mid[rows, :] = grad_middle
        low = grad_middle.astype(BF16)
        product = dot(ctx[rows, :], low, CONTRACT_ROWS)
        if i == 0:
            acc[...] = product
        elif i == 1:
            acc[...] += product
        else:
            dwp[...] = (acc[...] + product).astype(BF16)
        gctx[rows, :] = dot(low, w_ref[...], CONTRACT_LANES).astype(BF16)
        if i == 1:
            take_turn(2, 0)
            take_turn(2, 1)
    dg_ref[...] = grad_gain
    stored.append(mover.go(mid, gm_hbm))
    stored.append(mover.go(dwp, dwp_hbm))
    tok_in = mover.go(tok_hbm, cot)
    wide[1552:SORTED, :] = jnp.zeros((SORTED - 1552, 3 * D), BF16)
    qkv_in.wait()
    take_turn(3, 0)
    take_turn(3, 1)

    @pl.loop(0, SEQ_DEV)
    def _(pair):
        attend_back_pair(pair, len_ref[pair], qkv, gctx, lse_ref, wide)
        @pl.when(pair == 1)
        def _():
            take_turn(1, 0)
            take_turn(1, 1)

    stored.append(mover.go(wide.at[0:ROWS, :], gq_hbm))
    tok_in.wait()
    for rows in token_tiles():
        normal, _ = norm_parts(cot[rows, :].astype(F32))
        gctx[rows, :] = (normal * gain_one_ref[...].reshape(1, D)).astype(BF16)
    for i in range(3):
        cols = slice(i * D, i * D + D)
        qkv[0:D, cols] = dot(gctx[...], wide[0:ROWS, cols], CONTRACT_ROWS).astype(BF16)
    stored.append(mover.go(qkv.at[0:D, :], dwq_hbm))
    if small:
        take_turn(0, 0)
        take_turn(0, 1)
        wait_all(first_z + [z_copy(turn, i) for turn in TURNS[:3] for i in range(2)])
        for i in range(2):
            for e in range(EXPERTS):
                total = came_y[0, i, e].astype(F32)
                for k in range(3):
                    total = total + came_z[k, i, e].astype(F32)
                came_y[0, i, e] = total.astype(BF16)
        stored.append(mover.go(came_y.at[0], share_hbm))
    wait_all(sent + stored)


def rear(small, lengths, pos_col, gain_one, gain_two, w_proj, lse, *arrays):
    vmem = pl.BlockSpec(memory_space=pltpu.VMEM)
    any_space = pl.BlockSpec(memory_space=pl.ANY)
    dma = pltpu.SemaphoreType.DMA
    copies = 15
    return pl.pallas_call(
        functools.partial(rear_kernel, small),
        out_shape=(
            jax.ShapeDtypeStruct((TOK_DEV, D), F32),
            jax.ShapeDtypeStruct((ROWS, 3 * D), BF16),
            jax.ShapeDtypeStruct((D, 3 * D), BF16),
            jax.ShapeDtypeStruct((D, D), BF16),
            jax.ShapeDtypeStruct((1, D), F32),
            jax.ShapeDtypeStruct((2, EXPERTS, CHUNK, D), BF16),
            jax.ShapeDtypeStruct((SORTED, D), BF16),
            jax.ShapeDtypeStruct((SORTED, D), BF16),
        ),
        in_specs=[pl.BlockSpec(memory_space=pltpu.SMEM)] + [vmem] * 5 + [any_space] * len(arrays),
        out_specs=(any_space,) * 4 + (vmem,) + (any_space,) * 3,
        scratch_shapes=[
            pltpu.VMEM((SORTED, 3 * D), BF16),
            pltpu.VMEM((TOK_DEV, D), F32),
            pltpu.VMEM((TOK_DEV, D), BF16),
            pltpu.VMEM((ROWS, D), BF16),
            pltpu.VMEM((ROWS, D), BF16),
            pltpu.VMEM((ROWS, 3 * D), BF16),
            pltpu.VMEM((SORTED, D), BF16),
            pltpu.VMEM((SORTED, D), BF16),
            pltpu.VMEM((4, 2, EXPERTS, CHUNK, D), BF16),
            pltpu.VMEM((4, 2, EXPERTS, CHUNK, D), BF16),
            pltpu.VMEM((3, 2, EXPERTS, CHUNK, D), BF16),
            pltpu.VMEM((D, D), F32),
            pltpu.VMEM((D, D), BF16),
            dma((32,)),
            dma((copies,)),
            dma((copies,)),
            dma((3, 2)),
            dma((3, 2)),
        ],
        compiler_params=params(collective_id=2, has_side_effects=True),
        name="rear",
    )(lengths, pos_col, gain_one, gain_two, w_proj, lse, *arrays)


ORDERS = (("x", "y", "z"), ("y", "x", "z"))
WIDE = 4 * D
COLOUR = WIDE // 2
QUARTER = COLOUR // 4
GAIN_ROWS = 8


def last_kernel(
    small,
    group_ref,
    pos_ref,
    gain_ref,
    w_ref,
    dg_two_ref,
    tok_hbm,
    gq_hbm,
    gm_hbm,
    mid_hbm,
    out0_hbm,
    out1_hbm,
    out2_hbm,
    dwq_hbm,
    dwp_hbm,
    share_hbm,
    ig_hbm,
    bo_hbm,
    sum_ref,
    gains_ref,
    pieces_ref,
    tok,
    gq,
    gm,
    mid,
    outs,
    share,
    stage,
    near_rows,
    held,
    came_z,
    came_xy,
    gain_in,
    local_sems,
    send_sems,
    recv_sems,
):
    batch, ffn = lax.axis_index("batch"), lax.axis_index("ffn")
    z, y, x, c = batch // 2, batch % 2, ffn // 2, ffn % 2
    place = {"x": x, "y": y, "z": z}
    mover = Mover(local_sems)

    def peer(axis, k=1):
        if axis == "c":
            return (batch, ffn ^ 1)
        if axis == "x":
            return (batch, ffn ^ 2)
        if axis == "y":
            return (batch ^ 1, ffn)
        return (batch ^ (2 * k), ffn)

    flying = []
    top = [0, 0]
    left = [COLOUR * i for i in range(2)]
    rows, cols = [384] * 2, [COLOUR] * 2
    base = pl.multiple_of(c * 384, 16)
    if small:
        greet([peer("c"), peer("x")] + [(batch ^ j, ffn) for j in range(1, 8)])
        wire = Wire(send_sems, recv_sems)
        share_in = mover.go(share_hbm, share)
        give = pl.ds(pl.multiple_of((1 - c) * 384, 16), 384)
        keep = pl.ds(base, 384)
        to_core = [
            wire.send(dwq_hbm.at[give, :], near_rows.at[:, 0 : 3 * D], peer("c")),
            wire.send(dwp_hbm.at[give, :], near_rows.at[:, 3 * D : WIDE], peer("c")),
        ]
        kept = [
            mover.go(dwq_hbm.at[keep, :], held.at[:, 0 : 3 * D]),
            mover.go(dwp_hbm.at[keep, :], held.at[:, 3 * D : WIDE]),
        ]
    loads = [mover.go(tok_hbm, tok), mover.go(gq_hbm, gq), mover.go(gm_hbm, gm)]
    later = [mover.go(mid_hbm, mid)] + [
        mover.go(part, outs.at[i]) for i, part in enumerate((out0_hbm, out1_hbm, out2_hbm))
    ]
    handed = []

    def hand_out(i):
        for j in range(1, 8):
            handed.append(
                wire.send(stage.at[j, i], pieces_ref.at[batch, i], (batch ^ j, ffn))
            )

    if small:
        share_in.wait()
        for j in range(8):
            expert = group_ref[batch ^ j]
            for i in range(2):
                stage[j, i] = share[i, expert]
        hand_out(0)
        pieces_ref[batch] = stage[0]

    def core_done():
        wait_all(to_core + kept)
        for i in range(4):
            lanes = slice(i * D, i * D + D)
            held[:, lanes] = (
                held[:, lanes].astype(F32) + near_rows[:, lanes].astype(F32)
            ).astype(BF16)

    def sum_go(step):
        for i in range(2):
            axis = ORDERS[i][step]
            if axis == "z":
                live = pl.ds(top[i], rows[i])
                for k in (1, 2, 3):
                    there = pl.ds(pl.multiple_of(left[i] + (z ^ k) * QUARTER, 128), QUARTER)
                    flying.append(
                        wire.send(
                            held.at[live, there], came_z.at[i, k - 1, 0 : rows[i]], peer("z", k)
                        )
                    )
            else:
                half = rows[i] // 2
                there = pl.ds(pl.multiple_of(top[i] + (1 - place[axis]) * half, 16), half)
                flying.append(
                    wire.send(
                        held.at[there, pl.ds(left[i], cols[i])],
                        came_xy.at[i, 0 if axis == "x" else 1, 0:half, 0 : cols[i]],
                        peer(axis),
                    )
                )

    def sum_done(step):
        wait_all(flying)
        flying.clear()
        for i in range(2):
            axis = ORDERS[i][step]
            if axis == "z":
                left[i] = pl.multiple_of(left[i] + z * QUARTER, 128)
                cols[i] = QUARTER
                terms = [came_z[i, k, 0 : rows[i]] for k in range(3)]
            else:
                rows[i] = rows[i] // 2
                top[i] = pl.multiple_of(top[i] + place[axis] * rows[i], 16)
                terms = [came_xy[i, 0 if axis == "x" else 1, 0 : rows[i], 0 : cols[i]]]
            spot = (pl.ds(top[i], rows[i]), pl.ds(left[i], cols[i]))
            total = held[spot].astype(F32)
            for term in terms:
                total = total + term.astype(F32)
            held[spot] = total.astype(BF16)

    def spread_go(step):
        for i in range(2):
            axis = ORDERS[i][step]
            mine = sum_ref.at[
                pl.ds(pl.multiple_of(base + top[i], 16), rows[i]), pl.ds(left[i], cols[i])
            ]
            for k in (1, 2, 3) if axis == "z" else (1,):
                flying.append(wire.send(mine, mine, peer(axis, k)))

    def spread_done(step):
        wait_all(flying)
        flying.clear()
        for i in range(2):
            axis = ORDERS[i][step]
            if axis == "z":
                left[i] = COLOUR * i
                cols[i] = COLOUR
            else:
                top[i] = top[i] - place[axis] * rows[i]
                rows[i] = rows[i] * 2

    def gains_go(axis, slot):
        for k in (1, 2, 3) if axis == "z" else (1,):
            flying.append(wire.send(gains_ref, gain_in.at[slot + k - 1], peer(axis, k)))

    def gains_done(axis, slot):
        total = gains_ref[...]
        for k in (0, 1, 2) if axis == "z" else (0,):
            total = total + gain_in[slot + k]
        gains_ref[...] = total

    tiles = list(token_tiles())
    grad_gain = jnp.zeros((1, D), F32)
    stored = []

    def first_back(part):
        normal, inverse = norm_parts(tok[part, :].astype(F32))
        grad_normed = dot(gq[part, :], w_ref[...], CONTRACT_LANES)
        gain_part = jnp.sum(grad_normed * normal, axis=0, keepdims=True)
        pulled = norm_pull(grad_normed, gain_ref[...].reshape(1, D), normal, inverse)
        gm[part, :] = gm[part, :] + pulled
        stored.append(mover.go(gm.at[part], ig_hbm.at[part]))
        return gain_part

    def finish(part):
        mid[part, :] = mid[part, :] + unsort(pos_ref[part, 0:1], outs[0])
        stored.append(mover.go(mid.at[part], bo_hbm.at[part]))

    wait_all(loads)
    grad_gain = grad_gain + first_back(tiles[0])
    if small:
        core_done()
        sum_go(0)
    grad_gain = grad_gain + first_back(tiles[1])
    grad_gain = grad_gain + first_back(tiles[2])
    gains_ref[0:1, :] = grad_gain
    gains_ref[1:2, :] = dg_two_ref[...]
    gains_ref[2:GAIN_ROWS, :] = jnp.zeros((GAIN_ROWS - 2, D), F32)
    if small:
        gains_go("c", 0)
        sum_done(0)
        gains_done("c", 0)
        gains_go("x", 1)
        sum_go(1)
    wait_all(later)
    at = 0
    for size in SORT_TILES:
        part = slice(at, at + size)
        outs[0, part] = (
            outs[0, part].astype(F32) + outs[1, part].astype(F32) + outs[2, part].astype(F32)
        ).astype(BF16)
        at += size
    finish(tiles[0])
    if small:
        sum_done(1)
        gains_done("x", 1)
        gains_go("y", 2)
        sum_go(2)
    finish(tiles[1])
    if small:
        sum_done(2)
        gains_done("y", 2)
        for i in range(2):
            spot = (pl.ds(top[i], rows[i]), pl.ds(left[i], cols[i]))
            sum_ref[pl.ds(pl.multiple_of(base + top[i], 16), rows[i]), spot[1]] = held[spot]
        gains_go("z", 3)
        spread_go(2)
        hand_out(1)
    finish(tiles[2])
    if small:
        spread_done(2)
        gains_done("z", 3)
        spread_go(1)
        spread_done(1)
        spread_go(0)
        spread_done(0)
        mine = sum_ref.at[pl.ds(base, 384), :]
        wire.send(mine, mine, peer("c")).wait()
        wait_all(handed)
    wait_all(stored)


def last(small, group_map, pos_col, gain_one, w_qkv, dg_two, *arrays):
    vmem = pl.BlockSpec(memory_space=pltpu.VMEM)
    any_space = pl.BlockSpec(memory_space=pl.ANY)
    dma = pltpu.SemaphoreType.DMA
    copies = 2 + 14 + 10 + 10 + 6 + 1
    extra = dict(collective_id=3, has_side_effects=True) if small else {}
    return pl.pallas_call(
        functools.partial(last_kernel, small),
        out_shape=(
            jax.ShapeDtypeStruct((TOK_DEV, D), F32),
            jax.ShapeDtypeStruct((TOK_DEV, D), F32),
            jax.ShapeDtypeStruct((D, WIDE), BF16),
            jax.ShapeDtypeStruct((GAIN_ROWS, D), F32),
            jax.ShapeDtypeStruct((8, 2, CHUNK, D), BF16),
        ),
        in_specs=[pl.BlockSpec(memory_space=pltpu.SMEM)] + [vmem] * 4 + [any_space] * len(arrays),
        out_specs=(any_space,) * 2 + (vmem,) * 3,
        scratch_shapes=[
            pltpu.VMEM((TOK_DEV, D), BF16),
            pltpu.VMEM((ROWS, 3 * D), BF16),
            pltpu.VMEM((TOK_DEV, D), F32),
            pltpu.VMEM((TOK_DEV, D), F32),
            pltpu.VMEM((3, SORTED, D), BF16),
            pltpu.VMEM((2, EXPERTS, CHUNK, D), BF16),
            pltpu.VMEM((8, 2, CHUNK, D), BF16),
            pltpu.VMEM((384, WIDE), BF16),
            pltpu.VMEM((384, WIDE), BF16),
            pltpu.VMEM((2, 3, 96, QUARTER), BF16),
            pltpu.VMEM((2, 2, 192, COLOUR), BF16),
            pltpu.VMEM((6, GAIN_ROWS, D), F32),
            dma((16,)),
            dma((copies,)),
            dma((copies,)),
        ],
        compiler_params=params(**extra),
        name="last",
    )(group_map, pos_col, gain_one, w_qkv, dg_two, *arrays)


def close_kernel(
    sum_ref, gains_ref, pieces_ref, ig_ref, bo_ref, *outs
):
    qkv_ref, proj_ref, one_ref, two_ref, wi_ref, wb_ref, ig_out, bo_out = outs
    qkv_ref[...] = sum_ref[:, 0 : 3 * D].astype(F32)
    proj_ref[...] = sum_ref[:, 3 * D : WIDE].astype(F32)
    one_ref[...] = gains_ref[0:1, :].reshape(D)
    two_ref[...] = gains_ref[1:2, :].reshape(D)
    wi_ref[0] = pieces_ref[0, 0].astype(F32)
    wb_ref[0] = pieces_ref[0, 1].astype(F32)
    ig_out[...] = ig_ref[...]
    bo_out[...] = bo_ref[...]


def close(summed, gains, pieces, input_grad, block_out):
    row = pl.BlockSpec((CHUNK, D), lambda i: (i, 0))
    tokens = pl.BlockSpec((200, D), lambda i: (i, 0))
    weight = pl.BlockSpec((1, CHUNK, D), lambda i: (0, i, 0))
    rows = jax.ShapeDtypeStruct((TOK_DEV, D), F32)
    return pl.pallas_call(
        close_kernel,
        grid=(8,),
        out_shape=(
            jax.ShapeDtypeStruct((D, 3 * D), F32),
            jax.ShapeDtypeStruct((D, D), F32),
            jax.ShapeDtypeStruct((D,), F32),
            jax.ShapeDtypeStruct((D,), F32),
            jax.ShapeDtypeStruct((1, D, D), F32),
            jax.ShapeDtypeStruct((1, D, D), F32),
            rows,
            rows,
        ),
        in_specs=[
            pl.BlockSpec((CHUNK, WIDE), lambda i: (i, 0)),
            full((GAIN_ROWS, D)),
            pl.BlockSpec((1, 2, CHUNK, D), lambda i: (i, 0, 0, 0)),
            tokens,
            tokens,
        ],
        out_specs=(
            pl.BlockSpec((CHUNK, 3 * D), lambda i: (i, 0)),
            row,
            full((D,)),
            full((D,)),
            weight,
            weight,
            tokens,
            tokens,
        ),
        compiler_params=params(),
        name="close",
    )(summed, gains, pieces, input_grad, block_out)


def body(
    tokens,
    text_lengths,
    routes,
    group_map,
    gain_one,
    w_qkv,
    w_proj,
    gain_two,
    w_in,
    w_back,
    cotangent,
):
    n_batch = lax.axis_size("batch")
    own = lax.axis_index("batch")
    small = n_batch == 8
    routes_row = jnp.pad(routes.reshape(1, TOK_DEV), ((0, 0), (0, LANES - TOK_DEV)))
    qkv, context, lse, middle, g, x, wi_all, wb_all, offs, pos_col = front(
        small,
        text_lengths,
        group_map,
        routes_row,
        tokens,
        cotangent,
        gain_one,
        w_qkv,
        w_proj,
        gain_two,
        w_in,
        w_back,
    )
    if not small:
        own_expert = group_map[own]
        order = jnp.arange(n_batch, dtype=I32)
        rank = jnp.sum(jnp.where((group_map == own_expert) & (order < own), 1, 0))
        part = jnp.minimum(rank, 1)
        wi_part = lax.dynamic_slice(w_in[0], (0, part * HALF), (D, HALF))
        wb_part = lax.dynamic_slice(w_back[0], (part * HALF, 0), (HALF, D))
        wi_all = lax.all_gather(wi_part, "batch", axis=0)
        wb_all = lax.all_gather(wb_part, "batch", axis=0)

    def run(pair, x, *rest, **more):
        return experts(pair, offs, group_map, x, g, wi_all, wb_all, *rest, **more)

    def add(a, b):
        return (a.astype(F32) + b.astype(F32)).astype(BF16)

    out2, out3, gx2, gx3, dwi, dwb = run((2, 3), x)
    gx_half = add(gx2, swap(gx3, 1))
    gx_far = swap(gx_half, 2)
    x = tie(x, gx_half)
    if small:
        *earlier, going, staying = run((0, 1), x, (dwi, dwb), count=1, cut=True)
        came = lax.ppermute(going, "batch", [(b, b ^ 1) for b in range(8)])
        out0, out1, gx0, gx1, dwi, dwb = run((0, 1), x, (dwi, dwb), earlier, first=1, count=2)
    else:
        out0, out1, gx0, gx1, dwi, dwb = run((0, 1), x, (dwi, dwb))
        came = staying = jnp.zeros((2, 4, CHUNK, D), BF16)
    grad_middle, grad_qkv, dw_qkv, dw_proj, dg_two, share, out_near, out_far = rear(
        small,
        text_lengths,
        pos_col,
        gain_one,
        gain_two,
        w_proj,
        lse,
        gx0,
        gx1,
        gx_far,
        middle,
        cotangent,
        context,
        qkv,
        tokens,
        out1,
        out2,
        out3,
        dwi,
        dwb,
        came,
        staying,
    )
    input_grad, block_out, summed, gains, pieces = last(
        small,
        group_map,
        pos_col,
        gain_one,
        w_qkv,
        dg_two,
        tokens,
        grad_qkv,
        grad_middle,
        middle,
        out0,
        out_near,
        out_far,
        dw_qkv,
        dw_proj,
        share,
    )
    if small:
        summed_qkv, summed_proj, gain_a, gain_b, grad_w_in, grad_w_back, input_grad, block_out = close(
            summed, gains, pieces, input_grad, block_out
        )
        gains = (gain_a, gain_b)
    else:

        def settle_any(grad):
            share = lax.psum_scatter(grad, "batch", scatter_dimension=1, tiled=True)
            whole = lax.all_gather(share, "batch", axis=1, tiled=True)
            return lax.dynamic_index_in_dim(whole, own_expert, 0, keepdims=True).astype(F32)

        grad_w_in = settle_any(dwi)
        grad_w_back = settle_any(dwb)
        summed_qkv, summed_proj = lax.psum((dw_qkv, dw_proj), ("batch", "ffn"))
        gains = lax.psum(gains, ("batch", "ffn"))
    return (
        block_out,
        input_grad,
        gains[0],
        summed_qkv.astype(F32),
        summed_proj.astype(F32),
        gains[1],
        grad_w_in,
        grad_w_back,
    )


def solution(mesh):
    placed = (
        P(("batch", "ffn"), None),
        P(("batch", "ffn")),
        P(("batch", "ffn"), None),
        P(),
        P(),
        P(),
        P(),
        P(),
        P("batch", None, "ffn"),
        P("batch", "ffn", None),
        P(("batch", "ffn"), None),
    )
    return jax.shard_map(
        body,
        mesh=mesh,
        in_specs=placed,
        out_specs=(
            P(("batch", "ffn"), None),
            P(("batch", "ffn"), None),
            P(),
            P(),
            P(),
            P(),
            P("batch", None, "ffn"),
            P("batch", "ffn", None),
        ),
        check_vma=False,
    )
```

```python
import functools
import math

import jax
import jax.numpy as jnp
from jax import lax
from jax.experimental import pallas as pl
from jax.experimental.pallas import tpu as pltpu
from jax.sharding import PartitionSpec as P

D = 768
HEADS = 12
HEAD_DIM = 64
EXPERTS = 3
PATCHES = 197
SEQ_DEV = 6
SEQ_LEN = 261
TOK_DEV = 1566
ROWS = 1584
SORTED = 1616
WIN = 288
TILE = 528
LANES = 1664
EPS = 1e-05
F32 = jnp.float32
BF16 = jnp.bfloat16
I32 = jnp.int32
CONTRACT_LANES = (((1,), (1,)), ((), ()))
CONTRACT_ROWS = (((0,), (0,)), ((), ()))


def params(**extra):
    return pltpu.CompilerParams(vmem_limit_bytes=60 << 20, **extra)


def cost(flops, moved):
    return pl.CostEstimate(flops=int(flops), bytes_accessed=int(moved), transcendentals=0)


def dot(a, b, dims=(((1,), (0,)), ((), ()))):
    return lax.dot_general(a, b, dims, preferred_element_type=F32)


def full(shape):
    zeros = (0,) * len(shape)
    return pl.BlockSpec(shape, lambda *_: zeros)


def once(shape):
    zeros = (0,) * len(shape)
    return pl.BlockSpec(shape, lambda *_: zeros, pipeline_mode=pl.Buffered(1))


def row_mask(start, rows, limit):
    return start + lax.broadcasted_iota(I32, (rows, 1), 0) < limit


def norm_parts(values):
    average = jnp.mean(values, axis=-1, keepdims=True)
    centred = values - average
    variance = jnp.mean(centred * centred, axis=-1, keepdims=True)
    inverse = lax.rsqrt(variance + EPS)
    return centred * inverse, inverse


def norm_pull(grad_normed, gain, normal, inverse):
    scaled = grad_normed * gain
    mean_grad = jnp.mean(scaled, axis=-1, keepdims=True)
    mean_proj = jnp.mean(scaled * normal, axis=-1, keepdims=True)
    return inverse * (scaled - mean_grad - normal * mean_proj)


def route_rows(n_batch, gm_ref, routes_ref, pos_ref, col_ref, offs_ref):
    routes = routes_ref[...]
    lane = lax.broadcasted_iota(I32, (8, LANES), 1)
    sub = lax.broadcasted_iota(I32, (8, LANES), 0)
    expert = jnp.zeros((1, LANES), I32)
    for b in range(n_batch):
        expert = jnp.where(routes == b, gm_ref[b], expert)
    live = lane < TOK_DEV
    hot = jnp.where((jnp.broadcast_to(expert, (8, LANES)) == sub) & live, 1, 0)
    count = hot
    step = 1
    while step < LANES:
        count = count + jnp.where(lane >= step, pltpu.roll(count, step, 1), 0)
        step *= 2
    totals = [jnp.sum(hot[e : e + 1, :], axis=1, keepdims=True) for e in range(EXPERTS)]
    starts = [jnp.zeros((1, 1), I32)]
    for e in range(EXPERTS):
        starts.append(starts[-1] + (totals[e] + 15) // 16 * 16)
    pos = jnp.zeros((1, LANES), I32)
    for e in range(EXPERTS):
        pos = pos + jnp.where(hot[e : e + 1, :] > 0, count[e : e + 1, :] - 1 + starts[e], 0)
    pos = jnp.where(live[0:1, :], pos, -1)
    pos_ref[...] = pos
    wide = jnp.broadcast_to(pos.astype(F32), (128, LANES))
    col_ref[...] = jnp.transpose(wide).astype(I32)
    slot = lax.broadcasted_iota(I32, (1, 128), 1)
    offs = jnp.zeros((1, 128), I32)
    for e in range(EXPERTS + 1):
        offs = jnp.where(slot == e, starts[e], offs)
    offs_ref[...] = offs


SORT_TILES = (336, 336, 336, 336, 272)


def window(pair):
    first = pair * SEQ_LEN
    start = first // 16 * 16
    return start, first - start


def head_cols(hp, part):
    return pl.ds(pl.multiple_of(part * D + hp * 128, 128), 128)


def attend_pair(pair, length, qkv_ref, ctx_ref, lse_ref, stat):
    start, skip = window(pair)
    start = pl.multiple_of(start, 16)
    key = lax.broadcasted_iota(I32, (1, WIN), 1)
    seen = (key >= skip) & (key < skip + PATCHES + length)
    bias = jnp.where(seen, 0.0, -1e30)
    row = lax.broadcasted_iota(I32, (WIN, 1), 0)
    mine = (row >= skip) & (row < skip + SEQ_LEN)
    lane = lax.broadcasted_iota(I32, (WIN, 128), 1)
    stat[...] = jnp.zeros_like(stat)
    @pl.loop(0, HEADS // 2)
    def _(hp):
        q, k, v = [qkv_ref[pl.ds(start, WIN), head_cols(hp, part)] for part in range(3)]
        cols = head_cols(hp, 0)
        q = q * jnp.asarray(HEAD_DIM**-0.5, BF16)
        pieces = []
        for half in range(2):
            inside = (lane < 64) if half == 0 else (lane >= 64)
            qh = jnp.where(inside, q, jnp.zeros_like(q))
            scores = dot(qh, k, CONTRACT_LANES) + bias
            peak = jnp.max(scores, axis=1, keepdims=True)
            weight = jnp.exp(scores - peak).astype(BF16)
            vh = jnp.where(inside, v, jnp.ones_like(v))
            mixed = dot(weight, vh)
            total = pltpu.roll(mixed, 64, 1)
            pieces.append(mixed / total)
            one = total[:, 0:1] if half == 0 else mixed[:, 0:1]
            head = hp * 2 + half
            stat[0:WIN, :] = jnp.where(lane == head, peak + jnp.log(one), stat[0:WIN, :])
        ctx = jnp.where(lane < 64, pieces[0], pieces[1]).astype(BF16)
        old = ctx_ref[pl.ds(start, WIN), cols]
        ctx_ref[pl.ds(start, WIN), cols] = jnp.where(mine, ctx, old)
    lse_ref[pair] = jnp.transpose(stat[...])[0:16, :]


MESH = pl.DeviceIdType.MESH
HALF = 384
FF_DEV = 768
HOPS = [(way, hop) for hop in (1, 2, 3) for way in (1, -1)]


def front_kernel(
    small,
    n_batch,
    len_ref,
    group_ref,
    routes_ref,
    tok_ref,
    cot_ref,
    gain_one_ref,
    w_qkv_ref,
    w_proj_ref,
    gain_two_ref,
    w_in_ref,
    w_back_ref,
    qkv_hbm,
    ctx_hbm,
    lse_hbm,
    mid_hbm,
    g_hbm,
    x_hbm,
    wi_all,
    wb_all,
    offs_all,
    col_ref,
    qkv,
    ctx,
    lse,
    mid,
    g_sorted,
    x_sorted,
    held,
    stat,
    pos_ref,
    offs,
    wi_part,
    wb_part,
    local_sems,
    send_sems,
    recv_sems,
    hop_send,
    hop_recv,
    pass_send,
    pass_recv,
):
    batch, ffn = lax.axis_index("batch"), lax.axis_index("ffn")
    z, y = batch // 2, batch % 2
    near, far, cater = (batch, ffn ^ 1), (batch, ffn ^ 2), (batch, ffn ^ 3)
    across = (batch ^ 1, ffn)

    barrier = pltpu.get_barrier_semaphore()
    for device in [near, far, cater] + ([across] if small else []):
        pl.semaphore_signal(barrier, inc=1, device_id=device, device_id_type=MESH)
    if small:
        for way in (1, -1):

            @pl.when((z + way >= 0) & (z + way <= 3))
            def _(way=way):
                pl.semaphore_signal(
                    barrier, inc=1, device_id=(batch + 2 * way, ffn), device_id_type=MESH
                )

        inner = jnp.where((z == 0) | (z == 3), 1, 2)
        pl.semaphore_wait(barrier, 4 + inner)
    else:
        pl.semaphore_wait(barrier, 3)

    local_count = [0]
    waiting = []

    def local(src, dst):
        number = local_count[0]
        local_count[0] += 1
        copy = pltpu.make_async_copy(src, dst, local_sems.at[number])
        copy.start()
        waiting.append(copy)

    used = [0]

    def send(src, dst, device):
        number = used[0]
        used[0] += 1
        copy = pltpu.make_async_remote_copy(
            src_ref=src,
            dst_ref=dst,
            send_sem=send_sems.at[number],
            recv_sem=recv_sems.at[number],
            device_id=device,
            device_id_type=MESH,
        )
        copy.start()
        return copy

    part, whole = (wi_part, wb_part), (wi_all, wb_all)

    def valid(origin):
        return (origin >= 0) & (origin <= 3)

    def hop_copy(a, way, hop, origin, device):
        slot = whole[a].at[origin * 2 + y]
        number = HOPS.index((way, hop))
        return pltpu.make_async_remote_copy(
            src_ref=part[a] if hop == 1 else slot,
            dst_ref=slot,
            send_sem=hop_send.at[a, number],
            recv_sem=hop_recv.at[a, number],
            device_id=device,
            device_id_type=MESH,
        )

    def hop_go(a, hop, finish=False):
        for way in (1, -1):
            origin = z - way * (hop - 1)

            @pl.when(valid(origin) & valid(z + way))
            def _(way=way, origin=origin):
                copy = hop_copy(a, way, hop, origin, (batch + 2 * way, ffn))
                if finish:
                    copy.wait_send()
                else:
                    copy.start()

    def pass_copy(a, way, hop, origin, column):
        slot = whole[a].at[origin * 2 + column]
        number = HOPS.index((way, hop))
        return pltpu.make_async_remote_copy(
            src_ref=slot,
            dst_ref=slot,
            send_sem=pass_send.at[a, number],
            recv_sem=pass_recv.at[a, number],
            device_id=across,
            device_id_type=MESH,
        )

    def hop_came(a, hop):
        for way in (1, -1):
            origin = z - way * hop

            @pl.when(valid(origin))
            def _(way=way, origin=origin):
                hop_copy(a, way, hop, origin, (batch, ffn)).wait_recv()

        if hop < 3:
            hop_go(a, hop + 1)
        for way in (1, -1):
            origin = z - way * hop

            @pl.when(valid(origin))
            def _(way=way, origin=origin):
                pass_copy(a, way, hop, origin, y).start()

    own_over = []
    if small:
        rank = jnp.int32(0)
        for b in range(n_batch):
            same = (group_ref[b] == group_ref[batch]) & (b < batch)
            rank = rank + jnp.where(same, 1, 0)
        wi_part[...] = jnp.where(rank == 0, w_in_ref[0, :, 0:HALF], w_in_ref[0, :, HALF:FF_DEV])
        wb_part[...] = jnp.where(rank == 0, w_back_ref[0, 0:HALF, :], w_back_ref[0, HALF:FF_DEV, :])
        for a in range(2):
            hop_go(a, 1)
            own_over.append(send(part[a], whole[a].at[batch], across))
            local(part[a], whole[a].at[batch])

    exchanged = []
    route_rows(n_batch, group_ref, routes_ref, pos_ref, col_ref, offs)
    for slot, device in ((1, near), (2, far), (3, cater)):
        exchanged.append(send(offs, offs_all.at[pl.ds(slot, 1), :], device))
    local(offs, offs_all.at[pl.ds(0, 1), :])

    def sort_and_send(rows_ref, out_ref, out_hbm):
        pos = pos_ref[0:1, 0:ROWS]
        top = 0
        sent = []
        for size in SORT_TILES:
            want = top + lax.broadcasted_iota(I32, (size, ROWS), 0)
            hot = jnp.where(pos == want, 1.0, 0.0).astype(BF16)
            rows = pl.ds(top, size)
            out_ref[rows, :] = dot(hot, rows_ref[...]).astype(BF16)
            sent.append(send(out_ref.at[rows], out_hbm.at[2, rows], far))
            exchanged.append(send(out_ref.at[rows], out_hbm.at[1, rows], near))
            local(out_ref.at[rows], out_hbm.at[0, rows])
            top += size
        return sent

    def hand_on(sent, out_hbm):
        top = 0
        for copy, size in zip(sent, SORT_TILES):
            rows = pl.ds(top, size)
            copy.wait()
            exchanged.append(send(out_hbm.at[2, rows], out_hbm.at[3, rows], near))
            top += size

    held[1552:ROWS, :] = jnp.zeros((ROWS - 1552, D), BF16)
    held[0:TOK_DEV, :] = cot_ref[...]
    g_sent = sort_and_send(held, g_sorted, g_hbm)

    for i in range(3):
        top = min(TILE * (i + 1), TOK_DEV)
        rows = slice(TILE * i, top)
        normal, _ = norm_parts(tok_ref[rows, :].astype(F32))
        normed = (normal * gain_one_ref[...].reshape(1, D)).astype(BF16)
        qkv[rows, :] = dot(normed, w_qkv_ref[...]).astype(BF16)
    tail = slice(TOK_DEV, ROWS)
    qkv[tail, :] = jnp.zeros((ROWS - TOK_DEV, 3 * D), BF16)
    ctx[1552:ROWS, :] = jnp.zeros((ROWS - 1552, D), BF16)
    local(qkv, qkv_hbm)
    if small:
        hop_came(0, 1)

    @pl.loop(0, SEQ_DEV)
    def _(pair):
        attend_pair(pair, len_ref[pair], qkv, ctx, lse, stat)
        if small:

            @pl.when(pair == 1)
            def _():
                hop_came(1, 1)

            @pl.when(pair == 4)
            def _():
                hop_came(0, 2)

    local(ctx, ctx_hbm)
    local(lse, lse_hbm)
    for i in range(3):
        top = min(TILE * (i + 1), TOK_DEV)
        rows = slice(TILE * i, top)
        middle = tok_ref[rows, :].astype(F32) + dot(ctx[rows, :], w_proj_ref[...])
        mid[rows, :] = middle
        normal, _ = norm_parts(middle)
        held[rows, :] = (normal * gain_two_ref[...].reshape(1, D)).astype(BF16)
    local(mid, mid_hbm)
    if small:
        hop_came(1, 2)
    x_sent = sort_and_send(held, x_sorted, x_hbm)
    hand_on(g_sent, g_hbm)
    if small:
        hop_came(0, 3)
        hop_came(1, 3)
    hand_on(x_sent, x_hbm)
    for copy in exchanged + own_over:
        copy.wait()
    if small:
        for a in range(2):
            for hop in (1, 2, 3):
                hop_go(a, hop, finish=True)
            for way, hop in HOPS:
                origin = z - way * hop

                @pl.when(valid(origin))
                def _(a=a, way=way, hop=hop, origin=origin):
                    pass_copy(a, way, hop, origin, y).wait_send()
                    pass_copy(a, way, hop, origin, 1 - y).wait_recv()

    for copy in waiting:
        copy.wait()


def front(small, lengths, group_map, routes, tokens, *arrays):
    vmem = pl.BlockSpec(memory_space=pltpu.VMEM)
    any_space = pl.BlockSpec(memory_space=pl.ANY)
    tiles = len(SORT_TILES)
    copies = 6 * tiles + 2 + 3
    dma = pltpu.SemaphoreType.DMA
    return pl.pallas_call(
        functools.partial(front_kernel, small, group_map.shape[0]),
        out_shape=(
            jax.ShapeDtypeStruct((ROWS, 3 * D), BF16),
            jax.ShapeDtypeStruct((ROWS, D), BF16),
            jax.ShapeDtypeStruct((SEQ_DEV, 16, 384), F32),
            jax.ShapeDtypeStruct((TOK_DEV, D), F32),
            jax.ShapeDtypeStruct((4, SORTED, D), BF16),
            jax.ShapeDtypeStruct((4, SORTED, D), BF16),
            jax.ShapeDtypeStruct((8, D, HALF), BF16),
            jax.ShapeDtypeStruct((8, HALF, D), BF16),
            jax.ShapeDtypeStruct((4, 128), I32),
            jax.ShapeDtypeStruct((LANES, 128), I32),
        ),
        in_specs=[pl.BlockSpec(memory_space=pltpu.SMEM)] * 2 + [vmem] * (2 + len(arrays)),
        out_specs=(any_space,) * 8 + (vmem,) * 2,
        scratch_shapes=[
            pltpu.VMEM((ROWS, 3 * D), BF16),
            pltpu.VMEM((ROWS, D), BF16),
            pltpu.VMEM((SEQ_DEV, 16, 384), F32),
            pltpu.VMEM((TOK_DEV, D), F32),
            pltpu.VMEM((SORTED, D), BF16),
            pltpu.VMEM((SORTED, D), BF16),
            pltpu.VMEM((ROWS, D), BF16),
            pltpu.VMEM((384, 128), F32),
            pltpu.VMEM((1, LANES), I32),
            pltpu.VMEM((1, 128), I32),
            pltpu.VMEM((D, HALF), BF16),
            pltpu.VMEM((HALF, D), BF16),
            dma((2 * tiles + 7,)),
            dma((copies,)),
            dma((copies,)),
            dma((2, 6)),
            dma((2, 6)),
            dma((2, 6)),
            dma((2, 6)),
        ],
        compiler_params=params(collective_id=1, has_side_effects=True),
        name="front",
    )(lengths, group_map, routes, tokens, *arrays)


def gelu_both(u):
    below = 0.5 * (1.0 + lax.erf(u * (1.0 / math.sqrt(2.0))))
    density = jnp.exp(-0.5 * u * u) * (1.0 / math.sqrt(2.0 * math.pi))
    return u * below, below + u * density


MERGED = 2 * SORTED + 256
HEAD = 800
CHUNK = D // 8


def expert_kernel(sources, first, count, rows, carried, joined, cut, n_batch, offs_ref, group_ref, *refs):
    refs = list(refs)

    def take(count):
        head = refs[:count]
        del refs[:count]
        return head

    xs, gs = take(2), take(2)
    wi_hbm, wb_hbm = take(2)
    before = take(2) if carried else None
    earlier = take(4) if joined else None
    outs, gxs = take(2), take(2)
    dwi_ref, dwb_ref = take(2)
    xm, gm, wi, wb, acc_i, acc_b, hosts_ref, sems, join_sems = refs
    step = pl.program_id(0)
    expert = first + step
    slot = step % 2

    def join_copies():
        for number, (source, target) in enumerate(zip(earlier, outs + gxs)):
            yield pltpu.make_async_copy(source, target.at[0:HEAD, :], join_sems.at[number])

    def weight_copies(e, buffer, start):
        for p in range(2):
            host = hosts_ref[e * 2 + p]
            part = pl.ds(p * HALF, HALF)
            for number, source, target in (
                (0, wi_hbm.at[host], wi.at[buffer, :, part]),
                (1, wb_hbm.at[host], wb.at[buffer, part, :]),
            ):
                copy = pltpu.make_async_copy(source, target, sems.at[buffer, p, number])
                if start:
                    copy.start()
                else:
                    copy.wait()

    @pl.when(step == 0)
    def _():
        for e in range(EXPERTS):
            first_host, second_host = jnp.int32(n_batch), jnp.int32(n_batch)
            for b in reversed(range(n_batch)):
                hosting = group_ref[b] == e
                second_host = jnp.where(hosting, first_host, second_host)
                first_host = jnp.where(hosting, b, first_host)
            hosts_ref[2 * e] = first_host
            hosts_ref[2 * e + 1] = second_host
        weight_copies(first, 0, True)
        if joined:
            for copy in join_copies():
                copy.start()

    @pl.when(step + 1 < count)
    def _():
        weight_copies(expert + 1, 1 - slot, True)

    def blocks(count, act):
        @pl.loop(0, count)
        def _(i):
            act(pl.multiple_of(i * 16, 16))

    @pl.when((step == 0) & (rows == SORTED))
    def _():
        for s in range(2):
            live = pl.multiple_of(offs_ref[sources[s], EXPERTS], 16)

            def clear(at, s=s, live=live):
                spot = pl.ds(pl.multiple_of(live + at, 16), 16)
                outs[s][spot, :] = jnp.zeros((16, D), BF16)
                gxs[s][spot, :] = jnp.zeros((16, D), BF16)

            blocks((SORTED - live) // 16, clear)

    if carried:
        acc_i[...] = before[0][0].astype(F32)
        acc_b[...] = before[1][0].astype(F32)
    else:
        acc_i[...] = jnp.zeros_like(acc_i)
        acc_b[...] = jnp.zeros_like(acc_b)

    places = []
    total = jnp.int32(0)
    for s in range(2):
        begin = pl.multiple_of(offs_ref[sources[s], expert], 16)
        size = offs_ref[sources[s], expert + 1] - begin
        places.append((begin, total, size // 16))

        def gather(at, s=s, begin=begin, total=total):
            here = pl.ds(pl.multiple_of(begin + at, 16), 16)
            there = pl.ds(pl.multiple_of(total + at, 16), 16)
            xm[there, :] = xs[s][0, here, :]
            gm[there, :] = gs[s][0, here, :]

        blocks(size // 16, gather)
        total = total + size
    span = pl.multiple_of(total, 16)

    def blank(at):
        there = pl.ds(pl.multiple_of(span + at, 16), 16)
        xm[there, :] = jnp.zeros((16, D), BF16)
        gm[there, :] = jnp.zeros((16, D), BF16)

    blocks((256 - span % 256) // 16, blank)
    weight_copies(expert, slot, False)
    w_in, w_back = wi.at[slot], wb.at[slot]

    @pl.loop(0, (span + 255) // 256)
    def _(i):
        spot = pl.ds(pl.multiple_of(i * 256, 256), 256)
        x, g = xm[spot, :], gm[spot, :]
        inner = dot(x, w_in[...])
        hidden, slope = gelu_both(inner)
        hidden = hidden.astype(BF16)
        grad_hidden = dot(g, w_back[...], CONTRACT_LANES).astype(BF16)
        grad_inner = (grad_hidden.astype(F32) * slope).astype(BF16)
        xm[spot, :] = dot(hidden, w_back[...]).astype(BF16)
        gm[spot, :] = dot(grad_inner, w_in[...], CONTRACT_LANES).astype(BF16)
        acc_b[...] += dot(hidden, g, CONTRACT_ROWS)
        acc_i[...] += dot(x, grad_inner, CONTRACT_ROWS)

    if cut:
        y = lax.axis_index("batch") % 2
        for i, acc in enumerate((acc_i, acc_b)):
            for z in range(4):
                for ref, column in ((dwi_ref, 1 - y), (dwb_ref, y)):
                    part = pl.ds(pl.multiple_of((z * 2 + column) * CHUNK, 16), CHUNK)
                    ref[i, z] = acc[part, :].astype(BF16)
    else:
        dwi_ref[0] = acc_i[...].astype(BF16)
        dwb_ref[0] = acc_b[...].astype(BF16)
    if joined:

        @pl.when(step == 0)
        def _():
            for copy in join_copies():
                copy.wait()

    for s in range(2):
        begin, base, blocks_of = places[s]

        def hand_back(at, s=s, begin=begin, base=base):
            here = pl.ds(pl.multiple_of(begin + at, 16), 16)
            there = pl.ds(pl.multiple_of(base + at, 16), 16)
            outs[s][here, :] = xm[there, :]
            gxs[s][here, :] = gm[there, :]

        blocks(blocks_of, hand_back)


def experts(
    sources, offs, group_map, x, g, wi, wb, before=None, earlier=None, first=0, count=EXPERTS, cut=False
):
    rows = HEAD if cut else SORTED
    whole = once((rows, D))
    any_space = pl.BlockSpec(memory_space=pl.ANY)
    carried, joined = before is not None, earlier is not None
    out = jax.ShapeDtypeStruct((rows, D), BF16)

    def source(i):
        return pl.BlockSpec((1, rows, D), lambda e, *_: (i, 0, 0), pipeline_mode=pl.Buffered(1))

    carry = pl.BlockSpec((1, D, FF_DEV), lambda e, *_: (first + e, 0, 0))
    if cut:
        weight = once((2, 4, CHUNK, D))
        grad = jax.ShapeDtypeStruct((2, 4, CHUNK, D), BF16)
    else:
        weight = pl.BlockSpec((1, D, FF_DEV), lambda e, *_: (e, 0, 0))
        grad = jax.ShapeDtypeStruct((count, D, FF_DEV), BF16)
    picked = [source(i) for i in sources]
    kernel = functools.partial(
        expert_kernel, sources, first, count, rows, carried, joined, cut, group_map.shape[0]
    )
    return pl.pallas_call(
        kernel,
        grid_spec=pltpu.PrefetchScalarGridSpec(
            num_scalar_prefetch=2,
            grid=(count,),
            in_specs=picked
            + picked
            + [any_space] * 2
            + [carry] * (2 * carried)
            + [any_space] * (4 * joined),
            out_specs=[whole] * 4 + [weight] * 2,
            scratch_shapes=[
                pltpu.VMEM((MERGED, D), BF16),
                pltpu.VMEM((MERGED, D), BF16),
                pltpu.VMEM((2, D, FF_DEV), BF16),
                pltpu.VMEM((2, FF_DEV, D), BF16),
                pltpu.VMEM((D, FF_DEV), F32),
                pltpu.VMEM((FF_DEV, D), F32),
                pltpu.SMEM((2 * EXPERTS,), I32),
                pltpu.SemaphoreType.DMA((2, 2, 2)),
                pltpu.SemaphoreType.DMA((4,)),
            ],
        ),
        out_shape=(out,) * 4 + (grad,) * 2,
        compiler_params=params(),
        cost_estimate=cost(8 * count * SORTED * D * FF_DEV, 16 * SORTED * D),
        name="experts",
    )(offs, group_map, x, x, g, g, wi, wb, *(before or ()), *(earlier or ()))


def swap(rows, bit):
    pairs = [(f, f ^ bit) for f in range(4)]
    return lax.ppermute(rows, "ffn", pairs)


def tie(value, *others):
    return lax.optimization_barrier((value, *others))[0]


class Wire:
    def __init__(self, send_sems, recv_sems):
        self.send_sems, self.recv_sems, self.used = send_sems, recv_sems, 0

    def send(self, src, dst, device):
        number = self.used
        self.used += 1
        copy = pltpu.make_async_remote_copy(
            src_ref=src,
            dst_ref=dst,
            send_sem=self.send_sems.at[number],
            recv_sem=self.recv_sems.at[number],
            device_id=device,
            device_id_type=MESH,
        )
        copy.start()
        return copy


class Mover:
    def __init__(self, sems):
        self.sems, self.used = sems, 0

    def go(self, src, dst):
        number = self.used
        self.used += 1
        copy = pltpu.make_async_copy(src, dst, self.sems.at[number])
        copy.start()
        return copy


def greet(peers):
    barrier = pltpu.get_barrier_semaphore()
    for device in peers:
        pl.semaphore_signal(barrier, inc=1, device_id=device, device_id_type=MESH)
    pl.semaphore_wait(barrier, len(peers))


def wait_all(copies):
    for copy in copies:
        copy.wait()


def token_tiles():
    for i in range(3):
        yield slice(TILE * i, min(TILE * (i + 1), TOK_DEV))


def unsort(pos_col, src):
    want = lax.broadcasted_iota(I32, (pos_col.shape[0], SORTED), 1)
    hot = jnp.where(pos_col == want, 1.0, 0.0).astype(BF16)
    return dot(hot, src)


def attend_back_pair(pair, length, qkv_ref, gctx_ref, lse_ref, out_ref):
    start, skip = window(pair)
    start = pl.multiple_of(start, 16)
    row = lax.broadcasted_iota(I32, (WIN, 1), 0)
    mine = (row >= skip) & (row < skip + SEQ_LEN)
    bias = jnp.where((row >= skip) & (row < skip + PATCHES + length), 0.0, -1e30)
    lane = lax.broadcasted_iota(I32, (WIN, 128), 1)
    scale = jnp.asarray(HEAD_DIM**-0.5, BF16)
    @pl.loop(0, HEADS // 2)
    def _(hp):
        spots = [head_cols(hp, part) for part in range(3)]
        q, k, v = [qkv_ref[pl.ds(start, WIN), spot] for spot in spots]
        none = jnp.zeros_like(q)
        q = jnp.where(mine, q * scale, none)
        ks = k * scale
        go = jnp.where(mine, gctx_ref[pl.ds(start, WIN), spots[0]], none)
        low = lane < 64
        both_q = jnp.concatenate([jnp.where(low, q, none), jnp.where(low, none, q)], axis=0)
        both_go = jnp.concatenate([jnp.where(low, go, none), jnp.where(low, none, go)], axis=0)
        log_total = jnp.concatenate(
            [lse_ref[pair, pl.ds(hp * 2 + half, 1), 0:WIN] for half in range(2)], axis=1
        )
        probs = jnp.exp(dot(k, both_q, CONTRACT_LANES) + bias - log_total)
        grad_probs = dot(v, both_go, CONTRACT_LANES)
        delta = jnp.sum(probs * grad_probs, axis=0, keepdims=True)
        grad_scores = (probs * (grad_probs - delta)).astype(BF16)
        grad_v = dot(probs.astype(BF16), both_go)
        grad_k = dot(grad_scores, both_q)
        turned = dot(grad_scores, ks, CONTRACT_ROWS)
        grad_q = jnp.where(low, turned[0:WIN], turned[WIN : 2 * WIN])
        for spot, new in zip(spots, (grad_q, grad_k, grad_v)):
            old = out_ref[pl.ds(start, WIN), spot]
            out_ref[pl.ds(start, WIN), spot] = jnp.where(mine, new.astype(BF16), old)


TURNS = (2, 3, 1, 0)


def rear_kernel(
    small,
    len_ref,
    pos_ref,
    gain_one_ref,
    gain_two_ref,
    w_ref,
    lse_ref,
    gx0_hbm,
    gx1_hbm,
    gx2_hbm,
    mid_hbm,
    cot_hbm,
    ctx_hbm,
    qkv_hbm,
    tok_hbm,
    out1_hbm,
    out2_hbm,
    out3_hbm,
    dwi_hbm,
    dwb_hbm,
    first_came,
    first_own,
    gm_hbm,
    gq_hbm,
    dwq_hbm,
    dwp_hbm,
    dg_ref,
    share_hbm,
    near_hbm,
    far_hbm,
    wide,
    mid,
    cot,
    ctx,
    gctx,
    qkv,
    half_a,
    half_b,
    own_rows,
    came_y,
    came_z,
    acc,
    dwp,
    local_sems,
    send_sems,
    recv_sems,
    z_send,
    z_recv,
):
    batch, ffn = lax.axis_index("batch"), lax.axis_index("ffn")
    z, y = batch // 2, batch % 2
    near, far, across = (batch, ffn ^ 1), (batch, ffn ^ 2), (batch ^ 1, ffn)
    along = {k: (batch ^ (2 * k), ffn) for k in (1, 2, 3)}
    greet([near, far] + ([across] + list(along.values()) if small else []))
    wire, mover = Wire(send_sems, recv_sems), Mover(local_sems)

    parts_near = wire.send(gx1_hbm, wide.at[:, D : 2 * D], near)
    near_sent = wire.send(out3_hbm, half_b, near)
    half_in = mover.go(out2_hbm, half_a)
    over_y = {}
    own_in = {}
    if small:
        for turn in TURNS:
            there = pl.ds(pl.multiple_of(((z ^ turn) * 2 + 1 - y) * CHUNK, 16), CHUNK)
            over_y[turn] = [
                wire.send(grad.at[:, there, :], came_y.at[turn, i, 1:EXPERTS], across)
                for i, grad in enumerate((dwi_hbm, dwb_hbm))
            ]
    first_in = {}
    if small:
        for turn in TURNS:
            first_in[turn] = [
                mover.go(first_came.at[:, z ^ turn], came_y.at[turn, :, 0]),
                mover.go(first_own.at[:, z ^ turn], own_rows.at[turn, :, 0]),
            ]
    parts_in = [
        mover.go(part, wide.at[:, i * D : i * D + D])
        for i, part in ((0, gx0_hbm), (2, gx2_hbm))
    ]
    rows_in = [mover.go(mid_hbm, mid), mover.go(cot_hbm, cot), mover.go(ctx_hbm, ctx)]
    qkv_in = mover.go(qkv_hbm, qkv)
    if small:
        for turn in TURNS:
            here = pl.ds(pl.multiple_of(((z ^ turn) * 2 + y) * CHUNK, 16), CHUNK)
            own_in[turn] = [
                mover.go(grad.at[:, here, :], own_rows.at[turn, i, 1:EXPERTS])
                for i, grad in enumerate((dwi_hbm, dwb_hbm))
            ]
    sent = [wire.send(out1_hbm, near_hbm, near)]
    stored = []

    def z_copy(turn, i):
        return pltpu.make_async_remote_copy(
            src_ref=came_y.at[turn, i, 1:EXPERTS],
            dst_ref=came_z.at[turn - 1, i, 1:EXPERTS],
            send_sem=z_send.at[turn - 1, i],
            recv_sem=z_recv.at[turn - 1, i],
            device_id=along[turn],
            device_id_type=MESH,
        )

    def take_turn(turn, i):
        if not small:
            return
        over_y[turn][i].wait()
        own_in[turn][i].wait()
        for e in range(1, EXPERTS):
            came_y[turn, i, e] = (
                came_y[turn, i, e].astype(F32) + own_rows[turn, i, e].astype(F32)
            ).astype(BF16)
        if turn:
            z_copy(turn, i).start()

    first_z = []
    if small:
        for turn in TURNS:
            wait_all(first_in[turn])
            for i in range(2):
                came_y[turn, i, 0] = (
                    came_y[turn, i, 0].astype(F32) + own_rows[turn, i, 0].astype(F32)
                ).astype(BF16)
            if turn:
                first_z.append(
                    wire.send(came_y.at[turn, :, 0], came_z.at[turn - 1, :, 0], along[turn])
                )
    wait_all(parts_in + rows_in + [parts_near])
    top = 0
    for size in SORT_TILES:
        rows = slice(top, top + size)
        wide[rows, 0:D] = (
            wide[rows, 0:D].astype(F32)
            + wide[rows, D : 2 * D].astype(F32)
            + wide[rows, 2 * D : 3 * D].astype(F32)
        ).astype(BF16)
        top += size
    half_in.wait()
    near_sent.wait()
    half_a[...] = (half_a[...].astype(F32) + half_b[...].astype(F32)).astype(BF16)
    sent.append(wire.send(half_a, far_hbm, far))

    gctx[1552:ROWS, :] = jnp.zeros((ROWS - 1552, D), BF16)
    grad_gain = jnp.zeros((1, D), F32)
    for i, rows in enumerate(token_tiles()):
        grad_normed = unsort(pos_ref[rows, 0:1], wide[:, 0:D])
        normal, inverse = norm_parts(mid[rows, :])
        grad_gain = grad_gain + jnp.sum(grad_normed * normal, axis=0, keepdims=True)
        part = norm_pull(grad_normed, gain_two_ref[...].reshape(1, D), normal, inverse)
        grad_middle = cot[rows, :].astype(F32) + part
        mid[rows, :] = grad_middle
        low = grad_middle.astype(BF16)
        product = dot(ctx[rows, :], low, CONTRACT_ROWS)
        if i == 0:
            acc[...] = product
        elif i == 1:
            acc[...] += product
        else:
            dwp[...] = (acc[...] + product).astype(BF16)
        gctx[rows, :] = dot(low, w_ref[...], CONTRACT_LANES).astype(BF16)
        if i == 1:
            take_turn(2, 0)
            take_turn(2, 1)
    dg_ref[...] = grad_gain
    stored.append(mover.go(mid, gm_hbm))
    stored.append(mover.go(dwp, dwp_hbm))
    tok_in = mover.go(tok_hbm, cot)
    wide[1552:SORTED, :] = jnp.zeros((SORTED - 1552, 3 * D), BF16)
    qkv_in.wait()
    take_turn(3, 0)
    take_turn(3, 1)

    @pl.loop(0, SEQ_DEV)
    def _(pair):
        attend_back_pair(pair, len_ref[pair], qkv, gctx, lse_ref, wide)
        @pl.when(pair == 1)
        def _():
            take_turn(1, 0)
            take_turn(1, 1)

    stored.append(mover.go(wide.at[0:ROWS, :], gq_hbm))
    tok_in.wait()
    for rows in token_tiles():
        normal, _ = norm_parts(cot[rows, :].astype(F32))
        gctx[rows, :] = (normal * gain_one_ref[...].reshape(1, D)).astype(BF16)
    for i in range(3):
        part = slice(i * 256, i * 256 + 256)
        qkv[part, :] = dot(gctx[:, part], wide[0:ROWS, :], CONTRACT_ROWS).astype(BF16)
    stored.append(mover.go(qkv.at[0:D, :], dwq_hbm))
    if small:
        take_turn(0, 0)
        take_turn(0, 1)
        wait_all(first_z + [z_copy(turn, i) for turn in TURNS[:3] for i in range(2)])
        for i in range(2):
            for e in range(EXPERTS):
                total = came_y[0, i, e].astype(F32)
                for k in range(3):
                    total = total + came_z[k, i, e].astype(F32)
                came_y[0, i, e] = total.astype(BF16)
        stored.append(mover.go(came_y.at[0], share_hbm))
    wait_all(sent + stored)


def rear(small, lengths, pos_col, gain_one, gain_two, w_proj, lse, *arrays):
    vmem = pl.BlockSpec(memory_space=pltpu.VMEM)
    any_space = pl.BlockSpec(memory_space=pl.ANY)
    dma = pltpu.SemaphoreType.DMA
    copies = 15
    return pl.pallas_call(
        functools.partial(rear_kernel, small),
        out_shape=(
            jax.ShapeDtypeStruct((TOK_DEV, D), F32),
            jax.ShapeDtypeStruct((ROWS, 3 * D), BF16),
            jax.ShapeDtypeStruct((D, 3 * D), BF16),
            jax.ShapeDtypeStruct((D, D), BF16),
            jax.ShapeDtypeStruct((1, D), F32),
            jax.ShapeDtypeStruct((2, EXPERTS, CHUNK, D), BF16),
            jax.ShapeDtypeStruct((SORTED, D), BF16),
            jax.ShapeDtypeStruct((SORTED, D), BF16),
        ),
        in_specs=[pl.BlockSpec(memory_space=pltpu.SMEM)] + [vmem] * 5 + [any_space] * len(arrays),
        out_specs=(any_space,) * 4 + (vmem,) + (any_space,) * 3,
        scratch_shapes=[
            pltpu.VMEM((SORTED, 3 * D), BF16),
            pltpu.VMEM((TOK_DEV, D), F32),
            pltpu.VMEM((TOK_DEV, D), BF16),
            pltpu.VMEM((ROWS, D), BF16),
            pltpu.VMEM((ROWS, D), BF16),
            pltpu.VMEM((ROWS, 3 * D), BF16),
            pltpu.VMEM((SORTED, D), BF16),
            pltpu.VMEM((SORTED, D), BF16),
            pltpu.VMEM((4, 2, EXPERTS, CHUNK, D), BF16),
            pltpu.VMEM((4, 2, EXPERTS, CHUNK, D), BF16),
            pltpu.VMEM((3, 2, EXPERTS, CHUNK, D), BF16),
            pltpu.VMEM((D, D), F32),
            pltpu.VMEM((D, D), BF16),
            dma((32,)),
            dma((copies,)),
            dma((copies,)),
            dma((3, 2)),
            dma((3, 2)),
        ],
        compiler_params=params(collective_id=2, has_side_effects=True),
        name="rear",
    )(lengths, pos_col, gain_one, gain_two, w_proj, lse, *arrays)


ORDERS = (("x", "y", "z"), ("y", "x", "z")) * 2
WIDTHS = (1024, 1024, 512, 512)
LEFTS = (0, 1024, 2048, 2560)
SETS = ((0, 1), (2, 3))
WIDE = 4 * D
GAIN_ROWS = 8


def last_kernel(
    small,
    group_ref,
    pos_ref,
    gain_ref,
    w_ref,
    dg_two_ref,
    tok_hbm,
    gq_hbm,
    gm_hbm,
    mid_hbm,
    out0_hbm,
    out1_hbm,
    out2_hbm,
    dwq_hbm,
    dwp_hbm,
    share_hbm,
    ig_hbm,
    bo_hbm,
    sum_ref,
    gains_ref,
    pieces_ref,
    tok,
    gq,
    gm,
    mid,
    outs,
    share,
    stage,
    near_rows,
    held,
    came_z,
    came_xy,
    gain_in,
    local_sems,
    send_sems,
    recv_sems,
):
    batch, ffn = lax.axis_index("batch"), lax.axis_index("ffn")
    z, y, x, c = batch // 2, batch % 2, ffn // 2, ffn % 2
    place = {"x": x, "y": y, "z": z}
    mover = Mover(local_sems)

    def peer(axis, k=1):
        if axis == "c":
            return (batch, ffn ^ 1)
        if axis == "x":
            return (batch, ffn ^ 2)
        if axis == "y":
            return (batch ^ 1, ffn)
        return (batch ^ (2 * k), ffn)

    flying = ([], [])
    top = [0] * 4
    left = list(LEFTS)
    rows, cols = [384] * 4, list(WIDTHS)
    base = pl.multiple_of(c * 384, 16)
    if small:
        greet([peer("c"), peer("x")] + [(batch ^ j, ffn) for j in range(1, 8)])
        wire = Wire(send_sems, recv_sems)
        share_in = mover.go(share_hbm, share)
        give = pl.ds(pl.multiple_of((1 - c) * 384, 16), 384)
        keep = pl.ds(base, 384)
        pieces = (
            ((dwq_hbm, 0, 2048, 0),),
            ((dwq_hbm, 2048, 256, 2048), (dwp_hbm, 0, D, 3 * D)),
        )
        to_core, kept = [[], []], [[], []]
        for which in range(2):
            for ref, start, size, at in pieces[which]:
                lanes, spot = pl.ds(start, size), pl.ds(at, size)
                to_core[which].append(
                    wire.send(ref.at[give, lanes], near_rows.at[:, spot], peer("c"))
                )
                kept[which].append(mover.go(ref.at[keep, lanes], held.at[:, spot]))
    loads = [mover.go(tok_hbm, tok), mover.go(gq_hbm, gq), mover.go(gm_hbm, gm)]
    later = [mover.go(mid_hbm, mid)] + [
        mover.go(part, outs.at[i]) for i, part in enumerate((out0_hbm, out1_hbm, out2_hbm))
    ]
    handed = []

    def hand_out(i, *turns):
        for j in turns:
            handed.append(
                wire.send(stage.at[j, i], pieces_ref.at[batch, i], (batch ^ j, ffn))
            )

    if small:
        share_in.wait()
        for j in range(8):
            expert = group_ref[batch ^ j]
            for i in range(2):
                stage[j, i] = share[i, expert]
        hand_out(0, 4, 6, 5, 2)
        pieces_ref[batch] = stage[0]

    def core_done(which):
        wait_all(to_core[which] + kept[which])
        for i in SETS[which]:
            lanes = slice(LEFTS[i], LEFTS[i] + WIDTHS[i])
            held[:, lanes] = (
                held[:, lanes].astype(F32) + near_rows[:, lanes].astype(F32)
            ).astype(BF16)

    def sum_go(which, step):
        for i in SETS[which]:
            axis = ORDERS[i][step]
            quarter = WIDTHS[i] // 4
            if axis == "z":
                live = pl.ds(top[i], rows[i])
                for k in (2, 3, 1):
                    there = pl.ds(pl.multiple_of(left[i] + (z ^ k) * quarter, 128), quarter)
                    flying[which].append(
                        wire.send(
                            held.at[live, there],
                            came_z.at[i, k - 1, 0 : rows[i], 0:quarter],
                            peer("z", k),
                        )
                    )
            else:
                half = rows[i] // 2
                there = pl.ds(pl.multiple_of(top[i] + (1 - place[axis]) * half, 16), half)
                flying[which].append(
                    wire.send(
                        held.at[there, pl.ds(left[i], cols[i])],
                        came_xy.at[i, 0 if axis == "x" else 1, 0:half, 0 : cols[i]],
                        peer(axis),
                    )
                )

    def sum_done(which, step):
        wait_all(flying[which])
        flying[which].clear()
        for i in SETS[which]:
            axis = ORDERS[i][step]
            if axis == "z":
                cols[i] = WIDTHS[i] // 4
                left[i] = pl.multiple_of(left[i] + z * cols[i], 128)
                terms = [came_z[i, k, 0 : rows[i], 0 : cols[i]] for k in range(3)]
            else:
                rows[i] = rows[i] // 2
                top[i] = pl.multiple_of(top[i] + place[axis] * rows[i], 16)
                terms = [came_xy[i, 0 if axis == "x" else 1, 0 : rows[i], 0 : cols[i]]]
            spot = (pl.ds(top[i], rows[i]), pl.ds(left[i], cols[i]))
            total = held[spot].astype(F32)
            for term in terms:
                total = total + term.astype(F32)
            held[spot] = total.astype(BF16)
            if step == 2:
                lines = pl.ds(pl.multiple_of(base + top[i], 16), rows[i])
                sum_ref[lines, spot[1]] = total.astype(BF16)

    def spread_go(which, step):
        for i in SETS[which]:
            axis = ORDERS[i][step]
            mine = sum_ref.at[
                pl.ds(pl.multiple_of(base + top[i], 16), rows[i]), pl.ds(left[i], cols[i])
            ]
            for k in (2, 3, 1) if axis == "z" else (1,):
                flying[which].append(wire.send(mine, mine, peer(axis, k)))

    def spread_done(which, step):
        wait_all(flying[which])
        flying[which].clear()
        for i in SETS[which]:
            axis = ORDERS[i][step]
            if axis == "z":
                left[i] = LEFTS[i]
                cols[i] = WIDTHS[i]
            else:
                top[i] = top[i] - place[axis] * rows[i]
                rows[i] = rows[i] * 2

    def core_go(which):
        size = 2 * WIDTHS[SETS[which][0]]
        mine = sum_ref.at[pl.ds(base, 384), pl.ds(LEFTS[SETS[which][0]], size)]
        flying[which].append(wire.send(mine, mine, peer("c")))

    def gains_go(axis, slot):
        for k in (1, 2, 3) if axis == "z" else (1,):
            flying[0].append(wire.send(gains_ref, gain_in.at[slot + k - 1], peer(axis, k)))

    def gains_done(axis, slot):
        total = gains_ref[...]
        for k in (0, 1, 2) if axis == "z" else (0,):
            total = total + gain_in[slot + k]
        gains_ref[...] = total

    tiles = list(token_tiles())
    grad_gain = jnp.zeros((1, D), F32)
    stored = []

    def first_back(part):
        normal, inverse = norm_parts(tok[part, :].astype(F32))
        grad_normed = dot(gq[part, :], w_ref[...], CONTRACT_LANES)
        gain_part = jnp.sum(grad_normed * normal, axis=0, keepdims=True)
        pulled = norm_pull(grad_normed, gain_ref[...].reshape(1, D), normal, inverse)
        gm[part, :] = gm[part, :] + pulled
        stored.append(mover.go(gm.at[part], ig_hbm.at[part]))
        return gain_part

    def finish(part):
        mid[part, :] = mid[part, :] + unsort(pos_ref[part, 0:1], outs[0])
        stored.append(mover.go(mid.at[part], bo_hbm.at[part]))

    def finish_sums():
        wait_all(later)
        at = 0
        for size in SORT_TILES:
            part = slice(at, at + size)
            outs[0, part] = (
                outs[0, part].astype(F32) + outs[1, part].astype(F32) + outs[2, part].astype(F32)
            ).astype(BF16)
            at += size

    if small:
        for which in range(2):
            core_done(which)
            sum_go(which, 0)
    wait_all(loads)
    grad_gain = grad_gain + first_back(tiles[0])
    grad_gain = grad_gain + first_back(tiles[1])
    if small:
        for which in range(2):
            sum_done(which, 0)
            sum_go(which, 1)
    grad_gain = grad_gain + first_back(tiles[2])
    gains_ref[0:1, :] = grad_gain
    gains_ref[1:2, :] = dg_two_ref[...]
    gains_ref[2:GAIN_ROWS, :] = jnp.zeros((GAIN_ROWS - 2, D), F32)
    if small:
        gains_go("c", 0)
        for which in range(2):
            sum_done(which, 1)
            if which == 0:
                gains_done("c", 0)
                gains_go("x", 1)
            sum_go(which, 2)
    finish_sums()
    if small:
        for which in range(2):
            sum_done(which, 2)
            if which == 0:
                gains_done("x", 1)
                gains_go("y", 2)
            spread_go(which, 2)
    finish(tiles[0])
    finish(tiles[1])
    if small:
        for which in range(2):
            spread_done(which, 2)
            if which == 0:
                gains_done("y", 2)
                gains_go("z", 3)
            spread_go(which, 1)
        hand_out(0, 7, 3, 1)
        hand_out(1, 4, 6, 5, 7, 2, 3, 1)
    finish(tiles[2])
    if small:
        for which in range(2):
            spread_done(which, 1)
            if which == 0:
                gains_done("z", 3)
            spread_go(which, 0)
        for which in range(2):
            spread_done(which, 0)
            core_go(which)
        wait_all(flying[0] + flying[1] + handed)
    wait_all(stored)


def last(small, group_map, pos_col, gain_one, w_qkv, dg_two, *arrays):
    vmem = pl.BlockSpec(memory_space=pltpu.VMEM)
    any_space = pl.BlockSpec(memory_space=pl.ANY)
    dma = pltpu.SemaphoreType.DMA
    copies = 3 + 14 + 20 + 20 + 6 + 2
    extra = dict(collective_id=3, has_side_effects=True) if small else {}
    return pl.pallas_call(
        functools.partial(last_kernel, small),
        out_shape=(
            jax.ShapeDtypeStruct((TOK_DEV, D), F32),
            jax.ShapeDtypeStruct((TOK_DEV, D), F32),
            jax.ShapeDtypeStruct((D, WIDE), BF16),
            jax.ShapeDtypeStruct((GAIN_ROWS, D), F32),
            jax.ShapeDtypeStruct((8, 2, CHUNK, D), BF16),
        ),
        in_specs=[pl.BlockSpec(memory_space=pltpu.SMEM)] + [vmem] * 4 + [any_space] * len(arrays),
        out_specs=(any_space,) * 2 + (vmem,) * 3,
        scratch_shapes=[
            pltpu.VMEM((TOK_DEV, D), BF16),
            pltpu.VMEM((ROWS, 3 * D), BF16),
            pltpu.VMEM((TOK_DEV, D), F32),
            pltpu.VMEM((TOK_DEV, D), F32),
            pltpu.VMEM((3, SORTED, D), BF16),
            pltpu.VMEM((2, EXPERTS, CHUNK, D), BF16),
            pltpu.VMEM((8, 2, CHUNK, D), BF16),
            pltpu.VMEM((384, WIDE), BF16),
            pltpu.VMEM((384, WIDE), BF16),
            pltpu.VMEM((4, 3, 96, 256), BF16),
            pltpu.VMEM((4, 2, 192, 1024), BF16),
            pltpu.VMEM((6, GAIN_ROWS, D), F32),
            dma((20,)),
            dma((copies,)),
            dma((copies,)),
        ],
        compiler_params=params(**extra),
        name="last",
    )(group_map, pos_col, gain_one, w_qkv, dg_two, *arrays)


def close_kernel(
    sum_ref, gains_ref, pieces_ref, ig_ref, bo_ref, *outs
):
    qkv_ref, proj_ref, one_ref, two_ref, wi_ref, wb_ref, ig_out, bo_out = outs
    qkv_ref[...] = sum_ref[:, 0 : 3 * D].astype(F32)
    proj_ref[...] = sum_ref[:, 3 * D : WIDE].astype(F32)
    one_ref[...] = gains_ref[0:1, :].reshape(D)
    two_ref[...] = gains_ref[1:2, :].reshape(D)
    wi_ref[0] = pieces_ref[0, 0].astype(F32)
    wb_ref[0] = pieces_ref[0, 1].astype(F32)
    ig_out[...] = ig_ref[...]
    bo_out[...] = bo_ref[...]


def close(summed, gains, pieces, input_grad, block_out):
    row = pl.BlockSpec((CHUNK, D), lambda i: (i, 0))
    tokens = pl.BlockSpec((200, D), lambda i: (i, 0))
    weight = pl.BlockSpec((1, CHUNK, D), lambda i: (0, i, 0))
    rows = jax.ShapeDtypeStruct((TOK_DEV, D), F32)
    return pl.pallas_call(
        close_kernel,
        grid=(8,),
        out_shape=(
            jax.ShapeDtypeStruct((D, 3 * D), F32),
            jax.ShapeDtypeStruct((D, D), F32),
            jax.ShapeDtypeStruct((D,), F32),
            jax.ShapeDtypeStruct((D,), F32),
            jax.ShapeDtypeStruct((1, D, D), F32),
            jax.ShapeDtypeStruct((1, D, D), F32),
            rows,
            rows,
        ),
        in_specs=[
            pl.BlockSpec((CHUNK, WIDE), lambda i: (i, 0)),
            full((GAIN_ROWS, D)),
            pl.BlockSpec((1, 2, CHUNK, D), lambda i: (i, 0, 0, 0)),
            tokens,
            tokens,
        ],
        out_specs=(
            pl.BlockSpec((CHUNK, 3 * D), lambda i: (i, 0)),
            row,
            full((D,)),
            full((D,)),
            weight,
            weight,
            tokens,
            tokens,
        ),
        compiler_params=params(),
        name="close",
    )(summed, gains, pieces, input_grad, block_out)


def body(
    tokens,
    text_lengths,
    routes,
    group_map,
    gain_one,
    w_qkv,
    w_proj,
    gain_two,
    w_in,
    w_back,
    cotangent,
):
    n_batch = lax.axis_size("batch")
    own = lax.axis_index("batch")
    small = n_batch == 8
    routes_row = jnp.pad(routes.reshape(1, TOK_DEV), ((0, 0), (0, LANES - TOK_DEV)))
    qkv, context, lse, middle, g, x, wi_all, wb_all, offs, pos_col = front(
        small,
        text_lengths,
        group_map,
        routes_row,
        tokens,
        cotangent,
        gain_one,
        w_qkv,
        w_proj,
        gain_two,
        w_in,
        w_back,
    )
    if not small:
        own_expert = group_map[own]
        order = jnp.arange(n_batch, dtype=I32)
        rank = jnp.sum(jnp.where((group_map == own_expert) & (order < own), 1, 0))
        part = jnp.minimum(rank, 1)
        wi_part = lax.dynamic_slice(w_in[0], (0, part * HALF), (D, HALF))
        wb_part = lax.dynamic_slice(w_back[0], (part * HALF, 0), (HALF, D))
        wi_all = lax.all_gather(wi_part, "batch", axis=0)
        wb_all = lax.all_gather(wb_part, "batch", axis=0)

    def run(pair, x, *rest, **more):
        return experts(pair, offs, group_map, x, g, wi_all, wb_all, *rest, **more)

    def add(a, b):
        return (a.astype(F32) + b.astype(F32)).astype(BF16)

    out2, out3, gx2, gx3, dwi, dwb = run((2, 3), x)
    gx_half = add(gx2, swap(gx3, 1))
    gx_far = swap(gx_half, 2)
    x = tie(x, gx_half)
    if small:
        *earlier, going, staying = run((0, 1), x, (dwi, dwb), count=1, cut=True)
        came = lax.ppermute(going, "batch", [(b, b ^ 1) for b in range(8)])
        out0, out1, gx0, gx1, dwi, dwb = run((0, 1), x, (dwi, dwb), earlier, first=1, count=2)
    else:
        out0, out1, gx0, gx1, dwi, dwb = run((0, 1), x, (dwi, dwb))
        came = staying = jnp.zeros((2, 4, CHUNK, D), BF16)
    grad_middle, grad_qkv, dw_qkv, dw_proj, dg_two, share, out_near, out_far = rear(
        small,
        text_lengths,
        pos_col,
        gain_one,
        gain_two,
        w_proj,
        lse,
        gx0,
        gx1,
        gx_far,
        middle,
        cotangent,
        context,
        qkv,
        tokens,
        out1,
        out2,
        out3,
        dwi,
        dwb,
        came,
        staying,
    )
    input_grad, block_out, summed, gains, pieces = last(
        small,
        group_map,
        pos_col,
        gain_one,
        w_qkv,
        dg_two,
        tokens,
        grad_qkv,
        grad_middle,
        middle,
        out0,
        out_near,
        out_far,
        dw_qkv,
        dw_proj,
        share,
    )
    if small:
        summed_qkv, summed_proj, gain_a, gain_b, grad_w_in, grad_w_back, input_grad, block_out = close(
            summed, gains, pieces, input_grad, block_out
        )
        gains = (gain_a, gain_b)
    else:

        def settle_any(grad):
            share = lax.psum_scatter(grad, "batch", scatter_dimension=1, tiled=True)
            whole = lax.all_gather(share, "batch", axis=1, tiled=True)
            return lax.dynamic_index_in_dim(whole, own_expert, 0, keepdims=True).astype(F32)

        grad_w_in = settle_any(dwi)
        grad_w_back = settle_any(dwb)
        summed_qkv, summed_proj = lax.psum((dw_qkv, dw_proj), ("batch", "ffn"))
        gains = lax.psum(gains, ("batch", "ffn"))
    return (
        block_out,
        input_grad,
        gains[0],
        summed_qkv.astype(F32),
        summed_proj.astype(F32),
        gains[1],
        grad_w_in,
        grad_w_back,
    )


def solution(mesh):
    placed = (
        P(("batch", "ffn"), None),
        P(("batch", "ffn")),
        P(("batch", "ffn"), None),
        P(),
        P(),
        P(),
        P(),
        P(),
        P("batch", None, "ffn"),
        P("batch", "ffn", None),
        P(("batch", "ffn"), None),
    )
    return jax.shard_map(
        body,
        mesh=mesh,
        in_specs=placed,
        out_specs=(
            P(("batch", "ffn"), None),
            P(("batch", "ffn"), None),
            P(),
            P(),
            P(),
            P(),
            P("batch", None, "ffn"),
            P("batch", "ffn", None),
        ),
        check_vma=False,
    )
```

```python
import functools
import math

import jax
import jax.numpy as jnp
from jax import lax
from jax.experimental import pallas as pl
from jax.experimental.pallas import tpu as pltpu
from jax.sharding import PartitionSpec as P

D = 768
HEADS = 12
HEAD_DIM = 64
EXPERTS = 3
PATCHES = 197
SEQ_DEV = 6
SEQ_LEN = 261
TOK_DEV = 1566
ROWS = 1584
SORTED = 1616
WIN = 288
TILE = 528
LANES = 1664
EPS = 1e-05
F32 = jnp.float32
BF16 = jnp.bfloat16
I32 = jnp.int32
CONTRACT_LANES = (((1,), (1,)), ((), ()))
CONTRACT_ROWS = (((0,), (0,)), ((), ()))


def params(**extra):
    return pltpu.CompilerParams(vmem_limit_bytes=60 << 20, **extra)


def cost(flops, moved):
    return pl.CostEstimate(flops=int(flops), bytes_accessed=int(moved), transcendentals=0)


def dot(a, b, dims=(((1,), (0,)), ((), ()))):
    return lax.dot_general(a, b, dims, preferred_element_type=F32)


def full(shape):
    zeros = (0,) * len(shape)
    return pl.BlockSpec(shape, lambda *_: zeros)


def once(shape):
    zeros = (0,) * len(shape)
    return pl.BlockSpec(shape, lambda *_: zeros, pipeline_mode=pl.Buffered(1))


def row_mask(start, rows, limit):
    return start + lax.broadcasted_iota(I32, (rows, 1), 0) < limit


def norm_parts(values):
    average = jnp.mean(values, axis=-1, keepdims=True)
    centred = values - average
    variance = jnp.mean(centred * centred, axis=-1, keepdims=True)
    inverse = lax.rsqrt(variance + EPS)
    return centred * inverse, inverse


def norm_pull(grad_normed, gain, normal, inverse):
    scaled = grad_normed * gain
    mean_grad = jnp.mean(scaled, axis=-1, keepdims=True)
    mean_proj = jnp.mean(scaled * normal, axis=-1, keepdims=True)
    return inverse * (scaled - mean_grad - normal * mean_proj)


def route_rows(n_batch, gm_ref, routes_ref, pos_ref, col_ref, offs_ref):
    routes = routes_ref[...]
    lane = lax.broadcasted_iota(I32, (8, LANES), 1)
    sub = lax.broadcasted_iota(I32, (8, LANES), 0)
    expert = jnp.zeros((1, LANES), I32)
    for b in range(n_batch):
        expert = jnp.where(routes == b, gm_ref[b], expert)
    live = lane < TOK_DEV
    hot = jnp.where((jnp.broadcast_to(expert, (8, LANES)) == sub) & live, 1, 0)
    count = hot
    step = 1
    while step < LANES:
        count = count + jnp.where(lane >= step, pltpu.roll(count, step, 1), 0)
        step *= 2
    totals = [jnp.sum(hot[e : e + 1, :], axis=1, keepdims=True) for e in range(EXPERTS)]
    starts = [jnp.zeros((1, 1), I32)]
    for e in range(EXPERTS):
        starts.append(starts[-1] + (totals[e] + 15) // 16 * 16)
    pos = jnp.zeros((1, LANES), I32)
    for e in range(EXPERTS):
        pos = pos + jnp.where(hot[e : e + 1, :] > 0, count[e : e + 1, :] - 1 + starts[e], 0)
    pos = jnp.where(live[0:1, :], pos, -1)
    pos_ref[...] = pos
    wide = jnp.broadcast_to(pos.astype(F32), (128, LANES))
    col_ref[...] = jnp.transpose(wide).astype(I32)
    slot = lax.broadcasted_iota(I32, (1, 128), 1)
    offs = jnp.zeros((1, 128), I32)
    for e in range(EXPERTS + 1):
        offs = jnp.where(slot == e, starts[e], offs)
    offs_ref[...] = offs


SORT_TILES = (336, 336, 336, 336, 272)


def window(pair):
    first = pair * SEQ_LEN
    start = first // 16 * 16
    return start, first - start


def head_cols(hp, part):
    return pl.ds(pl.multiple_of(part * D + hp * 128, 128), 128)


def attend_pair(pair, length, qkv_ref, ctx_ref, lse_ref, stat):
    start, skip = window(pair)
    start = pl.multiple_of(start, 16)
    key = lax.broadcasted_iota(I32, (1, WIN), 1)
    seen = (key >= skip) & (key < skip + PATCHES + length)
    bias = jnp.where(seen, 0.0, -1e30)
    row = lax.broadcasted_iota(I32, (WIN, 1), 0)
    mine = (row >= skip) & (row < skip + SEQ_LEN)
    lane = lax.broadcasted_iota(I32, (WIN, 128), 1)
    stat[...] = jnp.zeros_like(stat)
    @pl.loop(0, HEADS // 2)
    def _(hp):
        q, k, v = [qkv_ref[pl.ds(start, WIN), head_cols(hp, part)] for part in range(3)]
        cols = head_cols(hp, 0)
        q = q * jnp.asarray(HEAD_DIM**-0.5, BF16)
        pieces = []
        for half in range(2):
            inside = (lane < 64) if half == 0 else (lane >= 64)
            qh = jnp.where(inside, q, jnp.zeros_like(q))
            scores = dot(qh, k, CONTRACT_LANES) + bias
            peak = jnp.max(scores, axis=1, keepdims=True)
            weight = jnp.exp(scores - peak).astype(BF16)
            vh = jnp.where(inside, v, jnp.ones_like(v))
            mixed = dot(weight, vh)
            total = pltpu.roll(mixed, 64, 1)
            pieces.append(mixed / total)
            one = total[:, 0:1] if half == 0 else mixed[:, 0:1]
            head = hp * 2 + half
            stat[0:WIN, :] = jnp.where(lane == head, peak + jnp.log(one), stat[0:WIN, :])
        ctx = jnp.where(lane < 64, pieces[0], pieces[1]).astype(BF16)
        old = ctx_ref[pl.ds(start, WIN), cols]
        ctx_ref[pl.ds(start, WIN), cols] = jnp.where(mine, ctx, old)
    lse_ref[pair] = jnp.transpose(stat[...])[0:16, :]


MESH = pl.DeviceIdType.MESH
HALF = 384
FF_DEV = 768
HOPS = [(way, hop) for hop in (1, 2, 3) for way in (1, -1)]


def front_kernel(
    small,
    n_batch,
    len_ref,
    group_ref,
    routes_ref,
    tok_ref,
    cot_ref,
    gain_one_ref,
    w_qkv_ref,
    w_proj_ref,
    gain_two_ref,
    w_in_ref,
    w_back_ref,
    qkv_hbm,
    ctx_hbm,
    lse_hbm,
    mid_hbm,
    g_hbm,
    x_hbm,
    wi_all,
    wb_all,
    offs_all,
    col_ref,
    qkv,
    ctx,
    lse,
    mid,
    g_sorted,
    x_sorted,
    held,
    stat,
    pos_ref,
    offs,
    wi_part,
    wb_part,
    local_sems,
    send_sems,
    recv_sems,
    hop_send,
    hop_recv,
    pass_send,
    pass_recv,
):
    batch, ffn = lax.axis_index("batch"), lax.axis_index("ffn")
    z, y = batch // 2, batch % 2
    near, far, cater = (batch, ffn ^ 1), (batch, ffn ^ 2), (batch, ffn ^ 3)
    across = (batch ^ 1, ffn)

    barrier = pltpu.get_barrier_semaphore()
    for device in [near, far, cater] + ([across] if small else []):
        pl.semaphore_signal(barrier, inc=1, device_id=device, device_id_type=MESH)
    if small:
        for way in (1, -1):

            @pl.when((z + way >= 0) & (z + way <= 3))
            def _(way=way):
                pl.semaphore_signal(
                    barrier, inc=1, device_id=(batch + 2 * way, ffn), device_id_type=MESH
                )

        inner = jnp.where((z == 0) | (z == 3), 1, 2)
        pl.semaphore_wait(barrier, 4 + inner)
    else:
        pl.semaphore_wait(barrier, 3)

    local_count = [0]
    waiting = []

    def local(src, dst):
        number = local_count[0]
        local_count[0] += 1
        copy = pltpu.make_async_copy(src, dst, local_sems.at[number])
        copy.start()
        waiting.append(copy)

    used = [0]

    def send(src, dst, device):
        number = used[0]
        used[0] += 1
        copy = pltpu.make_async_remote_copy(
            src_ref=src,
            dst_ref=dst,
            send_sem=send_sems.at[number],
            recv_sem=recv_sems.at[number],
            device_id=device,
            device_id_type=MESH,
        )
        copy.start()
        return copy

    part, whole = (wi_part, wb_part), (wi_all, wb_all)

    def valid(origin):
        return (origin >= 0) & (origin <= 3)

    def hop_copy(a, way, hop, origin, device):
        slot = whole[a].at[origin * 2 + y]
        number = HOPS.index((way, hop))
        return pltpu.make_async_remote_copy(
            src_ref=part[a] if hop == 1 else slot,
            dst_ref=slot,
            send_sem=hop_send.at[a, number],
            recv_sem=hop_recv.at[a, number],
            device_id=device,
            device_id_type=MESH,
        )

    def hop_go(a, hop, finish=False):
        for way in (1, -1):
            origin = z - way * (hop - 1)

            @pl.when(valid(origin) & valid(z + way))
            def _(way=way, origin=origin):
                copy = hop_copy(a, way, hop, origin, (batch + 2 * way, ffn))
                if finish:
                    copy.wait_send()
                else:
                    copy.start()

    def pass_copy(a, way, hop, origin, column):
        slot = whole[a].at[origin * 2 + column]
        number = HOPS.index((way, hop))
        return pltpu.make_async_remote_copy(
            src_ref=slot,
            dst_ref=slot,
            send_sem=pass_send.at[a, number],
            recv_sem=pass_recv.at[a, number],
            device_id=across,
            device_id_type=MESH,
        )

    def hop_came(a, hop):
        for way in (1, -1):
            origin = z - way * hop

            @pl.when(valid(origin))
            def _(way=way, origin=origin):
                hop_copy(a, way, hop, origin, (batch, ffn)).wait_recv()

        if hop < 3:
            hop_go(a, hop + 1)
        for way in (1, -1):
            origin = z - way * hop

            @pl.when(valid(origin))
            def _(way=way, origin=origin):
                pass_copy(a, way, hop, origin, y).start()

    own_over = []
    if small:
        rank = jnp.int32(0)
        for b in range(n_batch):
            same = (group_ref[b] == group_ref[batch]) & (b < batch)
            rank = rank + jnp.where(same, 1, 0)
        wi_part[...] = jnp.where(rank == 0, w_in_ref[0, :, 0:HALF], w_in_ref[0, :, HALF:FF_DEV])
        wb_part[...] = jnp.where(rank == 0, w_back_ref[0, 0:HALF, :], w_back_ref[0, HALF:FF_DEV, :])
        for a in range(2):
            hop_go(a, 1)
            own_over.append(send(part[a], whole[a].at[batch], across))
            local(part[a], whole[a].at[batch])

    exchanged = []
    route_rows(n_batch, group_ref, routes_ref, pos_ref, col_ref, offs)
    for slot, device in ((1, near), (2, far), (3, cater)):
        exchanged.append(send(offs, offs_all.at[pl.ds(slot, 1), :], device))
    local(offs, offs_all.at[pl.ds(0, 1), :])

    def sort_and_send(rows_ref, out_ref, out_hbm):
        pos = pos_ref[0:1, 0:ROWS]
        top = 0
        sent = []
        for size in SORT_TILES:
            want = top + lax.broadcasted_iota(I32, (size, ROWS), 0)
            hot = jnp.where(pos == want, 1.0, 0.0).astype(BF16)
            rows = pl.ds(top, size)
            out_ref[rows, :] = dot(hot, rows_ref[...]).astype(BF16)
            sent.append(send(out_ref.at[rows], out_hbm.at[2, rows], far))
            exchanged.append(send(out_ref.at[rows], out_hbm.at[1, rows], near))
            local(out_ref.at[rows], out_hbm.at[0, rows])
            top += size
        return sent

    def hand_on(sent, out_hbm):
        top = 0
        for copy, size in zip(sent, SORT_TILES):
            rows = pl.ds(top, size)
            copy.wait()
            exchanged.append(send(out_hbm.at[2, rows], out_hbm.at[3, rows], near))
            top += size

    held[1552:ROWS, :] = jnp.zeros((ROWS - 1552, D), BF16)
    held[0:TOK_DEV, :] = cot_ref[...]
    g_sent = sort_and_send(held, g_sorted, g_hbm)

    for i in range(3):
        top = min(TILE * (i + 1), TOK_DEV)
        rows = slice(TILE * i, top)
        normal, _ = norm_parts(tok_ref[rows, :].astype(F32))
        normed = (normal * gain_one_ref[...].reshape(1, D)).astype(BF16)
        qkv[rows, :] = dot(normed, w_qkv_ref[...]).astype(BF16)
    tail = slice(TOK_DEV, ROWS)
    qkv[tail, :] = jnp.zeros((ROWS - TOK_DEV, 3 * D), BF16)
    ctx[1552:ROWS, :] = jnp.zeros((ROWS - 1552, D), BF16)
    local(qkv, qkv_hbm)
    if small:
        hop_came(0, 1)

    @pl.loop(0, SEQ_DEV)
    def _(pair):
        attend_pair(pair, len_ref[pair], qkv, ctx, lse, stat)
        if small:

            @pl.when(pair == 1)
            def _():
                hop_came(1, 1)

            @pl.when(pair == 4)
            def _():
                hop_came(0, 2)

    local(ctx, ctx_hbm)
    local(lse, lse_hbm)
    for i in range(3):
        top = min(TILE * (i + 1), TOK_DEV)
        rows = slice(TILE * i, top)
        middle = tok_ref[rows, :].astype(F32) + dot(ctx[rows, :], w_proj_ref[...])
        mid[rows, :] = middle
        normal, _ = norm_parts(middle)
        held[rows, :] = (normal * gain_two_ref[...].reshape(1, D)).astype(BF16)
    local(mid, mid_hbm)
    if small:
        hop_came(1, 2)
    x_sent = sort_and_send(held, x_sorted, x_hbm)
    hand_on(g_sent, g_hbm)
    if small:
        hop_came(0, 3)
        hop_came(1, 3)
    hand_on(x_sent, x_hbm)
    for copy in exchanged + own_over:
        copy.wait()
    if small:
        for a in range(2):
            for hop in (1, 2, 3):
                hop_go(a, hop, finish=True)
            for way, hop in HOPS:
                origin = z - way * hop

                @pl.when(valid(origin))
                def _(a=a, way=way, hop=hop, origin=origin):
                    pass_copy(a, way, hop, origin, y).wait_send()
                    pass_copy(a, way, hop, origin, 1 - y).wait_recv()

    for copy in waiting:
        copy.wait()


def front(small, lengths, group_map, routes, tokens, *arrays):
    vmem = pl.BlockSpec(memory_space=pltpu.VMEM)
    any_space = pl.BlockSpec(memory_space=pl.ANY)
    tiles = len(SORT_TILES)
    copies = 6 * tiles + 2 + 3
    dma = pltpu.SemaphoreType.DMA
    return pl.pallas_call(
        functools.partial(front_kernel, small, group_map.shape[0]),
        out_shape=(
            jax.ShapeDtypeStruct((ROWS, 3 * D), BF16),
            jax.ShapeDtypeStruct((ROWS, D), BF16),
            jax.ShapeDtypeStruct((SEQ_DEV, 16, 384), F32),
            jax.ShapeDtypeStruct((TOK_DEV, D), F32),
            jax.ShapeDtypeStruct((4, SORTED, D), BF16),
            jax.ShapeDtypeStruct((4, SORTED, D), BF16),
            jax.ShapeDtypeStruct((8, D, HALF), BF16),
            jax.ShapeDtypeStruct((8, HALF, D), BF16),
            jax.ShapeDtypeStruct((4, 128), I32),
            jax.ShapeDtypeStruct((LANES, 128), I32),
        ),
        in_specs=[pl.BlockSpec(memory_space=pltpu.SMEM)] * 2 + [vmem] * (2 + len(arrays)),
        out_specs=(any_space,) * 8 + (vmem,) * 2,
        scratch_shapes=[
            pltpu.VMEM((ROWS, 3 * D), BF16),
            pltpu.VMEM((ROWS, D), BF16),
            pltpu.VMEM((SEQ_DEV, 16, 384), F32),
            pltpu.VMEM((TOK_DEV, D), F32),
            pltpu.VMEM((SORTED, D), BF16),
            pltpu.VMEM((SORTED, D), BF16),
            pltpu.VMEM((ROWS, D), BF16),
            pltpu.VMEM((384, 128), F32),
            pltpu.VMEM((1, LANES), I32),
            pltpu.VMEM((1, 128), I32),
            pltpu.VMEM((D, HALF), BF16),
            pltpu.VMEM((HALF, D), BF16),
            dma((2 * tiles + 7,)),
            dma((copies,)),
            dma((copies,)),
            dma((2, 6)),
            dma((2, 6)),
            dma((2, 6)),
            dma((2, 6)),
        ],
        compiler_params=params(collective_id=1, has_side_effects=True),
        name="front",
    )(lengths, group_map, routes, tokens, *arrays)


def gelu_both(u):
    below = 0.5 * (1.0 + lax.erf(u * (1.0 / math.sqrt(2.0))))
    density = jnp.exp(-0.5 * u * u) * (1.0 / math.sqrt(2.0 * math.pi))
    return u * below, below + u * density


MERGED = 2 * SORTED + 256
HEAD = 800
CHUNK = D // 8


def expert_kernel(sources, first, count, rows, carried, joined, cut, n_batch, offs_ref, group_ref, *refs):
    refs = list(refs)

    def take(count):
        head = refs[:count]
        del refs[:count]
        return head

    xs, gs = take(2), take(2)
    wi_hbm, wb_hbm = take(2)
    before = take(2) if carried else None
    earlier = take(4) if joined else None
    outs, gxs = take(2), take(2)
    dwi_ref, dwb_ref = take(2)
    xm, gm, wi, wb, acc_i, acc_b, hosts_ref, sems, join_sems = refs
    step = pl.program_id(0)
    expert = first + step
    slot = step % 2

    def join_copies():
        for number, (source, target) in enumerate(zip(earlier, outs + gxs)):
            yield pltpu.make_async_copy(source, target.at[0:HEAD, :], join_sems.at[number])

    def weight_copies(e, buffer, start):
        for p in range(2):
            host = hosts_ref[e * 2 + p]
            part = pl.ds(p * HALF, HALF)
            for number, source, target in (
                (0, wi_hbm.at[host], wi.at[buffer, :, part]),
                (1, wb_hbm.at[host], wb.at[buffer, part, :]),
            ):
                copy = pltpu.make_async_copy(source, target, sems.at[buffer, p, number])
                if start:
                    copy.start()
                else:
                    copy.wait()

    @pl.when(step == 0)
    def _():
        for e in range(EXPERTS):
            first_host, second_host = jnp.int32(n_batch), jnp.int32(n_batch)
            for b in reversed(range(n_batch)):
                hosting = group_ref[b] == e
                second_host = jnp.where(hosting, first_host, second_host)
                first_host = jnp.where(hosting, b, first_host)
            hosts_ref[2 * e] = first_host
            hosts_ref[2 * e + 1] = second_host
        weight_copies(first, 0, True)
        if joined:
            for copy in join_copies():
                copy.start()

    @pl.when(step + 1 < count)
    def _():
        weight_copies(expert + 1, 1 - slot, True)

    def blocks(count, act):
        @pl.loop(0, count)
        def _(i):
            act(pl.multiple_of(i * 16, 16))

    @pl.when((step == 0) & (rows == SORTED))
    def _():
        for s in range(2):
            live = pl.multiple_of(offs_ref[sources[s], EXPERTS], 16)

            def clear(at, s=s, live=live):
                spot = pl.ds(pl.multiple_of(live + at, 16), 16)
                outs[s][spot, :] = jnp.zeros((16, D), BF16)
                gxs[s][spot, :] = jnp.zeros((16, D), BF16)

            blocks((SORTED - live) // 16, clear)

    if carried:
        acc_i[...] = before[0][0].astype(F32)
        acc_b[...] = before[1][0].astype(F32)
    else:
        acc_i[...] = jnp.zeros_like(acc_i)
        acc_b[...] = jnp.zeros_like(acc_b)

    places = []
    total = jnp.int32(0)
    for s in range(2):
        begin = pl.multiple_of(offs_ref[sources[s], expert], 16)
        size = offs_ref[sources[s], expert + 1] - begin
        places.append((begin, total, size // 16))

        def gather(at, s=s, begin=begin, total=total):
            here = pl.ds(pl.multiple_of(begin + at, 16), 16)
            there = pl.ds(pl.multiple_of(total + at, 16), 16)
            xm[there, :] = xs[s][0, here, :]
            gm[there, :] = gs[s][0, here, :]

        blocks(size // 16, gather)
        total = total + size
    span = pl.multiple_of(total, 16)

    def blank(at):
        there = pl.ds(pl.multiple_of(span + at, 16), 16)
        xm[there, :] = jnp.zeros((16, D), BF16)
        gm[there, :] = jnp.zeros((16, D), BF16)

    blocks((256 - span % 256) // 16, blank)
    weight_copies(expert, slot, False)
    w_in, w_back = wi.at[slot], wb.at[slot]

    @pl.loop(0, (span + 255) // 256)
    def _(i):
        spot = pl.ds(pl.multiple_of(i * 256, 256), 256)
        x, g = xm[spot, :], gm[spot, :]
        inner = dot(x, w_in[...])
        hidden, slope = gelu_both(inner)
        hidden = hidden.astype(BF16)
        grad_hidden = dot(g, w_back[...], CONTRACT_LANES).astype(BF16)
        grad_inner = (grad_hidden.astype(F32) * slope).astype(BF16)
        xm[spot, :] = dot(hidden, w_back[...]).astype(BF16)
        gm[spot, :] = dot(grad_inner, w_in[...], CONTRACT_LANES).astype(BF16)
        acc_b[...] += dot(hidden, g, CONTRACT_ROWS)
        acc_i[...] += dot(x, grad_inner, CONTRACT_ROWS)

    if cut:
        y = lax.axis_index("batch") % 2
        for i, acc in enumerate((acc_i, acc_b)):
            for z in range(4):
                for ref, column in ((dwi_ref, 1 - y), (dwb_ref, y)):
                    part = pl.ds(pl.multiple_of((z * 2 + column) * CHUNK, 16), CHUNK)
                    ref[i, z] = acc[part, :].astype(BF16)
    else:
        dwi_ref[0] = acc_i[...].astype(BF16)
        dwb_ref[0] = acc_b[...].astype(BF16)
    if joined:

        @pl.when(step == 0)
        def _():
            for copy in join_copies():
                copy.wait()

    for s in range(2):
        begin, base, blocks_of = places[s]

        def hand_back(at, s=s, begin=begin, base=base):
            here = pl.ds(pl.multiple_of(begin + at, 16), 16)
            there = pl.ds(pl.multiple_of(base + at, 16), 16)
            outs[s][here, :] = xm[there, :]
            gxs[s][here, :] = gm[there, :]

        blocks(blocks_of, hand_back)


def experts(
    sources, offs, group_map, x, g, wi, wb, before=None, earlier=None, first=0, count=EXPERTS, cut=False
):
    rows = HEAD if cut else SORTED
    whole = once((rows, D))
    any_space = pl.BlockSpec(memory_space=pl.ANY)
    carried, joined = before is not None, earlier is not None
    out = jax.ShapeDtypeStruct((rows, D), BF16)

    def source(i):
        return pl.BlockSpec((1, rows, D), lambda e, *_: (i, 0, 0), pipeline_mode=pl.Buffered(1))

    carry = pl.BlockSpec((1, D, FF_DEV), lambda e, *_: (first + e, 0, 0))
    if cut:
        weight = once((2, 4, CHUNK, D))
        grad = jax.ShapeDtypeStruct((2, 4, CHUNK, D), BF16)
    else:
        weight = pl.BlockSpec((1, D, FF_DEV), lambda e, *_: (e, 0, 0))
        grad = jax.ShapeDtypeStruct((count, D, FF_DEV), BF16)
    picked = [source(i) for i in sources]
    kernel = functools.partial(
        expert_kernel, sources, first, count, rows, carried, joined, cut, group_map.shape[0]
    )
    return pl.pallas_call(
        kernel,
        grid_spec=pltpu.PrefetchScalarGridSpec(
            num_scalar_prefetch=2,
            grid=(count,),
            in_specs=picked
            + picked
            + [any_space] * 2
            + [carry] * (2 * carried)
            + [any_space] * (4 * joined),
            out_specs=[whole] * 4 + [weight] * 2,
            scratch_shapes=[
                pltpu.VMEM((MERGED, D), BF16),
                pltpu.VMEM((MERGED, D), BF16),
                pltpu.VMEM((2, D, FF_DEV), BF16),
                pltpu.VMEM((2, FF_DEV, D), BF16),
                pltpu.VMEM((D, FF_DEV), F32),
                pltpu.VMEM((FF_DEV, D), F32),
                pltpu.SMEM((2 * EXPERTS,), I32),
                pltpu.SemaphoreType.DMA((2, 2, 2)),
                pltpu.SemaphoreType.DMA((4,)),
            ],
        ),
        out_shape=(out,) * 4 + (grad,) * 2,
        compiler_params=params(),
        cost_estimate=cost(8 * count * SORTED * D * FF_DEV, 16 * SORTED * D),
        name="experts",
    )(offs, group_map, x, x, g, g, wi, wb, *(before or ()), *(earlier or ()))


def swap(rows, bit):
    pairs = [(f, f ^ bit) for f in range(4)]
    return lax.ppermute(rows, "ffn", pairs)


def tie(value, *others):
    return lax.optimization_barrier((value, *others))[0]


class Wire:
    def __init__(self, send_sems, recv_sems):
        self.send_sems, self.recv_sems, self.used = send_sems, recv_sems, 0

    def send(self, src, dst, device):
        number = self.used
        self.used += 1
        copy = pltpu.make_async_remote_copy(
            src_ref=src,
            dst_ref=dst,
            send_sem=self.send_sems.at[number],
            recv_sem=self.recv_sems.at[number],
            device_id=device,
            device_id_type=MESH,
        )
        copy.start()
        return copy


class Mover:
    def __init__(self, sems):
        self.sems, self.used = sems, 0

    def go(self, src, dst):
        number = self.used
        self.used += 1
        copy = pltpu.make_async_copy(src, dst, self.sems.at[number])
        copy.start()
        return copy


def greet(peers):
    barrier = pltpu.get_barrier_semaphore()
    for device in peers:
        pl.semaphore_signal(barrier, inc=1, device_id=device, device_id_type=MESH)
    pl.semaphore_wait(barrier, len(peers))


def wait_all(copies):
    for copy in copies:
        copy.wait()


def token_tiles():
    for i in range(3):
        yield slice(TILE * i, min(TILE * (i + 1), TOK_DEV))


def unsort(pos_col, src):
    want = lax.broadcasted_iota(I32, (pos_col.shape[0], SORTED), 1)
    hot = jnp.where(pos_col == want, 1.0, 0.0).astype(BF16)
    return dot(hot, src)


def attend_back_pair(pair, length, qkv_ref, gctx_ref, lse_ref, out_ref):
    start, skip = window(pair)
    start = pl.multiple_of(start, 16)
    row = lax.broadcasted_iota(I32, (WIN, 1), 0)
    mine = (row >= skip) & (row < skip + SEQ_LEN)
    bias = jnp.where((row >= skip) & (row < skip + PATCHES + length), 0.0, -1e30)
    lane = lax.broadcasted_iota(I32, (WIN, 128), 1)
    scale = jnp.asarray(HEAD_DIM**-0.5, BF16)
    @pl.loop(0, HEADS // 2)
    def _(hp):
        spots = [head_cols(hp, part) for part in range(3)]
        q, k, v = [qkv_ref[pl.ds(start, WIN), spot] for spot in spots]
        none = jnp.zeros_like(q)
        q = jnp.where(mine, q * scale, none)
        ks = k * scale
        go = jnp.where(mine, gctx_ref[pl.ds(start, WIN), spots[0]], none)
        low = lane < 64
        both_q = jnp.concatenate([jnp.where(low, q, none), jnp.where(low, none, q)], axis=0)
        both_go = jnp.concatenate([jnp.where(low, go, none), jnp.where(low, none, go)], axis=0)
        log_total = jnp.concatenate(
            [lse_ref[pair, pl.ds(hp * 2 + half, 1), 0:WIN] for half in range(2)], axis=1
        )
        probs = jnp.exp(dot(k, both_q, CONTRACT_LANES) + bias - log_total)
        grad_probs = dot(v, both_go, CONTRACT_LANES)
        delta = jnp.sum(probs * grad_probs, axis=0, keepdims=True)
        grad_scores = (probs * (grad_probs - delta)).astype(BF16)
        grad_v = dot(probs.astype(BF16), both_go)
        grad_k = dot(grad_scores, both_q)
        turned = dot(grad_scores, ks, CONTRACT_ROWS)
        grad_q = jnp.where(low, turned[0:WIN], turned[WIN : 2 * WIN])
        for spot, new in zip(spots, (grad_q, grad_k, grad_v)):
            old = out_ref[pl.ds(start, WIN), spot]
            out_ref[pl.ds(start, WIN), spot] = jnp.where(mine, new.astype(BF16), old)


TURNS = (2, 3, 1, 0)


def rear_kernel(
    small,
    len_ref,
    pos_ref,
    gain_one_ref,
    gain_two_ref,
    w_ref,
    lse_ref,
    gx0_hbm,
    gx1_hbm,
    gx2_hbm,
    mid_hbm,
    cot_hbm,
    ctx_hbm,
    qkv_hbm,
    tok_hbm,
    out1_hbm,
    out2_hbm,
    out3_hbm,
    dwi_hbm,
    dwb_hbm,
    first_came,
    first_own,
    gm_hbm,
    gq_hbm,
    dwq_hbm,
    dwp_hbm,
    dg_ref,
    share_hbm,
    near_hbm,
    far_hbm,
    wide,
    mid,
    cot,
    ctx,
    gctx,
    qkv,
    half_a,
    half_b,
    own_rows,
    came_y,
    came_z,
    acc,
    dwp,
    local_sems,
    send_sems,
    recv_sems,
    z_send,
    z_recv,
):
    batch, ffn = lax.axis_index("batch"), lax.axis_index("ffn")
    z, y = batch // 2, batch % 2
    near, far, across = (batch, ffn ^ 1), (batch, ffn ^ 2), (batch ^ 1, ffn)
    along = {k: (batch ^ (2 * k), ffn) for k in (1, 2, 3)}
    greet([near, far] + ([across] + list(along.values()) if small else []))
    wire, mover = Wire(send_sems, recv_sems), Mover(local_sems)

    parts_near = wire.send(gx1_hbm, wide.at[:, D : 2 * D], near)
    near_sent = wire.send(out3_hbm, half_b, near)
    half_in = mover.go(out2_hbm, half_a)
    over_y = {}
    own_in = {}
    if small:
        for turn in TURNS:
            there = pl.ds(pl.multiple_of(((z ^ turn) * 2 + 1 - y) * CHUNK, 16), CHUNK)
            over_y[turn] = [
                wire.send(grad.at[:, there, :], came_y.at[turn, i, 1:EXPERTS], across)
                for i, grad in enumerate((dwi_hbm, dwb_hbm))
            ]
    first_in = {}
    if small:
        for turn in TURNS:
            first_in[turn] = [
                mover.go(first_came.at[:, z ^ turn], came_y.at[turn, :, 0]),
                mover.go(first_own.at[:, z ^ turn], own_rows.at[turn, :, 0]),
            ]
    parts_in = [
        mover.go(part, wide.at[:, i * D : i * D + D])
        for i, part in ((0, gx0_hbm), (2, gx2_hbm))
    ]
    rows_in = [mover.go(mid_hbm, mid), mover.go(cot_hbm, cot), mover.go(ctx_hbm, ctx)]
    qkv_in = mover.go(qkv_hbm, qkv)
    if small:
        for turn in TURNS:
            here = pl.ds(pl.multiple_of(((z ^ turn) * 2 + y) * CHUNK, 16), CHUNK)
            own_in[turn] = [
                mover.go(grad.at[:, here, :], own_rows.at[turn, i, 1:EXPERTS])
                for i, grad in enumerate((dwi_hbm, dwb_hbm))
            ]
    sent = [wire.send(out1_hbm, near_hbm, near)]
    stored = []

    def z_copy(turn, i):
        return pltpu.make_async_remote_copy(
            src_ref=came_y.at[turn, i, 1:EXPERTS],
            dst_ref=came_z.at[turn - 1, i, 1:EXPERTS],
            send_sem=z_send.at[turn - 1, i],
            recv_sem=z_recv.at[turn - 1, i],
            device_id=along[turn],
            device_id_type=MESH,
        )

    def take_turn(turn, i):
        if not small:
            return
        over_y[turn][i].wait()
        own_in[turn][i].wait()
        for e in range(1, EXPERTS):
            came_y[turn, i, e] = (
                came_y[turn, i, e].astype(F32) + own_rows[turn, i, e].astype(F32)
            ).astype(BF16)
        if turn:
            z_copy(turn, i).start()

    first_z = []
    if small:
        for turn in TURNS:
            wait_all(first_in[turn])
            for i in range(2):
                came_y[turn, i, 0] = (
                    came_y[turn, i, 0].astype(F32) + own_rows[turn, i, 0].astype(F32)
                ).astype(BF16)
        first_z = [
            wire.send(came_y.at[turn, :, 0], came_z.at[turn - 1, :, 0], along[1])
            for turn in (1, 3)
        ]
    wait_all(parts_in + rows_in + [parts_near])
    top = 0
    for size in SORT_TILES:
        rows = slice(top, top + size)
        wide[rows, 0:D] = (
            wide[rows, 0:D].astype(F32)
            + wide[rows, D : 2 * D].astype(F32)
            + wide[rows, 2 * D : 3 * D].astype(F32)
        ).astype(BF16)
        top += size
    half_in.wait()
    near_sent.wait()
    half_a[...] = (half_a[...].astype(F32) + half_b[...].astype(F32)).astype(BF16)
    sent.append(wire.send(half_a, far_hbm, far))

    gctx[1552:ROWS, :] = jnp.zeros((ROWS - 1552, D), BF16)
    grad_gain = jnp.zeros((1, D), F32)
    for i, rows in enumerate(token_tiles()):
        grad_normed = unsort(pos_ref[rows, 0:1], wide[:, 0:D])
        normal, inverse = norm_parts(mid[rows, :])
        grad_gain = grad_gain + jnp.sum(grad_normed * normal, axis=0, keepdims=True)
        part = norm_pull(grad_normed, gain_two_ref[...].reshape(1, D), normal, inverse)
        grad_middle = cot[rows, :].astype(F32) + part
        mid[rows, :] = grad_middle
        low = grad_middle.astype(BF16)
        product = dot(ctx[rows, :], low, CONTRACT_ROWS)
        if i == 0:
            acc[...] = product
        elif i == 1:
            acc[...] += product
        else:
            dwp[...] = (acc[...] + product).astype(BF16)
        gctx[rows, :] = dot(low, w_ref[...], CONTRACT_LANES).astype(BF16)
        if small and i == 0:
            wait_all(first_z)
            for part_of in range(2):
                for turn, slot in ((2, 2), (0, 0)):
                    came_y[turn, part_of, 0] = (
                        came_y[turn, part_of, 0].astype(F32) + came_z[slot, part_of, 0].astype(F32)
                    ).astype(BF16)
            first_z = [wire.send(came_y.at[2, :, 0], came_z.at[1, :, 0], along[2])]
        if i == 1:
            take_turn(2, 0)
            take_turn(2, 1)
    dg_ref[...] = grad_gain
    stored.append(mover.go(mid, gm_hbm))
    stored.append(mover.go(dwp, dwp_hbm))
    tok_in = mover.go(tok_hbm, cot)
    wide[1552:SORTED, :] = jnp.zeros((SORTED - 1552, 3 * D), BF16)
    qkv_in.wait()
    take_turn(3, 0)
    take_turn(3, 1)

    @pl.loop(0, SEQ_DEV)
    def _(pair):
        attend_back_pair(pair, len_ref[pair], qkv, gctx, lse_ref, wide)
        @pl.when(pair == 1)
        def _():
            take_turn(1, 0)
            take_turn(1, 1)

    stored.append(mover.go(wide.at[0:ROWS, :], gq_hbm))
    tok_in.wait()
    for rows in token_tiles():
        normal, _ = norm_parts(cot[rows, :].astype(F32))
        gctx[rows, :] = (normal * gain_one_ref[...].reshape(1, D)).astype(BF16)
    for i in range(3):
        part = slice(i * 256, i * 256 + 256)
        qkv[part, :] = dot(gctx[:, part], wide[0:ROWS, :], CONTRACT_ROWS).astype(BF16)
    stored.append(mover.go(qkv.at[0:D, :], dwq_hbm))
    if small:
        take_turn(0, 0)
        take_turn(0, 1)
        wait_all(first_z + [z_copy(turn, i) for turn in TURNS[:3] for i in range(2)])
        for i in range(2):
            for e in range(EXPERTS):
                total = came_y[0, i, e].astype(F32)
                for k in range(3) if e else (1,):
                    total = total + came_z[k, i, e].astype(F32)
                came_y[0, i, e] = total.astype(BF16)
        stored.append(mover.go(came_y.at[0], share_hbm))
    wait_all(sent + stored)


def rear(small, lengths, pos_col, gain_one, gain_two, w_proj, lse, *arrays):
    vmem = pl.BlockSpec(memory_space=pltpu.VMEM)
    any_space = pl.BlockSpec(memory_space=pl.ANY)
    dma = pltpu.SemaphoreType.DMA
    copies = 15
    return pl.pallas_call(
        functools.partial(rear_kernel, small),
        out_shape=(
            jax.ShapeDtypeStruct((TOK_DEV, D), F32),
            jax.ShapeDtypeStruct((ROWS, 3 * D), BF16),
            jax.ShapeDtypeStruct((D, 3 * D), BF16),
            jax.ShapeDtypeStruct((D, D), BF16),
            jax.ShapeDtypeStruct((1, D), F32),
            jax.ShapeDtypeStruct((2, EXPERTS, CHUNK, D), BF16),
            jax.ShapeDtypeStruct((SORTED, D), BF16),
            jax.ShapeDtypeStruct((SORTED, D), BF16),
        ),
        in_specs=[pl.BlockSpec(memory_space=pltpu.SMEM)] + [vmem] * 5 + [any_space] * len(arrays),
        out_specs=(any_space,) * 4 + (vmem,) + (any_space,) * 3,
        scratch_shapes=[
            pltpu.VMEM((SORTED, 3 * D), BF16),
            pltpu.VMEM((TOK_DEV, D), F32),
            pltpu.VMEM((TOK_DEV, D), BF16),
            pltpu.VMEM((ROWS, D), BF16),
            pltpu.VMEM((ROWS, D), BF16),
            pltpu.VMEM((ROWS, 3 * D), BF16),
            pltpu.VMEM((SORTED, D), BF16),
            pltpu.VMEM((SORTED, D), BF16),
            pltpu.VMEM((4, 2, EXPERTS, CHUNK, D), BF16),
            pltpu.VMEM((4, 2, EXPERTS, CHUNK, D), BF16),
            pltpu.VMEM((3, 2, EXPERTS, CHUNK, D), BF16),
            pltpu.VMEM((D, D), F32),
            pltpu.VMEM((D, D), BF16),
            dma((32,)),
            dma((copies,)),
            dma((copies,)),
            dma((3, 2)),
            dma((3, 2)),
        ],
        compiler_params=params(collective_id=2, has_side_effects=True),
        name="rear",
    )(lengths, pos_col, gain_one, gain_two, w_proj, lse, *arrays)


ORDERS = (("x", "y", "z"), ("y", "x", "z")) * 2
WIDTHS = (1024, 1024, 512, 512)
LEFTS = (0, 1024, 2048, 2560)
SETS = ((0, 1), (2, 3))
WIDE = 4 * D
GAIN_ROWS = 8


def last_kernel(
    small,
    group_ref,
    pos_ref,
    gain_ref,
    w_ref,
    dg_two_ref,
    tok_hbm,
    gq_hbm,
    gm_hbm,
    mid_hbm,
    out0_hbm,
    out1_hbm,
    out2_hbm,
    dwq_hbm,
    dwp_hbm,
    share_hbm,
    ig_hbm,
    bo_hbm,
    sum_ref,
    gains_ref,
    pieces_ref,
    tok,
    gq,
    gm,
    mid,
    outs,
    share,
    stage,
    near_rows,
    held,
    came_z,
    came_xy,
    gain_in,
    local_sems,
    send_sems,
    recv_sems,
):
    batch, ffn = lax.axis_index("batch"), lax.axis_index("ffn")
    z, y, x, c = batch // 2, batch % 2, ffn // 2, ffn % 2
    place = {"x": x, "y": y, "z": z}
    mover = Mover(local_sems)

    def peer(axis, k=1):
        if axis == "c":
            return (batch, ffn ^ 1)
        if axis == "x":
            return (batch, ffn ^ 2)
        if axis == "y":
            return (batch ^ 1, ffn)
        return (batch ^ (2 * k), ffn)

    flying = ([], [])
    top = [0] * 4
    left = list(LEFTS)
    rows, cols = [384] * 4, list(WIDTHS)
    base = pl.multiple_of(c * 384, 16)
    if small:
        greet([peer("c"), peer("x")] + [(batch ^ j, ffn) for j in range(1, 8)])
        wire = Wire(send_sems, recv_sems)
        share_in = mover.go(share_hbm, share)
        give = pl.ds(pl.multiple_of((1 - c) * 384, 16), 384)
        keep = pl.ds(base, 384)
        pieces = (
            ((dwq_hbm, 0, 2048, 0),),
            ((dwq_hbm, 2048, 256, 2048), (dwp_hbm, 0, D, 3 * D)),
        )
        to_core, kept = [[], []], [[], []]
        for which in range(2):
            for ref, start, size, at in pieces[which]:
                lanes, spot = pl.ds(start, size), pl.ds(at, size)
                to_core[which].append(
                    wire.send(ref.at[give, lanes], near_rows.at[:, spot], peer("c"))
                )
                kept[which].append(mover.go(ref.at[keep, lanes], held.at[:, spot]))
    loads = [mover.go(tok_hbm, tok), mover.go(gq_hbm, gq), mover.go(gm_hbm, gm)]
    later = [mover.go(mid_hbm, mid)] + [
        mover.go(part, outs.at[i]) for i, part in enumerate((out0_hbm, out1_hbm, out2_hbm))
    ]
    handed = []

    def hand_out(i, *turns):
        for j in turns:
            handed.append(
                wire.send(stage.at[j, i], pieces_ref.at[batch, i], (batch ^ j, ffn))
            )

    if small:
        share_in.wait()
        for j in range(8):
            expert = group_ref[batch ^ j]
            for i in range(2):
                stage[j, i] = share[i, expert]
        hand_out(0, 4, 6, 5, 2)
        pieces_ref[batch] = stage[0]

    def core_done(which):
        wait_all(to_core[which] + kept[which])
        for i in SETS[which]:
            lanes = slice(LEFTS[i], LEFTS[i] + WIDTHS[i])
            held[:, lanes] = (
                held[:, lanes].astype(F32) + near_rows[:, lanes].astype(F32)
            ).astype(BF16)

    def sum_go(which, step):
        for i in SETS[which]:
            axis = ORDERS[i][step]
            quarter = WIDTHS[i] // 4
            if axis == "z":
                live = pl.ds(top[i], rows[i])
                for k in (2, 3, 1):
                    there = pl.ds(pl.multiple_of(left[i] + (z ^ k) * quarter, 128), quarter)
                    flying[which].append(
                        wire.send(
                            held.at[live, there],
                            came_z.at[i, k - 1, 0 : rows[i], 0:quarter],
                            peer("z", k),
                        )
                    )
            else:
                half = rows[i] // 2
                there = pl.ds(pl.multiple_of(top[i] + (1 - place[axis]) * half, 16), half)
                flying[which].append(
                    wire.send(
                        held.at[there, pl.ds(left[i], cols[i])],
                        came_xy.at[i, 0 if axis == "x" else 1, 0:half, 0 : cols[i]],
                        peer(axis),
                    )
                )

    def sum_done(which, step):
        wait_all(flying[which])
        flying[which].clear()
        for i in SETS[which]:
            axis = ORDERS[i][step]
            if axis == "z":
                cols[i] = WIDTHS[i] // 4
                left[i] = pl.multiple_of(left[i] + z * cols[i], 128)
                terms = [came_z[i, k, 0 : rows[i], 0 : cols[i]] for k in range(3)]
            else:
                rows[i] = rows[i] // 2
                top[i] = pl.multiple_of(top[i] + place[axis] * rows[i], 16)
                terms = [came_xy[i, 0 if axis == "x" else 1, 0 : rows[i], 0 : cols[i]]]
            spot = (pl.ds(top[i], rows[i]), pl.ds(left[i], cols[i]))
            total = held[spot].astype(F32)
            for term in terms:
                total = total + term.astype(F32)
            held[spot] = total.astype(BF16)
            if step == 2:
                lines = pl.ds(pl.multiple_of(base + top[i], 16), rows[i])
                sum_ref[lines, spot[1]] = total.astype(BF16)

    def spread_go(which, step):
        for i in SETS[which]:
            axis = ORDERS[i][step]
            mine = sum_ref.at[
                pl.ds(pl.multiple_of(base + top[i], 16), rows[i]), pl.ds(left[i], cols[i])
            ]
            for k in (2, 3, 1) if axis == "z" else (1,):
                flying[which].append(wire.send(mine, mine, peer(axis, k)))

    def spread_done(which, step):
        wait_all(flying[which])
        flying[which].clear()
        for i in SETS[which]:
            axis = ORDERS[i][step]
            if axis == "z":
                left[i] = LEFTS[i]
                cols[i] = WIDTHS[i]
            else:
                top[i] = top[i] - place[axis] * rows[i]
                rows[i] = rows[i] * 2

    def core_go(which):
        size = 2 * WIDTHS[SETS[which][0]]
        mine = sum_ref.at[pl.ds(base, 384), pl.ds(LEFTS[SETS[which][0]], size)]
        flying[which].append(wire.send(mine, mine, peer("c")))

    def gains_go(axis, slot):
        for k in (1, 2, 3) if axis == "z" else (1,):
            flying[0].append(wire.send(gains_ref, gain_in.at[slot + k - 1], peer(axis, k)))

    def gains_done(axis, slot):
        total = gains_ref[...]
        for k in (0, 1, 2) if axis == "z" else (0,):
            total = total + gain_in[slot + k]
        gains_ref[...] = total

    tiles = list(token_tiles())
    grad_gain = jnp.zeros((1, D), F32)
    stored = []

    def first_back(part):
        normal, inverse = norm_parts(tok[part, :].astype(F32))
        grad_normed = dot(gq[part, :], w_ref[...], CONTRACT_LANES)
        gain_part = jnp.sum(grad_normed * normal, axis=0, keepdims=True)
        pulled = norm_pull(grad_normed, gain_ref[...].reshape(1, D), normal, inverse)
        gm[part, :] = gm[part, :] + pulled
        stored.append(mover.go(gm.at[part], ig_hbm.at[part]))
        return gain_part

    def finish(part):
        mid[part, :] = mid[part, :] + unsort(pos_ref[part, 0:1], outs[0])
        stored.append(mover.go(mid.at[part], bo_hbm.at[part]))

    def finish_sums():
        wait_all(later)
        at = 0
        for size in SORT_TILES:
            part = slice(at, at + size)
            outs[0, part] = (
                outs[0, part].astype(F32) + outs[1, part].astype(F32) + outs[2, part].astype(F32)
            ).astype(BF16)
            at += size

    if small:
        for which in range(2):
            core_done(which)
            sum_go(which, 0)
    wait_all(loads)
    grad_gain = grad_gain + first_back(tiles[0])
    grad_gain = grad_gain + first_back(tiles[1])
    if small:
        for which in range(2):
            sum_done(which, 0)
            sum_go(which, 1)
    grad_gain = grad_gain + first_back(tiles[2])
    gains_ref[0:1, :] = grad_gain
    gains_ref[1:2, :] = dg_two_ref[...]
    gains_ref[2:GAIN_ROWS, :] = jnp.zeros((GAIN_ROWS - 2, D), F32)
    if small:
        gains_go("c", 0)
        for which in range(2):
            sum_done(which, 1)
            if which == 0:
                gains_done("c", 0)
                gains_go("x", 1)
            sum_go(which, 2)
    finish_sums()
    if small:
        for which in range(2):
            sum_done(which, 2)
            if which == 0:
                gains_done("x", 1)
                gains_go("y", 2)
            spread_go(which, 2)
    finish(tiles[0])
    finish(tiles[1])
    if small:
        for which in range(2):
            spread_done(which, 2)
            if which == 0:
                gains_done("y", 2)
                gains_go("z", 3)
            spread_go(which, 1)
        hand_out(0, 7, 3, 1)
        hand_out(1, 4, 6, 5, 7, 2, 3, 1)
    finish(tiles[2])
    if small:
        for which in range(2):
            spread_done(which, 1)
            if which == 0:
                gains_done("z", 3)
            spread_go(which, 0)
        for which in range(2):
            spread_done(which, 0)
            core_go(which)
        wait_all(flying[0] + flying[1] + handed)
    wait_all(stored)


def last(small, group_map, pos_col, gain_one, w_qkv, dg_two, *arrays):
    vmem = pl.BlockSpec(memory_space=pltpu.VMEM)
    any_space = pl.BlockSpec(memory_space=pl.ANY)
    dma = pltpu.SemaphoreType.DMA
    copies = 3 + 14 + 20 + 20 + 6 + 2
    extra = dict(collective_id=3, has_side_effects=True) if small else {}
    return pl.pallas_call(
        functools.partial(last_kernel, small),
        out_shape=(
            jax.ShapeDtypeStruct((TOK_DEV, D), F32),
            jax.ShapeDtypeStruct((TOK_DEV, D), F32),
            jax.ShapeDtypeStruct((D, WIDE), BF16),
            jax.ShapeDtypeStruct((GAIN_ROWS, D), F32),
            jax.ShapeDtypeStruct((8, 2, CHUNK, D), BF16),
        ),
        in_specs=[pl.BlockSpec(memory_space=pltpu.SMEM)] + [vmem] * 4 + [any_space] * len(arrays),
        out_specs=(any_space,) * 2 + (vmem,) * 3,
        scratch_shapes=[
            pltpu.VMEM((TOK_DEV, D), BF16),
            pltpu.VMEM((ROWS, 3 * D), BF16),
            pltpu.VMEM((TOK_DEV, D), F32),
            pltpu.VMEM((TOK_DEV, D), F32),
            pltpu.VMEM((3, SORTED, D), BF16),
            pltpu.VMEM((2, EXPERTS, CHUNK, D), BF16),
            pltpu.VMEM((8, 2, CHUNK, D), BF16),
            pltpu.VMEM((384, WIDE), BF16),
            pltpu.VMEM((384, WIDE), BF16),
            pltpu.VMEM((4, 3, 96, 256), BF16),
            pltpu.VMEM((4, 2, 192, 1024), BF16),
            pltpu.VMEM((6, GAIN_ROWS, D), F32),
            dma((20,)),
            dma((copies,)),
            dma((copies,)),
        ],
        compiler_params=params(**extra),
        name="last",
    )(group_map, pos_col, gain_one, w_qkv, dg_two, *arrays)


def close_kernel(
    sum_ref, gains_ref, pieces_ref, ig_ref, bo_ref, *outs
):
    qkv_ref, proj_ref, one_ref, two_ref, wi_ref, wb_ref, ig_out, bo_out = outs
    qkv_ref[...] = sum_ref[:, 0 : 3 * D].astype(F32)
    proj_ref[...] = sum_ref[:, 3 * D : WIDE].astype(F32)
    one_ref[...] = gains_ref[0:1, :].reshape(D)
    two_ref[...] = gains_ref[1:2, :].reshape(D)
    wi_ref[0] = pieces_ref[0, 0].astype(F32)
    wb_ref[0] = pieces_ref[0, 1].astype(F32)
    ig_out[...] = ig_ref[...]
    bo_out[...] = bo_ref[...]


def close(summed, gains, pieces, input_grad, block_out):
    row = pl.BlockSpec((CHUNK, D), lambda i: (i, 0))
    tokens = pl.BlockSpec((200, D), lambda i: (i, 0))
    weight = pl.BlockSpec((1, CHUNK, D), lambda i: (0, i, 0))
    rows = jax.ShapeDtypeStruct((TOK_DEV, D), F32)
    return pl.pallas_call(
        close_kernel,
        grid=(8,),
        out_shape=(
            jax.ShapeDtypeStruct((D, 3 * D), F32),
            jax.ShapeDtypeStruct((D, D), F32),
            jax.ShapeDtypeStruct((D,), F32),
            jax.ShapeDtypeStruct((D,), F32),
            jax.ShapeDtypeStruct((1, D, D), F32),
            jax.ShapeDtypeStruct((1, D, D), F32),
            rows,
            rows,
        ),
        in_specs=[
            pl.BlockSpec((CHUNK, WIDE), lambda i: (i, 0)),
            full((GAIN_ROWS, D)),
            pl.BlockSpec((1, 2, CHUNK, D), lambda i: (i, 0, 0, 0)),
            tokens,
            tokens,
        ],
        out_specs=(
            pl.BlockSpec((CHUNK, 3 * D), lambda i: (i, 0)),
            row,
            full((D,)),
            full((D,)),
            weight,
            weight,
            tokens,
            tokens,
        ),
        compiler_params=params(),
        name="close",
    )(summed, gains, pieces, input_grad, block_out)


def body(
    tokens,
    text_lengths,
    routes,
    group_map,
    gain_one,
    w_qkv,
    w_proj,
    gain_two,
    w_in,
    w_back,
    cotangent,
):
    n_batch = lax.axis_size("batch")
    own = lax.axis_index("batch")
    small = n_batch == 8
    routes_row = jnp.pad(routes.reshape(1, TOK_DEV), ((0, 0), (0, LANES - TOK_DEV)))
    qkv, context, lse, middle, g, x, wi_all, wb_all, offs, pos_col = front(
        small,
        text_lengths,
        group_map,
        routes_row,
        tokens,
        cotangent,
        gain_one,
        w_qkv,
        w_proj,
        gain_two,
        w_in,
        w_back,
    )
    if not small:
        own_expert = group_map[own]
        order = jnp.arange(n_batch, dtype=I32)
        rank = jnp.sum(jnp.where((group_map == own_expert) & (order < own), 1, 0))
        part = jnp.minimum(rank, 1)
        wi_part = lax.dynamic_slice(w_in[0], (0, part * HALF), (D, HALF))
        wb_part = lax.dynamic_slice(w_back[0], (part * HALF, 0), (HALF, D))
        wi_all = lax.all_gather(wi_part, "batch", axis=0)
        wb_all = lax.all_gather(wb_part, "batch", axis=0)

    def run(pair, x, *rest, **more):
        return experts(pair, offs, group_map, x, g, wi_all, wb_all, *rest, **more)

    def add(a, b):
        return (a.astype(F32) + b.astype(F32)).astype(BF16)

    out2, out3, gx2, gx3, dwi, dwb = run((2, 3), x)
    gx_half = add(gx2, swap(gx3, 1))
    gx_far = swap(gx_half, 2)
    x = tie(x, gx_half)
    if small:
        *earlier, going, staying = run((0, 1), x, (dwi, dwb), count=1, cut=True)
        came = lax.ppermute(going, "batch", [(b, b ^ 1) for b in range(8)])
        out0, out1, gx0, gx1, dwi, dwb = run((0, 1), x, (dwi, dwb), earlier, first=1, count=2)
    else:
        out0, out1, gx0, gx1, dwi, dwb = run((0, 1), x, (dwi, dwb))
        came = staying = jnp.zeros((2, 4, CHUNK, D), BF16)
    grad_middle, grad_qkv, dw_qkv, dw_proj, dg_two, share, out_near, out_far = rear(
        small,
        text_lengths,
        pos_col,
        gain_one,
        gain_two,
        w_proj,
        lse,
        gx0,
        gx1,
        gx_far,
        middle,
        cotangent,
        context,
        qkv,
        tokens,
        out1,
        out2,
        out3,
        dwi,
        dwb,
        came,
        staying,
    )
    input_grad, block_out, summed, gains, pieces = last(
        small,
        group_map,
        pos_col,
        gain_one,
        w_qkv,
        dg_two,
        tokens,
        grad_qkv,
        grad_middle,
        middle,
        out0,
        out_near,
        out_far,
        dw_qkv,
        dw_proj,
        share,
    )
    if small:
        summed_qkv, summed_proj, gain_a, gain_b, grad_w_in, grad_w_back, input_grad, block_out = close(
            summed, gains, pieces, input_grad, block_out
        )
        gains = (gain_a, gain_b)
    else:

        def settle_any(grad):
            share = lax.psum_scatter(grad, "batch", scatter_dimension=1, tiled=True)
            whole = lax.all_gather(share, "batch", axis=1, tiled=True)
            return lax.dynamic_index_in_dim(whole, own_expert, 0, keepdims=True).astype(F32)

        grad_w_in = settle_any(dwi)
        grad_w_back = settle_any(dwb)
        summed_qkv, summed_proj = lax.psum((dw_qkv, dw_proj), ("batch", "ffn"))
        gains = lax.psum(gains, ("batch", "ffn"))
    return (
        block_out,
        input_grad,
        gains[0],
        summed_qkv.astype(F32),
        summed_proj.astype(F32),
        gains[1],
        grad_w_in,
        grad_w_back,
    )


def solution(mesh):
    placed = (
        P(("batch", "ffn"), None),
        P(("batch", "ffn")),
        P(("batch", "ffn"), None),
        P(),
        P(),
        P(),
        P(),
        P(),
        P("batch", None, "ffn"),
        P("batch", "ffn", None),
        P(("batch", "ffn"), None),
    )
    return jax.shard_map(
        body,
        mesh=mesh,
        in_specs=placed,
        out_specs=(
            P(("batch", "ffn"), None),
            P(("batch", "ffn"), None),
            P(),
            P(),
            P(),
            P(),
            P("batch", None, "ffn"),
            P("batch", "ffn", None),
        ),
        check_vma=False,
    )
```

```python
import functools
import math

import jax
import jax.numpy as jnp
from jax import lax
from jax.experimental import pallas as pl
from jax.experimental.pallas import tpu as pltpu
from jax.sharding import PartitionSpec as P

D = 768
HEADS = 12
HEAD_DIM = 64
EXPERTS = 3
PATCHES = 197
SEQ_DEV = 6
SEQ_LEN = 261
TOK_DEV = 1566
ROWS = 1584
SORTED = 1616
WIN = 288
TILE = 528
LANES = 1664
EPS = 1e-05
F32 = jnp.float32
BF16 = jnp.bfloat16
I32 = jnp.int32
CONTRACT_LANES = (((1,), (1,)), ((), ()))
CONTRACT_ROWS = (((0,), (0,)), ((), ()))


def params(**extra):
    return pltpu.CompilerParams(vmem_limit_bytes=60 << 20, **extra)


def cost(flops, moved):
    return pl.CostEstimate(flops=int(flops), bytes_accessed=int(moved), transcendentals=0)


def dot(a, b, dims=(((1,), (0,)), ((), ()))):
    return lax.dot_general(a, b, dims, preferred_element_type=F32)


def full(shape):
    zeros = (0,) * len(shape)
    return pl.BlockSpec(shape, lambda *_: zeros)


def once(shape):
    zeros = (0,) * len(shape)
    return pl.BlockSpec(shape, lambda *_: zeros, pipeline_mode=pl.Buffered(1))


def row_mask(start, rows, limit):
    return start + lax.broadcasted_iota(I32, (rows, 1), 0) < limit


def norm_parts(values):
    average = jnp.mean(values, axis=-1, keepdims=True)
    centred = values - average
    variance = jnp.mean(centred * centred, axis=-1, keepdims=True)
    inverse = lax.rsqrt(variance + EPS)
    return centred * inverse, inverse


def norm_pull(grad_normed, gain, normal, inverse):
    scaled = grad_normed * gain
    mean_grad = jnp.mean(scaled, axis=-1, keepdims=True)
    mean_proj = jnp.mean(scaled * normal, axis=-1, keepdims=True)
    return inverse * (scaled - mean_grad - normal * mean_proj)


def route_rows(n_batch, gm_ref, routes_ref, pos_ref, col_ref, offs_ref):
    routes = routes_ref[...]
    lane = lax.broadcasted_iota(I32, (8, LANES), 1)
    sub = lax.broadcasted_iota(I32, (8, LANES), 0)
    expert = jnp.zeros((1, LANES), I32)
    for b in range(n_batch):
        expert = jnp.where(routes == b, gm_ref[b], expert)
    live = lane < TOK_DEV
    hot = jnp.where((jnp.broadcast_to(expert, (8, LANES)) == sub) & live, 1, 0)
    count = hot
    step = 1
    while step < LANES:
        count = count + jnp.where(lane >= step, pltpu.roll(count, step, 1), 0)
        step *= 2
    totals = [jnp.sum(hot[e : e + 1, :], axis=1, keepdims=True) for e in range(EXPERTS)]
    starts = [jnp.zeros((1, 1), I32)]
    for e in range(EXPERTS):
        starts.append(starts[-1] + (totals[e] + 15) // 16 * 16)
    pos = jnp.zeros((1, LANES), I32)
    for e in range(EXPERTS):
        pos = pos + jnp.where(hot[e : e + 1, :] > 0, count[e : e + 1, :] - 1 + starts[e], 0)
    pos = jnp.where(live[0:1, :], pos, -1)
    pos_ref[...] = pos
    wide = jnp.broadcast_to(pos.astype(F32), (128, LANES))
    col_ref[...] = jnp.transpose(wide).astype(I32)
    slot = lax.broadcasted_iota(I32, (1, 128), 1)
    offs = jnp.zeros((1, 128), I32)
    for e in range(EXPERTS + 1):
        offs = jnp.where(slot == e, starts[e], offs)
    offs_ref[...] = offs


SORT_TILES = (336, 336, 336, 336, 272)


def window(pair):
    first = pair * SEQ_LEN
    start = first // 16 * 16
    return start, first - start


def head_cols(hp, part):
    return pl.ds(pl.multiple_of(part * D + hp * 128, 128), 128)


def attend_pair(pair, length, qkv_ref, ctx_ref, lse_ref, stat):
    start, skip = window(pair)
    start = pl.multiple_of(start, 16)
    key = lax.broadcasted_iota(I32, (1, WIN), 1)
    seen = (key >= skip) & (key < skip + PATCHES + length)
    bias = jnp.where(seen, 0.0, -1e30)
    row = lax.broadcasted_iota(I32, (WIN, 1), 0)
    mine = (row >= skip) & (row < skip + SEQ_LEN)
    lane = lax.broadcasted_iota(I32, (WIN, 128), 1)
    stat[...] = jnp.zeros_like(stat)
    @pl.loop(0, HEADS // 2)
    def _(hp):
        q, k, v = [qkv_ref[pl.ds(start, WIN), head_cols(hp, part)] for part in range(3)]
        cols = head_cols(hp, 0)
        q = q * jnp.asarray(HEAD_DIM**-0.5, BF16)
        pieces = []
        for half in range(2):
            inside = (lane < 64) if half == 0 else (lane >= 64)
            qh = jnp.where(inside, q, jnp.zeros_like(q))
            scores = dot(qh, k, CONTRACT_LANES) + bias
            peak = jnp.max(scores, axis=1, keepdims=True)
            weight = jnp.exp(scores - peak).astype(BF16)
            vh = jnp.where(inside, v, jnp.ones_like(v))
            mixed = dot(weight, vh)
            total = pltpu.roll(mixed, 64, 1)
            pieces.append(mixed / total)
            one = total[:, 0:1] if half == 0 else mixed[:, 0:1]
            head = hp * 2 + half
            stat[0:WIN, :] = jnp.where(lane == head, peak + jnp.log(one), stat[0:WIN, :])
        ctx = jnp.where(lane < 64, pieces[0], pieces[1]).astype(BF16)
        old = ctx_ref[pl.ds(start, WIN), cols]
        ctx_ref[pl.ds(start, WIN), cols] = jnp.where(mine, ctx, old)
    lse_ref[pair] = jnp.transpose(stat[...])[0:16, :]


MESH = pl.DeviceIdType.MESH
HALF = 384
FF_DEV = 768
HOPS = [(way, hop) for hop in (1, 2, 3) for way in (1, -1)]


def front_kernel(
    small,
    n_batch,
    len_ref,
    group_ref,
    routes_ref,
    tok_ref,
    cot_ref,
    gain_one_ref,
    w_qkv_hbm,
    w_proj_hbm,
    gain_two_ref,
    w_in_ref,
    w_back_ref,
    qkv_hbm,
    ctx_hbm,
    lse_hbm,
    mid_hbm,
    g_hbm,
    x_hbm,
    wi_all,
    wb_all,
    offs_all,
    col_ref,
    qkv,
    ctx,
    lse,
    mid,
    g_sorted,
    x_sorted,
    held,
    stat,
    pos_ref,
    offs,
    wi_part,
    wb_part,
    w_qkv_ref,
    w_proj_ref,
    weight_sems,
    local_sems,
    send_sems,
    recv_sems,
    hop_send,
    hop_recv,
    pass_send,
    pass_recv,
):
    batch, ffn = lax.axis_index("batch"), lax.axis_index("ffn")
    z, y = batch // 2, batch % 2
    near, far, cater = (batch, ffn ^ 1), (batch, ffn ^ 2), (batch, ffn ^ 3)
    across = (batch ^ 1, ffn)

    barrier = pltpu.get_barrier_semaphore()
    for device in [near, far, cater] + ([across] if small else []):
        pl.semaphore_signal(barrier, inc=1, device_id=device, device_id_type=MESH)
    if small:
        for way in (1, -1):

            @pl.when((z + way >= 0) & (z + way <= 3))
            def _(way=way):
                pl.semaphore_signal(
                    barrier, inc=1, device_id=(batch + 2 * way, ffn), device_id_type=MESH
                )

        inner = jnp.where((z == 0) | (z == 3), 1, 2)
        pl.semaphore_wait(barrier, 4 + inner)
    else:
        pl.semaphore_wait(barrier, 3)

    weights_in = [
        pltpu.make_async_copy(w_qkv_hbm, w_qkv_ref, weight_sems.at[0]),
        pltpu.make_async_copy(w_proj_hbm, w_proj_ref, weight_sems.at[1]),
    ]
    for copy in weights_in:
        copy.start()
    local_count = [0]
    waiting = []

    def local(src, dst):
        number = local_count[0]
        local_count[0] += 1
        copy = pltpu.make_async_copy(src, dst, local_sems.at[number])
        copy.start()
        waiting.append(copy)

    used = [0]

    def send(src, dst, device):
        number = used[0]
        used[0] += 1
        copy = pltpu.make_async_remote_copy(
            src_ref=src,
            dst_ref=dst,
            send_sem=send_sems.at[number],
            recv_sem=recv_sems.at[number],
            device_id=device,
            device_id_type=MESH,
        )
        copy.start()
        return copy

    part, whole = (wi_part, wb_part), (wi_all, wb_all)

    def valid(origin):
        return (origin >= 0) & (origin <= 3)

    def hop_copy(a, way, hop, origin, device):
        slot = whole[a].at[origin * 2 + y]
        number = HOPS.index((way, hop))
        return pltpu.make_async_remote_copy(
            src_ref=part[a] if hop == 1 else slot,
            dst_ref=slot,
            send_sem=hop_send.at[a, number],
            recv_sem=hop_recv.at[a, number],
            device_id=device,
            device_id_type=MESH,
        )

    def hop_go(a, hop, finish=False):
        for way in (1, -1):
            origin = z - way * (hop - 1)

            @pl.when(valid(origin) & valid(z + way))
            def _(way=way, origin=origin):
                copy = hop_copy(a, way, hop, origin, (batch + 2 * way, ffn))
                if finish:
                    copy.wait_send()
                else:
                    copy.start()

    def pass_copy(a, way, hop, origin, column):
        slot = whole[a].at[origin * 2 + column]
        number = HOPS.index((way, hop))
        return pltpu.make_async_remote_copy(
            src_ref=slot,
            dst_ref=slot,
            send_sem=pass_send.at[a, number],
            recv_sem=pass_recv.at[a, number],
            device_id=across,
            device_id_type=MESH,
        )

    def hop_came(a, hop):
        for way in (1, -1):
            origin = z - way * hop

            @pl.when(valid(origin))
            def _(way=way, origin=origin):
                hop_copy(a, way, hop, origin, (batch, ffn)).wait_recv()

        if hop < 3:
            hop_go(a, hop + 1)
        for way in (1, -1):
            origin = z - way * hop

            @pl.when(valid(origin))
            def _(way=way, origin=origin):
                pass_copy(a, way, hop, origin, y).start()

    own_over = []
    if small:
        rank = jnp.int32(0)
        for b in range(n_batch):
            same = (group_ref[b] == group_ref[batch]) & (b < batch)
            rank = rank + jnp.where(same, 1, 0)
        wi_part[...] = jnp.where(rank == 0, w_in_ref[0, :, 0:HALF], w_in_ref[0, :, HALF:FF_DEV])
        wb_part[...] = jnp.where(rank == 0, w_back_ref[0, 0:HALF, :], w_back_ref[0, HALF:FF_DEV, :])
        for a in range(2):
            hop_go(a, 1)
            own_over.append(send(part[a], whole[a].at[batch], across))
            local(part[a], whole[a].at[batch])

    exchanged = []
    route_rows(n_batch, group_ref, routes_ref, pos_ref, col_ref, offs)
    for slot, device in ((1, near), (2, far), (3, cater)):
        exchanged.append(send(offs, offs_all.at[pl.ds(slot, 1), :], device))
    local(offs, offs_all.at[pl.ds(0, 1), :])

    def sort_and_send(rows_ref, out_ref, out_hbm):
        pos = pos_ref[0:1, 0:ROWS]
        top = 0
        sent = []
        for size in SORT_TILES:
            want = top + lax.broadcasted_iota(I32, (size, ROWS), 0)
            hot = jnp.where(pos == want, 1.0, 0.0).astype(BF16)
            rows = pl.ds(top, size)
            out_ref[rows, :] = dot(hot, rows_ref[...]).astype(BF16)
            sent.append(send(out_ref.at[rows], out_hbm.at[2, rows], far))
            exchanged.append(send(out_ref.at[rows], out_hbm.at[1, rows], near))
            local(out_ref.at[rows], out_hbm.at[0, rows])
            top += size
        return sent

    def hand_on(sent, out_hbm):
        top = 0
        for copy, size in zip(sent, SORT_TILES):
            rows = pl.ds(top, size)
            copy.wait()
            exchanged.append(send(out_hbm.at[2, rows], out_hbm.at[3, rows], near))
            top += size

    held[1552:ROWS, :] = jnp.zeros((ROWS - 1552, D), BF16)
    held[0:TOK_DEV, :] = cot_ref[...]
    g_sent = sort_and_send(held, g_sorted, g_hbm)
    for copy in weights_in:
        copy.wait()

    for i in range(3):
        top = min(TILE * (i + 1), TOK_DEV)
        rows = slice(TILE * i, top)
        normal, _ = norm_parts(tok_ref[rows, :].astype(F32))
        normed = (normal * gain_one_ref[...].reshape(1, D)).astype(BF16)
        qkv[rows, :] = dot(normed, w_qkv_ref[...]).astype(BF16)
    tail = slice(TOK_DEV, ROWS)
    qkv[tail, :] = jnp.zeros((ROWS - TOK_DEV, 3 * D), BF16)
    ctx[1552:ROWS, :] = jnp.zeros((ROWS - 1552, D), BF16)
    local(qkv, qkv_hbm)
    if small:
        hop_came(0, 1)

    @pl.loop(0, SEQ_DEV)
    def _(pair):
        attend_pair(pair, len_ref[pair], qkv, ctx, lse, stat)
        if small:

            @pl.when(pair == 1)
            def _():
                hop_came(1, 1)

            @pl.when(pair == 4)
            def _():
                hop_came(0, 2)

    local(ctx, ctx_hbm)
    local(lse, lse_hbm)
    for i in range(3):
        top = min(TILE * (i + 1), TOK_DEV)
        rows = slice(TILE * i, top)
        middle = tok_ref[rows, :].astype(F32) + dot(ctx[rows, :], w_proj_ref[...])
        mid[rows, :] = middle
        normal, _ = norm_parts(middle)
        held[rows, :] = (normal * gain_two_ref[...].reshape(1, D)).astype(BF16)
    local(mid, mid_hbm)
    if small:
        hop_came(1, 2)
    x_sent = sort_and_send(held, x_sorted, x_hbm)
    hand_on(g_sent, g_hbm)
    if small:
        hop_came(0, 3)
        hop_came(1, 3)
    hand_on(x_sent, x_hbm)
    for copy in exchanged + own_over:
        copy.wait()
    if small:
        for a in range(2):
            for hop in (1, 2, 3):
                hop_go(a, hop, finish=True)
            for way, hop in HOPS:
                origin = z - way * hop

                @pl.when(valid(origin))
                def _(a=a, way=way, hop=hop, origin=origin):
                    pass_copy(a, way, hop, origin, y).wait_send()
                    pass_copy(a, way, hop, origin, 1 - y).wait_recv()

    for copy in waiting:
        copy.wait()


def front(small, lengths, group_map, routes, tokens, *arrays):
    vmem = pl.BlockSpec(memory_space=pltpu.VMEM)
    any_space = pl.BlockSpec(memory_space=pl.ANY)
    tiles = len(SORT_TILES)
    copies = 6 * tiles + 2 + 3
    dma = pltpu.SemaphoreType.DMA
    return pl.pallas_call(
        functools.partial(front_kernel, small, group_map.shape[0]),
        out_shape=(
            jax.ShapeDtypeStruct((ROWS, 3 * D), BF16),
            jax.ShapeDtypeStruct((ROWS, D), BF16),
            jax.ShapeDtypeStruct((SEQ_DEV, 16, 384), F32),
            jax.ShapeDtypeStruct((TOK_DEV, D), F32),
            jax.ShapeDtypeStruct((4, SORTED, D), BF16),
            jax.ShapeDtypeStruct((4, SORTED, D), BF16),
            jax.ShapeDtypeStruct((8, D, HALF), BF16),
            jax.ShapeDtypeStruct((8, HALF, D), BF16),
            jax.ShapeDtypeStruct((4, 128), I32),
            jax.ShapeDtypeStruct((LANES, 128), I32),
        ),
        in_specs=[pl.BlockSpec(memory_space=pltpu.SMEM)] * 2
        + [vmem] * 4
        + [any_space] * 2
        + [vmem] * 3,
        out_specs=(any_space,) * 8 + (vmem,) * 2,
        scratch_shapes=[
            pltpu.VMEM((ROWS, 3 * D), BF16),
            pltpu.VMEM((ROWS, D), BF16),
            pltpu.VMEM((SEQ_DEV, 16, 384), F32),
            pltpu.VMEM((TOK_DEV, D), F32),
            pltpu.VMEM((SORTED, D), BF16),
            pltpu.VMEM((SORTED, D), BF16),
            pltpu.VMEM((ROWS, D), BF16),
            pltpu.VMEM((384, 128), F32),
            pltpu.VMEM((1, LANES), I32),
            pltpu.VMEM((1, 128), I32),
            pltpu.VMEM((D, HALF), BF16),
            pltpu.VMEM((HALF, D), BF16),
            pltpu.VMEM((D, 3 * D), BF16),
            pltpu.VMEM((D, D), BF16),
            dma((2,)),
            dma((2 * tiles + 7,)),
            dma((copies,)),
            dma((copies,)),
            dma((2, 6)),
            dma((2, 6)),
            dma((2, 6)),
            dma((2, 6)),
        ],
        compiler_params=params(collective_id=1, has_side_effects=True),
        name="front",
    )(lengths, group_map, routes, tokens, *arrays)


def gelu_both(u):
    below = 0.5 * (1.0 + lax.erf(u * (1.0 / math.sqrt(2.0))))
    density = jnp.exp(-0.5 * u * u) * (1.0 / math.sqrt(2.0 * math.pi))
    return u * below, below + u * density


MERGED = 2 * SORTED + 256
HEAD = 800
CHUNK = D // 8


def expert_kernel(sources, first, count, rows, carried, joined, cut, n_batch, offs_ref, group_ref, *refs):
    refs = list(refs)

    def take(count):
        head = refs[:count]
        del refs[:count]
        return head

    xs, gs = take(2), take(2)
    wi_hbm, wb_hbm = take(2)
    before = take(2) if carried else None
    earlier = take(4) if joined else None
    outs, gxs = take(2), take(2)
    dwi_ref, dwb_ref = take(2)
    xm, gm, wi, wb, acc_i, acc_b, hosts_ref, sems, join_sems = refs
    step = pl.program_id(0)
    expert = first + step
    slot = step % 2

    def join_copies():
        for number, (source, target) in enumerate(zip(earlier, outs + gxs)):
            yield pltpu.make_async_copy(source, target.at[0:HEAD, :], join_sems.at[number])

    def weight_copies(e, buffer, start):
        for p in range(2):
            host = hosts_ref[e * 2 + p]
            part = pl.ds(p * HALF, HALF)
            for number, source, target in (
                (0, wi_hbm.at[host], wi.at[buffer, :, part]),
                (1, wb_hbm.at[host], wb.at[buffer, part, :]),
            ):
                copy = pltpu.make_async_copy(source, target, sems.at[buffer, p, number])
                if start:
                    copy.start()
                else:
                    copy.wait()

    @pl.when(step == 0)
    def _():
        for e in range(EXPERTS):
            first_host, second_host = jnp.int32(n_batch), jnp.int32(n_batch)
            for b in reversed(range(n_batch)):
                hosting = group_ref[b] == e
                second_host = jnp.where(hosting, first_host, second_host)
                first_host = jnp.where(hosting, b, first_host)
            hosts_ref[2 * e] = first_host
            hosts_ref[2 * e + 1] = second_host
        weight_copies(first, 0, True)
        if joined:
            for copy in join_copies():
                copy.start()

    @pl.when(step + 1 < count)
    def _():
        weight_copies(expert + 1, 1 - slot, True)

    def blocks(count, act):
        @pl.loop(0, count)
        def _(i):
            act(pl.multiple_of(i * 16, 16))

    @pl.when((step == 0) & (rows == SORTED))
    def _():
        for s in range(2):
            live = pl.multiple_of(offs_ref[sources[s], EXPERTS], 16)

            def clear(at, s=s, live=live):
                spot = pl.ds(pl.multiple_of(live + at, 16), 16)
                outs[s][spot, :] = jnp.zeros((16, D), BF16)
                gxs[s][spot, :] = jnp.zeros((16, D), BF16)

            blocks((SORTED - live) // 16, clear)

    if carried:
        acc_i[...] = before[0][0].astype(F32)
        acc_b[...] = before[1][0].astype(F32)
    else:
        acc_i[...] = jnp.zeros_like(acc_i)
        acc_b[...] = jnp.zeros_like(acc_b)

    places = []
    total = jnp.int32(0)
    for s in range(2):
        begin = pl.multiple_of(offs_ref[sources[s], expert], 16)
        size = offs_ref[sources[s], expert + 1] - begin
        places.append((begin, total, size // 16))

        def gather(at, s=s, begin=begin, total=total):
            here = pl.ds(pl.multiple_of(begin + at, 16), 16)
            there = pl.ds(pl.multiple_of(total + at, 16), 16)
            xm[there, :] = xs[s][0, here, :]
            gm[there, :] = gs[s][0, here, :]

        blocks(size // 16, gather)
        total = total + size
    span = pl.multiple_of(total, 16)

    def blank(at):
        there = pl.ds(pl.multiple_of(span + at, 16), 16)
        xm[there, :] = jnp.zeros((16, D), BF16)
        gm[there, :] = jnp.zeros((16, D), BF16)

    blocks((256 - span % 256) // 16, blank)
    weight_copies(expert, slot, False)
    w_in, w_back = wi.at[slot], wb.at[slot]

    @pl.loop(0, (span + 255) // 256)
    def _(i):
        spot = pl.ds(pl.multiple_of(i * 256, 256), 256)
        x, g = xm[spot, :], gm[spot, :]
        inner = dot(x, w_in[...])
        hidden, slope = gelu_both(inner)
        hidden = hidden.astype(BF16)
        grad_hidden = dot(g, w_back[...], CONTRACT_LANES).astype(BF16)
        grad_inner = (grad_hidden.astype(F32) * slope).astype(BF16)
        xm[spot, :] = dot(hidden, w_back[...]).astype(BF16)
        gm[spot, :] = dot(grad_inner, w_in[...], CONTRACT_LANES).astype(BF16)
        acc_b[...] += dot(hidden, g, CONTRACT_ROWS)
        acc_i[...] += dot(x, grad_inner, CONTRACT_ROWS)

    if cut:
        y = lax.axis_index("batch") % 2
        for i, acc in enumerate((acc_i, acc_b)):
            for z in range(4):
                for ref, column in ((dwi_ref, 1 - y), (dwb_ref, y)):
                    part = pl.ds(pl.multiple_of((z * 2 + column) * CHUNK, 16), CHUNK)
                    ref[i, z] = acc[part, :].astype(BF16)
    else:
        dwi_ref[0] = acc_i[...].astype(BF16)
        dwb_ref[0] = acc_b[...].astype(BF16)
    if joined:

        @pl.when(step == 0)
        def _():
            for copy in join_copies():
                copy.wait()

    for s in range(2):
        begin, base, blocks_of = places[s]

        def hand_back(at, s=s, begin=begin, base=base):
            here = pl.ds(pl.multiple_of(begin + at, 16), 16)
            there = pl.ds(pl.multiple_of(base + at, 16), 16)
            outs[s][here, :] = xm[there, :]
            gxs[s][here, :] = gm[there, :]

        blocks(blocks_of, hand_back)


def experts(
    sources, offs, group_map, x, g, wi, wb, before=None, earlier=None, first=0, count=EXPERTS, cut=False
):
    rows = HEAD if cut else SORTED
    whole = once((rows, D))
    any_space = pl.BlockSpec(memory_space=pl.ANY)
    carried, joined = before is not None, earlier is not None
    out = jax.ShapeDtypeStruct((rows, D), BF16)

    def source(i):
        return pl.BlockSpec((1, rows, D), lambda e, *_: (i, 0, 0), pipeline_mode=pl.Buffered(1))

    carry = pl.BlockSpec((1, D, FF_DEV), lambda e, *_: (first + e, 0, 0))
    if cut:
        weight = once((2, 4, CHUNK, D))
        grad = jax.ShapeDtypeStruct((2, 4, CHUNK, D), BF16)
    else:
        weight = pl.BlockSpec((1, D, FF_DEV), lambda e, *_: (e, 0, 0))
        grad = jax.ShapeDtypeStruct((count, D, FF_DEV), BF16)
    picked = [source(i) for i in sources]
    kernel = functools.partial(
        expert_kernel, sources, first, count, rows, carried, joined, cut, group_map.shape[0]
    )
    return pl.pallas_call(
        kernel,
        grid_spec=pltpu.PrefetchScalarGridSpec(
            num_scalar_prefetch=2,
            grid=(count,),
            in_specs=picked
            + picked
            + [any_space] * 2
            + [carry] * (2 * carried)
            + [any_space] * (4 * joined),
            out_specs=[whole] * 4 + [weight] * 2,
            scratch_shapes=[
                pltpu.VMEM((MERGED, D), BF16),
                pltpu.VMEM((MERGED, D), BF16),
                pltpu.VMEM((2, D, FF_DEV), BF16),
                pltpu.VMEM((2, FF_DEV, D), BF16),
                pltpu.VMEM((D, FF_DEV), F32),
                pltpu.VMEM((FF_DEV, D), F32),
                pltpu.SMEM((2 * EXPERTS,), I32),
                pltpu.SemaphoreType.DMA((2, 2, 2)),
                pltpu.SemaphoreType.DMA((4,)),
            ],
        ),
        out_shape=(out,) * 4 + (grad,) * 2,
        compiler_params=params(),
        cost_estimate=cost(8 * count * SORTED * D * FF_DEV, 16 * SORTED * D),
        name="experts",
    )(offs, group_map, x, x, g, g, wi, wb, *(before or ()), *(earlier or ()))


def swap(rows, bit):
    pairs = [(f, f ^ bit) for f in range(4)]
    return lax.ppermute(rows, "ffn", pairs)


def tie(value, *others):
    return lax.optimization_barrier((value, *others))[0]


class Wire:
    def __init__(self, send_sems, recv_sems):
        self.send_sems, self.recv_sems, self.used = send_sems, recv_sems, 0

    def send(self, src, dst, device):
        number = self.used
        self.used += 1
        copy = pltpu.make_async_remote_copy(
            src_ref=src,
            dst_ref=dst,
            send_sem=self.send_sems.at[number],
            recv_sem=self.recv_sems.at[number],
            device_id=device,
            device_id_type=MESH,
        )
        copy.start()
        return copy


class Mover:
    def __init__(self, sems):
        self.sems, self.used = sems, 0

    def go(self, src, dst):
        number = self.used
        self.used += 1
        copy = pltpu.make_async_copy(src, dst, self.sems.at[number])
        copy.start()
        return copy


def greet(peers):
    barrier = pltpu.get_barrier_semaphore()
    for device in peers:
        pl.semaphore_signal(barrier, inc=1, device_id=device, device_id_type=MESH)
    pl.semaphore_wait(barrier, len(peers))


def wait_all(copies):
    for copy in copies:
        copy.wait()


def token_tiles():
    for i in range(3):
        yield slice(TILE * i, min(TILE * (i + 1), TOK_DEV))


def unsort(pos_col, src):
    want = lax.broadcasted_iota(I32, (pos_col.shape[0], SORTED), 1)
    hot = jnp.where(pos_col == want, 1.0, 0.0).astype(BF16)
    return dot(hot, src)


def attend_back_pair(pair, length, qkv_ref, gctx_ref, lse_ref, out_ref):
    start, skip = window(pair)
    start = pl.multiple_of(start, 16)
    row = lax.broadcasted_iota(I32, (WIN, 1), 0)
    mine = (row >= skip) & (row < skip + SEQ_LEN)
    bias = jnp.where((row >= skip) & (row < skip + PATCHES + length), 0.0, -1e30)
    lane = lax.broadcasted_iota(I32, (WIN, 128), 1)
    scale = jnp.asarray(HEAD_DIM**-0.5, BF16)
    @pl.loop(0, HEADS // 2)
    def _(hp):
        spots = [head_cols(hp, part) for part in range(3)]
        q, k, v = [qkv_ref[pl.ds(start, WIN), spot] for spot in spots]
        none = jnp.zeros_like(q)
        q = jnp.where(mine, q * scale, none)
        ks = k * scale
        go = jnp.where(mine, gctx_ref[pl.ds(start, WIN), spots[0]], none)
        low = lane < 64
        both_q = jnp.concatenate([jnp.where(low, q, none), jnp.where(low, none, q)], axis=0)
        both_go = jnp.concatenate([jnp.where(low, go, none), jnp.where(low, none, go)], axis=0)
        log_total = jnp.concatenate(
            [lse_ref[pair, pl.ds(hp * 2 + half, 1), 0:WIN] for half in range(2)], axis=1
        )
        probs = jnp.exp(dot(k, both_q, CONTRACT_LANES) + bias - log_total)
        grad_probs = dot(v, both_go, CONTRACT_LANES)
        delta = jnp.sum(probs * grad_probs, axis=0, keepdims=True)
        grad_scores = (probs * (grad_probs - delta)).astype(BF16)
        grad_v = dot(probs.astype(BF16), both_go)
        grad_k = dot(grad_scores, both_q)
        turned = dot(grad_scores, ks, CONTRACT_ROWS)
        grad_q = jnp.where(low, turned[0:WIN], turned[WIN : 2 * WIN])
        for spot, new in zip(spots, (grad_q, grad_k, grad_v)):
            old = out_ref[pl.ds(start, WIN), spot]
            out_ref[pl.ds(start, WIN), spot] = jnp.where(mine, new.astype(BF16), old)


TURNS = (2, 3, 1, 0)


def rear_kernel(
    small,
    len_ref,
    pos_ref,
    gain_one_ref,
    gain_two_ref,
    w_ref,
    lse_ref,
    gx0_hbm,
    gx1_hbm,
    gx2_hbm,
    mid_hbm,
    cot_hbm,
    ctx_hbm,
    qkv_hbm,
    tok_hbm,
    out1_hbm,
    out2_hbm,
    out3_hbm,
    dwi_hbm,
    dwb_hbm,
    first_came,
    first_own,
    gm_hbm,
    gq_hbm,
    dwq_hbm,
    dwp_hbm,
    dg_ref,
    share_hbm,
    near_hbm,
    far_hbm,
    wide,
    mid,
    cot,
    ctx,
    gctx,
    qkv,
    half_a,
    half_b,
    own_rows,
    came_y,
    came_z,
    acc,
    dwp,
    local_sems,
    send_sems,
    recv_sems,
    z_send,
    z_recv,
):
    batch, ffn = lax.axis_index("batch"), lax.axis_index("ffn")
    z, y = batch // 2, batch % 2
    near, far, across = (batch, ffn ^ 1), (batch, ffn ^ 2), (batch ^ 1, ffn)
    along = {k: (batch ^ (2 * k), ffn) for k in (1, 2, 3)}
    greet([near, far] + ([across] + list(along.values()) if small else []))
    wire, mover = Wire(send_sems, recv_sems), Mover(local_sems)

    parts_near = wire.send(gx1_hbm, wide.at[:, D : 2 * D], near)
    near_sent = wire.send(out3_hbm, half_b, near)
    half_in = mover.go(out2_hbm, half_a)
    over_y = {}
    own_in = {}
    if small:
        for turn in TURNS:
            there = pl.ds(pl.multiple_of(((z ^ turn) * 2 + 1 - y) * CHUNK, 16), CHUNK)
            over_y[turn] = [
                wire.send(grad.at[:, there, :], came_y.at[turn, i, 1:EXPERTS], across)
                for i, grad in enumerate((dwi_hbm, dwb_hbm))
            ]
    first_in = {}
    if small:
        for turn in TURNS:
            first_in[turn] = [
                mover.go(first_came.at[:, z ^ turn], came_y.at[turn, :, 0]),
                mover.go(first_own.at[:, z ^ turn], own_rows.at[turn, :, 0]),
            ]
    parts_in = [
        mover.go(part, wide.at[:, i * D : i * D + D])
        for i, part in ((0, gx0_hbm), (2, gx2_hbm))
    ]
    rows_in = [mover.go(mid_hbm, mid), mover.go(cot_hbm, cot), mover.go(ctx_hbm, ctx)]
    qkv_in = mover.go(qkv_hbm, qkv)
    if small:
        for turn in TURNS:
            here = pl.ds(pl.multiple_of(((z ^ turn) * 2 + y) * CHUNK, 16), CHUNK)
            own_in[turn] = [
                mover.go(grad.at[:, here, :], own_rows.at[turn, i, 1:EXPERTS])
                for i, grad in enumerate((dwi_hbm, dwb_hbm))
            ]
    sent = [wire.send(out1_hbm, near_hbm, near)]
    stored = []

    def z_copy(turn, i):
        return pltpu.make_async_remote_copy(
            src_ref=came_y.at[turn, i, 1:EXPERTS],
            dst_ref=came_z.at[turn - 1, i, 1:EXPERTS],
            send_sem=z_send.at[turn - 1, i],
            recv_sem=z_recv.at[turn - 1, i],
            device_id=along[turn],
            device_id_type=MESH,
        )

    def take_turn(turn, i):
        if not small:
            return
        over_y[turn][i].wait()
        own_in[turn][i].wait()
        for e in range(1, EXPERTS):
            came_y[turn, i, e] = (
                came_y[turn, i, e].astype(F32) + own_rows[turn, i, e].astype(F32)
            ).astype(BF16)
        if turn:
            z_copy(turn, i).start()

    first_z = []
    if small:
        for turn in TURNS:
            wait_all(first_in[turn])
            for i in range(2):
                came_y[turn, i, 0] = (
                    came_y[turn, i, 0].astype(F32) + own_rows[turn, i, 0].astype(F32)
                ).astype(BF16)
            if turn:
                first_z.append(
                    wire.send(came_y.at[turn, :, 0], came_z.at[turn - 1, :, 0], along[turn])
                )
    wait_all(parts_in + rows_in + [parts_near])
    top = 0
    for size in SORT_TILES:
        rows = slice(top, top + size)
        wide[rows, 0:D] = (
            wide[rows, 0:D].astype(F32)
            + wide[rows, D : 2 * D].astype(F32)
            + wide[rows, 2 * D : 3 * D].astype(F32)
        ).astype(BF16)
        top += size
    half_in.wait()
    near_sent.wait()
    half_a[...] = (half_a[...].astype(F32) + half_b[...].astype(F32)).astype(BF16)
    sent.append(wire.send(half_a, far_hbm, far))

    gctx[1552:ROWS, :] = jnp.zeros((ROWS - 1552, D), BF16)
    grad_gain = jnp.zeros((1, D), F32)
    for i, rows in enumerate(token_tiles()):
        grad_normed = unsort(pos_ref[rows, 0:1], wide[:, 0:D])
        normal, inverse = norm_parts(mid[rows, :])
        grad_gain = grad_gain + jnp.sum(grad_normed * normal, axis=0, keepdims=True)
        part = norm_pull(grad_normed, gain_two_ref[...].reshape(1, D), normal, inverse)
        grad_middle = cot[rows, :].astype(F32) + part
        mid[rows, :] = grad_middle
        low = grad_middle.astype(BF16)
        product = dot(ctx[rows, :], low, CONTRACT_ROWS)
        if i == 0:
            acc[...] = product
        elif i == 1:
            acc[...] += product
        else:
            dwp[...] = (acc[...] + product).astype(BF16)
        gctx[rows, :] = dot(low, w_ref[...], CONTRACT_LANES).astype(BF16)
        if i == 1:
            take_turn(2, 0)
            take_turn(2, 1)
    dg_ref[...] = grad_gain
    stored.append(mover.go(mid, gm_hbm))
    stored.append(mover.go(dwp, dwp_hbm))
    tok_in = mover.go(tok_hbm, cot)
    wide[1552:SORTED, :] = jnp.zeros((SORTED - 1552, 3 * D), BF16)
    qkv_in.wait()
    take_turn(3, 0)
    take_turn(3, 1)

    @pl.loop(0, SEQ_DEV)
    def _(pair):
        attend_back_pair(pair, len_ref[pair], qkv, gctx, lse_ref, wide)
        @pl.when(pair == 1)
        def _():
            take_turn(1, 0)
            take_turn(1, 1)

    stored.append(mover.go(wide.at[0:ROWS, :], gq_hbm))
    tok_in.wait()
    for rows in token_tiles():
        normal, _ = norm_parts(cot[rows, :].astype(F32))
        gctx[rows, :] = (normal * gain_one_ref[...].reshape(1, D)).astype(BF16)
    for i in range(3):
        part = slice(i * 256, i * 256 + 256)
        qkv[part, :] = dot(gctx[:, part], wide[0:ROWS, :], CONTRACT_ROWS).astype(BF16)
    stored.append(mover.go(qkv.at[0:D, :], dwq_hbm))
    if small:
        take_turn(0, 0)
        take_turn(0, 1)
        wait_all(first_z + [z_copy(turn, i) for turn in TURNS[:3] for i in range(2)])
        for i in range(2):
            for e in range(EXPERTS):
                total = came_y[0, i, e].astype(F32)
                for k in range(3):
                    total = total + came_z[k, i, e].astype(F32)
                came_y[0, i, e] = total.astype(BF16)
        stored.append(mover.go(came_y.at[0], share_hbm))
    wait_all(sent + stored)


def rear(small, lengths, pos_col, gain_one, gain_two, w_proj, lse, *arrays):
    vmem = pl.BlockSpec(memory_space=pltpu.VMEM)
    any_space = pl.BlockSpec(memory_space=pl.ANY)
    dma = pltpu.SemaphoreType.DMA
    copies = 15
    return pl.pallas_call(
        functools.partial(rear_kernel, small),
        out_shape=(
            jax.ShapeDtypeStruct((TOK_DEV, D), F32),
            jax.ShapeDtypeStruct((ROWS, 3 * D), BF16),
            jax.ShapeDtypeStruct((D, 3 * D), BF16),
            jax.ShapeDtypeStruct((D, D), BF16),
            jax.ShapeDtypeStruct((1, D), F32),
            jax.ShapeDtypeStruct((2, EXPERTS, CHUNK, D), BF16),
            jax.ShapeDtypeStruct((SORTED, D), BF16),
            jax.ShapeDtypeStruct((SORTED, D), BF16),
        ),
        in_specs=[pl.BlockSpec(memory_space=pltpu.SMEM)] + [vmem] * 5 + [any_space] * len(arrays),
        out_specs=(any_space,) * 4 + (vmem,) + (any_space,) * 3,
        scratch_shapes=[
            pltpu.VMEM((SORTED, 3 * D), BF16),
            pltpu.VMEM((TOK_DEV, D), F32),
            pltpu.VMEM((TOK_DEV, D), BF16),
            pltpu.VMEM((ROWS, D), BF16),
            pltpu.VMEM((ROWS, D), BF16),
            pltpu.VMEM((ROWS, 3 * D), BF16),
            pltpu.VMEM((SORTED, D), BF16),
            pltpu.VMEM((SORTED, D), BF16),
            pltpu.VMEM((4, 2, EXPERTS, CHUNK, D), BF16),
            pltpu.VMEM((4, 2, EXPERTS, CHUNK, D), BF16),
            pltpu.VMEM((3, 2, EXPERTS, CHUNK, D), BF16),
            pltpu.VMEM((D, D), F32),
            pltpu.VMEM((D, D), BF16),
            dma((32,)),
            dma((copies,)),
            dma((copies,)),
            dma((3, 2)),
            dma((3, 2)),
        ],
        compiler_params=params(collective_id=2, has_side_effects=True),
        name="rear",
    )(lengths, pos_col, gain_one, gain_two, w_proj, lse, *arrays)


ORDERS = (("x", "y", "z"), ("y", "x", "z")) * 2
WIDTHS = (1024, 1024, 512, 512)
LEFTS = (0, 1024, 2048, 2560)
SETS = ((0, 1), (2, 3))
WIDE = 4 * D
GAIN_ROWS = 8


def last_kernel(
    small,
    group_ref,
    pos_ref,
    gain_ref,
    w_ref,
    dg_two_ref,
    tok_hbm,
    gq_hbm,
    gm_hbm,
    mid_hbm,
    out0_hbm,
    out1_hbm,
    out2_hbm,
    dwq_hbm,
    dwp_hbm,
    share_hbm,
    ig_hbm,
    bo_hbm,
    sum_ref,
    gains_ref,
    pieces_ref,
    tok,
    gq,
    gm,
    mid,
    outs,
    share,
    stage,
    near_rows,
    held,
    came_z,
    came_xy,
    gain_in,
    local_sems,
    send_sems,
    recv_sems,
):
    batch, ffn = lax.axis_index("batch"), lax.axis_index("ffn")
    z, y, x, c = batch // 2, batch % 2, ffn // 2, ffn % 2
    place = {"x": x, "y": y, "z": z}
    mover = Mover(local_sems)

    def peer(axis, k=1):
        if axis == "c":
            return (batch, ffn ^ 1)
        if axis == "x":
            return (batch, ffn ^ 2)
        if axis == "y":
            return (batch ^ 1, ffn)
        return (batch ^ (2 * k), ffn)

    flying = ([], [])
    top = [0] * 4
    left = list(LEFTS)
    rows, cols = [384] * 4, list(WIDTHS)
    base = pl.multiple_of(c * 384, 16)
    if small:
        greet([peer("c"), peer("x")] + [(batch ^ j, ffn) for j in range(1, 8)])
        wire = Wire(send_sems, recv_sems)
        share_in = mover.go(share_hbm, share)
        give = pl.ds(pl.multiple_of((1 - c) * 384, 16), 384)
        keep = pl.ds(base, 384)
        pieces = (
            ((dwq_hbm, 0, 2048, 0),),
            ((dwq_hbm, 2048, 256, 2048), (dwp_hbm, 0, D, 3 * D)),
        )
        to_core, kept = [[], []], [[], []]
        for which in range(2):
            for ref, start, size, at in pieces[which]:
                lanes, spot = pl.ds(start, size), pl.ds(at, size)
                to_core[which].append(
                    wire.send(ref.at[give, lanes], near_rows.at[:, spot], peer("c"))
                )
                kept[which].append(mover.go(ref.at[keep, lanes], held.at[:, spot]))
    loads = [mover.go(tok_hbm, tok), mover.go(gq_hbm, gq), mover.go(gm_hbm, gm)]
    later = [mover.go(mid_hbm, mid)] + [
        mover.go(part, outs.at[i]) for i, part in enumerate((out0_hbm, out1_hbm, out2_hbm))
    ]
    handed = []

    def hand_out(i, *turns):
        for j in turns:
            handed.append(
                wire.send(stage.at[j, i], pieces_ref.at[batch, i], (batch ^ j, ffn))
            )

    if small:
        share_in.wait()
        for j in range(8):
            expert = group_ref[batch ^ j]
            for i in range(2):
                stage[j, i] = share[i, expert]
        hand_out(0, 4, 6, 5, 2)
        pieces_ref[batch] = stage[0]

    def core_done(which):
        wait_all(to_core[which] + kept[which])
        for i in SETS[which]:
            lanes = slice(LEFTS[i], LEFTS[i] + WIDTHS[i])
            held[:, lanes] = (
                held[:, lanes].astype(F32) + near_rows[:, lanes].astype(F32)
            ).astype(BF16)

    def sum_go(which, step):
        for i in SETS[which]:
            axis = ORDERS[i][step]
            quarter = WIDTHS[i] // 4
            if axis == "z":
                live = pl.ds(top[i], rows[i])
                for k in (2, 3, 1):
                    there = pl.ds(pl.multiple_of(left[i] + (z ^ k) * quarter, 128), quarter)
                    flying[which].append(
                        wire.send(
                            held.at[live, there],
                            came_z.at[i, k - 1, 0 : rows[i], 0:quarter],
                            peer("z", k),
                        )
                    )
            else:
                half = rows[i] // 2
                there = pl.ds(pl.multiple_of(top[i] + (1 - place[axis]) * half, 16), half)
                flying[which].append(
                    wire.send(
                        held.at[there, pl.ds(left[i], cols[i])],
                        came_xy.at[i, 0 if axis == "x" else 1, 0:half, 0 : cols[i]],
                        peer(axis),
                    )
                )

    def sum_done(which, step):
        wait_all(flying[which])
        flying[which].clear()
        for i in SETS[which]:
            axis = ORDERS[i][step]
            if axis == "z":
                cols[i] = WIDTHS[i] // 4
                left[i] = pl.multiple_of(left[i] + z * cols[i], 128)
                terms = [came_z[i, k, 0 : rows[i], 0 : cols[i]] for k in range(3)]
            else:
                rows[i] = rows[i] // 2
                top[i] = pl.multiple_of(top[i] + place[axis] * rows[i], 16)
                terms = [came_xy[i, 0 if axis == "x" else 1, 0 : rows[i], 0 : cols[i]]]
            spot = (pl.ds(top[i], rows[i]), pl.ds(left[i], cols[i]))
            total = held[spot].astype(F32)
            for term in terms:
                total = total + term.astype(F32)
            held[spot] = total.astype(BF16)
            if step == 2:
                lines = pl.ds(pl.multiple_of(base + top[i], 16), rows[i])
                sum_ref[lines, spot[1]] = total.astype(BF16)

    def spread_go(which, step):
        for i in SETS[which]:
            axis = ORDERS[i][step]
            mine = sum_ref.at[
                pl.ds(pl.multiple_of(base + top[i], 16), rows[i]), pl.ds(left[i], cols[i])
            ]
            for k in (2, 3, 1) if axis == "z" else (1,):
                flying[which].append(wire.send(mine, mine, peer(axis, k)))

    def spread_done(which, step):
        wait_all(flying[which])
        flying[which].clear()
        for i in SETS[which]:
            axis = ORDERS[i][step]
            if axis == "z":
                left[i] = LEFTS[i]
                cols[i] = WIDTHS[i]
            else:
                top[i] = top[i] - place[axis] * rows[i]
                rows[i] = rows[i] * 2

    def core_go(which):
        size = 2 * WIDTHS[SETS[which][0]]
        mine = sum_ref.at[pl.ds(base, 384), pl.ds(LEFTS[SETS[which][0]], size)]
        flying[which].append(wire.send(mine, mine, peer("c")))

    def gains_go(axis, slot):
        for k in (1, 2, 3) if axis == "z" else (1,):
            flying[0].append(wire.send(gains_ref, gain_in.at[slot + k - 1], peer(axis, k)))

    def gains_done(axis, slot):
        total = gains_ref[...]
        for k in (0, 1, 2) if axis == "z" else (0,):
            total = total + gain_in[slot + k]
        gains_ref[...] = total

    tiles = list(token_tiles())
    grad_gain = jnp.zeros((1, D), F32)
    stored = []

    def first_back(part):
        normal, inverse = norm_parts(tok[part, :].astype(F32))
        grad_normed = dot(gq[part, :], w_ref[...], CONTRACT_LANES)
        gain_part = jnp.sum(grad_normed * normal, axis=0, keepdims=True)
        pulled = norm_pull(grad_normed, gain_ref[...].reshape(1, D), normal, inverse)
        gm[part, :] = gm[part, :] + pulled
        stored.append(mover.go(gm.at[part], ig_hbm.at[part]))
        return gain_part

    def finish(part):
        mid[part, :] = mid[part, :] + unsort(pos_ref[part, 0:1], outs[0])
        stored.append(mover.go(mid.at[part], bo_hbm.at[part]))

    def finish_sums():
        wait_all(later)
        at = 0
        for size in SORT_TILES:
            part = slice(at, at + size)
            outs[0, part] = (
                outs[0, part].astype(F32) + outs[1, part].astype(F32) + outs[2, part].astype(F32)
            ).astype(BF16)
            at += size

    if small:
        for which in range(2):
            core_done(which)
            sum_go(which, 0)
    wait_all(loads)
    grad_gain = grad_gain + first_back(tiles[0])
    grad_gain = grad_gain + first_back(tiles[1])
    if small:
        for which in range(2):
            sum_done(which, 0)
            sum_go(which, 1)
    grad_gain = grad_gain + first_back(tiles[2])
    gains_ref[0:1, :] = grad_gain
    gains_ref[1:2, :] = dg_two_ref[...]
    gains_ref[2:GAIN_ROWS, :] = jnp.zeros((GAIN_ROWS - 2, D), F32)
    if small:
        gains_go("c", 0)
        for which in range(2):
            sum_done(which, 1)
            if which == 0:
                gains_done("c", 0)
                gains_go("x", 1)
            sum_go(which, 2)
    finish_sums()
    if small:
        for which in range(2):
            sum_done(which, 2)
            if which == 0:
                gains_done("x", 1)
                gains_go("y", 2)
            spread_go(which, 2)
    finish(tiles[0])
    finish(tiles[1])
    if small:
        for which in range(2):
            spread_done(which, 2)
            if which == 0:
                gains_done("y", 2)
                gains_go("z", 3)
            spread_go(which, 1)
        hand_out(0, 7, 3, 1)
        hand_out(1, 4, 6, 5, 7, 2, 3, 1)
    finish(tiles[2])
    if small:
        for which in range(2):
            spread_done(which, 1)
            if which == 0:
                gains_done("z", 3)
            spread_go(which, 0)
        for which in range(2):
            spread_done(which, 0)
            core_go(which)
        wait_all(flying[0] + flying[1] + handed)
    wait_all(stored)


def last(small, group_map, pos_col, gain_one, w_qkv, dg_two, *arrays):
    vmem = pl.BlockSpec(memory_space=pltpu.VMEM)
    any_space = pl.BlockSpec(memory_space=pl.ANY)
    dma = pltpu.SemaphoreType.DMA
    copies = 3 + 14 + 20 + 20 + 6 + 2
    extra = dict(collective_id=3, has_side_effects=True) if small else {}
    return pl.pallas_call(
        functools.partial(last_kernel, small),
        out_shape=(
            jax.ShapeDtypeStruct((TOK_DEV, D), F32),
            jax.ShapeDtypeStruct((TOK_DEV, D), F32),
            jax.ShapeDtypeStruct((D, WIDE), BF16),
            jax.ShapeDtypeStruct((GAIN_ROWS, D), F32),
            jax.ShapeDtypeStruct((8, 2, CHUNK, D), BF16),
        ),
        in_specs=[pl.BlockSpec(memory_space=pltpu.SMEM)] + [vmem] * 4 + [any_space] * len(arrays),
        out_specs=(any_space,) * 2 + (vmem,) * 3,
        scratch_shapes=[
            pltpu.VMEM((TOK_DEV, D), BF16),
            pltpu.VMEM((ROWS, 3 * D), BF16),
            pltpu.VMEM((TOK_DEV, D), F32),
            pltpu.VMEM((TOK_DEV, D), F32),
            pltpu.VMEM((3, SORTED, D), BF16),
            pltpu.VMEM((2, EXPERTS, CHUNK, D), BF16),
            pltpu.VMEM((8, 2, CHUNK, D), BF16),
            pltpu.VMEM((384, WIDE), BF16),
            pltpu.VMEM((384, WIDE), BF16),
            pltpu.VMEM((4, 3, 96, 256), BF16),
            pltpu.VMEM((4, 2, 192, 1024), BF16),
            pltpu.VMEM((6, GAIN_ROWS, D), F32),
            dma((20,)),
            dma((copies,)),
            dma((copies,)),
        ],
        compiler_params=params(**extra),
        name="last",
    )(group_map, pos_col, gain_one, w_qkv, dg_two, *arrays)


def close_kernel(
    sum_ref, gains_ref, pieces_ref, ig_ref, bo_ref, *outs
):
    qkv_ref, proj_ref, one_ref, two_ref, wi_ref, wb_ref, ig_out, bo_out = outs
    qkv_ref[...] = sum_ref[:, 0 : 3 * D].astype(F32)
    proj_ref[...] = sum_ref[:, 3 * D : WIDE].astype(F32)
    one_ref[...] = gains_ref[0:1, :].reshape(D)
    two_ref[...] = gains_ref[1:2, :].reshape(D)
    wi_ref[0] = pieces_ref[0, 0].astype(F32)
    wb_ref[0] = pieces_ref[0, 1].astype(F32)
    ig_out[...] = ig_ref[...]
    bo_out[...] = bo_ref[...]


def close(summed, gains, pieces, input_grad, block_out):
    row = pl.BlockSpec((CHUNK, D), lambda i: (i, 0))
    tokens = pl.BlockSpec((200, D), lambda i: (i, 0))
    weight = pl.BlockSpec((1, CHUNK, D), lambda i: (0, i, 0))
    rows = jax.ShapeDtypeStruct((TOK_DEV, D), F32)
    return pl.pallas_call(
        close_kernel,
        grid=(8,),
        out_shape=(
            jax.ShapeDtypeStruct((D, 3 * D), F32),
            jax.ShapeDtypeStruct((D, D), F32),
            jax.ShapeDtypeStruct((D,), F32),
            jax.ShapeDtypeStruct((D,), F32),
            jax.ShapeDtypeStruct((1, D, D), F32),
            jax.ShapeDtypeStruct((1, D, D), F32),
            rows,
            rows,
        ),
        in_specs=[
            pl.BlockSpec((CHUNK, WIDE), lambda i: (i, 0)),
            full((GAIN_ROWS, D)),
            pl.BlockSpec((1, 2, CHUNK, D), lambda i: (i, 0, 0, 0)),
            tokens,
            tokens,
        ],
        out_specs=(
            pl.BlockSpec((CHUNK, 3 * D), lambda i: (i, 0)),
            row,
            full((D,)),
            full((D,)),
            weight,
            weight,
            tokens,
            tokens,
        ),
        compiler_params=params(),
        name="close",
    )(summed, gains, pieces, input_grad, block_out)


def body(
    tokens,
    text_lengths,
    routes,
    group_map,
    gain_one,
    w_qkv,
    w_proj,
    gain_two,
    w_in,
    w_back,
    cotangent,
):
    n_batch = lax.axis_size("batch")
    own = lax.axis_index("batch")
    small = n_batch == 8
    routes_row = jnp.pad(routes.reshape(1, TOK_DEV), ((0, 0), (0, LANES - TOK_DEV)))
    qkv, context, lse, middle, g, x, wi_all, wb_all, offs, pos_col = front(
        small,
        text_lengths,
        group_map,
        routes_row,
        tokens,
        cotangent,
        gain_one,
        w_qkv,
        w_proj,
        gain_two,
        w_in,
        w_back,
    )
    if not small:
        own_expert = group_map[own]
        order = jnp.arange(n_batch, dtype=I32)
        rank = jnp.sum(jnp.where((group_map == own_expert) & (order < own), 1, 0))
        part = jnp.minimum(rank, 1)
        wi_part = lax.dynamic_slice(w_in[0], (0, part * HALF), (D, HALF))
        wb_part = lax.dynamic_slice(w_back[0], (part * HALF, 0), (HALF, D))
        wi_all = lax.all_gather(wi_part, "batch", axis=0)
        wb_all = lax.all_gather(wb_part, "batch", axis=0)

    def run(pair, x, *rest, **more):
        return experts(pair, offs, group_map, x, g, wi_all, wb_all, *rest, **more)

    def add(a, b):
        return (a.astype(F32) + b.astype(F32)).astype(BF16)

    out2, out3, gx2, gx3, dwi, dwb = run((2, 3), x)
    gx_half = add(gx2, swap(gx3, 1))
    gx_far = swap(gx_half, 2)
    x = tie(x, gx_half)
    if small:
        *earlier, going, staying = run((0, 1), x, (dwi, dwb), count=1, cut=True)
        came = lax.ppermute(going, "batch", [(b, b ^ 1) for b in range(8)])
        out0, out1, gx0, gx1, dwi, dwb = run((0, 1), x, (dwi, dwb), earlier, first=1, count=2)
    else:
        out0, out1, gx0, gx1, dwi, dwb = run((0, 1), x, (dwi, dwb))
        came = staying = jnp.zeros((2, 4, CHUNK, D), BF16)
    grad_middle, grad_qkv, dw_qkv, dw_proj, dg_two, share, out_near, out_far = rear(
        small,
        text_lengths,
        pos_col,
        gain_one,
        gain_two,
        w_proj,
        lse,
        gx0,
        gx1,
        gx_far,
        middle,
        cotangent,
        context,
        qkv,
        tokens,
        out1,
        out2,
        out3,
        dwi,
        dwb,
        came,
        staying,
    )
    input_grad, block_out, summed, gains, pieces = last(
        small,
        group_map,
        pos_col,
        gain_one,
        w_qkv,
        dg_two,
        tokens,
        grad_qkv,
        grad_middle,
        middle,
        out0,
        out_near,
        out_far,
        dw_qkv,
        dw_proj,
        share,
    )
    if small:
        summed_qkv, summed_proj, gain_a, gain_b, grad_w_in, grad_w_back, input_grad, block_out = close(
            summed, gains, pieces, input_grad, block_out
        )
        gains = (gain_a, gain_b)
    else:

        def settle_any(grad):
            share = lax.psum_scatter(grad, "batch", scatter_dimension=1, tiled=True)
            whole = lax.all_gather(share, "batch", axis=1, tiled=True)
            return lax.dynamic_index_in_dim(whole, own_expert, 0, keepdims=True).astype(F32)

        grad_w_in = settle_any(dwi)
        grad_w_back = settle_any(dwb)
        summed_qkv, summed_proj = lax.psum((dw_qkv, dw_proj), ("batch", "ffn"))
        gains = lax.psum(gains, ("batch", "ffn"))
    return (
        block_out,
        input_grad,
        gains[0],
        summed_qkv.astype(F32),
        summed_proj.astype(F32),
        gains[1],
        grad_w_in,
        grad_w_back,
    )


def solution(mesh):
    placed = (
        P(("batch", "ffn"), None),
        P(("batch", "ffn")),
        P(("batch", "ffn"), None),
        P(),
        P(),
        P(),
        P(),
        P(),
        P("batch", None, "ffn"),
        P("batch", "ffn", None),
        P(("batch", "ffn"), None),
    )
    return jax.shard_map(
        body,
        mesh=mesh,
        in_specs=placed,
        out_specs=(
            P(("batch", "ffn"), None),
            P(("batch", "ffn"), None),
            P(),
            P(),
            P(),
            P(),
            P("batch", None, "ffn"),
            P("batch", "ffn", None),
        ),
        check_vma=False,
    )
```
